32 devices in a mesh: fsdp: 2 (over x), ctx: 4 (over y, core), tp: 4 (over z).
Axes of the slice: x: 2, y: 2, z: 4, core: 2. Of those that a mesh axis runs over, the one named last changes fastest.
Arguments:
- hidden: float32 [2, 2048, 1280], P('fsdp', 'ctx'), may hold values from -96 to 96
- cotangent: float32 [2, 2048, 1280], P('fsdp', 'ctx'), may hold values from -6 to 6
- lengths: int32 [2], P('fsdp'), may hold values from 1024 to 2048, as said below
- query_weight: float32 [2, 1280, 1280], P(None, 'fsdp', 'tp'), may hold values from -0.25 to 0.25
- key_weight: float32 [2, 1280, 1280], P(None, 'fsdp', 'tp'), may hold values from -0.25 to 0.25
- value_weight: float32 [2, 1280, 1280], P(None, 'fsdp', 'tp'), may hold values from -0.15625 to 0.15625
- output_weight: float32 [2, 1280, 1280], P(None, 'tp', 'fsdp'), may hold values from -1 to 1
- inner_weight: float32 [2, 1280, 5120], P(None, 'fsdp', 'tp'), may hold values from -0.15625 to 0.15625
- outer_weight: float32 [2, 5120, 1280], P(None, 'tp', 'fsdp'), may hold values from -0.078125 to 0.078125
- query_bias: float32 [2, 1280], P(None, 'tp'), may hold values from -3 to 3
- value_bias: float32 [2, 1280], P(None, 'tp'), may hold values from -3 to 3
- inner_bias: float32 [2, 5120], P(None, 'tp'), may hold values from -3 to 3
- output_bias: float32 [2, 1280], P(None, 'fsdp'), may hold values from -3 to 3
- outer_bias: float32 [2, 1280], P(None, 'fsdp'), may hold values from -3 to 3
- first_gain: float32 [2, 1280], P(None, 'fsdp'), may hold values from 0.1 to 1.9
- first_shift: float32 [2, 1280], P(None, 'fsdp'), may hold values from -3 to 3
- second_gain: float32 [2, 1280], P(None, 'fsdp'), may hold values from 0.1 to 1.9
- second_shift: float32 [2, 1280], P(None, 'fsdp'), may hold values from -3 to 3
Outputs:
- output: float32 [2, 2048, 1280], P('fsdp', 'ctx')
- grad_hidden: float32 [2, 2048, 1280], P('fsdp', 'ctx')
- grad_query_weight: float32 [2, 1280, 1280], P(None, 'fsdp', 'tp')
- grad_key_weight: float32 [2, 1280, 1280], P(None, 'fsdp', 'tp')
- grad_value_weight: float32 [2, 1280, 1280], P(None, 'fsdp', 'tp')
- grad_output_weight: float32 [2, 1280, 1280], P(None, 'tp', 'fsdp')
- grad_inner_weight: float32 [2, 1280, 5120], P(None, 'fsdp', 'tp')
- grad_outer_weight: float32 [2, 5120, 1280], P(None, 'tp', 'fsdp')
- grad_query_bias: float32 [2, 1280], P(None, 'tp')
- grad_value_bias: float32 [2, 1280], P(None, 'tp')
- grad_inner_bias: float32 [2, 5120], P(None, 'tp')
- grad_output_bias: float32 [2, 1280], P(None, 'fsdp')
- grad_outer_bias: float32 [2, 1280], P(None, 'fsdp')
- grad_first_gain: float32 [2, 1280], P(None, 'fsdp')
- grad_first_shift: float32 [2, 1280], P(None, 'fsdp')
- grad_second_gain: float32 [2, 1280], P(None, 'fsdp')
- grad_second_shift: float32 [2, 1280], P(None, 'fsdp')
The draws below stay inside these ranges and needn't reach their ends.
Inputs may be any that keep to these rules, and one draw needn't show every extreme that they name: `lengths`: every clip has 1024 to 2048 valid frames, and some clip is full.
All inputs are finite; a program needn't handle non-finite values.
Results may differ from the reference program's by a relative error of at most 0.017.
The reference program's roundings to bfloat16 on the way count: a program that leaves them out, or rounds other values in their place, can miss the bound.
Values may be sent and summed in bfloat16 or wider, within the bound.
A program may use at most 256 MiB of HBM per device.

```python
import math
import jax
import jax.numpy as jnp
from jax import lax

D = 1280
HEADS = 16
HD = 80
FF = 5120
LAYERS = 2
FRAMES = 2048
CLIPS = 2


def draw_hidden(key, part):
    key_rows, key_cols, key_entries = jax.random.split(key, 3)
    row_scale = jnp.exp(jax.random.uniform(key_rows, (CLIPS, FRAMES, 1), jnp.float32, math.log(0.4), math.log(4.0)))
    col_scale = jnp.exp(jax.random.uniform(key_cols, (CLIPS, 1, D), jnp.float32, math.log(0.4), math.log(4.0)))
    entries = jnp.clip(jax.random.normal(key_entries, (CLIPS, FRAMES, D), jnp.float32), -6.0, 6.0)
    return (entries * row_scale * col_scale).astype(jnp.float32)


def draw_lengths(key, part):
    key_lengths, key_pick = jax.random.split(key, 2)
    drawn = jax.random.randint(key_lengths, (CLIPS,), FRAMES // 2, FRAMES + 1)
    chosen = jax.random.randint(key_pick, (), 0, CLIPS)
    return jnp.where(jnp.arange(CLIPS) == chosen, FRAMES, drawn).astype(jnp.int32)


def shard_levels(key, dims, cuts, smallest, high):
    factor_of, own = 1.0, jax.random.fold_in(key, 6)
    for axis_at, parts in cuts:
        draws = jnp.exp(jax.random.uniform(jax.random.fold_in(own, axis_at), (parts,), jnp.float32, smallest / len(cuts), high / len(cuts)))
        factor_of = factor_of * jnp.repeat(draws, dims[axis_at] // parts).reshape([-1 if axis == axis_at else 1 for axis in range(len(dims))])
    return factor_of


def noise(stream_key, extent, width, reach, pieces=(), dtype=jnp.bfloat16):
    result = width * jax.random.normal(stream_key, extent, jnp.float32)
    if pieces:
        result = result * shard_levels(stream_key, extent, pieces, -0.22, 0.18)
    return jnp.clip(result, -reach, reach).astype(dtype)


def setup_inputs(seed: int = 0) -> dict:
    keys = jax.random.split(jax.random.key(seed), 19)
    hidden = draw_hidden(jax.random.fold_in(keys[18], 71), 0)
    cotangent = noise(keys[1], (CLIPS, FRAMES, D), 1.0, 6.0, ((0, 2), (1, 4)), jnp.float32)
    lengths = draw_lengths(jax.random.fold_in(keys[18], 71), 0)
    query_weight = noise(keys[3], (LAYERS, D, D), (D // 2) ** -0.5, 0.25, ((1, 2), (2, 4)), jnp.float32)
    key_weight = noise(keys[4], (LAYERS, D, D), (D // 2) ** -0.5, 0.25, ((1, 2), (2, 4)), jnp.float32)
    value_weight = noise(keys[5], (LAYERS, D, D), D ** -0.5, 0.15625, ((1, 2), (2, 4)), jnp.float32)
    output_weight = noise(keys[6], (LAYERS, D, D), (D // 32) ** -0.5, 1.0, ((1, 4), (2, 2)), jnp.float32)
    inner_weight = noise(keys[7], (LAYERS, D, FF), D ** -0.5, 0.15625, ((1, 2), (2, 4)), jnp.float32)
    outer_weight = noise(keys[8], (LAYERS, FF, D), FF ** -0.5, 0.078125, ((1, 4), (2, 2)), jnp.float32)
    query_bias = noise(keys[9], (LAYERS, D), 0.5, 3.0, ((1, 4),), jnp.float32)
    value_bias = noise(keys[10], (LAYERS, D), 0.5, 3.0, ((1, 4),), jnp.float32)
    inner_bias = noise(keys[11], (LAYERS, FF), 0.5, 3.0, ((1, 4),), jnp.float32)
    output_bias = noise(keys[12], (LAYERS, D), 0.5, 3.0, ((1, 2),), jnp.float32)
    outer_bias = noise(keys[13], (LAYERS, D), 0.5, 3.0, ((1, 2),), jnp.float32)
    first_gain = jnp.clip(1.0 + 0.18 * jax.random.normal(keys[14], (LAYERS, D), jnp.float32), 0.1, 1.9)
    first_shift = noise(keys[15], (LAYERS, D), 0.5, 3.0, ((1, 2),), jnp.float32)
    second_gain = jnp.clip(1.0 + 0.18 * jax.random.normal(keys[16], (LAYERS, D), jnp.float32), 0.1, 1.9)
    second_shift = noise(keys[17], (LAYERS, D), 0.5, 3.0, ((1, 2),), jnp.float32)
    return {"hidden": hidden, "cotangent": cotangent, "lengths": lengths, "query_weight": query_weight, "key_weight": key_weight, "value_weight": value_weight, "output_weight": output_weight, "inner_weight": inner_weight, "outer_weight": outer_weight, "query_bias": query_bias, "value_bias": value_bias, "inner_bias": inner_bias, "output_bias": output_bias, "outer_bias": outer_bias, "first_gain": first_gain, "first_shift": first_shift, "second_gain": second_gain, "second_shift": second_shift}


@jax.custom_vjp
def low(v):
    return lax.optimization_barrier(v.astype(jnp.bfloat16)).astype(jnp.float32)

@jax.custom_vjp
def low_back(v):
    return v

def low_keep(v):
    return (low(v), None)

def low_pass(kept, grad):
    return (grad,)

def back_keep(v):
    return (v, None)

def back_low(kept, grad):
    return (low(grad),)
low.defvjp(low_keep, low_pass)
low_back.defvjp(back_keep, back_low)
EPSILON = 1e-05
NEGATIVE = -1e+30

def norm_parts(values):
    average = lax.optimization_barrier(jnp.mean(values, axis=-1, keepdims=True))
    centered = values - average
    spread = lax.optimization_barrier(jnp.mean(centered * centered, axis=-1, keepdims=True))
    return centered * lax.rsqrt(spread + EPSILON)

def gelu_exact(values):
    return 0.5 * values * (1.0 + lax.erf(values * (1.0 / math.sqrt(2.0))))

def rounded(values):
    return low(low_back(values))

def project(left_side, right_side):
    return jnp.einsum('bfd,de->bfe', left_side, right_side, precision=lax.Precision.HIGHEST)

def attend_one(packed):
    queries, key_rows, values, length = packed
    scores = jnp.dot(queries, key_rows.T, precision=lax.Precision.HIGHEST) * (1.0 / math.sqrt(HD))
    scores = low_back(scores)
    valid_keys = jnp.arange(FRAMES) < length
    scores = jnp.where(valid_keys[None, :], scores, NEGATIVE)
    highest = lax.optimization_barrier(jnp.max(scores, axis=-1, keepdims=True))
    raised = jnp.exp(scores - highest)
    weights_soft = raised / lax.optimization_barrier(jnp.sum(raised, axis=-1, keepdims=True))
    return jnp.dot(low(weights_soft), values, precision=lax.Precision.HIGHEST)

def split_heads(values, clip_count):
    return values.reshape(clip_count, FRAMES, HEADS, HD).transpose(0, 2, 1, 3).reshape(clip_count * HEADS, FRAMES, HD)

def merge_heads(values, clip_count):
    return values.reshape(clip_count, HEADS, FRAMES, HD).transpose(0, 2, 1, 3).reshape(clip_count, FRAMES, HEADS * HD)

def one_layer(hidden, lengths, query_weight, key_weight, value_weight, output_weight, inner_weight, outer_weight, query_bias, value_bias, inner_bias, output_bias, outer_bias, first_gain, first_shift, second_gain, second_shift):
    clip_count = hidden.shape[0]
    normed = low(norm_parts(hidden) * low(first_gain) + low(first_shift))
    queries = rounded(project(normed, low(query_weight)) + query_bias)
    key_rows = rounded(project(normed, low(key_weight)))
    values = rounded(project(normed, low(value_weight)) + value_bias)
    lengths_rep = jnp.repeat(lengths, HEADS)
    attended = lax.map(jax.checkpoint(attend_one), (split_heads(queries, clip_count), split_heads(key_rows, clip_count), split_heads(values, clip_count), lengths_rep))
    attended = rounded(merge_heads(attended, clip_count))
    middle = hidden + low_back(project(attended, low(output_weight))) + low(output_bias)
    normed_two = low(norm_parts(middle) * low(second_gain) + low(second_shift))
    inner_pre = low_back(project(normed_two, low(inner_weight)) + inner_bias)
    active = low(gelu_exact(inner_pre))
    return middle + low_back(project(active, low(outer_weight))) + low(outer_bias)

def reference(hidden, cotangent, lengths, query_weight, key_weight, value_weight, output_weight, inner_weight, outer_weight, query_bias, value_bias, inner_bias, output_bias, outer_bias, first_gain, first_shift, second_gain, second_shift):
    parameters = (query_weight, key_weight, value_weight, output_weight, inner_weight, outer_weight, query_bias, value_bias, inner_bias, output_bias, outer_bias, first_gain, first_shift, second_gain, second_shift)

    def forward(residual, *layer_params):
        for layer_index in range(LAYERS):
            residual = one_layer(residual, lengths, *[member[layer_index] for member in layer_params])
        return residual
    output, pullback = jax.vjp(forward, hidden, *parameters)
    gradients = pullback(cotangent)
    return (output, gradients[0], gradients[1], gradients[2], gradients[3], gradients[4], gradients[5], gradients[6], gradients[7], gradients[8], gradients[9], gradients[10], gradients[11], gradients[12], gradients[13], gradients[14], gradients[15])
```

```python
import math

import jax
import jax.numpy as jnp
from jax import lax
from jax.sharding import PartitionSpec as P

HD = 80
LAYERS = 2


EPSILON = 1e-05
NEGATIVE = -1e30
ROOT_HALF = 1.0 / math.sqrt(2.0)
DENSITY = 1.0 / math.sqrt(2.0 * math.pi)
LOW = jnp.bfloat16
WIDE = jnp.float32


def norm_parts(values):
    average = jnp.mean(values, axis=-1, keepdims=True)
    centered = values - average
    spread = jnp.mean(centered * centered, axis=-1, keepdims=True)
    inverse = lax.rsqrt(spread + EPSILON)
    return (centered * inverse, inverse)


def norm_back(upstream, normal_hat, inverse, gain_full):
    scaled = upstream * gain_full
    first_mean = jnp.mean(scaled, axis=-1, keepdims=True)
    second_mean = jnp.mean(scaled * normal_hat, axis=-1, keepdims=True)
    return inverse * (scaled - first_mean - normal_hat * second_mean)


def gelu_value(values):
    return 0.5 * values * (1.0 + lax.erf(values * ROOT_HALF))


def gelu_slope(values):
    return 0.5 * (1.0 + lax.erf(values * ROOT_HALF)) + values * DENSITY * jnp.exp(
        -0.5 * values * values
    )


def matmul(left_side, right_side):
    return jnp.dot(left_side, right_side, preferred_element_type=WIDE)


def contract_rows(left_side, right_side):
    return lax.dot_general(
        left_side, right_side, (((0,), (0,)), ((), ())), preferred_element_type=WIDE
    )


def contract_cols(left_side, right_side):
    return lax.dot_general(
        left_side, right_side, (((1,), (1,)), ((), ())), preferred_element_type=WIDE
    )


def scatter_rows(partial):
    return lax.psum_scatter(partial.astype(LOW), "tp", scatter_dimension=0, tiled=True).astype(WIDE)


def gather_rows(own):
    return lax.all_gather(own, "tp", axis=0, tiled=True)


def per_device(
    hidden,
    cotangent,
    lengths,
    query_weight,
    key_weight,
    value_weight,
    output_weight,
    inner_weight,
    outer_weight,
    query_bias,
    value_bias,
    inner_bias,
    output_bias,
    outer_bias,
    first_gain,
    first_shift,
    second_gain,
    second_shift,
):
    clip_count, frames_local, width = hidden.shape
    rows = clip_count * frames_local
    frames_all = frames_local * lax.axis_size("ctx")
    tp_size = lax.axis_size("tp")
    own_rows = rows // tp_size
    columns = query_weight.shape[2]
    heads_local = columns // HD
    scale = 1.0 / math.sqrt(HD)
    valid_keys = jnp.arange(frames_all)[None, :] < lengths[:, None]
    own_start = lax.axis_index("tp") * own_rows

    def own_slice(full):
        return lax.dynamic_slice_in_dim(full, own_start, own_rows, axis=0)

    small = jnp.concatenate(
        [output_bias, outer_bias, first_gain, first_shift, second_gain, second_shift], axis=0
    ).astype(LOW)
    small = lax.all_gather(small, "fsdp", axis=1, tiled=True).astype(WIDE)

    def vector(kind, layer):
        return small[kind * LAYERS + layer]

    def fetch(layer):
        qkv = jnp.concatenate(
            [query_weight[layer], key_weight[layer], value_weight[layer]], axis=1
        ).astype(LOW)
        qkv = lax.all_gather(qkv, "fsdp", axis=0, tiled=True)
        out = lax.all_gather(output_weight[layer].astype(LOW), "fsdp", axis=1, tiled=True)
        inner = lax.all_gather(inner_weight[layer].astype(LOW), "fsdp", axis=0, tiled=True)
        outer = lax.all_gather(outer_weight[layer].astype(LOW), "fsdp", axis=1, tiled=True)
        return (qkv, out, inner, outer)

    def scores_of(query_block, key_block, mask_row):
        scores = (
            jnp.einsum(
                "qhd,khd->hqk",
                query_block.reshape(frames_local, heads_local, HD),
                key_block.reshape(frames_all, heads_local, HD),
                preferred_element_type=WIDE,
            )
            * scale
        )
        return jnp.where(mask_row[None, None, :], scores, NEGATIVE)

    def attend(packed):
        query_block, key_block, value_block, mask_row = packed
        scores = scores_of(query_block, key_block, mask_row)
        highest = jnp.max(scores, axis=-1, keepdims=True)
        raised = jnp.exp(scores - highest)
        total = jnp.sum(raised, axis=-1, keepdims=True)
        weights_soft = (raised / total).astype(LOW)
        attended = jnp.einsum(
            "hqk,khd->qhd",
            weights_soft,
            value_block.reshape(frames_all, heads_local, HD),
            preferred_element_type=WIDE,
        )
        return (attended.reshape(frames_local, columns), (highest + jnp.log(total))[:, :, 0])

    def attend_back(packed):
        query_block, key_block, value_block, grad_block, log_total, mask_row = packed
        scores = scores_of(query_block, key_block, mask_row)
        weights_full = jnp.exp(scores - log_total[:, :, None])
        grad_heads = grad_block.reshape(frames_local, heads_local, HD)
        grad_weights = jnp.einsum(
            "qhd,khd->hqk",
            grad_heads,
            value_block.reshape(frames_all, heads_local, HD),
            preferred_element_type=WIDE,
        )
        row_terms = jnp.sum(weights_full * grad_weights, axis=-1, keepdims=True)
        grad_scores = (weights_full * (grad_weights - row_terms)).astype(LOW)
        grad_query = (
            jnp.einsum(
                "hqk,khd->qhd",
                grad_scores,
                key_block.reshape(frames_all, heads_local, HD),
                preferred_element_type=WIDE,
            )
            * scale
        )
        grad_key = (
            jnp.einsum(
                "hqk,qhd->khd",
                grad_scores,
                query_block.reshape(frames_local, heads_local, HD),
                preferred_element_type=WIDE,
            )
            * scale
        )
        grad_value = jnp.einsum(
            "hqk,qhd->khd",
            weights_full.astype(LOW),
            grad_heads,
            preferred_element_type=WIDE,
        )
        return (
            grad_query.reshape(frames_local, columns),
            grad_key.reshape(frames_all, columns),
            grad_value.reshape(frames_all, columns),
        )

    def clips(values):
        return values.reshape(clip_count, -1, values.shape[-1])

    weights = [fetch(layer) for layer in range(LAYERS)]

    residual = own_slice(hidden.reshape(rows, width))
    kept = []
    for layer in range(LAYERS):
        w_qkv, w_out, w_inner, w_outer = weights[layer]
        if layer == 0:
            hat_full, _ = norm_parts(hidden.reshape(rows, width))
            normed = (hat_full * vector(2, layer) + vector(3, layer)).astype(LOW)
            hat_first, inverse_first = norm_parts(residual)
        else:
            hat_first, inverse_first = norm_parts(residual)
            normed = gather_rows((hat_first * vector(2, layer) + vector(3, layer)).astype(LOW))
        bias_qkv = jnp.concatenate(
            [query_bias[layer], jnp.zeros_like(query_bias[layer]), value_bias[layer]]
        )
        qkv = (matmul(normed, w_qkv) + bias_qkv).astype(LOW)
        queries = qkv[:, :columns]
        key_value = lax.all_gather(clips(qkv[:, columns:]), "ctx", axis=1, tiled=True)
        key_all = key_value[:, :, :columns]
        value_all = key_value[:, :, columns:]
        attended, log_total = lax.map(attend, (clips(queries), key_all, value_all, valid_keys))
        attended = attended.reshape(rows, columns).astype(LOW)
        middle = residual + scatter_rows(matmul(attended, w_out)) + vector(0, layer)
        hat_second, inverse_second = norm_parts(middle)
        normed_two = gather_rows((hat_second * vector(4, layer) + vector(5, layer)).astype(LOW))
        inner_pre = matmul(normed_two, w_inner) + inner_bias[layer]
        active = gelu_value(inner_pre).astype(LOW)
        residual = middle + scatter_rows(matmul(active, w_outer)) + vector(1, layer)
        kept.append(
            (
                hat_first,
                inverse_first,
                normed,
                queries,
                key_all,
                value_all,
                log_total,
                attended,
                hat_second,
                inverse_second,
                normed_two,
                inner_pre,
                active,
            )
        )
    output = gather_rows(residual)

    grad_own = own_slice(cotangent.reshape(rows, width))
    grad_low = cotangent.reshape(rows, width).astype(LOW)
    grads = [None] * LAYERS
    vectors = [None] * LAYERS
    biases = [None] * LAYERS
    for layer in reversed(range(LAYERS)):
        w_qkv, w_out, w_inner, w_outer = weights[layer]
        (
            hat_first,
            inverse_first,
            normed,
            queries,
            key_all,
            value_all,
            log_total,
            attended,
            hat_second,
            inverse_second,
            normed_two,
            inner_pre,
            active,
        ) = kept[layer]
        if layer != LAYERS - 1:
            grad_low = gather_rows(grad_own.astype(LOW))
        grad_active = contract_cols(grad_low, w_outer)
        grad_inner = (grad_active * gelu_slope(inner_pre)).astype(LOW)
        grad_normed_two = scatter_rows(contract_cols(grad_inner, w_inner))
        grad_outer_w = contract_rows(active, grad_low)
        grad_inner_w = contract_rows(normed_two, grad_inner)
        grad_middle = grad_own + norm_back(
            grad_normed_two, hat_second, inverse_second, vector(4, layer)
        )
        grad_mid_low = gather_rows(grad_middle.astype(LOW))
        grad_attended = contract_cols(grad_mid_low, w_out).astype(LOW)
        grad_output_w = contract_rows(attended, grad_mid_low)
        grad_query, grad_key_part, grad_value_part = lax.map(
            attend_back,
            (clips(queries), key_all, value_all, clips(grad_attended), log_total, valid_keys),
        )
        grad_kv_part = jnp.concatenate([grad_key_part, grad_value_part], axis=-1).astype(LOW)
        grad_kv = lax.psum_scatter(grad_kv_part, "ctx", scatter_dimension=1, tiled=True)
        grad_qkv = jnp.concatenate(
            [grad_query.reshape(rows, columns).astype(LOW), grad_kv.reshape(rows, 2 * columns)],
            axis=1,
        )
        grad_normed = scatter_rows(contract_cols(grad_qkv, w_qkv))
        grad_in = grad_middle + norm_back(grad_normed, hat_first, inverse_first, vector(2, layer))
        by_rows = jnp.concatenate([contract_rows(normed, grad_qkv), grad_inner_w], axis=1)
        by_cols = jnp.concatenate([grad_output_w, grad_outer_w], axis=0)
        by_rows = lax.psum_scatter(
            by_rows.astype(LOW), ("fsdp", "ctx"), scatter_dimension=0, tiled=True
        )
        by_rows = lax.all_gather(by_rows, "ctx", axis=0, tiled=True).astype(WIDE)
        by_cols = lax.psum_scatter(
            by_cols.astype(LOW), ("fsdp", "ctx"), scatter_dimension=1, tiled=True
        )
        by_cols = lax.all_gather(by_cols, "ctx", axis=1, tiled=True).astype(WIDE)
        grads[layer] = (by_rows, by_cols)
        vectors[layer] = jnp.stack(
            [
                jnp.sum(grad_middle, axis=0),
                jnp.sum(grad_own, axis=0),
                jnp.sum(grad_normed * hat_first, axis=0),
                jnp.sum(grad_normed, axis=0),
                jnp.sum(grad_normed_two * hat_second, axis=0),
                jnp.sum(grad_normed_two, axis=0),
            ]
        )
        biases[layer] = jnp.concatenate(
            [
                jnp.sum(grad_qkv.astype(WIDE), axis=0),
                jnp.sum(grad_inner.astype(WIDE), axis=0),
            ]
        )
        grad_own = grad_in
    grad_hidden = gather_rows(grad_own)

    vector_sums = lax.psum(jnp.stack(vectors, axis=1), ("fsdp", "ctx", "tp"))
    bias_sums = lax.psum(jnp.stack(biases), ("fsdp", "ctx"))
    shard = output_bias.shape[1]
    vector_sums = lax.dynamic_slice_in_dim(
        vector_sums, lax.axis_index("fsdp") * shard, shard, axis=2
    )

    def stacked_rows(start, size):
        return jnp.stack([grads[layer][0][:, start : start + size] for layer in range(LAYERS)])

    def stacked_cols(start, size):
        return jnp.stack([grads[layer][1][start : start + size] for layer in range(LAYERS)])

    hidden_local = inner_weight.shape[2]
    return (
        output.reshape(hidden.shape),
        grad_hidden.reshape(hidden.shape),
        stacked_rows(0, columns),
        stacked_rows(columns, columns),
        stacked_rows(2 * columns, columns),
        stacked_cols(0, columns),
        stacked_rows(3 * columns, hidden_local),
        stacked_cols(columns, hidden_local),
        bias_sums[:, :columns],
        bias_sums[:, 2 * columns : 3 * columns],
        bias_sums[:, 3 * columns :],
        vector_sums[0],
        vector_sums[1],
        vector_sums[2],
        vector_sums[3],
        vector_sums[4],
        vector_sums[5],
    )


def solution(mesh):
    in_specs = (
        P("fsdp", "ctx", None),
        P("fsdp", "ctx", None),
        P("fsdp"),
        P(None, "fsdp", "tp"),
        P(None, "fsdp", "tp"),
        P(None, "fsdp", "tp"),
        P(None, "tp", "fsdp"),
        P(None, "fsdp", "tp"),
        P(None, "tp", "fsdp"),
        P(None, "tp"),
        P(None, "tp"),
        P(None, "tp"),
        P(None, "fsdp"),
        P(None, "fsdp"),
        P(None, "fsdp"),
        P(None, "fsdp"),
        P(None, "fsdp"),
        P(None, "fsdp"),
    )
    out_specs = (
        P("fsdp", "ctx", None),
        P("fsdp", "ctx", None),
        P(None, "fsdp", "tp"),
        P(None, "fsdp", "tp"),
        P(None, "fsdp", "tp"),
        P(None, "tp", "fsdp"),
        P(None, "fsdp", "tp"),
        P(None, "tp", "fsdp"),
        P(None, "tp"),
        P(None, "tp"),
        P(None, "tp"),
        P(None, "fsdp"),
        P(None, "fsdp"),
        P(None, "fsdp"),
        P(None, "fsdp"),
        P(None, "fsdp"),
        P(None, "fsdp"),
    )
    return jax.shard_map(
        per_device, mesh=mesh, in_specs=in_specs, out_specs=out_specs, check_vma=False
    )
```

```python
import functools
import math
import jax
import jax.numpy as jnp
from jax import lax
from jax.experimental import pallas as pl
from jax.experimental.pallas import tpu as pltpu
from jax.sharding import PartitionSpec as P

MESH = pl.DeviceIdType.MESH
LOW = jnp.bfloat16
WIDE = jnp.float32
EPSILON = 1e-05
NEGATIVE = -1e30
HD = 80
PIECES = 4
LAYERS = 2
ROOT_HALF = 1.0 / math.sqrt(2.0)
DENSITY = 1.0 / math.sqrt(2.0 * math.pi)


def norm_parts(values):
    average = jnp.mean(values, axis=-1, keepdims=True)
    centered = values - average
    spread = jnp.mean(centered * centered, axis=-1, keepdims=True)
    inverse = lax.rsqrt(spread + EPSILON)
    return (centered * inverse, inverse)


def norm_back(upstream, normal_hat, inverse, gain_full):
    scaled = upstream * gain_full
    first_mean = jnp.mean(scaled, axis=-1, keepdims=True)
    second_mean = jnp.mean(scaled * normal_hat, axis=-1, keepdims=True)
    return inverse * (scaled - first_mean - normal_hat * second_mean)


def line_exchange(n, own, pieces, partial, gathered, from_left, from_right, total, sems, finish):
    rs_send, rs_recv, ag_send, ag_recv = sems
    me = lax.axis_index("tp")
    piece = own // pieces
    to_right, to_left = {"tp": lax.rem(me + 1, n)}, {"tp": lax.rem(me + n - 1, n)}
    has_left, has_right = me > 0, me < n - 1

    barrier = pltpu.get_barrier_semaphore()

    @pl.when(has_left)
    def _():
        pl.semaphore_signal(barrier, inc=1, device_id=to_left, device_id_type=MESH)

    @pl.when(has_right)
    def _():
        pl.semaphore_signal(barrier, inc=1, device_id=to_right, device_id_type=MESH)

    pl.semaphore_wait(barrier, has_left.astype(jnp.int32) + has_right.astype(jnp.int32))

    def rows_of(shard, step):
        return pl.ds(pl.multiple_of(shard * own + step * piece, piece), piece)

    def reduce_copy(way, src, shard, step):
        rows = rows_of(shard, step)
        landing = from_left if way == 0 else from_right
        return pltpu.make_async_remote_copy(
            src_ref=src.at[rows],
            dst_ref=landing.at[rows],
            send_sem=rs_send.at[way, shard, step],
            recv_sem=rs_recv.at[way, shard, step],
            device_id=to_right if way == 0 else to_left,
            device_id_type=MESH,
        )

    def gather_copy(way, shard, step):
        rows = rows_of(shard, step)
        return pltpu.make_async_remote_copy(
            src_ref=gathered.at[rows],
            dst_ref=gathered.at[rows],
            send_sem=ag_send.at[way, shard, step],
            recv_sem=ag_recv.at[way, shard, step],
            device_id=to_right if way == 0 else to_left,
            device_id_type=MESH,
        )

    def reduce_step(step):
        for k in range(n - 1):
            for way in range(2):
                shard = n - 1 - k if way == 0 else k
                landing = from_left if way == 0 else from_right
                first = me == 0 if way == 0 else me == n - 1
                inside = (me > 0) & (me < shard) if way == 0 else (me < n - 1) & (me > shard)

                @pl.when(first)
                def _():
                    reduce_copy(way, partial, shard, step).start()

                @pl.when(inside)
                def _():
                    rows = rows_of(shard, step)
                    reduce_copy(way, partial, shard, step).wait_recv()
                    landing[rows, :] = (
                        partial[rows, :].astype(WIDE) + landing[rows, :].astype(WIDE)
                    ).astype(LOW)
                    reduce_copy(way, landing, shard, step).start()

    def finish_step(step):
        rows = rows_of(me, step)
        total[...] = partial[rows, :].astype(WIDE)

        @pl.when(has_left)
        def _():
            reduce_copy(0, partial, me, step).wait_recv()
            total[...] += from_left[rows, :].astype(WIDE)

        @pl.when(has_right)
        def _():
            reduce_copy(1, partial, me, step).wait_recv()
            total[...] += from_right[rows, :].astype(WIDE)

        own_rows = pl.ds(pl.multiple_of(step * piece, piece), piece)
        gathered[rows, :] = finish(own_rows, total[...])

        @pl.when(has_right)
        def _():
            gather_copy(0, me, step).start()

        @pl.when(has_left)
        def _():
            gather_copy(1, me, step).start()

    def forward_step(step):
        for k in range(1, n):
            for way in range(2):
                shard = me - k if way == 0 else me + k
                there = shard >= 0 if way == 0 else shard <= n - 1
                further = has_right if way == 0 else has_left

                @pl.when(there)
                def _():
                    gather_copy(way, shard, step).wait_recv()

                @pl.when(there & further)
                def _():
                    gather_copy(way, shard, step).start()

    def body(step, carry):
        @pl.when(step < pieces)
        def _():
            reduce_step(step)

        @pl.when((step >= 1) & (step <= pieces))
        def _():
            finish_step(step - 1)

        @pl.when(step >= 2)
        def _():
            forward_step(step - 2)

        return carry

    lax.fori_loop(0, pieces + 2, body, 0)

    def drain(step, carry):
        for k in range(n - 1):
            for way in range(2):
                shard = n - 1 - k if way == 0 else k
                sends = me < shard if way == 0 else me > shard

                @pl.when(sends)
                def _():
                    reduce_copy(way, partial, shard, step).wait_send()

        for k in range(n):
            for way in range(2):
                shard = me - k if way == 0 else me + k
                there = shard >= 0 if way == 0 else shard <= n - 1
                further = has_right if way == 0 else has_left

                @pl.when(there & further)
                def _():
                    gather_copy(way, shard, step).wait_send()

        return carry

    lax.fori_loop(0, pieces, drain, 0)


def exchange_scratch(n, rows, width, pieces):
    return [
        pltpu.VMEM((rows, width), LOW),
        pltpu.VMEM((rows, width), LOW),
        pltpu.VMEM((rows // n // pieces, width), WIDE),
        pltpu.SemaphoreType.DMA((2, n, pieces)),
        pltpu.SemaphoreType.DMA((2, n, pieces)),
        pltpu.SemaphoreType.DMA((2, n, pieces)),
        pltpu.SemaphoreType.DMA((2, n, pieces)),
    ]


def forward_exchange_kernel(
    n, pieces, partial, residual, bias, gain, shift, gathered, middle, from_left, from_right, total, *sems
):
    def finish(rows, value):
        mid = value + residual[rows, :] + bias[...]
        middle[rows, :] = mid
        hat, _ = norm_parts(mid)
        return (hat * gain[...] + shift[...]).astype(LOW)

    line_exchange(
        n, residual.shape[0], pieces, partial, gathered, from_left, from_right, total, sems, finish
    )


def backward_exchange_kernel(
    n, pieces, partial, grad_out, normal_in, gain, gathered, grad_in, sums, from_left, from_right, total, *sems
):
    sums[...] = jnp.zeros_like(sums)

    def finish(rows, upstream):
        hat, inverse = norm_parts(normal_in[rows, :])
        grad = grad_out[rows, :] + norm_back(upstream, hat, inverse, gain[...])
        grad_in[rows, :] = grad
        sums[0:1, :] += jnp.sum(upstream * hat, axis=0, keepdims=True)
        sums[1:2, :] += jnp.sum(upstream, axis=0, keepdims=True)
        sums[2:3, :] += jnp.sum(grad, axis=0, keepdims=True)
        return grad.astype(LOW)

    line_exchange(
        n, grad_out.shape[0], pieces, partial, gathered, from_left, from_right, total, sems, finish
    )


def in_vmem(count):
    return [pl.BlockSpec(memory_space=pltpu.VMEM)] * count


def forward_exchange(partial, residual, bias, gain, shift, n, collective_id):
    rows, width = partial.shape
    return pl.pallas_call(
        functools.partial(forward_exchange_kernel, n, PIECES),
        out_shape=(
            jax.ShapeDtypeStruct((rows, width), LOW),
            jax.ShapeDtypeStruct(residual.shape, WIDE),
        ),
        in_specs=in_vmem(5),
        out_specs=tuple(in_vmem(2)),
        scratch_shapes=exchange_scratch(n, rows, width, PIECES),
        compiler_params=pltpu.CompilerParams(
            collective_id=collective_id, has_side_effects=True, vmem_limit_bytes=40 << 20
        ),
        name="forward_exchange",
    )(partial, residual, bias[None, :], gain[None, :], shift[None, :])


def backward_exchange(partial, grad_out, normal_in, gain, n, collective_id):
    rows, width = partial.shape
    return pl.pallas_call(
        functools.partial(backward_exchange_kernel, n, PIECES),
        out_shape=(
            jax.ShapeDtypeStruct((rows, width), LOW),
            jax.ShapeDtypeStruct(grad_out.shape, WIDE),
            jax.ShapeDtypeStruct((8, width), WIDE),
        ),
        in_specs=in_vmem(4),
        out_specs=tuple(in_vmem(3)),
        scratch_shapes=exchange_scratch(n, rows, width, PIECES),
        compiler_params=pltpu.CompilerParams(
            collective_id=collective_id, has_side_effects=True, vmem_limit_bytes=40 << 20
        ),
        name="backward_exchange",
    )(partial, grad_out, normal_in, gain[None, :])


def attend_kernel(scale, length, qkv, out, out_wide, log_total, held, high, low_sum, sems_send, sems_recv):
    columns = qkv.shape[0] // 3
    frames = qkv.shape[1]
    heads = columns // HD
    me = lax.axis_index("ctx")

    def partner(r):
        return {"ctx": jnp.bitwise_xor(me, r)}

    barrier = pltpu.get_barrier_semaphore()
    for r in (1, 2):
        pl.semaphore_signal(barrier, inc=1, device_id=partner(r), device_id_type=MESH)
    pl.semaphore_wait(barrier, 2)

    def send(slot, part, to):
        rows = pl.ds(part * columns, columns)
        src = qkv.at[pl.ds((1 + part) * columns, columns)] if slot != 3 else held.at[1, rows]
        return pltpu.make_async_remote_copy(
            src_ref=src,
            dst_ref=held.at[slot - 1, rows],
            send_sem=sems_send.at[slot - 1, part],
            recv_sem=sems_recv.at[slot - 1, part],
            device_id=partner(to),
            device_id_type=MESH,
        )

    for part in range(2):
        send(2, part, 2).start()
    for part in range(2):
        send(1, part, 1).start()

    high[...] = jnp.full_like(high, NEGATIVE)
    low_sum[...] = jnp.zeros_like(low_sum)
    out_wide[...] = jnp.zeros_like(out_wide)
    limit = length[0]

    def block(keys_ref, key_row, value_row, slot):
        owner = jnp.bitwise_xor(me, slot)
        left = limit - owner * frames
        valid = lax.broadcasted_iota(jnp.int32, (frames, frames), 0) < left
        for h in range(heads):
            rows = pl.ds(h * HD, HD)
            keys = keys_ref[pl.ds(key_row + h * HD, HD), :]
            values = keys_ref[pl.ds(value_row + h * HD, HD), :]
            scores = lax.dot_general(
                keys, qkv[rows, :], (((0,), (0,)), ((), ())), preferred_element_type=WIDE
            )
            scores = jnp.where(valid, scores * scale, NEGATIVE)
            before = high[h : h + 1, :]
            now = jnp.maximum(before, jnp.max(scores, axis=0, keepdims=True))
            shrink = jnp.exp(before - now)
            raised = jnp.exp(scores - now)
            low_sum[h : h + 1, :] = low_sum[h : h + 1, :] * shrink + jnp.sum(
                raised, axis=0, keepdims=True
            )
            high[h : h + 1, :] = now
            out_wide[rows, :] = out_wide[rows, :] * shrink + jnp.dot(
                values, raised.astype(LOW), preferred_element_type=WIDE
            )

    block(qkv, columns, 2 * columns, 0)
    for part in range(2):
        send(1, part, 1).wait_recv()
    block(held.at[0], 0, columns, 1)
    for part in range(2):
        send(2, part, 2).wait_recv()
        send(3, part, 1).start()
    block(held.at[1], 0, columns, 2)
    for part in range(2):
        send(3, part, 1).wait_recv()
    block(held.at[2], 0, columns, 3)
    for h in range(heads):
        rows = pl.ds(h * HD, HD)
        total = low_sum[h : h + 1, :]
        done = out_wide[rows, :] / total
        out_wide[rows, :] = done
        out[rows, :] = done.astype(LOW)
        log_total[h : h + 1, :] = high[h : h + 1, :] + jnp.log(total)
    for slot in (1, 2, 3):
        for part in range(2):
            send(slot, part, 2 if slot == 2 else 1).wait_send()


def attend(qkv, length, scale, collective_id):
    columns, frames = qkv.shape[0] // 3, qkv.shape[1]
    return pl.pallas_call(
        functools.partial(attend_kernel, scale),
        out_shape=(
            jax.ShapeDtypeStruct((columns, frames), LOW),
            jax.ShapeDtypeStruct((columns, frames), WIDE),
            jax.ShapeDtypeStruct((8, frames), WIDE),
            jax.ShapeDtypeStruct((3, 2 * columns, frames), LOW),
        ),
        in_specs=[pl.BlockSpec(memory_space=pltpu.SMEM)] + in_vmem(1),
        out_specs=tuple(in_vmem(4)),
        scratch_shapes=[
            pltpu.VMEM((8, frames), WIDE),
            pltpu.VMEM((8, frames), WIDE),
            pltpu.SemaphoreType.DMA((3, 2)),
            pltpu.SemaphoreType.DMA((3, 2)),
        ],
        compiler_params=pltpu.CompilerParams(
            collective_id=collective_id, has_side_effects=True, vmem_limit_bytes=56 << 20
        ),
        name="attend",
    )(length, qkv)


def attend_back_kernel(
    scale, length, qkv, held, grad, out_wide, log_total, grad_qkv, mine, parts, landed, acc, sems_send, sems_recv
):
    columns = qkv.shape[0] // 3
    frames = qkv.shape[1]
    heads = columns // HD
    me = lax.axis_index("ctx")

    def partner(r):
        return {"ctx": jnp.bitwise_xor(me, r)}

    barrier = pltpu.get_barrier_semaphore()
    for r in (1, 2):
        pl.semaphore_signal(barrier, inc=1, device_id=partner(r), device_id_type=MESH)
    pl.semaphore_wait(barrier, 2)

    def send(at, part, to):
        rows = pl.ds(part * columns, columns)
        return pltpu.make_async_remote_copy(
            src_ref=parts.at[at, rows],
            dst_ref=landed.at[at, rows],
            send_sem=sems_send.at[at, part],
            recv_sem=sems_recv.at[at, part],
            device_id=partner(to),
            device_id_type=MESH,
        )

    acc[...] = jnp.zeros_like(acc)
    limit = length[0]

    def block(keys_ref, key_row, value_row, slot, store):
        owner = jnp.bitwise_xor(me, slot)
        left = limit - owner * frames
        valid = lax.broadcasted_iota(jnp.int32, (frames, frames), 0) < left
        for h in range(heads):
            rows = pl.ds(h * HD, HD)
            keys = keys_ref[pl.ds(key_row + h * HD, HD), :]
            values = keys_ref[pl.ds(value_row + h * HD, HD), :]
            queries = qkv[rows, :]
            upstream = grad[rows, :]
            scores = lax.dot_general(
                keys, queries, (((0,), (0,)), ((), ())), preferred_element_type=WIDE
            )
            weights = jnp.where(valid, jnp.exp(scores * scale - log_total[h : h + 1, :]), 0.0)
            grad_weights = lax.dot_general(
                values, upstream, (((0,), (0,)), ((), ())), preferred_element_type=WIDE
            )
            row_terms = jnp.sum(
                upstream.astype(WIDE) * out_wide[rows, :], axis=0, keepdims=True
            )
            grad_scores = (weights * (grad_weights - row_terms)).astype(LOW)
            acc[rows, :] += jnp.dot(keys, grad_scores, preferred_element_type=WIDE)
            grad_keys = (
                lax.dot_general(
                    queries, grad_scores, (((1,), (1,)), ((), ())), preferred_element_type=WIDE
                )
                * scale
            )
            grad_values = lax.dot_general(
                upstream, weights.astype(LOW), (((1,), (1,)), ((), ())), preferred_element_type=WIDE
            )
            store(h * HD, grad_keys, grad_values)

    def store_part(at):
        def store(row, grad_keys, grad_values):
            parts[at, pl.ds(row, HD), :] = grad_keys.astype(LOW)
            parts[at, pl.ds(columns + row, HD), :] = grad_values.astype(LOW)

        return store

    def store_mine(row, grad_keys, grad_values):
        mine[pl.ds(row, HD), :] = grad_keys
        mine[pl.ds(columns + row, HD), :] = grad_values

    def store_joined(row, grad_keys, grad_values):
        for start, value in ((row, grad_keys), (columns + row, grad_values)):
            rows = pl.ds(start, HD)
            parts[1, rows, :] = (value + landed[0, rows, :].astype(WIDE)).astype(LOW)

    block(held.at[2], 0, columns, 3, store_part(0))
    for part in range(2):
        send(0, part, 1).start()
    for part in range(2):
        send(0, part, 1).wait_recv()
    block(held.at[1], 0, columns, 2, store_joined)
    for part in range(2):
        send(1, part, 2).start()
    block(held.at[0], 0, columns, 1, store_part(2))
    for part in range(2):
        send(2, part, 1).start()
    block(qkv, columns, 2 * columns, 0, store_mine)
    grad_qkv[0:columns, :] = (acc[...] * scale).astype(LOW)
    for part in range(2):
        send(2, part, 1).wait_recv()
    for part in range(2):
        send(1, part, 2).wait_recv()
    grad_qkv[columns:, :] = (
        mine[...] + landed[1].astype(WIDE) + landed[2].astype(WIDE)
    ).astype(LOW)
    for at in range(3):
        for part in range(2):
            send(at, part, 2 if at == 1 else 1).wait_send()


def attend_back(qkv, held, grad, out_wide, log_total, length, scale, collective_id):
    columns, frames = qkv.shape[0] // 3, qkv.shape[1]
    return pl.pallas_call(
        functools.partial(attend_back_kernel, scale),
        out_shape=jax.ShapeDtypeStruct((3 * columns, frames), LOW),
        in_specs=[pl.BlockSpec(memory_space=pltpu.SMEM)] + in_vmem(5),
        out_specs=in_vmem(1)[0],
        scratch_shapes=[
            pltpu.VMEM((2 * columns, frames), WIDE),
            pltpu.VMEM((3, 2 * columns, frames), LOW),
            pltpu.VMEM((3, 2 * columns, frames), LOW),
            pltpu.VMEM((columns, frames), WIDE),
            pltpu.SemaphoreType.DMA((3, 2)),
            pltpu.SemaphoreType.DMA((3, 2)),
        ],
        compiler_params=pltpu.CompilerParams(
            collective_id=collective_id, has_side_effects=True, vmem_limit_bytes=56 << 20
        ),
        name="attend_back",
    )(length, qkv, held, grad, out_wide, log_total)


def gelu_value(values):
    return 0.5 * values * (1.0 + lax.erf(values * ROOT_HALF))


def gelu_slope(values):
    return 0.5 * (1.0 + lax.erf(values * ROOT_HALF)) + values * DENSITY * jnp.exp(
        -0.5 * values * values
    )


def product(left_side, right_side, left_axis, right_axis):
    return lax.dot_general(
        left_side,
        right_side,
        (((left_axis,), (right_axis,)), ((), ())),
        preferred_element_type=WIDE,
    )


def per_device(
    hidden,
    cotangent,
    lengths,
    query_weight,
    key_weight,
    value_weight,
    output_weight,
    inner_weight,
    outer_weight,
    query_bias,
    value_bias,
    inner_bias,
    output_bias,
    outer_bias,
    first_gain,
    first_shift,
    second_gain,
    second_shift,
):
    clip_count, rows, width = hidden.shape
    assert clip_count == 1
    assert lax.axis_size("ctx") == 4
    tp_size = lax.axis_size("tp")
    own_rows = rows // tp_size
    columns = query_weight.shape[2]
    hidden_local = inner_weight.shape[2]
    scale = 1.0 / math.sqrt(HD)
    own_start = lax.axis_index("tp") * own_rows

    def own_slice(full):
        return lax.dynamic_slice_in_dim(full, own_start, own_rows, axis=0)

    small = jnp.concatenate(
        [output_bias, outer_bias, first_gain, first_shift, second_gain, second_shift], axis=0
    ).astype(LOW)
    small = lax.all_gather(small, "fsdp", axis=1, tiled=True).astype(WIDE)

    def vector(kind, layer):
        return small[kind * LAYERS + layer]

    def fetch(layer):
        qkv = jnp.concatenate(
            [query_weight[layer], key_weight[layer], value_weight[layer]], axis=1
        ).astype(LOW)
        qkv = lax.all_gather(qkv, "fsdp", axis=0, tiled=True)
        out = lax.all_gather(output_weight[layer].astype(LOW), "fsdp", axis=1, tiled=True)
        inner = lax.all_gather(inner_weight[layer].astype(LOW), "fsdp", axis=0, tiled=True)
        outer = lax.all_gather(outer_weight[layer].astype(LOW), "fsdp", axis=1, tiled=True)
        return (qkv, out, inner, outer)

    weights = [fetch(layer) for layer in range(LAYERS)]

    hidden_rows = hidden.reshape(rows, width)
    residual = own_slice(hidden_rows)
    hat_full, _ = norm_parts(hidden_rows)
    normed = (hat_full * vector(2, 0) + vector(3, 0)).astype(LOW)
    kept = []
    for layer in range(LAYERS):
        w_qkv, w_out, w_inner, w_outer = weights[layer]
        bias_qkv = jnp.concatenate(
            [query_bias[layer], jnp.zeros_like(query_bias[layer]), value_bias[layer]]
        )
        qkv = (product(w_qkv, normed, 0, 1) + bias_qkv[:, None]).astype(LOW)
        attended, attended_wide, log_total, held = attend(qkv, lengths, scale, 2 * layer)
        branch = product(attended, w_out, 0, 0).astype(LOW)
        normed_two, middle = forward_exchange(
            branch, residual, vector(0, layer), vector(4, layer), vector(5, layer), tp_size, 2 * layer + 4
        )
        inner_pre = product(normed_two, w_inner, 1, 0) + inner_bias[layer]
        active = gelu_value(inner_pre).astype(LOW)
        kept.append(
            (residual, normed, qkv, attended, attended_wide, log_total, held, middle, normed_two, inner_pre, active)
        )
        branch = product(active, w_outer, 1, 0).astype(LOW)
        if layer + 1 < LAYERS:
            normed, residual = forward_exchange(
                branch,
                middle,
                vector(1, layer),
                vector(2, layer + 1),
                vector(3, layer + 1),
                tp_size,
                2 * layer + 5,
            )
        else:
            branch = lax.psum_scatter(branch, "tp", scatter_dimension=0, tiled=True).astype(WIDE)
            residual = middle + branch + vector(1, layer)
            output = lax.all_gather(residual.astype(LOW), "tp", axis=0, tiled=True).astype(WIDE)

    grad_rows = cotangent.reshape(rows, width)
    grad_own = own_slice(grad_rows)
    grad_low = grad_rows.astype(LOW)
    outer_bias_sum = jnp.sum(grad_own, axis=0)
    grads = [None] * LAYERS
    vectors = [None] * LAYERS
    biases = [None] * LAYERS
    for layer in reversed(range(LAYERS)):
        w_qkv, w_out, w_inner, w_outer = weights[layer]
        (
            residual,
            normed,
            qkv,
            attended,
            attended_wide,
            log_total,
            held,
            middle,
            normed_two,
            inner_pre,
            active,
        ) = kept[layer]
        grad_active = product(grad_low, w_outer, 1, 1)
        grad_inner = (grad_active * gelu_slope(inner_pre)).astype(LOW)
        branch = product(grad_inner, w_inner, 1, 1).astype(LOW)
        grad_mid_low, grad_middle, sums_two = backward_exchange(
            branch, grad_own, middle, vector(4, layer), tp_size, 2 * layer + 8
        )
        grad_outer_w = product(active, grad_low, 0, 0)
        grad_inner_w = product(normed_two, grad_inner, 0, 0)
        grad_attended = product(w_out, grad_mid_low, 1, 1).astype(LOW)
        grad_qkv = attend_back(
            qkv, held, grad_attended, attended_wide, log_total, lengths, scale, 2 * layer + 12
        )
        grad_output_w = product(attended, grad_mid_low, 1, 0)
        branch = product(grad_qkv, w_qkv, 0, 1).astype(LOW)
        grad_low, grad_own, sums_one = backward_exchange(
            branch, grad_middle, residual, vector(2, layer), tp_size, 2 * layer + 9
        )
        by_rows = jnp.concatenate([product(normed, grad_qkv, 0, 1), grad_inner_w], axis=1)
        by_cols = jnp.concatenate([grad_output_w, grad_outer_w], axis=0)
        by_rows = lax.psum_scatter(
            by_rows.astype(LOW), ("fsdp", "ctx"), scatter_dimension=0, tiled=True
        )
        by_rows = lax.all_gather(by_rows, "ctx", axis=0, tiled=True).astype(WIDE)
        by_cols = lax.psum_scatter(
            by_cols.astype(LOW), ("fsdp", "ctx"), scatter_dimension=1, tiled=True
        )
        by_cols = lax.all_gather(by_cols, "ctx", axis=1, tiled=True).astype(WIDE)
        grads[layer] = (by_rows, by_cols)
        vectors[layer] = jnp.stack(
            [sums_two[2], outer_bias_sum, sums_one[0], sums_one[1], sums_two[0], sums_two[1]]
        )
        outer_bias_sum = sums_one[2]
        biases[layer] = jnp.concatenate(
            [
                jnp.sum(grad_qkv.astype(WIDE), axis=1),
                jnp.sum(grad_inner.astype(WIDE), axis=0),
            ]
        )
    grad_hidden = grad_low.astype(WIDE)

    vector_sums = lax.psum(jnp.stack(vectors, axis=1), ("fsdp", "ctx", "tp"))
    bias_sums = lax.psum(jnp.stack(biases), ("fsdp", "ctx"))
    shard = output_bias.shape[1]
    vector_sums = lax.dynamic_slice_in_dim(
        vector_sums, lax.axis_index("fsdp") * shard, shard, axis=2
    )

    def stacked_rows(start, size):
        return jnp.stack([grads[layer][0][:, start : start + size] for layer in range(LAYERS)])

    def stacked_cols(start, size):
        return jnp.stack([grads[layer][1][start : start + size] for layer in range(LAYERS)])

    return (
        output.reshape(hidden.shape),
        grad_hidden.reshape(hidden.shape),
        stacked_rows(0, columns),
        stacked_rows(columns, columns),
        stacked_rows(2 * columns, columns),
        stacked_cols(0, columns),
        stacked_rows(3 * columns, hidden_local),
        stacked_cols(columns, hidden_local),
        bias_sums[:, :columns],
        bias_sums[:, 2 * columns : 3 * columns],
        bias_sums[:, 3 * columns :],
        vector_sums[0],
        vector_sums[1],
        vector_sums[2],
        vector_sums[3],
        vector_sums[4],
        vector_sums[5],
    )


def solution(mesh):
    in_specs = (
        P("fsdp", "ctx", None),
        P("fsdp", "ctx", None),
        P("fsdp"),
        P(None, "fsdp", "tp"),
        P(None, "fsdp", "tp"),
        P(None, "fsdp", "tp"),
        P(None, "tp", "fsdp"),
        P(None, "fsdp", "tp"),
        P(None, "tp", "fsdp"),
        P(None, "tp"),
        P(None, "tp"),
        P(None, "tp"),
        P(None, "fsdp"),
        P(None, "fsdp"),
        P(None, "fsdp"),
        P(None, "fsdp"),
        P(None, "fsdp"),
        P(None, "fsdp"),
    )
    out_specs = (
        P("fsdp", "ctx", None),
        P("fsdp", "ctx", None),
        P(None, "fsdp", "tp"),
        P(None, "fsdp", "tp"),
        P(None, "fsdp", "tp"),
        P(None, "tp", "fsdp"),
        P(None, "fsdp", "tp"),
        P(None, "tp", "fsdp"),
        P(None, "tp"),
        P(None, "tp"),
        P(None, "tp"),
        P(None, "fsdp"),
        P(None, "fsdp"),
        P(None, "fsdp"),
        P(None, "fsdp"),
        P(None, "fsdp"),
        P(None, "fsdp"),
    )
    return jax.shard_map(
        per_device, mesh=mesh, in_specs=in_specs, out_specs=out_specs, check_vma=False
    )
```

```python
import functools
import math
import jax
import jax.numpy as jnp
from jax import lax
from jax.experimental import pallas as pl
from jax.experimental.pallas import tpu as pltpu
from jax.sharding import PartitionSpec as P

MESH = pl.DeviceIdType.MESH
LOW = jnp.bfloat16
WIDE = jnp.float32
EPSILON = 1e-05
NEGATIVE = -1e30
HD = 80
PIECES = 4
LAYERS = 2
ROOT_HALF = 1.0 / math.sqrt(2.0)
DENSITY = 1.0 / math.sqrt(2.0 * math.pi)
REDUCE_LAG = 2
GATHER_LAG = 3


def norm_parts(values):
    average = jnp.mean(values, axis=-1, keepdims=True)
    centered = values - average
    spread = jnp.mean(centered * centered, axis=-1, keepdims=True)
    inverse = lax.rsqrt(spread + EPSILON)
    return (centered * inverse, inverse)


def norm_back(upstream, normal_hat, inverse, gain_full):
    scaled = upstream * gain_full
    first_mean = jnp.mean(scaled, axis=-1, keepdims=True)
    second_mean = jnp.mean(scaled * normal_hat, axis=-1, keepdims=True)
    return inverse * (scaled - first_mean - normal_hat * second_mean)


def line_exchange(n, own, pieces, partial, gathered, from_left, from_right, total, sems, finish):
    rs_send, rs_recv, ag_send, ag_recv = sems
    me = lax.axis_index("tp")
    piece = own // pieces
    to_right, to_left = {"tp": lax.rem(me + 1, n)}, {"tp": lax.rem(me + n - 1, n)}
    has_left, has_right = me > 0, me < n - 1

    barrier = pltpu.get_barrier_semaphore()

    @pl.when(has_left)
    def _():
        pl.semaphore_signal(barrier, inc=1, device_id=to_left, device_id_type=MESH)

    @pl.when(has_right)
    def _():
        pl.semaphore_signal(barrier, inc=1, device_id=to_right, device_id_type=MESH)

    pl.semaphore_wait(barrier, has_left.astype(jnp.int32) + has_right.astype(jnp.int32))

    def rows_of(shard, step):
        return pl.ds(pl.multiple_of(shard * own + step * piece, piece), piece)

    def reduce_copy(way, src, shard, step):
        rows = rows_of(shard, step)
        landing = from_left if way == 0 else from_right
        return pltpu.make_async_remote_copy(
            src_ref=src.at[rows],
            dst_ref=landing.at[rows],
            send_sem=rs_send.at[way, shard, step],
            recv_sem=rs_recv.at[way, shard, step],
            device_id=to_right if way == 0 else to_left,
            device_id_type=MESH,
        )

    def gather_copy(way, shard, step):
        rows = rows_of(shard, step)
        return pltpu.make_async_remote_copy(
            src_ref=gathered.at[rows],
            dst_ref=gathered.at[rows],
            send_sem=ag_send.at[way, shard, step],
            recv_sem=ag_recv.at[way, shard, step],
            device_id=to_right if way == 0 else to_left,
            device_id_type=MESH,
        )

    def reduce_one(way, shard, step):
        landing = from_left if way == 0 else from_right
        first = me == 0 if way == 0 else me == n - 1

        @pl.when(first)
        def _():
            reduce_copy(way, partial, shard, step).start()

        @pl.when(jnp.logical_not(first))
        def _():
            rows = rows_of(shard, step)
            reduce_copy(way, partial, shard, step).wait_recv()
            landing[rows, :] = (
                partial[rows, :].astype(WIDE) + landing[rows, :].astype(WIDE)
            ).astype(LOW)
            reduce_copy(way, landing, shard, step).start()

    def finish_one(step):
        rows = rows_of(me, step)
        total[...] = partial[rows, :].astype(WIDE)

        @pl.when(has_left)
        def _():
            reduce_copy(0, partial, me, step).wait_recv()
            total[...] += from_left[rows, :].astype(WIDE)

        @pl.when(has_right)
        def _():
            reduce_copy(1, partial, me, step).wait_recv()
            total[...] += from_right[rows, :].astype(WIDE)

        own_rows = pl.ds(pl.multiple_of(step * piece, piece), piece)
        gathered[rows, :] = finish(own_rows, total[...])

        @pl.when(has_right)
        def _():
            gather_copy(0, me, step).start()

        @pl.when(has_left)
        def _():
            gather_copy(1, me, step).start()

    def forward_one(way, shard, step):
        gather_copy(way, shard, step).wait_recv()

        @pl.when(has_right if way == 0 else has_left)
        def _():
            gather_copy(way, shard, step).start()

    period = n - 1

    def finish_at(device):
        from_start = jnp.where(device > 0, n - 1 - device + REDUCE_LAG * device, 0)
        from_end = jnp.where(device < n - 1, device + REDUCE_LAG * (n - 1 - device), 0)
        return jnp.maximum(from_start, from_end)

    def split(tick, start, length):
        since = tick - start
        clipped = jnp.maximum(since, 0)
        return (since >= 0) & (clipped < length), lax.div(clipped, period), lax.rem(clipped, period)

    def body(tick, carry):
        for way in range(2):
            hops = me if way == 0 else n - 1 - me
            due, step, k = split(tick, REDUCE_LAG * hops, pieces * period)
            shard = n - 1 - k if way == 0 else k
            mine = me < shard if way == 0 else me > shard

            @pl.when(due & mine)
            def _():
                reduce_one(way, shard, step)

        due, step, k = split(tick, finish_at(me), pieces * period)

        @pl.when(due & (k == 0))
        def _():
            finish_one(step)

        for hops in range(1, n):
            for way in range(2):
                shard = me - hops if way == 0 else me + hops
                there = shard >= 0 if way == 0 else shard <= n - 1
                due, step, k = split(
                    tick, finish_at(shard) + GATHER_LAG * hops, pieces * period
                )

                @pl.when(there & due & (k == 0))
                def _():
                    forward_one(way, shard, step)

        return carry

    ticks = period * (pieces - 1) + max(REDUCE_LAG, 1) * (n - 1) + GATHER_LAG * (n - 1) + 1
    lax.fori_loop(0, ticks, body, 0)

    def drain(step, carry):
        for k in range(n - 1):
            for way in range(2):
                shard = n - 1 - k if way == 0 else k
                sends = me < shard if way == 0 else me > shard

                @pl.when(sends)
                def _():
                    reduce_copy(way, partial, shard, step).wait_send()

        for k in range(n):
            for way in range(2):
                shard = me - k if way == 0 else me + k
                there = shard >= 0 if way == 0 else shard <= n - 1
                further = has_right if way == 0 else has_left

                @pl.when(there & further)
                def _():
                    gather_copy(way, shard, step).wait_send()

        return carry

    lax.fori_loop(0, pieces, drain, 0)


def exchange_scratch(n, rows, width, pieces):
    return [
        pltpu.VMEM((rows, width), LOW),
        pltpu.VMEM((rows, width), LOW),
        pltpu.VMEM((rows // n // pieces, width), WIDE),
        pltpu.SemaphoreType.DMA((2, n, pieces)),
        pltpu.SemaphoreType.DMA((2, n, pieces)),
        pltpu.SemaphoreType.DMA((2, n, pieces)),
        pltpu.SemaphoreType.DMA((2, n, pieces)),
    ]


def forward_exchange_kernel(
    n, pieces, partial, residual, bias, gain, shift, gathered, middle, from_left, from_right, total, *sems
):
    def finish(rows, value):
        mid = value + residual[rows, :] + bias[...]
        middle[rows, :] = mid
        hat, _ = norm_parts(mid)
        return (hat * gain[...] + shift[...]).astype(LOW)

    line_exchange(
        n, residual.shape[0], pieces, partial, gathered, from_left, from_right, total, sems, finish
    )


def backward_exchange_kernel(
    n, pieces, partial, grad_out, normal_in, gain, gathered, grad_in, sums, from_left, from_right, total, *sems
):
    sums[...] = jnp.zeros_like(sums)

    def finish(rows, upstream):
        hat, inverse = norm_parts(normal_in[rows, :])
        grad = grad_out[rows, :] + norm_back(upstream, hat, inverse, gain[...])
        grad_in[rows, :] = grad
        sums[0:1, :] += jnp.sum(upstream * hat, axis=0, keepdims=True)
        sums[1:2, :] += jnp.sum(upstream, axis=0, keepdims=True)
        sums[2:3, :] += jnp.sum(grad, axis=0, keepdims=True)
        return grad.astype(LOW)

    line_exchange(
        n, grad_out.shape[0], pieces, partial, gathered, from_left, from_right, total, sems, finish
    )


def in_vmem(count):
    return [pl.BlockSpec(memory_space=pltpu.VMEM)] * count


def forward_exchange(partial, residual, bias, gain, shift, n, collective_id):
    rows, width = partial.shape
    return pl.pallas_call(
        functools.partial(forward_exchange_kernel, n, PIECES),
        out_shape=(
            jax.ShapeDtypeStruct((rows, width), LOW),
            jax.ShapeDtypeStruct(residual.shape, WIDE),
        ),
        in_specs=in_vmem(5),
        out_specs=tuple(in_vmem(2)),
        scratch_shapes=exchange_scratch(n, rows, width, PIECES),
        compiler_params=pltpu.CompilerParams(
            collective_id=collective_id, has_side_effects=True, vmem_limit_bytes=40 << 20
        ),
        name="forward_exchange",
    )(partial, residual, bias[None, :], gain[None, :], shift[None, :])


def backward_exchange(partial, grad_out, normal_in, gain, n, collective_id):
    rows, width = partial.shape
    return pl.pallas_call(
        functools.partial(backward_exchange_kernel, n, PIECES),
        out_shape=(
            jax.ShapeDtypeStruct((rows, width), LOW),
            jax.ShapeDtypeStruct(grad_out.shape, WIDE),
            jax.ShapeDtypeStruct((8, width), WIDE),
        ),
        in_specs=in_vmem(4),
        out_specs=tuple(in_vmem(3)),
        scratch_shapes=exchange_scratch(n, rows, width, PIECES),
        compiler_params=pltpu.CompilerParams(
            collective_id=collective_id, has_side_effects=True, vmem_limit_bytes=40 << 20
        ),
        name="backward_exchange",
    )(partial, grad_out, normal_in, gain[None, :])


def attend_kernel(scale, length, qkv, out, out_wide, log_total, held, high, low_sum, sems_send, sems_recv):
    columns = qkv.shape[0] // 3
    frames = qkv.shape[1]
    heads = columns // HD
    me = lax.axis_index("ctx")

    def partner(r):
        return {"ctx": jnp.bitwise_xor(me, r)}

    barrier = pltpu.get_barrier_semaphore()
    for r in (1, 2):
        pl.semaphore_signal(barrier, inc=1, device_id=partner(r), device_id_type=MESH)
    pl.semaphore_wait(barrier, 2)

    def send(slot, part, to):
        rows = pl.ds(part * columns, columns)
        src = qkv.at[pl.ds((1 + part) * columns, columns)] if slot != 3 else held.at[1, rows]
        return pltpu.make_async_remote_copy(
            src_ref=src,
            dst_ref=held.at[slot - 1, rows],
            send_sem=sems_send.at[slot - 1, part],
            recv_sem=sems_recv.at[slot - 1, part],
            device_id=partner(to),
            device_id_type=MESH,
        )

    for part in range(2):
        send(2, part, 2).start()
    for part in range(2):
        send(1, part, 1).start()

    high[...] = jnp.full_like(high, NEGATIVE)
    low_sum[...] = jnp.zeros_like(low_sum)
    out_wide[...] = jnp.zeros_like(out_wide)
    limit = length[0]

    def block(keys_ref, key_row, value_row, slot):
        owner = jnp.bitwise_xor(me, slot)
        left = limit - owner * frames
        valid = lax.broadcasted_iota(jnp.int32, (frames, frames), 0) < left
        for h in range(heads):
            rows = pl.ds(h * HD, HD)
            keys = keys_ref[pl.ds(key_row + h * HD, HD), :]
            values = keys_ref[pl.ds(value_row + h * HD, HD), :]
            scores = lax.dot_general(
                keys, qkv[rows, :], (((0,), (0,)), ((), ())), preferred_element_type=WIDE
            )
            scores = jnp.where(valid, scores * scale, NEGATIVE)
            before = high[h : h + 1, :]
            now = jnp.maximum(before, jnp.max(scores, axis=0, keepdims=True))
            shrink = jnp.exp(before - now)
            raised = jnp.exp(scores - now)
            low_sum[h : h + 1, :] = low_sum[h : h + 1, :] * shrink + jnp.sum(
                raised, axis=0, keepdims=True
            )
            high[h : h + 1, :] = now
            out_wide[rows, :] = out_wide[rows, :] * shrink + jnp.dot(
                values, raised.astype(LOW), preferred_element_type=WIDE
            )

    block(qkv, columns, 2 * columns, 0)
    for part in range(2):
        send(1, part, 1).wait_recv()
    block(held.at[0], 0, columns, 1)
    for part in range(2):
        send(2, part, 2).wait_recv()
        send(3, part, 1).start()
    block(held.at[1], 0, columns, 2)
    for part in range(2):
        send(3, part, 1).wait_recv()
    block(held.at[2], 0, columns, 3)
    for h in range(heads):
        rows = pl.ds(h * HD, HD)
        total = low_sum[h : h + 1, :]
        done = out_wide[rows, :] / total
        out_wide[rows, :] = done
        out[rows, :] = done.astype(LOW)
        log_total[h : h + 1, :] = high[h : h + 1, :] + jnp.log(total)
    for slot in (1, 2, 3):
        for part in range(2):
            send(slot, part, 2 if slot == 2 else 1).wait_send()


def attend(qkv, length, scale, collective_id):
    columns, frames = qkv.shape[0] // 3, qkv.shape[1]
    return pl.pallas_call(
        functools.partial(attend_kernel, scale),
        out_shape=(
            jax.ShapeDtypeStruct((columns, frames), LOW),
            jax.ShapeDtypeStruct((columns, frames), WIDE),
            jax.ShapeDtypeStruct((8, frames), WIDE),
            jax.ShapeDtypeStruct((3, 2 * columns, frames), LOW),
        ),
        in_specs=[pl.BlockSpec(memory_space=pltpu.SMEM)] + in_vmem(1),
        out_specs=tuple(in_vmem(4)),
        scratch_shapes=[
            pltpu.VMEM((8, frames), WIDE),
            pltpu.VMEM((8, frames), WIDE),
            pltpu.SemaphoreType.DMA((3, 2)),
            pltpu.SemaphoreType.DMA((3, 2)),
        ],
        compiler_params=pltpu.CompilerParams(
            collective_id=collective_id, has_side_effects=True, vmem_limit_bytes=56 << 20
        ),
        name="attend",
    )(length, qkv)


def attend_back_kernel(
    scale, length, qkv, held, grad, out_wide, log_total, grad_qkv, mine, parts, landed, acc, sems_send, sems_recv
):
    columns = qkv.shape[0] // 3
    frames = qkv.shape[1]
    heads = columns // HD
    me = lax.axis_index("ctx")

    def partner(r):
        return {"ctx": jnp.bitwise_xor(me, r)}

    barrier = pltpu.get_barrier_semaphore()
    for r in (1, 2):
        pl.semaphore_signal(barrier, inc=1, device_id=partner(r), device_id_type=MESH)
    pl.semaphore_wait(barrier, 2)

    def send(at, part, to):
        rows = pl.ds(part * columns, columns)
        return pltpu.make_async_remote_copy(
            src_ref=parts.at[at, rows],
            dst_ref=landed.at[at, rows],
            send_sem=sems_send.at[at, part],
            recv_sem=sems_recv.at[at, part],
            device_id=partner(to),
            device_id_type=MESH,
        )

    acc[...] = jnp.zeros_like(acc)
    limit = length[0]

    def block(keys_ref, key_row, value_row, slot, store):
        owner = jnp.bitwise_xor(me, slot)
        left = limit - owner * frames
        valid = lax.broadcasted_iota(jnp.int32, (frames, frames), 0) < left
        for h in range(heads):
            rows = pl.ds(h * HD, HD)
            keys = keys_ref[pl.ds(key_row + h * HD, HD), :]
            values = keys_ref[pl.ds(value_row + h * HD, HD), :]
            queries = qkv[rows, :]
            upstream = grad[rows, :]
            scores = lax.dot_general(
                keys, queries, (((0,), (0,)), ((), ())), preferred_element_type=WIDE
            )
            weights = jnp.where(valid, jnp.exp(scores * scale - log_total[h : h + 1, :]), 0.0)
            grad_weights = lax.dot_general(
                values, upstream, (((0,), (0,)), ((), ())), preferred_element_type=WIDE
            )
            row_terms = jnp.sum(
                upstream.astype(WIDE) * out_wide[rows, :], axis=0, keepdims=True
            )
            grad_scores = (weights * (grad_weights - row_terms)).astype(LOW)
            acc[rows, :] += jnp.dot(keys, grad_scores, preferred_element_type=WIDE)
            grad_keys = (
                lax.dot_general(
                    queries, grad_scores, (((1,), (1,)), ((), ())), preferred_element_type=WIDE
                )
                * scale
            )
            grad_values = lax.dot_general(
                upstream, weights.astype(LOW), (((1,), (1,)), ((), ())), preferred_element_type=WIDE
            )
            store(h * HD, grad_keys, grad_values)

    def store_part(at):
        def store(row, grad_keys, grad_values):
            parts[at, pl.ds(row, HD), :] = grad_keys.astype(LOW)
            parts[at, pl.ds(columns + row, HD), :] = grad_values.astype(LOW)

        return store

    def store_mine(row, grad_keys, grad_values):
        mine[pl.ds(row, HD), :] = grad_keys
        mine[pl.ds(columns + row, HD), :] = grad_values

    def store_joined(row, grad_keys, grad_values):
        for start, value in ((row, grad_keys), (columns + row, grad_values)):
            rows = pl.ds(start, HD)
            parts[1, rows, :] = (value + landed[0, rows, :].astype(WIDE)).astype(LOW)

    block(held.at[2], 0, columns, 3, store_part(0))
    for part in range(2):
        send(0, part, 1).start()
    for part in range(2):
        send(0, part, 1).wait_recv()
    block(held.at[1], 0, columns, 2, store_joined)
    for part in range(2):
        send(1, part, 2).start()
    block(held.at[0], 0, columns, 1, store_part(2))
    for part in range(2):
        send(2, part, 1).start()
    block(qkv, columns, 2 * columns, 0, store_mine)
    grad_qkv[0:columns, :] = (acc[...] * scale).astype(LOW)
    for part in range(2):
        send(2, part, 1).wait_recv()
    for part in range(2):
        send(1, part, 2).wait_recv()
    grad_qkv[columns:, :] = (
        mine[...] + landed[1].astype(WIDE) + landed[2].astype(WIDE)
    ).astype(LOW)
    for at in range(3):
        for part in range(2):
            send(at, part, 2 if at == 1 else 1).wait_send()


def attend_back(qkv, held, grad, out_wide, log_total, length, scale, collective_id):
    columns, frames = qkv.shape[0] // 3, qkv.shape[1]
    return pl.pallas_call(
        functools.partial(attend_back_kernel, scale),
        out_shape=jax.ShapeDtypeStruct((3 * columns, frames), LOW),
        in_specs=[pl.BlockSpec(memory_space=pltpu.SMEM)] + in_vmem(5),
        out_specs=in_vmem(1)[0],
        scratch_shapes=[
            pltpu.VMEM((2 * columns, frames), WIDE),
            pltpu.VMEM((3, 2 * columns, frames), LOW),
            pltpu.VMEM((3, 2 * columns, frames), LOW),
            pltpu.VMEM((columns, frames), WIDE),
            pltpu.SemaphoreType.DMA((3, 2)),
            pltpu.SemaphoreType.DMA((3, 2)),
        ],
        compiler_params=pltpu.CompilerParams(
            collective_id=collective_id, has_side_effects=True, vmem_limit_bytes=56 << 20
        ),
        name="attend_back",
    )(length, qkv, held, grad, out_wide, log_total)


def gelu_value(values):
    return 0.5 * values * (1.0 + lax.erf(values * ROOT_HALF))


def gelu_slope(values):
    return 0.5 * (1.0 + lax.erf(values * ROOT_HALF)) + values * DENSITY * jnp.exp(
        -0.5 * values * values
    )


def product(left_side, right_side, left_axis, right_axis):
    return lax.dot_general(
        left_side,
        right_side,
        (((left_axis,), (right_axis,)), ((), ())),
        preferred_element_type=WIDE,
    )


def per_device(
    hidden,
    cotangent,
    lengths,
    query_weight,
    key_weight,
    value_weight,
    output_weight,
    inner_weight,
    outer_weight,
    query_bias,
    value_bias,
    inner_bias,
    output_bias,
    outer_bias,
    first_gain,
    first_shift,
    second_gain,
    second_shift,
):
    clip_count, rows, width = hidden.shape
    assert clip_count == 1
    assert lax.axis_size("ctx") == 4
    tp_size = lax.axis_size("tp")
    own_rows = rows // tp_size
    columns = query_weight.shape[2]
    hidden_local = inner_weight.shape[2]
    scale = 1.0 / math.sqrt(HD)
    own_start = lax.axis_index("tp") * own_rows

    def own_slice(full):
        return lax.dynamic_slice_in_dim(full, own_start, own_rows, axis=0)

    small = jnp.concatenate(
        [output_bias, outer_bias, first_gain, first_shift, second_gain, second_shift], axis=0
    ).astype(LOW)
    small = lax.all_gather(small, "fsdp", axis=1, tiled=True).astype(WIDE)

    def vector(kind, layer):
        return small[kind * LAYERS + layer]

    def fetch(layer):
        qkv = jnp.concatenate(
            [query_weight[layer], key_weight[layer], value_weight[layer]], axis=1
        ).astype(LOW)
        qkv = lax.all_gather(qkv, "fsdp", axis=0, tiled=True)
        out = lax.all_gather(output_weight[layer].astype(LOW), "fsdp", axis=1, tiled=True)
        inner = lax.all_gather(inner_weight[layer].astype(LOW), "fsdp", axis=0, tiled=True)
        outer = lax.all_gather(outer_weight[layer].astype(LOW), "fsdp", axis=1, tiled=True)
        return (qkv, out, inner, outer)

    weights = [fetch(layer) for layer in range(LAYERS)]

    hidden_rows = hidden.reshape(rows, width)
    residual = own_slice(hidden_rows)
    hat_full, _ = norm_parts(hidden_rows)
    normed = (hat_full * vector(2, 0) + vector(3, 0)).astype(LOW)
    kept = []
    for layer in range(LAYERS):
        w_qkv, w_out, w_inner, w_outer = weights[layer]
        bias_qkv = jnp.concatenate(
            [query_bias[layer], jnp.zeros_like(query_bias[layer]), value_bias[layer]]
        )
        qkv = (product(w_qkv, normed, 0, 1) + bias_qkv[:, None]).astype(LOW)
        attended, attended_wide, log_total, held = attend(qkv, lengths, scale, 2 * layer)
        branch = product(attended, w_out, 0, 0).astype(LOW)
        normed_two, middle = forward_exchange(
            branch, residual, vector(0, layer), vector(4, layer), vector(5, layer), tp_size, 2 * layer + 4
        )
        inner_pre = product(normed_two, w_inner, 1, 0) + inner_bias[layer]
        active = gelu_value(inner_pre).astype(LOW)
        kept.append(
            (residual, normed, qkv, attended, attended_wide, log_total, held, middle, normed_two, inner_pre, active)
        )
        branch = product(active, w_outer, 1, 0).astype(LOW)
        if layer + 1 < LAYERS:
            normed, residual = forward_exchange(
                branch,
                middle,
                vector(1, layer),
                vector(2, layer + 1),
                vector(3, layer + 1),
                tp_size,
                2 * layer + 5,
            )
        else:
            branch = lax.psum_scatter(branch, "tp", scatter_dimension=0, tiled=True).astype(WIDE)
            residual = middle + branch + vector(1, layer)
            output = lax.all_gather(residual.astype(LOW), "tp", axis=0, tiled=True).astype(WIDE)

    grad_rows = cotangent.reshape(rows, width)
    grad_own = own_slice(grad_rows)
    grad_low = grad_rows.astype(LOW)
    outer_bias_sum = jnp.sum(grad_own, axis=0)
    grads = [None] * LAYERS
    vectors = [None] * LAYERS
    biases = [None] * LAYERS
    for layer in reversed(range(LAYERS)):
        w_qkv, w_out, w_inner, w_outer = weights[layer]
        (
            residual,
            normed,
            qkv,
            attended,
            attended_wide,
            log_total,
            held,
            middle,
            normed_two,
            inner_pre,
            active,
        ) = kept[layer]
        grad_active = product(grad_low, w_outer, 1, 1)
        grad_inner = (grad_active * gelu_slope(inner_pre)).astype(LOW)
        branch = product(grad_inner, w_inner, 1, 1).astype(LOW)
        grad_mid_low, grad_middle, sums_two = backward_exchange(
            branch, grad_own, middle, vector(4, layer), tp_size, 2 * layer + 8
        )
        grad_outer_w = product(active, grad_low, 0, 0)
        grad_inner_w = product(normed_two, grad_inner, 0, 0)
        grad_attended = product(w_out, grad_mid_low, 1, 1).astype(LOW)
        grad_qkv = attend_back(
            qkv, held, grad_attended, attended_wide, log_total, lengths, scale, 2 * layer + 12
        )
        grad_output_w = product(attended, grad_mid_low, 1, 0)
        branch = product(grad_qkv, w_qkv, 0, 1).astype(LOW)
        by_rows = jnp.concatenate(
            [product(normed, grad_qkv, 0, 1).astype(LOW), grad_inner_w.astype(LOW)], axis=1
        )
        by_cols = jnp.concatenate([grad_output_w.astype(LOW), grad_outer_w.astype(LOW)], axis=0)
        branch, by_rows, by_cols = lax.optimization_barrier((branch, by_rows, by_cols))
        grad_low, grad_own, sums_one = backward_exchange(
            branch, grad_middle, residual, vector(2, layer), tp_size, 2 * layer + 9
        )
        by_rows = lax.psum_scatter(
            by_rows, ("fsdp", "ctx"), scatter_dimension=0, tiled=True
        )
        by_rows = lax.all_gather(by_rows, "ctx", axis=0, tiled=True).astype(WIDE)
        by_cols = lax.psum_scatter(
            by_cols, ("fsdp", "ctx"), scatter_dimension=1, tiled=True
        )
        by_cols = lax.all_gather(by_cols, "ctx", axis=1, tiled=True).astype(WIDE)
        grads[layer] = (by_rows, by_cols)
        own_sums = jnp.concatenate(
            [
                jnp.sum(grad_qkv.astype(WIDE), axis=1),
                jnp.sum(grad_inner.astype(WIDE), axis=0),
            ]
        )
        placed = jnp.where(
            jnp.arange(tp_size)[:, None] == lax.axis_index("tp"), own_sums[None, :], 0.0
        )
        vector_parts = jnp.stack(
            [sums_two[2], outer_bias_sum, sums_one[0], sums_one[1], sums_two[0], sums_two[1]]
        )
        outer_bias_sum = sums_one[2]
        summed = lax.psum(
            jnp.concatenate([placed.reshape(-1), vector_parts.reshape(-1)]), ("fsdp", "ctx", "tp")
        )
        biases[layer] = lax.dynamic_slice_in_dim(
            summed, lax.axis_index("tp") * own_sums.shape[0], own_sums.shape[0]
        )
        vectors[layer] = summed[placed.size :].reshape(vector_parts.shape)
    grad_hidden = grad_low.astype(WIDE)

    vector_sums = jnp.stack(vectors, axis=1)
    bias_sums = jnp.stack(biases)
    shard = output_bias.shape[1]
    vector_sums = lax.dynamic_slice_in_dim(
        vector_sums, lax.axis_index("fsdp") * shard, shard, axis=2
    )

    def stacked_rows(start, size):
        return jnp.stack([grads[layer][0][:, start : start + size] for layer in range(LAYERS)])

    def stacked_cols(start, size):
        return jnp.stack([grads[layer][1][start : start + size] for layer in range(LAYERS)])

    return (
        output.reshape(hidden.shape),
        grad_hidden.reshape(hidden.shape),
        stacked_rows(0, columns),
        stacked_rows(columns, columns),
        stacked_rows(2 * columns, columns),
        stacked_cols(0, columns),
        stacked_rows(3 * columns, hidden_local),
        stacked_cols(columns, hidden_local),
        bias_sums[:, :columns],
        bias_sums[:, 2 * columns : 3 * columns],
        bias_sums[:, 3 * columns :],
        vector_sums[0],
        vector_sums[1],
        vector_sums[2],
        vector_sums[3],
        vector_sums[4],
        vector_sums[5],
    )


def solution(mesh):
    in_specs = (
        P("fsdp", "ctx", None),
        P("fsdp", "ctx", None),
        P("fsdp"),
        P(None, "fsdp", "tp"),
        P(None, "fsdp", "tp"),
        P(None, "fsdp", "tp"),
        P(None, "tp", "fsdp"),
        P(None, "fsdp", "tp"),
        P(None, "tp", "fsdp"),
        P(None, "tp"),
        P(None, "tp"),
        P(None, "tp"),
        P(None, "fsdp"),
        P(None, "fsdp"),
        P(None, "fsdp"),
        P(None, "fsdp"),
        P(None, "fsdp"),
        P(None, "fsdp"),
    )
    out_specs = (
        P("fsdp", "ctx", None),
        P("fsdp", "ctx", None),
        P(None, "fsdp", "tp"),
        P(None, "fsdp", "tp"),
        P(None, "fsdp", "tp"),
        P(None, "tp", "fsdp"),
        P(None, "fsdp", "tp"),
        P(None, "tp", "fsdp"),
        P(None, "tp"),
        P(None, "tp"),
        P(None, "tp"),
        P(None, "fsdp"),
        P(None, "fsdp"),
        P(None, "fsdp"),
        P(None, "fsdp"),
        P(None, "fsdp"),
        P(None, "fsdp"),
    )
    return jax.shard_map(
        per_device, mesh=mesh, in_specs=in_specs, out_specs=out_specs, check_vma=False
    )
```

```python
import functools
import math
import jax
import jax.numpy as jnp
from jax import lax
from jax.experimental import pallas as pl
from jax.experimental.pallas import tpu as pltpu
from jax.sharding import PartitionSpec as P

MESH = pl.DeviceIdType.MESH
LOW = jnp.bfloat16
WIDE = jnp.float32
EPSILON = 1e-05
NEGATIVE = -1e30
HD = 80
PIECES = 4
LAYERS = 2
ROOT_HALF = 1.0 / math.sqrt(2.0)
DENSITY = 1.0 / math.sqrt(2.0 * math.pi)
REDUCE_LAG = 2
GATHER_LAG = 3


def norm_parts(values):
    average = jnp.mean(values, axis=-1, keepdims=True)
    centered = values - average
    spread = jnp.mean(centered * centered, axis=-1, keepdims=True)
    inverse = lax.rsqrt(spread + EPSILON)
    return (centered * inverse, inverse)


def norm_back(upstream, normal_hat, inverse, gain_full):
    scaled = upstream * gain_full
    first_mean = jnp.mean(scaled, axis=-1, keepdims=True)
    second_mean = jnp.mean(scaled * normal_hat, axis=-1, keepdims=True)
    return inverse * (scaled - first_mean - normal_hat * second_mean)


def line_exchange(n, own, pieces, partial, gathered, from_left, from_right, total, sems, finish, side=None):
    rs_send, rs_recv, ag_send, ag_recv = sems
    me = lax.axis_index("tp")
    piece = own // pieces
    to_right, to_left = {"tp": lax.rem(me + 1, n)}, {"tp": lax.rem(me + n - 1, n)}
    has_left, has_right = me > 0, me < n - 1

    barrier = pltpu.get_barrier_semaphore()

    @pl.when(has_left)
    def _():
        pl.semaphore_signal(barrier, inc=1, device_id=to_left, device_id_type=MESH)

    @pl.when(has_right)
    def _():
        pl.semaphore_signal(barrier, inc=1, device_id=to_right, device_id_type=MESH)

    peers = has_left.astype(jnp.int32) + has_right.astype(jnp.int32)
    if side is not None:
        for peer in side.peers:
            pl.semaphore_signal(barrier, inc=1, device_id=peer, device_id_type=MESH)
        peers = peers + len(side.peers)
    pl.semaphore_wait(barrier, peers)
    if side is not None:
        side.start()

    def rows_of(shard, step):
        return pl.ds(pl.multiple_of(shard * own + step * piece, piece), piece)

    def reduce_copy(way, src, shard, step):
        rows = rows_of(shard, step)
        landing = from_left if way == 0 else from_right
        return pltpu.make_async_remote_copy(
            src_ref=src.at[rows],
            dst_ref=landing.at[rows],
            send_sem=rs_send.at[way, shard, step],
            recv_sem=rs_recv.at[way, shard, step],
            device_id=to_right if way == 0 else to_left,
            device_id_type=MESH,
        )

    def gather_copy(way, shard, step):
        rows = rows_of(shard, step)
        return pltpu.make_async_remote_copy(
            src_ref=gathered.at[rows],
            dst_ref=gathered.at[rows],
            send_sem=ag_send.at[way, shard, step],
            recv_sem=ag_recv.at[way, shard, step],
            device_id=to_right if way == 0 else to_left,
            device_id_type=MESH,
        )

    def reduce_one(way, shard, step):
        landing = from_left if way == 0 else from_right
        first = me == 0 if way == 0 else me == n - 1

        @pl.when(first)
        def _():
            reduce_copy(way, partial, shard, step).start()

        @pl.when(jnp.logical_not(first))
        def _():
            rows = rows_of(shard, step)
            reduce_copy(way, partial, shard, step).wait_recv()
            landing[rows, :] = (
                partial[rows, :].astype(WIDE) + landing[rows, :].astype(WIDE)
            ).astype(LOW)
            reduce_copy(way, landing, shard, step).start()

    def finish_one(step):
        rows = rows_of(me, step)
        total[...] = partial[rows, :].astype(WIDE)

        @pl.when(has_left)
        def _():
            reduce_copy(0, partial, me, step).wait_recv()
            total[...] += from_left[rows, :].astype(WIDE)

        @pl.when(has_right)
        def _():
            reduce_copy(1, partial, me, step).wait_recv()
            total[...] += from_right[rows, :].astype(WIDE)

        own_rows = pl.ds(pl.multiple_of(step * piece, piece), piece)
        gathered[rows, :] = finish(own_rows, total[...])

        @pl.when(has_right)
        def _():
            gather_copy(0, me, step).start()

        @pl.when(has_left)
        def _():
            gather_copy(1, me, step).start()

    def forward_one(way, shard, step):
        gather_copy(way, shard, step).wait_recv()

        @pl.when(has_right if way == 0 else has_left)
        def _():
            gather_copy(way, shard, step).start()

    period = n - 1

    def finish_at(device):
        from_start = jnp.where(device > 0, n - 1 - device + REDUCE_LAG * device, 0)
        from_end = jnp.where(device < n - 1, device + REDUCE_LAG * (n - 1 - device), 0)
        return jnp.maximum(from_start, from_end)

    def split(tick, start, length):
        since = tick - start
        clipped = jnp.maximum(since, 0)
        return (since >= 0) & (clipped < length), lax.div(clipped, period), lax.rem(clipped, period)

    def body(tick, carry):
        for way in range(2):
            hops = me if way == 0 else n - 1 - me
            due, step, k = split(tick, REDUCE_LAG * hops, pieces * period)
            shard = n - 1 - k if way == 0 else k
            mine = me < shard if way == 0 else me > shard

            @pl.when(due & mine)
            def _():
                reduce_one(way, shard, step)

        due, step, k = split(tick, finish_at(me), pieces * period)

        @pl.when(due & (k == 0))
        def _():
            finish_one(step)

        for hops in range(1, n):
            for way in range(2):
                shard = me - hops if way == 0 else me + hops
                there = shard >= 0 if way == 0 else shard <= n - 1
                due, step, k = split(
                    tick, finish_at(shard) + GATHER_LAG * hops, pieces * period
                )

                @pl.when(there & due & (k == 0))
                def _():
                    forward_one(way, shard, step)

        if side is not None:
            side.at(tick)
        return carry

    ticks = period * (pieces - 1) + max(REDUCE_LAG, 1) * (n - 1) + GATHER_LAG * (n - 1) + 1
    if side is not None:
        ticks = max(ticks, side.ticks)
    lax.fori_loop(0, ticks, body, 0)
    if side is not None:
        side.drain()

    def drain(step, carry):
        for k in range(n - 1):
            for way in range(2):
                shard = n - 1 - k if way == 0 else k
                sends = me < shard if way == 0 else me > shard

                @pl.when(sends)
                def _():
                    reduce_copy(way, partial, shard, step).wait_send()

        for k in range(n):
            for way in range(2):
                shard = me - k if way == 0 else me + k
                there = shard >= 0 if way == 0 else shard <= n - 1
                further = has_right if way == 0 else has_left

                @pl.when(there & further)
                def _():
                    gather_copy(way, shard, step).wait_send()

        return carry

    lax.fori_loop(0, pieces, drain, 0)


def exchange_scratch(n, rows, width, pieces):
    return [
        pltpu.VMEM((rows, width), LOW),
        pltpu.VMEM((rows, width), LOW),
        pltpu.VMEM((rows // n // pieces, width), WIDE),
        pltpu.SemaphoreType.DMA((2, n, pieces)),
        pltpu.SemaphoreType.DMA((2, n, pieces)),
        pltpu.SemaphoreType.DMA((2, n, pieces)),
        pltpu.SemaphoreType.DMA((2, n, pieces)),
    ]


def forward_exchange_kernel(
    n, pieces, partial, residual, bias, gain, shift, gathered, middle, from_left, from_right, total, *sems
):
    def finish(rows, value):
        mid = value + residual[rows, :] + bias[...]
        middle[rows, :] = mid
        hat, _ = norm_parts(mid)
        return (hat * gain[...] + shift[...]).astype(LOW)

    line_exchange(
        n, residual.shape[0], pieces, partial, gathered, from_left, from_right, total, sems, finish
    )


def backward_exchange_kernel(
    n, pieces, partial, grad_out, normal_in, gain, gathered, grad_in, sums, from_left, from_right, total, *sems, side=None
):
    sums[...] = jnp.zeros_like(sums)

    def finish(rows, upstream):
        hat, inverse = norm_parts(normal_in[rows, :])
        grad = grad_out[rows, :] + norm_back(upstream, hat, inverse, gain[...])
        grad_in[rows, :] = grad
        sums[0:1, :] += jnp.sum(upstream * hat, axis=0, keepdims=True)
        sums[1:2, :] += jnp.sum(upstream, axis=0, keepdims=True)
        sums[2:3, :] += jnp.sum(grad, axis=0, keepdims=True)
        return grad.astype(LOW)

    line_exchange(
        n, grad_out.shape[0], pieces, partial, gathered, from_left, from_right, total, sems, finish, side
    )


def in_vmem(count):
    return [pl.BlockSpec(memory_space=pltpu.VMEM)] * count


CHUNKS = 10


class GradientSum:
    LAGS = (1, 5, 9, 12)

    def __init__(self, arrays, outs, landings, sems):
        self.arrays, self.outs, self.landings = arrays, outs, landings
        self.sends, self.recvs = sems
        self.half = lax.axis_index("fsdp")
        self.ctx = lax.axis_index("ctx")
        self.core = lax.rem(self.ctx, 2)
        pair = {"ctx": jnp.bitwise_xor(self.ctx, 1)}
        across = {"ctx": jnp.bitwise_xor(self.ctx, 2)}
        other = {"fsdp": 1 - self.half}
        self.peers = (pair, across, other)
        self.ticks = 2 * (CHUNKS - 1) + self.LAGS[3] + 1

    def view(self, which, half, core, chunk):
        rows, cols = self.arrays[which].shape
        if which == 0:
            part = rows // 4
            height = part // CHUNKS
            start = half * (2 * part) + core * part + chunk * height
            return pl.ds(pl.multiple_of(start, 16), height), slice(None)
        part = rows // 2
        height = part // CHUNKS
        start = core * part + chunk * height
        width = cols // 2
        return (
            pl.ds(pl.multiple_of(start, 16), height),
            pl.ds(pl.multiple_of(half * width, 128), width),
        )

    def out_rows(self, which, core, chunk):
        part = self.outs[which].shape[0] // 2
        height = part // CHUNKS
        return pl.ds(pl.multiple_of(core * part + chunk * height, 8), height)

    def copy(self, which, stage, chunk, half=0):
        pair, across, other = self.peers
        landing = self.landings[which]
        if stage == 0:
            src = self.arrays[which].at[self.view(which, half, 1 - self.core, chunk)]
            slot, peer = half, pair
        elif stage == 1:
            src = landing.at[1 - self.half, chunk]
            slot, peer = 2, other
        elif stage == 2:
            src = landing.at[2, chunk]
            slot, peer = 3, across
        else:
            src = landing.at[3, chunk]
            slot, peer = 4, pair
        return pltpu.make_async_remote_copy(
            src_ref=src,
            dst_ref=landing.at[slot, chunk],
            send_sem=self.sends.at[which, slot, chunk],
            recv_sem=self.recvs.at[which, slot, chunk],
            device_id=peer,
            device_id_type=MESH,
        )

    def start(self):
        def body(chunk, carry):
            for which in range(2):
                for half in range(2):
                    self.copy(which, 0, chunk, half).start()
            return carry

        lax.fori_loop(0, CHUNKS, body, 0)

    def when_due(self, tick, lag, action):
        since = tick - lag
        clipped = jnp.maximum(since, 0)
        chunk = lax.div(clipped, 2)

        @pl.when((since >= 0) & (lax.rem(clipped, 2) == 0) & (chunk < CHUNKS))
        def _():
            for which in range(2):
                action(which, chunk)

    def at(self, tick):
        def joined(which, chunk):
            landing = self.landings[which]
            for half in range(2):
                self.copy(which, 0, chunk, half).wait_recv()
                rows, cols = self.view(which, half, self.core, chunk)
                landing[half, chunk] = (
                    self.arrays[which][rows, cols].astype(WIDE) + landing[half, chunk].astype(WIDE)
                ).astype(LOW)
            self.copy(which, 1, chunk).start()

        def crossed(which, chunk):
            landing = self.landings[which]
            self.copy(which, 1, chunk).wait_recv()
            landing[2, chunk] = (
                landing[self.half, chunk].astype(WIDE) + landing[2, chunk].astype(WIDE)
            ).astype(LOW)
            self.copy(which, 2, chunk).start()

        def summed(which, chunk):
            landing = self.landings[which]
            self.copy(which, 2, chunk).wait_recv()
            low = (landing[2, chunk].astype(WIDE) + landing[3, chunk].astype(WIDE)).astype(LOW)
            landing[3, chunk] = low
            self.outs[which][self.out_rows(which, self.core, chunk), :] = low.astype(WIDE)
            self.copy(which, 3, chunk).start()

        def shared(which, chunk):
            self.copy(which, 3, chunk).wait_recv()
            self.outs[which][self.out_rows(which, 1 - self.core, chunk), :] = self.landings[which][
                4, chunk
            ].astype(WIDE)

        for lag, action in zip(self.LAGS, (joined, crossed, summed, shared)):
            self.when_due(tick, lag, action)

    def drain(self):
        def body(chunk, carry):
            for which in range(2):
                for half in range(2):
                    self.copy(which, 0, chunk, half).wait_send()
                for stage in range(1, 4):
                    self.copy(which, stage, chunk).wait_send()
            return carry

        lax.fori_loop(0, CHUNKS, body, 0)


def gradient_shapes(by_rows, by_cols):
    rows, cols = by_rows.shape
    rows_two, cols_two = by_cols.shape
    outs = (
        jax.ShapeDtypeStruct((rows // 2, cols), WIDE),
        jax.ShapeDtypeStruct((rows_two, cols_two // 2), WIDE),
    )
    landings = [
        pltpu.VMEM((5, CHUNKS, rows // 4 // CHUNKS, cols), LOW),
        pltpu.VMEM((5, CHUNKS, rows_two // 2 // CHUNKS, cols_two // 2), LOW),
    ]
    return outs, landings


def backward_gradient_kernel(
    n, pieces, partial, grad_out, normal_in, gain, by_rows, by_cols, gathered, grad_in, sums, out_rows, out_cols,
    from_left, from_right, total, rs_send, rs_recv, ag_send, ag_recv, landing_rows, landing_cols, side_send, side_recv
):
    side = GradientSum(
        (by_rows, by_cols), (out_rows, out_cols), (landing_rows, landing_cols), (side_send, side_recv)
    )
    backward_exchange_kernel(
        n, pieces, partial, grad_out, normal_in, gain, gathered, grad_in, sums, from_left, from_right, total,
        rs_send, rs_recv, ag_send, ag_recv, side=side
    )


def sum_all_kernel(axes, shared_rows, values, out, landing, sends, recvs):
    steps = [(axis, 1 << b) for axis, size in axes for b in range(size.bit_length() - 1)]

    def peer(axis, k):
        return {axis: jnp.bitwise_xor(lax.axis_index(axis), k)}

    barrier = pltpu.get_barrier_semaphore()
    for axis, k in steps:
        pl.semaphore_signal(barrier, inc=1, device_id=peer(axis, k), device_id_type=MESH)
    pl.semaphore_wait(barrier, len(steps))
    out[...] = values[...]
    for at, (axis, k) in enumerate(steps):
        rows = pl.ds(0, shared_rows) if axis == "tp" else pl.ds(0, values.shape[0])
        landing[at, 0, rows] = out[rows, :]
        copy = pltpu.make_async_remote_copy(
            src_ref=landing.at[at, 0, rows],
            dst_ref=landing.at[at, 1, rows],
            send_sem=sends.at[at],
            recv_sem=recvs.at[at],
            device_id=peer(axis, k),
            device_id_type=MESH,
        )
        copy.start()
        copy.wait()
        out[rows, :] = landing[at, 0, rows] + landing[at, 1, rows]


def sum_all(values, shared_rows, axes, collective_id):
    steps = sum(size.bit_length() - 1 for _, size in axes)
    return pl.pallas_call(
        functools.partial(sum_all_kernel, axes, shared_rows),
        out_shape=jax.ShapeDtypeStruct(values.shape, WIDE),
        in_specs=in_vmem(1),
        out_specs=in_vmem(1)[0],
        scratch_shapes=[
            pltpu.VMEM((steps, 2) + values.shape, WIDE),
            pltpu.SemaphoreType.DMA((steps,)),
            pltpu.SemaphoreType.DMA((steps,)),
        ],
        compiler_params=pltpu.CompilerParams(collective_id=collective_id, has_side_effects=True),
        name="sum_all",
    )(values)


def forward_exchange(partial, residual, bias, gain, shift, n, collective_id):
    rows, width = partial.shape
    return pl.pallas_call(
        functools.partial(forward_exchange_kernel, n, PIECES),
        out_shape=(
            jax.ShapeDtypeStruct((rows, width), LOW),
            jax.ShapeDtypeStruct(residual.shape, WIDE),
        ),
        in_specs=in_vmem(5),
        out_specs=tuple(in_vmem(2)),
        scratch_shapes=exchange_scratch(n, rows, width, PIECES),
        compiler_params=pltpu.CompilerParams(
            collective_id=collective_id, has_side_effects=True, vmem_limit_bytes=40 << 20
        ),
        name="forward_exchange",
    )(partial, residual, bias[None, :], gain[None, :], shift[None, :])


def backward_exchange(partial, grad_out, normal_in, gain, n, collective_id, by_rows=None, by_cols=None):
    rows, width = partial.shape
    out_shape = (
        jax.ShapeDtypeStruct((rows, width), LOW),
        jax.ShapeDtypeStruct(grad_out.shape, WIDE),
        jax.ShapeDtypeStruct((8, width), WIDE),
    )
    scratch = exchange_scratch(n, rows, width, PIECES)
    kernel, extra = backward_exchange_kernel, ()
    if by_rows is not None:
        outs, landings = gradient_shapes(by_rows, by_cols)
        out_shape = out_shape + outs
        scratch = scratch + landings + [pltpu.SemaphoreType.DMA((2, 5, CHUNKS))] * 2
        kernel, extra = backward_gradient_kernel, (by_rows, by_cols)
    return pl.pallas_call(
        functools.partial(kernel, n, PIECES),
        out_shape=out_shape,
        in_specs=in_vmem(4 + len(extra)),
        out_specs=tuple(in_vmem(len(out_shape))),
        scratch_shapes=scratch,
        compiler_params=pltpu.CompilerParams(
            collective_id=collective_id, has_side_effects=True, vmem_limit_bytes=56 << 20
        ),
        name="backward_exchange",
    )(partial, grad_out, normal_in, gain[None, :], *extra)


def attend_kernel(scale, length, qkv, out, out_wide, log_total, held, high, low_sum, sems_send, sems_recv):
    columns = qkv.shape[0] // 3
    frames = qkv.shape[1]
    heads = columns // HD
    me = lax.axis_index("ctx")

    def partner(r):
        return {"ctx": jnp.bitwise_xor(me, r)}

    barrier = pltpu.get_barrier_semaphore()
    for r in (1, 2):
        pl.semaphore_signal(barrier, inc=1, device_id=partner(r), device_id_type=MESH)
    pl.semaphore_wait(barrier, 2)

    def send(slot, part, to):
        rows = pl.ds(part * columns, columns)
        src = qkv.at[pl.ds((1 + part) * columns, columns)] if slot != 3 else held.at[1, rows]
        return pltpu.make_async_remote_copy(
            src_ref=src,
            dst_ref=held.at[slot - 1, rows],
            send_sem=sems_send.at[slot - 1, part],
            recv_sem=sems_recv.at[slot - 1, part],
            device_id=partner(to),
            device_id_type=MESH,
        )

    for part in range(2):
        send(2, part, 2).start()
    for part in range(2):
        send(1, part, 1).start()

    high[...] = jnp.full_like(high, NEGATIVE)
    low_sum[...] = jnp.zeros_like(low_sum)
    out_wide[...] = jnp.zeros_like(out_wide)
    limit = length[0]

    def block(keys_ref, key_row, value_row, slot):
        owner = jnp.bitwise_xor(me, slot)
        left = limit - owner * frames
        valid = lax.broadcasted_iota(jnp.int32, (frames, frames), 0) < left
        for h in range(heads):
            rows = pl.ds(h * HD, HD)
            keys = keys_ref[pl.ds(key_row + h * HD, HD), :]
            values = keys_ref[pl.ds(value_row + h * HD, HD), :]
            scores = lax.dot_general(
                keys, qkv[rows, :], (((0,), (0,)), ((), ())), preferred_element_type=WIDE
            )
            scores = jnp.where(valid, scores * scale, NEGATIVE)
            before = high[h : h + 1, :]
            now = jnp.maximum(before, jnp.max(scores, axis=0, keepdims=True))
            shrink = jnp.exp(before - now)
            raised = jnp.exp(scores - now)
            low_sum[h : h + 1, :] = low_sum[h : h + 1, :] * shrink + jnp.sum(
                raised, axis=0, keepdims=True
            )
            high[h : h + 1, :] = now
            out_wide[rows, :] = out_wide[rows, :] * shrink + jnp.dot(
                values, raised.astype(LOW), preferred_element_type=WIDE
            )

    block(qkv, columns, 2 * columns, 0)
    for part in range(2):
        send(1, part, 1).wait_recv()
    block(held.at[0], 0, columns, 1)
    for part in range(2):
        send(2, part, 2).wait_recv()
        send(3, part, 1).start()
    block(held.at[1], 0, columns, 2)
    for part in range(2):
        send(3, part, 1).wait_recv()
    block(held.at[2], 0, columns, 3)
    for h in range(heads):
        rows = pl.ds(h * HD, HD)
        total = low_sum[h : h + 1, :]
        done = out_wide[rows, :] / total
        out_wide[rows, :] = done
        out[rows, :] = done.astype(LOW)
        log_total[h : h + 1, :] = high[h : h + 1, :] + jnp.log(total)
    for slot in (1, 2, 3):
        for part in range(2):
            send(slot, part, 2 if slot == 2 else 1).wait_send()


def attend(qkv, length, scale, collective_id):
    columns, frames = qkv.shape[0] // 3, qkv.shape[1]
    return pl.pallas_call(
        functools.partial(attend_kernel, scale),
        out_shape=(
            jax.ShapeDtypeStruct((columns, frames), LOW),
            jax.ShapeDtypeStruct((columns, frames), WIDE),
            jax.ShapeDtypeStruct((8, frames), WIDE),
            jax.ShapeDtypeStruct((3, 2 * columns, frames), LOW),
        ),
        in_specs=[pl.BlockSpec(memory_space=pltpu.SMEM)] + in_vmem(1),
        out_specs=tuple(in_vmem(4)),
        scratch_shapes=[
            pltpu.VMEM((8, frames), WIDE),
            pltpu.VMEM((8, frames), WIDE),
            pltpu.SemaphoreType.DMA((3, 2)),
            pltpu.SemaphoreType.DMA((3, 2)),
        ],
        compiler_params=pltpu.CompilerParams(
            collective_id=collective_id, has_side_effects=True, vmem_limit_bytes=56 << 20
        ),
        name="attend",
    )(length, qkv)


def attend_back_kernel(
    scale, length, qkv, held, grad, out_wide, log_total, grad_qkv, mine, parts, landed, acc, sems_send, sems_recv
):
    columns = qkv.shape[0] // 3
    frames = qkv.shape[1]
    heads = columns // HD
    me = lax.axis_index("ctx")

    def partner(r):
        return {"ctx": jnp.bitwise_xor(me, r)}

    barrier = pltpu.get_barrier_semaphore()
    for r in (1, 2):
        pl.semaphore_signal(barrier, inc=1, device_id=partner(r), device_id_type=MESH)
    pl.semaphore_wait(barrier, 2)

    def send(at, part, to):
        rows = pl.ds(part * columns, columns)
        return pltpu.make_async_remote_copy(
            src_ref=parts.at[at, rows],
            dst_ref=landed.at[at, rows],
            send_sem=sems_send.at[at, part],
            recv_sem=sems_recv.at[at, part],
            device_id=partner(to),
            device_id_type=MESH,
        )

    acc[...] = jnp.zeros_like(acc)
    limit = length[0]

    def block(keys_ref, key_row, value_row, slot, store):
        owner = jnp.bitwise_xor(me, slot)
        left = limit - owner * frames
        valid = lax.broadcasted_iota(jnp.int32, (frames, frames), 0) < left
        for h in range(heads):
            rows = pl.ds(h * HD, HD)
            keys = keys_ref[pl.ds(key_row + h * HD, HD), :]
            values = keys_ref[pl.ds(value_row + h * HD, HD), :]
            queries = qkv[rows, :]
            upstream = grad[rows, :]
            scores = lax.dot_general(
                keys, queries, (((0,), (0,)), ((), ())), preferred_element_type=WIDE
            )
            weights = jnp.where(valid, jnp.exp(scores * scale - log_total[h : h + 1, :]), 0.0)
            grad_weights = lax.dot_general(
                values, upstream, (((0,), (0,)), ((), ())), preferred_element_type=WIDE
            )
            row_terms = jnp.sum(
                upstream.astype(WIDE) * out_wide[rows, :], axis=0, keepdims=True
            )
            grad_scores = (weights * (grad_weights - row_terms)).astype(LOW)
            acc[rows, :] += jnp.dot(keys, grad_scores, preferred_element_type=WIDE)
            grad_keys = (
                lax.dot_general(
                    queries, grad_scores, (((1,), (1,)), ((), ())), preferred_element_type=WIDE
                )
                * scale
            )
            grad_values = lax.dot_general(
                upstream, weights.astype(LOW), (((1,), (1,)), ((), ())), preferred_element_type=WIDE
            )
            store(h * HD, grad_keys, grad_values)

    def store_part(at):
        def store(row, grad_keys, grad_values):
            parts[at, pl.ds(row, HD), :] = grad_keys.astype(LOW)
            parts[at, pl.ds(columns + row, HD), :] = grad_values.astype(LOW)

        return store

    def store_mine(row, grad_keys, grad_values):
        mine[pl.ds(row, HD), :] = grad_keys
        mine[pl.ds(columns + row, HD), :] = grad_values

    def store_joined(row, grad_keys, grad_values):
        for start, value in ((row, grad_keys), (columns + row, grad_values)):
            rows = pl.ds(start, HD)
            parts[1, rows, :] = (value + landed[0, rows, :].astype(WIDE)).astype(LOW)

    block(held.at[2], 0, columns, 3, store_part(0))
    for part in range(2):
        send(0, part, 1).start()
    for part in range(2):
        send(0, part, 1).wait_recv()
    block(held.at[1], 0, columns, 2, store_joined)
    for part in range(2):
        send(1, part, 2).start()
    block(held.at[0], 0, columns, 1, store_part(2))
    for part in range(2):
        send(2, part, 1).start()
    block(qkv, columns, 2 * columns, 0, store_mine)
    grad_qkv[0:columns, :] = (acc[...] * scale).astype(LOW)
    for part in range(2):
        send(2, part, 1).wait_recv()
    for part in range(2):
        send(1, part, 2).wait_recv()
    grad_qkv[columns:, :] = (
        mine[...] + landed[1].astype(WIDE) + landed[2].astype(WIDE)
    ).astype(LOW)
    for at in range(3):
        for part in range(2):
            send(at, part, 2 if at == 1 else 1).wait_send()


def attend_back(qkv, held, grad, out_wide, log_total, length, scale, collective_id):
    columns, frames = qkv.shape[0] // 3, qkv.shape[1]
    return pl.pallas_call(
        functools.partial(attend_back_kernel, scale),
        out_shape=jax.ShapeDtypeStruct((3 * columns, frames), LOW),
        in_specs=[pl.BlockSpec(memory_space=pltpu.SMEM)] + in_vmem(5),
        out_specs=in_vmem(1)[0],
        scratch_shapes=[
            pltpu.VMEM((2 * columns, frames), WIDE),
            pltpu.VMEM((3, 2 * columns, frames), LOW),
            pltpu.VMEM((3, 2 * columns, frames), LOW),
            pltpu.VMEM((columns, frames), WIDE),
            pltpu.SemaphoreType.DMA((3, 2)),
            pltpu.SemaphoreType.DMA((3, 2)),
        ],
        compiler_params=pltpu.CompilerParams(
            collective_id=collective_id, has_side_effects=True, vmem_limit_bytes=56 << 20
        ),
        name="attend_back",
    )(length, qkv, held, grad, out_wide, log_total)


def gelu_value(values):
    return 0.5 * values * (1.0 + lax.erf(values * ROOT_HALF))


def gelu_slope(values):
    return 0.5 * (1.0 + lax.erf(values * ROOT_HALF)) + values * DENSITY * jnp.exp(
        -0.5 * values * values
    )


def product(left_side, right_side, left_axis, right_axis):
    return lax.dot_general(
        left_side,
        right_side,
        (((left_axis,), (right_axis,)), ((), ())),
        preferred_element_type=WIDE,
    )


def per_device(
    hidden,
    cotangent,
    lengths,
    query_weight,
    key_weight,
    value_weight,
    output_weight,
    inner_weight,
    outer_weight,
    query_bias,
    value_bias,
    inner_bias,
    output_bias,
    outer_bias,
    first_gain,
    first_shift,
    second_gain,
    second_shift,
):
    clip_count, rows, width = hidden.shape
    assert clip_count == 1
    assert lax.axis_size("ctx") == 4
    tp_size = lax.axis_size("tp")
    own_rows = rows // tp_size
    columns = query_weight.shape[2]
    hidden_local = inner_weight.shape[2]
    scale = 1.0 / math.sqrt(HD)
    own_start = lax.axis_index("tp") * own_rows

    def own_slice(full):
        return lax.dynamic_slice_in_dim(full, own_start, own_rows, axis=0)

    small = jnp.concatenate(
        [output_bias, outer_bias, first_gain, first_shift, second_gain, second_shift], axis=0
    ).astype(LOW)
    small = lax.all_gather(small, "fsdp", axis=1, tiled=True).astype(WIDE)

    def vector(kind, layer):
        return small[kind * LAYERS + layer]

    def fetch(layer):
        qkv = jnp.concatenate(
            [query_weight[layer], key_weight[layer], value_weight[layer]], axis=1
        ).astype(LOW)
        qkv = lax.all_gather(qkv, "fsdp", axis=0, tiled=True)
        out = lax.all_gather(output_weight[layer].astype(LOW), "fsdp", axis=1, tiled=True)
        inner = lax.all_gather(inner_weight[layer].astype(LOW), "fsdp", axis=0, tiled=True)
        outer = lax.all_gather(outer_weight[layer].astype(LOW), "fsdp", axis=1, tiled=True)
        return (qkv, out, inner, outer)

    weights = [fetch(layer) for layer in range(LAYERS)]

    hidden_rows = hidden.reshape(rows, width)
    residual = own_slice(hidden_rows)
    hat_full, _ = norm_parts(hidden_rows)
    normed = (hat_full * vector(2, 0) + vector(3, 0)).astype(LOW)
    kept = []
    for layer in range(LAYERS):
        w_qkv, w_out, w_inner, w_outer = weights[layer]
        bias_qkv = jnp.concatenate(
            [query_bias[layer], jnp.zeros_like(query_bias[layer]), value_bias[layer]]
        )
        qkv = (product(w_qkv, normed, 0, 1) + bias_qkv[:, None]).astype(LOW)
        attended, attended_wide, log_total, held = attend(qkv, lengths, scale, 2 * layer)
        branch = product(attended, w_out, 0, 0).astype(LOW)
        normed_two, middle = forward_exchange(
            branch, residual, vector(0, layer), vector(4, layer), vector(5, layer), tp_size, 2 * layer + 4
        )
        inner_pre = product(normed_two, w_inner, 1, 0) + inner_bias[layer]
        active = gelu_value(inner_pre).astype(LOW)
        kept.append(
            (residual, normed, qkv, attended, attended_wide, log_total, held, middle, normed_two, inner_pre, active)
        )
        branch = product(active, w_outer, 1, 0).astype(LOW)
        if layer + 1 < LAYERS:
            normed, residual = forward_exchange(
                branch,
                middle,
                vector(1, layer),
                vector(2, layer + 1),
                vector(3, layer + 1),
                tp_size,
                2 * layer + 5,
            )
        else:
            branch = lax.psum_scatter(branch, "tp", scatter_dimension=0, tiled=True).astype(WIDE)
            residual = middle + branch + vector(1, layer)
            output = lax.all_gather(residual.astype(LOW), "tp", axis=0, tiled=True).astype(WIDE)

    def exchange_back(branch, grad_out, normal_in, gain, collective_id, by_rows, by_cols):
        if lax.axis_size("fsdp") == 2:
            return backward_exchange(
                branch, grad_out, normal_in, gain, tp_size, collective_id, by_rows, by_cols
            )
        first = backward_exchange(branch, grad_out, normal_in, gain, tp_size, collective_id)
        by_rows = lax.psum_scatter(by_rows, ("fsdp", "ctx"), scatter_dimension=0, tiled=True)
        by_rows = lax.all_gather(by_rows, "ctx", axis=0, tiled=True).astype(WIDE)
        by_cols = lax.psum_scatter(by_cols, ("fsdp", "ctx"), scatter_dimension=1, tiled=True)
        by_cols = lax.all_gather(by_cols, "ctx", axis=1, tiled=True).astype(WIDE)
        return (*first, by_rows, by_cols)

    grad_rows = cotangent.reshape(rows, width)
    grad_own = own_slice(grad_rows)
    grad_low = grad_rows.astype(LOW)
    outer_bias_sum = jnp.sum(grad_own, axis=0)
    grads = [None] * LAYERS
    vectors = [None] * LAYERS
    biases = [None] * LAYERS
    for layer in reversed(range(LAYERS)):
        w_qkv, w_out, w_inner, w_outer = weights[layer]
        (
            residual,
            normed,
            qkv,
            attended,
            attended_wide,
            log_total,
            held,
            middle,
            normed_two,
            inner_pre,
            active,
        ) = kept[layer]
        grad_active = product(grad_low, w_outer, 1, 1)
        grad_inner = (grad_active * gelu_slope(inner_pre)).astype(LOW)
        branch = product(grad_inner, w_inner, 1, 1).astype(LOW)
        grad_outer_w = product(active, grad_low, 0, 0).astype(LOW)
        grad_inner_w = product(normed_two, grad_inner, 0, 0).astype(LOW)
        grad_mid_low, grad_middle, sums_two, *summed_two = exchange_back(
            branch, grad_own, middle, vector(4, layer), 2 * layer + 8, grad_inner_w, grad_outer_w
        )
        grad_attended = product(w_out, grad_mid_low, 1, 1).astype(LOW)
        grad_qkv = attend_back(
            qkv, held, grad_attended, attended_wide, log_total, lengths, scale, 2 * layer + 12
        )
        grad_output_w = product(attended, grad_mid_low, 1, 0).astype(LOW)
        branch = product(grad_qkv, w_qkv, 0, 1).astype(LOW)
        grad_qkv_w = product(normed, grad_qkv, 0, 1).astype(LOW)
        grad_low, grad_own, sums_one, *summed_one = exchange_back(
            branch, grad_middle, residual, vector(2, layer), 2 * layer + 9, grad_qkv_w, grad_output_w
        )
        grads[layer] = (*summed_one, *summed_two)
        vectors[layer] = [
            sums_two[2], outer_bias_sum, sums_one[0], sums_one[1], sums_two[0], sums_two[1]
        ]
        outer_bias_sum = sums_one[2]
        biases[layer] = jnp.concatenate(
            [
                jnp.sum(grad_qkv.astype(WIDE), axis=1),
                jnp.sum(grad_inner.astype(WIDE), axis=0),
            ]
        )
    grad_hidden = grad_low.astype(WIDE)

    flat_biases = jnp.concatenate(biases)
    bias_rows = -(-flat_biases.size // width)
    flat_biases = jnp.pad(flat_biases, (0, bias_rows * width - flat_biases.size))
    vector_count = 6 * LAYERS
    shared_rows = -(-vector_count // 8) * 8
    total_rows = shared_rows + -(-bias_rows // 8) * 8
    small_sums = jnp.concatenate(
        [
            jnp.stack([row for parts in zip(*vectors) for row in parts]),
            jnp.zeros((shared_rows - vector_count, width), WIDE),
            flat_biases.reshape(bias_rows, width),
            jnp.zeros((total_rows - shared_rows - bias_rows, width), WIDE),
        ]
    )
    small_sums = sum_all(
        small_sums, shared_rows, tuple((axis, lax.axis_size(axis)) for axis in ("ctx", "fsdp", "tp")), 16
    )
    shard = output_bias.shape[1]
    vector_sums = lax.dynamic_slice_in_dim(
        small_sums[:vector_count].reshape(6, LAYERS, width), lax.axis_index("fsdp") * shard, shard, axis=2
    )
    bias_sums = small_sums[shared_rows:].reshape(-1)[: LAYERS * biases[0].size].reshape(LAYERS, -1)

    def stacked(which, start=0, size=None):
        size = grads[0][which].shape[1] if size is None else size
        return jnp.stack([grads[layer][which][:, start : start + size] for layer in range(LAYERS)])

    return (
        output.reshape(hidden.shape),
        grad_hidden.reshape(hidden.shape),
        stacked(0, 0, columns),
        stacked(0, columns, columns),
        stacked(0, 2 * columns, columns),
        stacked(1),
        stacked(2),
        stacked(3),
        bias_sums[:, :columns],
        bias_sums[:, 2 * columns : 3 * columns],
        bias_sums[:, 3 * columns :],
        vector_sums[0],
        vector_sums[1],
        vector_sums[2],
        vector_sums[3],
        vector_sums[4],
        vector_sums[5],
    )


def solution(mesh):
    in_specs = (
        P("fsdp", "ctx", None),
        P("fsdp", "ctx", None),
        P("fsdp"),
        P(None, "fsdp", "tp"),
        P(None, "fsdp", "tp"),
        P(None, "fsdp", "tp"),
        P(None, "tp", "fsdp"),
        P(None, "fsdp", "tp"),
        P(None, "tp", "fsdp"),
        P(None, "tp"),
        P(None, "tp"),
        P(None, "tp"),
        P(None, "fsdp"),
        P(None, "fsdp"),
        P(None, "fsdp"),
        P(None, "fsdp"),
        P(None, "fsdp"),
        P(None, "fsdp"),
    )
    out_specs = (
        P("fsdp", "ctx", None),
        P("fsdp", "ctx", None),
        P(None, "fsdp", "tp"),
        P(None, "fsdp", "tp"),
        P(None, "fsdp", "tp"),
        P(None, "tp", "fsdp"),
        P(None, "fsdp", "tp"),
        P(None, "tp", "fsdp"),
        P(None, "tp"),
        P(None, "tp"),
        P(None, "tp"),
        P(None, "fsdp"),
        P(None, "fsdp"),
        P(None, "fsdp"),
        P(None, "fsdp"),
        P(None, "fsdp"),
        P(None, "fsdp"),
    )
    return jax.shard_map(
        per_device, mesh=mesh, in_specs=in_specs, out_specs=out_specs, check_vma=False
    )
```

```python
import functools
import math
import jax
import jax.numpy as jnp
from jax import lax
from jax.experimental import pallas as pl
from jax.experimental.pallas import tpu as pltpu
from jax.sharding import PartitionSpec as P

MESH = pl.DeviceIdType.MESH
LOW = jnp.bfloat16
WIDE = jnp.float32
EPSILON = 1e-05
NEGATIVE = -1e30
HD = 80
PIECES = 4
LAYERS = 2
ROOT_HALF = 1.0 / math.sqrt(2.0)
DENSITY = 1.0 / math.sqrt(2.0 * math.pi)
REDUCE_LAG = 2
GATHER_LAG = 3


def norm_parts(values):
    average = jnp.mean(values, axis=-1, keepdims=True)
    centered = values - average
    spread = jnp.mean(centered * centered, axis=-1, keepdims=True)
    inverse = lax.rsqrt(spread + EPSILON)
    return (centered * inverse, inverse)


def norm_back(upstream, normal_hat, inverse, gain_full):
    scaled = upstream * gain_full
    first_mean = jnp.mean(scaled, axis=-1, keepdims=True)
    second_mean = jnp.mean(scaled * normal_hat, axis=-1, keepdims=True)
    return inverse * (scaled - first_mean - normal_hat * second_mean)


def line_exchange(n, own, pieces, partial, gathered, from_left, from_right, total, sems, finish, side=None):
    rs_send, rs_recv, ag_send, ag_recv = sems
    me = lax.axis_index("tp")
    piece = own // pieces
    to_right, to_left = {"tp": lax.rem(me + 1, n)}, {"tp": lax.rem(me + n - 1, n)}
    has_left, has_right = me > 0, me < n - 1

    barrier = pltpu.get_barrier_semaphore()

    @pl.when(has_left)
    def _():
        pl.semaphore_signal(barrier, inc=1, device_id=to_left, device_id_type=MESH)

    @pl.when(has_right)
    def _():
        pl.semaphore_signal(barrier, inc=1, device_id=to_right, device_id_type=MESH)

    peers = has_left.astype(jnp.int32) + has_right.astype(jnp.int32)
    if side is not None:
        for peer in side.peers:
            pl.semaphore_signal(barrier, inc=1, device_id=peer, device_id_type=MESH)
        peers = peers + len(side.peers)
    pl.semaphore_wait(barrier, peers)
    if side is not None:
        side.start()

    def rows_of(shard, step):
        return pl.ds(pl.multiple_of(shard * own + step * piece, piece), piece)

    def reduce_copy(way, src, shard, step):
        rows = rows_of(shard, step)
        landing = from_left if way == 0 else from_right
        return pltpu.make_async_remote_copy(
            src_ref=src.at[rows],
            dst_ref=landing.at[rows],
            send_sem=rs_send.at[way, shard, step],
            recv_sem=rs_recv.at[way, shard, step],
            device_id=to_right if way == 0 else to_left,
            device_id_type=MESH,
        )

    def gather_copy(way, shard, step):
        rows = rows_of(shard, step)
        return pltpu.make_async_remote_copy(
            src_ref=gathered.at[rows],
            dst_ref=gathered.at[rows],
            send_sem=ag_send.at[way, shard, step],
            recv_sem=ag_recv.at[way, shard, step],
            device_id=to_right if way == 0 else to_left,
            device_id_type=MESH,
        )

    def reduce_one(way, shard, step):
        landing = from_left if way == 0 else from_right
        first = me == 0 if way == 0 else me == n - 1

        @pl.when(first)
        def _():
            reduce_copy(way, partial, shard, step).start()

        @pl.when(jnp.logical_not(first))
        def _():
            rows = rows_of(shard, step)
            reduce_copy(way, partial, shard, step).wait_recv()
            landing[rows, :] = (
                partial[rows, :].astype(WIDE) + landing[rows, :].astype(WIDE)
            ).astype(LOW)
            reduce_copy(way, landing, shard, step).start()

    def finish_one(step):
        rows = rows_of(me, step)
        total[...] = partial[rows, :].astype(WIDE)

        @pl.when(has_left)
        def _():
            reduce_copy(0, partial, me, step).wait_recv()
            total[...] += from_left[rows, :].astype(WIDE)

        @pl.when(has_right)
        def _():
            reduce_copy(1, partial, me, step).wait_recv()
            total[...] += from_right[rows, :].astype(WIDE)

        own_rows = pl.ds(pl.multiple_of(step * piece, piece), piece)
        gathered[rows, :] = finish(own_rows, total[...])

        @pl.when(has_right)
        def _():
            gather_copy(0, me, step).start()

        @pl.when(has_left)
        def _():
            gather_copy(1, me, step).start()

    def forward_one(way, shard, step):
        gather_copy(way, shard, step).wait_recv()

        @pl.when(has_right if way == 0 else has_left)
        def _():
            gather_copy(way, shard, step).start()

    period = n - 1

    def finish_at(device):
        from_start = jnp.where(device > 0, n - 1 - device + REDUCE_LAG * device, 0)
        from_end = jnp.where(device < n - 1, device + REDUCE_LAG * (n - 1 - device), 0)
        return jnp.maximum(from_start, from_end)

    def split(tick, start, length):
        since = tick - start
        clipped = jnp.maximum(since, 0)
        return (since >= 0) & (clipped < length), lax.div(clipped, period), lax.rem(clipped, period)

    def body(tick, carry):
        for way in range(2):
            hops = me if way == 0 else n - 1 - me
            due, step, k = split(tick, REDUCE_LAG * hops, pieces * period)
            shard = n - 1 - k if way == 0 else k
            mine = me < shard if way == 0 else me > shard

            @pl.when(due & mine)
            def _():
                reduce_one(way, shard, step)

        due, step, k = split(tick, finish_at(me), pieces * period)

        @pl.when(due & (k == 0))
        def _():
            finish_one(step)

        for hops in range(1, n):
            for way in range(2):
                shard = me - hops if way == 0 else me + hops
                there = shard >= 0 if way == 0 else shard <= n - 1
                due, step, k = split(
                    tick, finish_at(shard) + GATHER_LAG * hops, pieces * period
                )

                @pl.when(there & due & (k == 0))
                def _():
                    forward_one(way, shard, step)

        if side is not None:
            side.at(tick)
        return carry

    ticks = period * (pieces - 1) + max(REDUCE_LAG, 1) * (n - 1) + GATHER_LAG * (n - 1) + 1
    if side is not None:
        ticks = max(ticks, side.ticks)
    lax.fori_loop(0, ticks, body, 0)
    if side is not None:
        side.drain()

    def drain(step, carry):
        for k in range(n - 1):
            for way in range(2):
                shard = n - 1 - k if way == 0 else k
                sends = me < shard if way == 0 else me > shard

                @pl.when(sends)
                def _():
                    reduce_copy(way, partial, shard, step).wait_send()

        for k in range(n):
            for way in range(2):
                shard = me - k if way == 0 else me + k
                there = shard >= 0 if way == 0 else shard <= n - 1
                further = has_right if way == 0 else has_left

                @pl.when(there & further)
                def _():
                    gather_copy(way, shard, step).wait_send()

        return carry

    lax.fori_loop(0, pieces, drain, 0)


def exchange_scratch(n, rows, width, pieces):
    return [
        pltpu.VMEM((rows, width), LOW),
        pltpu.VMEM((rows, width), LOW),
        pltpu.VMEM((rows // n // pieces, width), WIDE),
        pltpu.SemaphoreType.DMA((2, n, pieces)),
        pltpu.SemaphoreType.DMA((2, n, pieces)),
        pltpu.SemaphoreType.DMA((2, n, pieces)),
        pltpu.SemaphoreType.DMA((2, n, pieces)),
    ]


def forward_exchange_kernel(
    n, pieces, partial, residual, bias, gain, shift, gathered, middle, from_left, from_right, total, *sems
):
    def finish(rows, value):
        mid = value + residual[rows, :] + bias[...]
        middle[rows, :] = mid
        hat, _ = norm_parts(mid)
        return (hat * gain[...] + shift[...]).astype(LOW)

    line_exchange(
        n, residual.shape[0], pieces, partial, gathered, from_left, from_right, total, sems, finish
    )


def backward_exchange_kernel(
    n, pieces, partial, grad_out, normal_in, gain, gathered, grad_in, sums, from_left, from_right, total, *sems, side=None
):
    sums[...] = jnp.zeros_like(sums)

    def finish(rows, upstream):
        hat, inverse = norm_parts(normal_in[rows, :])
        grad = grad_out[rows, :] + norm_back(upstream, hat, inverse, gain[...])
        grad_in[rows, :] = grad
        sums[0:1, :] += jnp.sum(upstream * hat, axis=0, keepdims=True)
        sums[1:2, :] += jnp.sum(upstream, axis=0, keepdims=True)
        sums[2:3, :] += jnp.sum(grad, axis=0, keepdims=True)
        return grad.astype(LOW)

    line_exchange(
        n, grad_out.shape[0], pieces, partial, gathered, from_left, from_right, total, sems, finish, side
    )


def in_vmem(count):
    return [pl.BlockSpec(memory_space=pltpu.VMEM)] * count


class GradientSum:
    LAGS = (0, 3, 6, 9)

    def __init__(self, arrays, outs, landings, sems):
        self.chunks = landings[0].shape[1]
        self.arrays, self.outs, self.landings = arrays, outs, landings
        self.sends, self.recvs = sems
        self.half = lax.axis_index("fsdp")
        self.ctx = lax.axis_index("ctx")
        self.core = lax.rem(self.ctx, 2)
        pair = {"ctx": jnp.bitwise_xor(self.ctx, 1)}
        across = {"ctx": jnp.bitwise_xor(self.ctx, 2)}
        other = {"fsdp": 1 - self.half}
        self.peers = (pair, across, other)
        self.ticks = 2 * (self.chunks - 1) + self.LAGS[3] + 1

    def view(self, which, half, core, chunk):
        rows, cols = self.arrays[which].shape
        if which == 0:
            part = rows // 4
            height = part // self.chunks
            start = half * (2 * part) + core * part + chunk * height
            return pl.ds(pl.multiple_of(start, 16), height), slice(None)
        part = rows // 2
        height = part // self.chunks
        start = core * part + chunk * height
        width = cols // 2
        return (
            pl.ds(pl.multiple_of(start, 16), height),
            pl.ds(pl.multiple_of(half * width, 128), width),
        )

    def out_rows(self, which, core, chunk):
        part = self.outs[which].shape[0] // 2
        height = part // self.chunks
        return pl.ds(pl.multiple_of(core * part + chunk * height, 8), height)

    def copy(self, which, stage, chunk, half=0):
        pair, across, other = self.peers
        landing = self.landings[which]
        if stage == 0:
            src = self.arrays[which].at[self.view(which, half, 1 - self.core, chunk)]
            slot, peer = half, pair
        elif stage == 1:
            src = landing.at[1 - self.half, chunk]
            slot, peer = 2, other
        elif stage == 2:
            src = landing.at[2, chunk]
            slot, peer = 3, across
        else:
            src = landing.at[3, chunk]
            slot, peer = 4, pair
        return pltpu.make_async_remote_copy(
            src_ref=src,
            dst_ref=landing.at[slot, chunk],
            send_sem=self.sends.at[which, slot, chunk],
            recv_sem=self.recvs.at[which, slot, chunk],
            device_id=peer,
            device_id_type=MESH,
        )

    def start(self):
        def body(chunk, carry):
            for which in range(2):
                for half in range(2):
                    self.copy(which, 0, chunk, half).start()
            return carry

        lax.fori_loop(0, self.chunks, body, 0)

    def when_due(self, tick, lag, action):
        since = tick - lag
        clipped = jnp.maximum(since, 0)
        chunk = lax.div(clipped, 2)

        @pl.when((since >= 0) & (lax.rem(clipped, 2) == 0) & (chunk < self.chunks))
        def _():
            for which in range(2):
                action(which, chunk)

    def at(self, tick):
        def joined(which, chunk):
            landing = self.landings[which]
            for half in range(2):
                self.copy(which, 0, chunk, half).wait_recv()
                rows, cols = self.view(which, half, self.core, chunk)
                landing[half, chunk] = (
                    self.arrays[which][rows, cols].astype(WIDE) + landing[half, chunk].astype(WIDE)
                ).astype(LOW)
            self.copy(which, 1, chunk).start()

        def crossed(which, chunk):
            landing = self.landings[which]
            self.copy(which, 1, chunk).wait_recv()
            landing[2, chunk] = (
                landing[self.half, chunk].astype(WIDE) + landing[2, chunk].astype(WIDE)
            ).astype(LOW)
            self.copy(which, 2, chunk).start()

        def summed(which, chunk):
            landing = self.landings[which]
            self.copy(which, 2, chunk).wait_recv()
            low = (landing[2, chunk].astype(WIDE) + landing[3, chunk].astype(WIDE)).astype(LOW)
            landing[3, chunk] = low
            self.outs[which][self.out_rows(which, self.core, chunk), :] = low.astype(WIDE)
            self.copy(which, 3, chunk).start()

        def shared(which, chunk):
            self.copy(which, 3, chunk).wait_recv()
            self.outs[which][self.out_rows(which, 1 - self.core, chunk), :] = self.landings[which][
                4, chunk
            ].astype(WIDE)

        for lag, action in zip(self.LAGS, (joined, crossed, summed, shared)):
            self.when_due(tick, lag, action)

    def drain(self):
        def body(chunk, carry):
            for which in range(2):
                for half in range(2):
                    self.copy(which, 0, chunk, half).wait_send()
                for stage in range(1, 4):
                    self.copy(which, stage, chunk).wait_send()
            return carry

        lax.fori_loop(0, self.chunks, body, 0)


def gradient_shapes(by_rows, by_cols):
    rows, cols = by_rows.shape
    rows_two, cols_two = by_cols.shape
    chunks = 10 if rows_two >= rows else 5
    outs = (
        jax.ShapeDtypeStruct((rows // 2, cols), WIDE),
        jax.ShapeDtypeStruct((rows_two, cols_two // 2), WIDE),
    )
    landings = [
        pltpu.VMEM((5, chunks, rows // 4 // chunks, cols), LOW),
        pltpu.VMEM((5, chunks, rows_two // 2 // chunks, cols_two // 2), LOW),
    ]
    return outs, landings, pltpu.SemaphoreType.DMA((2, 5, chunks))


def backward_gradient_kernel(
    n, pieces, partial, grad_out, normal_in, gain, by_rows, by_cols, gathered, grad_in, sums, out_rows, out_cols,
    from_left, from_right, total, rs_send, rs_recv, ag_send, ag_recv, landing_rows, landing_cols, side_send, side_recv
):
    side = GradientSum(
        (by_rows, by_cols), (out_rows, out_cols), (landing_rows, landing_cols), (side_send, side_recv)
    )
    backward_exchange_kernel(
        n, pieces, partial, grad_out, normal_in, gain, gathered, grad_in, sums, from_left, from_right, total,
        rs_send, rs_recv, ag_send, ag_recv, side=side
    )


def sum_all_kernel(axes, shared_rows, values, out, landing, sends, recvs):
    steps = [(axis, 1 << b) for axis, size in axes for b in range(size.bit_length() - 1)]

    def peer(axis, k):
        return {axis: jnp.bitwise_xor(lax.axis_index(axis), k)}

    barrier = pltpu.get_barrier_semaphore()
    for axis, k in steps:
        pl.semaphore_signal(barrier, inc=1, device_id=peer(axis, k), device_id_type=MESH)
    pl.semaphore_wait(barrier, len(steps))
    out[...] = values[...]
    for at, (axis, k) in enumerate(steps):
        rows = pl.ds(0, shared_rows) if axis == "tp" else pl.ds(0, values.shape[0])
        landing[at, 0, rows] = out[rows, :]
        copy = pltpu.make_async_remote_copy(
            src_ref=landing.at[at, 0, rows],
            dst_ref=landing.at[at, 1, rows],
            send_sem=sends.at[at],
            recv_sem=recvs.at[at],
            device_id=peer(axis, k),
            device_id_type=MESH,
        )
        copy.start()
        copy.wait()
        out[rows, :] = landing[at, 0, rows] + landing[at, 1, rows]


def sum_all(values, shared_rows, axes, collective_id):
    steps = sum(size.bit_length() - 1 for _, size in axes)
    return pl.pallas_call(
        functools.partial(sum_all_kernel, axes, shared_rows),
        out_shape=jax.ShapeDtypeStruct(values.shape, WIDE),
        in_specs=in_vmem(1),
        out_specs=in_vmem(1)[0],
        scratch_shapes=[
            pltpu.VMEM((steps, 2) + values.shape, WIDE),
            pltpu.SemaphoreType.DMA((steps,)),
            pltpu.SemaphoreType.DMA((steps,)),
        ],
        compiler_params=pltpu.CompilerParams(collective_id=collective_id, has_side_effects=True),
        name="sum_all",
    )(values)


FETCH_PARTS = 2


def fetch_kernel(by_column, *refs):
    count = len(by_column)
    shards, small, outs, out_small = refs[:count], refs[count], refs[count + 1 : -5], refs[-5]
    sends, recvs, small_send, small_recv = refs[-4:]
    half = lax.axis_index("fsdp")
    ctx = lax.axis_index("ctx")
    pair, across = jnp.bitwise_xor(ctx, 1), jnp.bitwise_xor(ctx, 2)
    peers = ({"fsdp": 1 - half}, {"ctx": across}, {"ctx": pair}, {"ctx": pair})

    barrier = pltpu.get_barrier_semaphore()
    for peer in peers[:3]:
        pl.semaphore_signal(barrier, inc=1, device_id=peer, device_id_type=MESH)
    pl.semaphore_wait(barrier, 3)

    def rows_of(which, quarter, part, base=0):
        height = shards[which].shape[0] // 4 // FETCH_PARTS
        return pl.ds(pl.multiple_of(base + (quarter * FETCH_PARTS + part) * height, 16), height)

    def place(which, side, quarter, part):
        rows, cols = shards[which].shape
        if by_column[which]:
            return outs[which].at[rows_of(which, quarter, part), pl.ds(pl.multiple_of(side * cols, 128), cols)]
        return outs[which].at[rows_of(which, quarter, part, side * rows)]

    def copy(which, stage, part, arriving=False):
        quarter = (ctx, ctx, ctx, across)[stage]
        src = shards[which].at[rows_of(which, quarter, part)]
        dst = place(which, half, quarter, part)
        if stage > 0:
            src = dst = place(which, 1 - half, quarter, part)
        if arriving:
            quarter = (ctx, across, pair, jnp.bitwise_xor(ctx, 3))[stage]
            dst = place(which, 1 - half, quarter, part)
        return pltpu.make_async_remote_copy(
            src_ref=src,
            dst_ref=dst,
            send_sem=sends.at[which, stage, part],
            recv_sem=recvs.at[which, stage, part],
            device_id=peers[stage],
            device_id_type=MESH,
        )

    def small_copy(side):
        cols = small.shape[1]
        return pltpu.make_async_remote_copy(
            src_ref=small,
            dst_ref=out_small.at[:, pl.ds(pl.multiple_of(side * cols, 128), cols)],
            send_sem=small_send,
            recv_sem=small_recv,
            device_id=peers[0],
            device_id_type=MESH,
        )

    each = [(which, part) for which in range(count) for part in range(FETCH_PARTS)]
    for which, part in each:
        copy(which, 0, part).start()
    small_copy(half).start()
    for shard, out, column in zip((*shards, small), (*outs, out_small), (*by_column, True)):
        rows, cols = shard.shape
        if column:
            out[:, pl.ds(pl.multiple_of(half * cols, 128), cols)] = shard[...]
        else:
            out[pl.ds(pl.multiple_of(half * rows, 16), rows), :] = shard[...]
    for at in range(len(each) + 1):
        if at < len(each):
            copy(each[at][0], 0, each[at][1], True).wait_recv()
            copy(each[at][0], 1, each[at][1]).start()
            copy(each[at][0], 2, each[at][1]).start()
        if at > 0:
            copy(each[at - 1][0], 1, each[at - 1][1], True).wait_recv()
            copy(each[at - 1][0], 3, each[at - 1][1]).start()
    small_copy(1 - half).wait_recv()
    for stage in (2, 3):
        for which, part in each:
            copy(which, stage, part, True).wait_recv()
    for stage in range(4):
        for which, part in each:
            copy(which, stage, part).wait_send()
    small_copy(half).wait_send()


def fetch_first(shards, by_column, small, collective_id):
    def whole(shape, column):
        return (shape[0], 2 * shape[1]) if column else (2 * shape[0], shape[1])

    shapes = [whole(shard.shape, column) for shard, column in zip(shards, by_column)]
    shapes.append(whole(small.shape, True))
    sems = pltpu.SemaphoreType.DMA((len(shards), 4, FETCH_PARTS))
    return pl.pallas_call(
        functools.partial(fetch_kernel, by_column),
        out_shape=tuple(jax.ShapeDtypeStruct(shape, LOW) for shape in shapes),
        in_specs=in_vmem(len(shapes)),
        out_specs=tuple(in_vmem(len(shapes))),
        scratch_shapes=[sems, sems, pltpu.SemaphoreType.DMA, pltpu.SemaphoreType.DMA],
        compiler_params=pltpu.CompilerParams(
            collective_id=collective_id, has_side_effects=True, vmem_limit_bytes=40 << 20
        ),
        name="fetch_first",
    )(*shards, small)


def forward_exchange(partial, residual, bias, gain, shift, n, collective_id):
    rows, width = partial.shape
    return pl.pallas_call(
        functools.partial(forward_exchange_kernel, n, PIECES),
        out_shape=(
            jax.ShapeDtypeStruct((rows, width), LOW),
            jax.ShapeDtypeStruct(residual.shape, WIDE),
        ),
        in_specs=in_vmem(5),
        out_specs=tuple(in_vmem(2)),
        scratch_shapes=exchange_scratch(n, rows, width, PIECES),
        compiler_params=pltpu.CompilerParams(
            collective_id=collective_id, has_side_effects=True, vmem_limit_bytes=40 << 20
        ),
        name="forward_exchange",
    )(partial, residual, bias[None, :], gain[None, :], shift[None, :])


def backward_exchange(partial, grad_out, normal_in, gain, n, collective_id, by_rows=None, by_cols=None):
    rows, width = partial.shape
    out_shape = (
        jax.ShapeDtypeStruct((rows, width), LOW),
        jax.ShapeDtypeStruct(grad_out.shape, WIDE),
        jax.ShapeDtypeStruct((8, width), WIDE),
    )
    scratch = exchange_scratch(n, rows, width, PIECES)
    kernel, extra = backward_exchange_kernel, ()
    if by_rows is not None:
        outs, landings, sems = gradient_shapes(by_rows, by_cols)
        out_shape = out_shape + outs
        scratch = scratch + landings + [sems] * 2
        kernel, extra = backward_gradient_kernel, (by_rows, by_cols)
    return pl.pallas_call(
        functools.partial(kernel, n, PIECES),
        out_shape=out_shape,
        in_specs=in_vmem(4 + len(extra)),
        out_specs=tuple(in_vmem(len(out_shape))),
        scratch_shapes=scratch,
        compiler_params=pltpu.CompilerParams(
            collective_id=collective_id, has_side_effects=True, vmem_limit_bytes=56 << 20
        ),
        name="backward_exchange",
    )(partial, grad_out, normal_in, gain[None, :], *extra)


GROUPS = 2
PARTS = 2 * GROUPS


def part_rows(columns, part, base=0):
    size = columns // GROUPS
    return pl.ds(base + (part % 2) * columns + (part // 2) * size, size)


def group_parts(group):
    return (2 * group, 2 * group + 1)


def group_heads(heads, group):
    assert heads % GROUPS == 0
    size = heads // GROUPS
    return range(heads) if group is None else range(group * size, (group + 1) * size)


def attend_kernel(scale, length, qkv, out, out_wide, log_total, held, high, low_sum, sems_send, sems_recv):
    columns = qkv.shape[0] // 3
    frames = qkv.shape[1]
    heads = columns // HD
    me = lax.axis_index("ctx")

    def partner(r):
        return {"ctx": jnp.bitwise_xor(me, r)}

    barrier = pltpu.get_barrier_semaphore()
    for r in (1, 2):
        pl.semaphore_signal(barrier, inc=1, device_id=partner(r), device_id_type=MESH)
    pl.semaphore_wait(barrier, 2)

    def send(slot, part, to):
        rows, own_rows = part_rows(columns, part), part_rows(columns, part, columns)
        src = qkv.at[own_rows] if slot != 3 else held.at[1, rows]
        return pltpu.make_async_remote_copy(
            src_ref=src,
            dst_ref=held.at[slot - 1, rows],
            send_sem=sems_send.at[slot - 1, part],
            recv_sem=sems_recv.at[slot - 1, part],
            device_id=partner(to),
            device_id_type=MESH,
        )

    for part in range(PARTS):
        send(2, part, 2).start()
    for part in range(PARTS):
        send(1, part, 1).start()

    high[...] = jnp.full_like(high, NEGATIVE)
    low_sum[...] = jnp.zeros_like(low_sum)
    out_wide[...] = jnp.zeros_like(out_wide)
    limit = length[0]

    def block(keys_ref, key_row, value_row, slot, group=None):
        owner = jnp.bitwise_xor(me, slot)
        left = limit - owner * frames
        valid = lax.broadcasted_iota(jnp.int32, (frames, frames), 0) < left
        for h in group_heads(heads, group):
            rows = pl.ds(h * HD, HD)
            keys = keys_ref[pl.ds(key_row + h * HD, HD), :]
            values = keys_ref[pl.ds(value_row + h * HD, HD), :]
            scores = lax.dot_general(
                keys, qkv[rows, :], (((0,), (0,)), ((), ())), preferred_element_type=WIDE
            )
            scores = jnp.where(valid, scores * scale, NEGATIVE)
            before = high[h : h + 1, :]
            now = jnp.maximum(before, jnp.max(scores, axis=0, keepdims=True))
            shrink = jnp.exp(before - now)
            raised = jnp.exp(scores - now)
            low_sum[h : h + 1, :] = low_sum[h : h + 1, :] * shrink + jnp.sum(
                raised, axis=0, keepdims=True
            )
            high[h : h + 1, :] = now
            out_wide[rows, :] = out_wide[rows, :] * shrink + jnp.dot(
                values, raised.astype(LOW), preferred_element_type=WIDE
            )

    block(qkv, columns, 2 * columns, 0)
    for part in range(PARTS):
        send(1, part, 1).wait_recv()
    block(held.at[0], 0, columns, 1)
    for group in range(GROUPS):
        for part in group_parts(group):
            send(2, part, 2).wait_recv()
            send(3, part, 1).start()
        block(held.at[1], 0, columns, 2, group)
    for group in range(GROUPS):
        for part in group_parts(group):
            send(3, part, 1).wait_recv()
        block(held.at[2], 0, columns, 3, group)
    for h in range(heads):
        rows = pl.ds(h * HD, HD)
        total = low_sum[h : h + 1, :]
        done = out_wide[rows, :] / total
        out_wide[rows, :] = done
        out[rows, :] = done.astype(LOW)
        log_total[h : h + 1, :] = high[h : h + 1, :] + jnp.log(total)
    for slot in (1, 2, 3):
        for part in range(PARTS):
            send(slot, part, 2 if slot == 2 else 1).wait_send()


def attend(qkv, length, scale, collective_id):
    columns, frames = qkv.shape[0] // 3, qkv.shape[1]
    return pl.pallas_call(
        functools.partial(attend_kernel, scale),
        out_shape=(
            jax.ShapeDtypeStruct((columns, frames), LOW),
            jax.ShapeDtypeStruct((columns, frames), WIDE),
            jax.ShapeDtypeStruct((8, frames), WIDE),
            jax.ShapeDtypeStruct((3, 2 * columns, frames), LOW),
        ),
        in_specs=[pl.BlockSpec(memory_space=pltpu.SMEM)] + in_vmem(1),
        out_specs=tuple(in_vmem(4)),
        scratch_shapes=[
            pltpu.VMEM((8, frames), WIDE),
            pltpu.VMEM((8, frames), WIDE),
            pltpu.SemaphoreType.DMA((3, PARTS)),
            pltpu.SemaphoreType.DMA((3, PARTS)),
        ],
        compiler_params=pltpu.CompilerParams(
            collective_id=collective_id, has_side_effects=True, vmem_limit_bytes=56 << 20
        ),
        name="attend",
    )(length, qkv)


class LineGather:
    def __init__(self, own, gathered, sends, recvs):
        self.own, self.gathered, self.sends, self.recvs = own, gathered, sends, recvs
        self.n = gathered.shape[0] // own.shape[0]
        self.me = lax.axis_index("tp")
        self.further = (self.me < self.n - 1, self.me > 0)
        self.peers = ({"tp": lax.rem(self.me + 1, self.n)}, {"tp": lax.rem(self.me + self.n - 1, self.n)})

    def greet(self, barrier):
        for way in range(2):

            @pl.when(self.further[way])
            def _():
                pl.semaphore_signal(barrier, inc=1, device_id=self.peers[way], device_id_type=MESH)

        return self.further[0].astype(jnp.int32) + self.further[1].astype(jnp.int32)

    def rows(self, shard):
        size = self.own.shape[0]
        return pl.ds(pl.multiple_of(shard * size, size), size)

    def there(self, way, hops):
        return self.me - hops >= 0 if way == 0 else self.me + hops <= self.n - 1

    def send(self, way, hops):
        shard = self.me - hops if way == 0 else self.me + hops
        rows = self.rows(shard)
        return pltpu.make_async_remote_copy(
            src_ref=self.own if hops == 0 else self.gathered.at[rows],
            dst_ref=self.gathered.at[rows],
            send_sem=self.sends.at[way, hops],
            recv_sem=self.recvs.at[way, hops],
            device_id=self.peers[way],
            device_id_type=MESH,
        )

    def arrival(self, way, hops):
        rows = self.rows(self.me - hops if way == 0 else self.me + hops)
        return pltpu.make_async_remote_copy(
            src_ref=self.gathered.at[rows],
            dst_ref=self.gathered.at[rows],
            send_sem=self.sends.at[way, hops],
            recv_sem=self.recvs.at[way, hops - 1],
            device_id=self.peers[way],
            device_id_type=MESH,
        )

    def hop(self, hops):
        for way in range(2):
            if hops > 0:

                @pl.when(self.there(way, hops))
                def _():
                    self.arrival(way, hops).wait_recv()

            if hops < self.n - 1:

                @pl.when(self.there(way, hops) & self.further[way])
                def _():
                    self.send(way, hops).start()

    def drain(self):
        for hops in range(self.n - 1):
            for way in range(2):

                @pl.when(self.there(way, hops) & self.further[way])
                def _():
                    self.send(way, hops).wait_send()


def attend_back_kernel(scale, sharing, length, qkv, held, grad, out_wide, log_total, *refs):
    if sharing:
        own, grad_qkv, gathered, mine, parts, landed, acc, sems_send, sems_recv, sends, recvs = refs
        share = LineGather(own, gathered, sends, recvs)
    else:
        grad_qkv, mine, parts, landed, acc, sems_send, sems_recv = refs
        share = None
    columns = qkv.shape[0] // 3
    frames = qkv.shape[1]
    heads = columns // HD
    me = lax.axis_index("ctx")

    def partner(r):
        return {"ctx": jnp.bitwise_xor(me, r)}

    barrier = pltpu.get_barrier_semaphore()
    for r in (1, 2):
        pl.semaphore_signal(barrier, inc=1, device_id=partner(r), device_id_type=MESH)
    waiting = 2
    if share is not None:
        waiting = waiting + share.greet(barrier)
    pl.semaphore_wait(barrier, waiting)
    if share is not None:
        share.hop(0)
        gathered[share.rows(share.me), :] = own[...]

    def send(at, part, to):
        rows = part_rows(columns, part)
        return pltpu.make_async_remote_copy(
            src_ref=parts.at[at, rows],
            dst_ref=landed.at[at, rows],
            send_sem=sems_send.at[at, part],
            recv_sem=sems_recv.at[at, part],
            device_id=partner(to),
            device_id_type=MESH,
        )

    acc[...] = jnp.zeros_like(acc)
    limit = length[0]

    def block(keys_ref, key_row, value_row, slot, store, group=None):
        owner = jnp.bitwise_xor(me, slot)
        left = limit - owner * frames
        valid = lax.broadcasted_iota(jnp.int32, (frames, frames), 0) < left
        for h in group_heads(heads, group):
            rows = pl.ds(h * HD, HD)
            keys = keys_ref[pl.ds(key_row + h * HD, HD), :]
            values = keys_ref[pl.ds(value_row + h * HD, HD), :]
            queries = qkv[rows, :]
            upstream = grad[rows, :]
            scores = lax.dot_general(
                keys, queries, (((0,), (0,)), ((), ())), preferred_element_type=WIDE
            )
            weights = jnp.where(valid, jnp.exp(scores * scale - log_total[h : h + 1, :]), 0.0)
            grad_weights = lax.dot_general(
                values, upstream, (((0,), (0,)), ((), ())), preferred_element_type=WIDE
            )
            row_terms = jnp.sum(
                upstream.astype(WIDE) * out_wide[rows, :], axis=0, keepdims=True
            )
            grad_scores = (weights * (grad_weights - row_terms)).astype(LOW)
            acc[rows, :] += jnp.dot(keys, grad_scores, preferred_element_type=WIDE)
            grad_keys = (
                lax.dot_general(
                    queries, grad_scores, (((1,), (1,)), ((), ())), preferred_element_type=WIDE
                )
                * scale
            )
            grad_values = lax.dot_general(
                upstream, weights.astype(LOW), (((1,), (1,)), ((), ())), preferred_element_type=WIDE
            )
            store(h * HD, grad_keys, grad_values)

    def store_part(at):
        def store(row, grad_keys, grad_values):
            parts[at, pl.ds(row, HD), :] = grad_keys.astype(LOW)
            parts[at, pl.ds(columns + row, HD), :] = grad_values.astype(LOW)

        return store

    def store_mine(row, grad_keys, grad_values):
        mine[pl.ds(row, HD), :] = grad_keys
        mine[pl.ds(columns + row, HD), :] = grad_values

    def store_joined(row, grad_keys, grad_values):
        for start, value in ((row, grad_keys), (columns + row, grad_values)):
            rows = pl.ds(start, HD)
            parts[1, rows, :] = (value + landed[0, rows, :].astype(WIDE)).astype(LOW)

    for group in range(GROUPS):
        block(held.at[2], 0, columns, 3, store_part(0), group)
        for part in group_parts(group):
            send(0, part, 1).start()
    for group in range(GROUPS):
        for part in group_parts(group):
            send(0, part, 1).wait_recv()
        block(held.at[1], 0, columns, 2, store_joined, group)
        for part in group_parts(group):
            send(1, part, 2).start()
        if share is not None and group == 0:
            share.hop(1)
    for group in range(GROUPS):
        block(held.at[0], 0, columns, 1, store_part(2), group)
        for part in group_parts(group):
            send(2, part, 1).start()
        if share is not None and group == 0:
            share.hop(2)
    block(qkv, columns, 2 * columns, 0, store_mine)
    grad_qkv[0:columns, :] = (acc[...] * scale).astype(LOW)
    for part in range(PARTS):
        send(2, part, 1).wait_recv()
    for part in range(PARTS):
        send(1, part, 2).wait_recv()
    grad_qkv[columns:, :] = (
        mine[...] + landed[1].astype(WIDE) + landed[2].astype(WIDE)
    ).astype(LOW)
    for at in range(3):
        for part in range(PARTS):
            send(at, part, 2 if at == 1 else 1).wait_send()
    if share is not None:
        for hops in range(3, share.n):
            share.hop(hops)
        share.drain()


def attend_back(qkv, held, grad, out_wide, log_total, length, scale, collective_id, own=None):
    columns, frames = qkv.shape[0] // 3, qkv.shape[1]
    out_shape = (jax.ShapeDtypeStruct((3 * columns, frames), LOW),)
    extra, sems = (), []
    if own is not None:
        n = lax.axis_size("tp")
        assert n >= 3
        out_shape += (jax.ShapeDtypeStruct((n * own.shape[0], own.shape[1]), LOW),)
        extra, sems = (own,), [pltpu.SemaphoreType.DMA((2, n))] * 2
    return pl.pallas_call(
        functools.partial(attend_back_kernel, scale, own is not None),
        out_shape=out_shape,
        in_specs=[pl.BlockSpec(memory_space=pltpu.SMEM)] + in_vmem(5 + len(extra)),
        out_specs=tuple(in_vmem(len(out_shape))),
        scratch_shapes=[
            pltpu.VMEM((2 * columns, frames), WIDE),
            pltpu.VMEM((3, 2 * columns, frames), LOW),
            pltpu.VMEM((3, 2 * columns, frames), LOW),
            pltpu.VMEM((columns, frames), WIDE),
            pltpu.SemaphoreType.DMA((3, PARTS)),
            pltpu.SemaphoreType.DMA((3, PARTS)),
            *sems,
        ],
        compiler_params=pltpu.CompilerParams(
            collective_id=collective_id, has_side_effects=True, vmem_limit_bytes=56 << 20
        ),
        name="attend_back",
    )(length, qkv, held, grad, out_wide, log_total, *extra)


def gelu_value(values):
    return 0.5 * values * (1.0 + lax.erf(values * ROOT_HALF))


def gelu_slope(values):
    return 0.5 * (1.0 + lax.erf(values * ROOT_HALF)) + values * DENSITY * jnp.exp(
        -0.5 * values * values
    )


def product(left_side, right_side, left_axis, right_axis):
    return lax.dot_general(
        left_side,
        right_side,
        (((left_axis,), (right_axis,)), ((), ())),
        preferred_element_type=WIDE,
    )


def per_device(
    hidden,
    cotangent,
    lengths,
    query_weight,
    key_weight,
    value_weight,
    output_weight,
    inner_weight,
    outer_weight,
    query_bias,
    value_bias,
    inner_bias,
    output_bias,
    outer_bias,
    first_gain,
    first_shift,
    second_gain,
    second_shift,
):
    clip_count, rows, width = hidden.shape
    assert clip_count == 1
    assert lax.axis_size("ctx") == 4
    tp_size = lax.axis_size("tp")
    own_rows = rows // tp_size
    columns = query_weight.shape[2]
    hidden_local = inner_weight.shape[2]
    scale = 1.0 / math.sqrt(HD)
    own_start = lax.axis_index("tp") * own_rows

    def own_slice(full):
        return lax.dynamic_slice_in_dim(full, own_start, own_rows, axis=0)

    small = jnp.concatenate(
        [output_bias, outer_bias, first_gain, first_shift, second_gain, second_shift], axis=0
    ).astype(LOW)
    small = jnp.pad(small, ((0, -small.shape[0] % 16), (0, 0)))

    def qkv_shard(layer):
        return jnp.concatenate(
            [query_weight[layer], key_weight[layer], value_weight[layer]], axis=1
        ).astype(LOW)

    projections = output_weight.astype(LOW).reshape(-1, output_weight.shape[2])
    if lax.axis_size("fsdp") == 2:
        qkv_first, projections, inner_first, small = fetch_first(
            (qkv_shard(0), projections, inner_weight[0].astype(LOW)), (False, True, False), small, 17
        )
        small, outer_weight, inner_weight, query_weight, key_weight, value_weight = lax.optimization_barrier(
            (small, outer_weight, inner_weight, query_weight, key_weight, value_weight)
        )
    else:
        qkv_first = lax.all_gather(qkv_shard(0), "fsdp", axis=0, tiled=True)
        inner_first = lax.all_gather(inner_weight[0].astype(LOW), "fsdp", axis=0, tiled=True)
        projections = lax.all_gather(projections, "fsdp", axis=1, tiled=True)
        small = lax.all_gather(small, "fsdp", axis=1, tiled=True)
    small = small.astype(WIDE)
    projections = projections.reshape(LAYERS, columns, width)

    def vector(kind, layer):
        return small[kind * LAYERS + layer]

    def fetch(layer):
        qkv, inner = qkv_first, inner_first
        if layer > 0:
            qkv = lax.all_gather(qkv_shard(layer), "fsdp", axis=0, tiled=True)
            inner = lax.all_gather(inner_weight[layer].astype(LOW), "fsdp", axis=0, tiled=True)
        out = projections[layer]
        outer = lax.all_gather(outer_weight[layer].astype(LOW), "fsdp", axis=1, tiled=True)
        return (qkv, out, inner, outer)

    weights = [fetch(layer) for layer in range(LAYERS)]

    hidden_rows = hidden.reshape(rows, width)
    residual = own_slice(hidden_rows)
    hat_full, _ = norm_parts(hidden_rows)
    normed = (hat_full * vector(2, 0) + vector(3, 0)).astype(LOW)
    kept = []
    for layer in range(LAYERS):
        w_qkv, w_out, w_inner, w_outer = weights[layer]
        bias_qkv = jnp.concatenate(
            [query_bias[layer], jnp.zeros_like(query_bias[layer]), value_bias[layer]]
        )
        qkv = (product(w_qkv, normed, 0, 1) + bias_qkv[:, None]).astype(LOW)
        attended, attended_wide, log_total, held = attend(qkv, lengths, scale, 2 * layer)
        branch = product(attended, w_out, 0, 0).astype(LOW)
        normed_two, middle = forward_exchange(
            branch, residual, vector(0, layer), vector(4, layer), vector(5, layer), tp_size, 2 * layer + 4
        )
        inner_pre = product(normed_two, w_inner, 1, 0) + inner_bias[layer]
        active = gelu_value(inner_pre).astype(LOW)
        kept.append(
            (residual, normed, qkv, attended, attended_wide, log_total, held, middle, normed_two, inner_pre, active)
        )
        branch = product(active, w_outer, 1, 0).astype(LOW)
        if layer + 1 < LAYERS:
            normed, residual = forward_exchange(
                branch,
                middle,
                vector(1, layer),
                vector(2, layer + 1),
                vector(3, layer + 1),
                tp_size,
                2 * layer + 5,
            )
        else:
            last_branch, last_middle = branch, middle

    def exchange_back(branch, grad_out, normal_in, gain, collective_id, by_rows, by_cols):
        if lax.axis_size("fsdp") == 2:
            return backward_exchange(
                branch, grad_out, normal_in, gain, tp_size, collective_id, by_rows, by_cols
            )
        first = backward_exchange(branch, grad_out, normal_in, gain, tp_size, collective_id)
        by_rows = lax.psum_scatter(by_rows, ("fsdp", "ctx"), scatter_dimension=0, tiled=True)
        by_rows = lax.all_gather(by_rows, "ctx", axis=0, tiled=True).astype(WIDE)
        by_cols = lax.psum_scatter(by_cols, ("fsdp", "ctx"), scatter_dimension=1, tiled=True)
        by_cols = lax.all_gather(by_cols, "ctx", axis=1, tiled=True).astype(WIDE)
        return (*first, by_rows, by_cols)

    grad_rows = cotangent.reshape(rows, width)
    grad_own = own_slice(grad_rows)
    grad_low = grad_rows.astype(LOW)
    outer_bias_sum = jnp.sum(grad_own, axis=0)
    grads = [None] * LAYERS
    vectors = [None] * LAYERS
    biases = [None] * LAYERS
    for layer in reversed(range(LAYERS)):
        w_qkv, w_out, w_inner, w_outer = weights[layer]
        (
            residual,
            normed,
            qkv,
            attended,
            attended_wide,
            log_total,
            held,
            middle,
            normed_two,
            inner_pre,
            active,
        ) = kept[layer]
        grad_active = product(grad_low, w_outer, 1, 1)
        grad_inner = (grad_active * gelu_slope(inner_pre)).astype(LOW)
        branch = product(grad_inner, w_inner, 1, 1).astype(LOW)
        grad_outer_w = product(active, grad_low, 0, 0).astype(LOW)
        grad_inner_w = product(normed_two, grad_inner, 0, 0).astype(LOW)
        grad_mid_low, grad_middle, sums_two, *summed_two = exchange_back(
            branch, grad_own, middle, vector(4, layer), 2 * layer + 8, grad_inner_w, grad_outer_w
        )
        if layer == LAYERS - 1:
            last_branch, grad_mid_low = lax.optimization_barrier((last_branch, grad_mid_low))
            last_branch = lax.psum_scatter(last_branch, "tp", scatter_dimension=0, tiled=True)
        grad_attended = product(w_out, grad_mid_low, 1, 1).astype(LOW)
        grad_qkv, *shared = attend_back(
            qkv,
            held,
            grad_attended,
            attended_wide,
            log_total,
            lengths,
            scale,
            2 * layer + 12,
            last_rows if layer == 0 else None,
        )
        grad_output_w = product(attended, grad_mid_low, 1, 0).astype(LOW)
        branch = product(grad_qkv, w_qkv, 0, 1).astype(LOW)
        grad_qkv_w = product(normed, grad_qkv, 0, 1).astype(LOW)
        if layer == LAYERS - 1:
            last_branch, branch = lax.optimization_barrier((last_branch, branch))
            last_rows = (last_middle + last_branch.astype(WIDE) + vector(1, layer)).astype(LOW)
        if layer == 0:
            output = shared[0].astype(WIDE)
        grad_low, grad_own, sums_one, *summed_one = exchange_back(
            branch, grad_middle, residual, vector(2, layer), 2 * layer + 9, grad_qkv_w, grad_output_w
        )
        grads[layer] = (*summed_one, *summed_two)
        vectors[layer] = [
            sums_two[2], outer_bias_sum, sums_one[0], sums_one[1], sums_two[0], sums_two[1]
        ]
        outer_bias_sum = sums_one[2]
        biases[layer] = jnp.concatenate(
            [
                jnp.sum(grad_qkv.astype(WIDE), axis=1),
                jnp.sum(grad_inner.astype(WIDE), axis=0),
            ]
        )
    grad_hidden = grad_low.astype(WIDE)

    flat_biases = jnp.concatenate(biases)
    bias_rows = -(-flat_biases.size // width)
    flat_biases = jnp.pad(flat_biases, (0, bias_rows * width - flat_biases.size))
    vector_count = 6 * LAYERS
    shared_rows = -(-vector_count // 8) * 8
    total_rows = shared_rows + -(-bias_rows // 8) * 8
    small_sums = jnp.concatenate(
        [
            jnp.stack([row for parts in zip(*vectors) for row in parts]),
            jnp.zeros((shared_rows - vector_count, width), WIDE),
            flat_biases.reshape(bias_rows, width),
            jnp.zeros((total_rows - shared_rows - bias_rows, width), WIDE),
        ]
    )
    small_sums = sum_all(
        small_sums, shared_rows, tuple((axis, lax.axis_size(axis)) for axis in ("ctx", "fsdp", "tp")), 16
    )
    shard = output_bias.shape[1]
    vector_sums = lax.dynamic_slice_in_dim(
        small_sums[:vector_count].reshape(6, LAYERS, width), lax.axis_index("fsdp") * shard, shard, axis=2
    )
    bias_sums = small_sums[shared_rows:].reshape(-1)[: LAYERS * biases[0].size].reshape(LAYERS, -1)

    def stacked(which, start=0, size=None):
        size = grads[0][which].shape[1] if size is None else size
        return jnp.stack([grads[layer][which][:, start : start + size] for layer in range(LAYERS)])

    return (
        output.reshape(hidden.shape),
        grad_hidden.reshape(hidden.shape),
        stacked(0, 0, columns),
        stacked(0, columns, columns),
        stacked(0, 2 * columns, columns),
        stacked(1),
        stacked(2),
        stacked(3),
        bias_sums[:, :columns],
        bias_sums[:, 2 * columns : 3 * columns],
        bias_sums[:, 3 * columns :],
        vector_sums[0],
        vector_sums[1],
        vector_sums[2],
        vector_sums[3],
        vector_sums[4],
        vector_sums[5],
    )


def solution(mesh):
    in_specs = (
        P("fsdp", "ctx", None),
        P("fsdp", "ctx", None),
        P("fsdp"),
        P(None, "fsdp", "tp"),
        P(None, "fsdp", "tp"),
        P(None, "fsdp", "tp"),
        P(None, "tp", "fsdp"),
        P(None, "fsdp", "tp"),
        P(None, "tp", "fsdp"),
        P(None, "tp"),
        P(None, "tp"),
        P(None, "tp"),
        P(None, "fsdp"),
        P(None, "fsdp"),
        P(None, "fsdp"),
        P(None, "fsdp"),
        P(None, "fsdp"),
        P(None, "fsdp"),
    )
    out_specs = (
        P("fsdp", "ctx", None),
        P("fsdp", "ctx", None),
        P(None, "fsdp", "tp"),
        P(None, "fsdp", "tp"),
        P(None, "fsdp", "tp"),
        P(None, "tp", "fsdp"),
        P(None, "fsdp", "tp"),
        P(None, "tp", "fsdp"),
        P(None, "tp"),
        P(None, "tp"),
        P(None, "tp"),
        P(None, "fsdp"),
        P(None, "fsdp"),
        P(None, "fsdp"),
        P(None, "fsdp"),
        P(None, "fsdp"),
        P(None, "fsdp"),
    )
    return jax.shard_map(
        per_device, mesh=mesh, in_specs=in_specs, out_specs=out_specs, check_vma=False
    )
```

```python
import functools
import math
import jax
import jax.numpy as jnp
from jax import lax
from jax.experimental import pallas as pl
from jax.experimental.pallas import tpu as pltpu
from jax.sharding import PartitionSpec as P

MESH = pl.DeviceIdType.MESH
LOW = jnp.bfloat16
WIDE = jnp.float32
EPSILON = 1e-05
NEGATIVE = -1e30
HD = 80
PIECES = 4
LAYERS = 2
ROOT_HALF = 1.0 / math.sqrt(2.0)
DENSITY = 1.0 / math.sqrt(2.0 * math.pi)
REDUCE_LAG = 2
GATHER_LAG = 3


def norm_parts(values):
    average = jnp.mean(values, axis=-1, keepdims=True)
    centered = values - average
    spread = jnp.mean(centered * centered, axis=-1, keepdims=True)
    inverse = lax.rsqrt(spread + EPSILON)
    return (centered * inverse, inverse)


def norm_back(upstream, normal_hat, inverse, gain_full):
    scaled = upstream * gain_full
    first_mean = jnp.mean(scaled, axis=-1, keepdims=True)
    second_mean = jnp.mean(scaled * normal_hat, axis=-1, keepdims=True)
    return inverse * (scaled - first_mean - normal_hat * second_mean)


def line_exchange(n, own, pieces, partial, gathered, from_left, from_right, total, sems, finish, side=None):
    rs_send, rs_recv, ag_send, ag_recv = sems
    me = lax.axis_index("tp")
    piece = own // pieces
    to_right, to_left = {"tp": lax.rem(me + 1, n)}, {"tp": lax.rem(me + n - 1, n)}
    has_left, has_right = me > 0, me < n - 1

    barrier = pltpu.get_barrier_semaphore()

    @pl.when(has_left)
    def _():
        pl.semaphore_signal(barrier, inc=1, device_id=to_left, device_id_type=MESH)

    @pl.when(has_right)
    def _():
        pl.semaphore_signal(barrier, inc=1, device_id=to_right, device_id_type=MESH)

    peers = has_left.astype(jnp.int32) + has_right.astype(jnp.int32)
    if side is not None:
        for peer in side.peers:
            pl.semaphore_signal(barrier, inc=1, device_id=peer, device_id_type=MESH)
        peers = peers + len(side.peers)
    pl.semaphore_wait(barrier, peers)
    if side is not None:
        side.start()

    def rows_of(shard, step):
        return pl.ds(pl.multiple_of(shard * own + step * piece, piece), piece)

    def reduce_copy(way, src, shard, step):
        rows = rows_of(shard, step)
        landing = from_left if way == 0 else from_right
        return pltpu.make_async_remote_copy(
            src_ref=src.at[rows],
            dst_ref=landing.at[rows],
            send_sem=rs_send.at[way, shard, step],
            recv_sem=rs_recv.at[way, shard, step],
            device_id=to_right if way == 0 else to_left,
            device_id_type=MESH,
        )

    def gather_copy(way, shard, step):
        rows = rows_of(shard, step)
        return pltpu.make_async_remote_copy(
            src_ref=gathered.at[rows],
            dst_ref=gathered.at[rows],
            send_sem=ag_send.at[way, shard, step],
            recv_sem=ag_recv.at[way, shard, step],
            device_id=to_right if way == 0 else to_left,
            device_id_type=MESH,
        )

    def reduce_one(way, shard, step):
        landing = from_left if way == 0 else from_right
        first = me == 0 if way == 0 else me == n - 1

        @pl.when(first)
        def _():
            reduce_copy(way, partial, shard, step).start()

        @pl.when(jnp.logical_not(first))
        def _():
            rows = rows_of(shard, step)
            reduce_copy(way, partial, shard, step).wait_recv()
            landing[rows, :] = (
                partial[rows, :].astype(WIDE) + landing[rows, :].astype(WIDE)
            ).astype(LOW)
            reduce_copy(way, landing, shard, step).start()

    def finish_one(step):
        rows = rows_of(me, step)
        total[...] = partial[rows, :].astype(WIDE)

        @pl.when(has_left)
        def _():
            reduce_copy(0, partial, me, step).wait_recv()
            total[...] += from_left[rows, :].astype(WIDE)

        @pl.when(has_right)
        def _():
            reduce_copy(1, partial, me, step).wait_recv()
            total[...] += from_right[rows, :].astype(WIDE)

        own_rows = pl.ds(pl.multiple_of(step * piece, piece), piece)
        gathered[rows, :] = finish(own_rows, total[...])

        @pl.when(has_right)
        def _():
            gather_copy(0, me, step).start()

        @pl.when(has_left)
        def _():
            gather_copy(1, me, step).start()

    def forward_one(way, shard, step):
        gather_copy(way, shard, step).wait_recv()

        @pl.when(has_right if way == 0 else has_left)
        def _():
            gather_copy(way, shard, step).start()

    period = n - 1

    def finish_at(device):
        from_start = jnp.where(device > 0, n - 1 - device + REDUCE_LAG * device, 0)
        from_end = jnp.where(device < n - 1, device + REDUCE_LAG * (n - 1 - device), 0)
        return jnp.maximum(from_start, from_end)

    def split(tick, start, length):
        since = tick - start
        clipped = jnp.maximum(since, 0)
        return (since >= 0) & (clipped < length), lax.div(clipped, period), lax.rem(clipped, period)

    def body(tick, carry):
        for way in range(2):
            hops = me if way == 0 else n - 1 - me
            due, step, k = split(tick, REDUCE_LAG * hops, pieces * period)
            shard = n - 1 - k if way == 0 else k
            mine = me < shard if way == 0 else me > shard

            @pl.when(due & mine)
            def _():
                reduce_one(way, shard, step)

        due, step, k = split(tick, finish_at(me), pieces * period)

        @pl.when(due & (k == 0))
        def _():
            finish_one(step)

        for hops in range(1, n):
            for way in range(2):
                shard = me - hops if way == 0 else me + hops
                there = shard >= 0 if way == 0 else shard <= n - 1
                due, step, k = split(
                    tick, finish_at(shard) + GATHER_LAG * hops, pieces * period
                )

                @pl.when(there & due & (k == 0))
                def _():
                    forward_one(way, shard, step)

        if side is not None:
            side.at(tick)
        return carry

    ticks = period * (pieces - 1) + max(REDUCE_LAG, 1) * (n - 1) + GATHER_LAG * (n - 1) + 1
    if side is not None:
        ticks = max(ticks, side.ticks)
    lax.fori_loop(0, ticks, body, 0)
    if side is not None:
        side.drain()

    def drain(step, carry):
        for k in range(n - 1):
            for way in range(2):
                shard = n - 1 - k if way == 0 else k
                sends = me < shard if way == 0 else me > shard

                @pl.when(sends)
                def _():
                    reduce_copy(way, partial, shard, step).wait_send()

        for k in range(n):
            for way in range(2):
                shard = me - k if way == 0 else me + k
                there = shard >= 0 if way == 0 else shard <= n - 1
                further = has_right if way == 0 else has_left

                @pl.when(there & further)
                def _():
                    gather_copy(way, shard, step).wait_send()

        return carry

    lax.fori_loop(0, pieces, drain, 0)


def exchange_scratch(n, rows, width, pieces):
    return [
        pltpu.VMEM((rows, width), LOW),
        pltpu.VMEM((rows, width), LOW),
        pltpu.VMEM((rows // n // pieces, width), WIDE),
        pltpu.SemaphoreType.DMA((2, n, pieces)),
        pltpu.SemaphoreType.DMA((2, n, pieces)),
        pltpu.SemaphoreType.DMA((2, n, pieces)),
        pltpu.SemaphoreType.DMA((2, n, pieces)),
    ]


def forward_exchange_kernel(
    n, pieces, partial, residual, bias, gain, shift, gathered, middle, from_left, from_right, total, *sems
):
    def finish(rows, value):
        mid = value + residual[rows, :] + bias[...]
        middle[rows, :] = mid
        hat, _ = norm_parts(mid)
        return (hat * gain[...] + shift[...]).astype(LOW)

    line_exchange(
        n, residual.shape[0], pieces, partial, gathered, from_left, from_right, total, sems, finish
    )


def backward_exchange_kernel(
    n, pieces, partial, grad_out, normal_in, gain, gathered, grad_in, sums, from_left, from_right, total, *sems, side=None
):
    sums[...] = jnp.zeros_like(sums)

    def finish(rows, upstream):
        hat, inverse = norm_parts(normal_in[rows, :])
        grad = grad_out[rows, :] + norm_back(upstream, hat, inverse, gain[...])
        grad_in[rows, :] = grad
        sums[0:1, :] += jnp.sum(upstream * hat, axis=0, keepdims=True)
        sums[1:2, :] += jnp.sum(upstream, axis=0, keepdims=True)
        sums[2:3, :] += jnp.sum(grad, axis=0, keepdims=True)
        return grad.astype(LOW)

    line_exchange(
        n, grad_out.shape[0], pieces, partial, gathered, from_left, from_right, total, sems, finish, side
    )


def in_vmem(count):
    return [pl.BlockSpec(memory_space=pltpu.VMEM)] * count


class GradientSum:
    LAGS = (0, 3, 6, 9)

    def __init__(self, by_column, arrays, outs, landings, sems):
        self.by_column = by_column
        self.chunks = landings[0].shape[1]
        self.arrays, self.outs, self.landings = arrays, outs, landings
        self.sends, self.recvs = sems
        self.half = lax.axis_index("fsdp")
        self.ctx = lax.axis_index("ctx")
        self.core = lax.rem(self.ctx, 2)
        pair = {"ctx": jnp.bitwise_xor(self.ctx, 1)}
        across = {"ctx": jnp.bitwise_xor(self.ctx, 2)}
        other = {"fsdp": 1 - self.half}
        self.peers = (pair, across, other)
        self.ticks = 2 * (self.chunks - 1) + self.LAGS[3] + 1

    def view(self, which, half, core, chunk):
        rows, cols = self.arrays[which].shape
        if not self.by_column[which]:
            part = rows // 4
            height = part // self.chunks
            start = half * (2 * part) + core * part + chunk * height
            return pl.ds(pl.multiple_of(start, 16), height), slice(None)
        part = rows // 2
        height = part // self.chunks
        start = core * part + chunk * height
        width = cols // 2
        return (
            pl.ds(pl.multiple_of(start, 16), height),
            pl.ds(pl.multiple_of(half * width, 128), width),
        )

    def out_rows(self, which, core, chunk):
        part = self.outs[which].shape[0] // 2
        height = part // self.chunks
        return pl.ds(pl.multiple_of(core * part + chunk * height, 16), height)

    def copy(self, which, stage, chunk, half=0):
        pair, across, other = self.peers
        landing = self.landings[which]
        if stage == 0:
            src = self.arrays[which].at[self.view(which, half, 1 - self.core, chunk)]
            slot, peer = half, pair
        elif stage == 1:
            src = landing.at[1 - self.half, chunk]
            slot, peer = 2, other
        elif stage == 2:
            src = landing.at[2, chunk]
            slot, peer = 3, across
        else:
            src = landing.at[3, chunk]
            slot, peer = 4, pair
        return pltpu.make_async_remote_copy(
            src_ref=src,
            dst_ref=landing.at[slot, chunk],
            send_sem=self.sends.at[which, slot, chunk],
            recv_sem=self.recvs.at[which, slot, chunk],
            device_id=peer,
            device_id_type=MESH,
        )

    def start(self):
        def body(chunk, carry):
            for which in range(2):
                for half in range(2):
                    self.copy(which, 0, chunk, half).start()
            return carry

        lax.fori_loop(0, self.chunks, body, 0)

    def when_due(self, tick, lag, action):
        since = tick - lag
        clipped = jnp.maximum(since, 0)
        chunk = lax.div(clipped, 2)

        @pl.when((since >= 0) & (lax.rem(clipped, 2) == 0) & (chunk < self.chunks))
        def _():
            for which in range(2):
                action(which, chunk)

    def at(self, tick):
        def joined(which, chunk):
            landing = self.landings[which]
            for half in range(2):
                self.copy(which, 0, chunk, half).wait_recv()
                rows, cols = self.view(which, half, self.core, chunk)
                landing[half, chunk] = (
                    self.arrays[which][rows, cols].astype(WIDE) + landing[half, chunk].astype(WIDE)
                ).astype(LOW)
            self.copy(which, 1, chunk).start()

        def crossed(which, chunk):
            landing = self.landings[which]
            self.copy(which, 1, chunk).wait_recv()
            landing[2, chunk] = (
                landing[self.half, chunk].astype(WIDE) + landing[2, chunk].astype(WIDE)
            ).astype(LOW)
            self.copy(which, 2, chunk).start()

        def summed(which, chunk):
            landing = self.landings[which]
            self.copy(which, 2, chunk).wait_recv()
            low = (landing[2, chunk].astype(WIDE) + landing[3, chunk].astype(WIDE)).astype(LOW)
            landing[3, chunk] = low
            self.outs[which][self.out_rows(which, self.core, chunk), :] = low
            self.copy(which, 3, chunk).start()

        def shared(which, chunk):
            self.copy(which, 3, chunk).wait_recv()
            self.outs[which][self.out_rows(which, 1 - self.core, chunk), :] = self.landings[which][
                4, chunk
            ]

        for lag, action in zip(self.LAGS, (joined, crossed, summed, shared)):
            self.when_due(tick, lag, action)

    def drain(self):
        def body(chunk, carry):
            for which in range(2):
                for half in range(2):
                    self.copy(which, 0, chunk, half).wait_send()
                for stage in range(1, 4):
                    self.copy(which, stage, chunk).wait_send()
            return carry

        lax.fori_loop(0, self.chunks, body, 0)


def gradient_shapes(arrays, by_column):
    chunks = 10 if arrays[0].shape == arrays[1].shape else 5
    outs, landings = (), []
    for array, column in zip(arrays, by_column):
        rows, cols = array.shape
        rows, cols = (rows, cols // 2) if column else (rows // 2, cols)
        outs += (jax.ShapeDtypeStruct((rows, cols), LOW),)
        landings.append(pltpu.VMEM((5, chunks, rows // 2 // chunks, cols), LOW))
    return outs, landings, pltpu.SemaphoreType.DMA((2, 5, chunks))


def backward_gradient_kernel(
    by_column, n, pieces, partial, grad_out, normal_in, gain, first, second, gathered, grad_in, sums, out_first,
    out_second, from_left, from_right, total, rs_send, rs_recv, ag_send, ag_recv, landing_first, landing_second,
    side_send, side_recv
):
    side = GradientSum(
        by_column, (first, second), (out_first, out_second), (landing_first, landing_second), (side_send, side_recv)
    )
    backward_exchange_kernel(
        n, pieces, partial, grad_out, normal_in, gain, gathered, grad_in, sums, from_left, from_right, total,
        rs_send, rs_recv, ag_send, ag_recv, side=side
    )


def sum_all_kernel(axes, vectors, biases, out, staged, landing, sends, recvs):
    half = lax.axis_index("fsdp")
    shared, width = vectors.shape[0], out.shape[1]
    steps = [("fsdp", 1)] + [(axis, 1 << b) for axis, size in axes for b in range(size.bit_length() - 1)]

    def peer(axis, k):
        return {axis: jnp.bitwise_xor(lax.axis_index(axis), k)}

    barrier = pltpu.get_barrier_semaphore()
    for axis, k in steps:
        pl.semaphore_signal(barrier, inc=1, device_id=peer(axis, k), device_id_type=MESH)
    for side in range(2):
        staged[side, 0:shared, :] = vectors[:, side * width : (side + 1) * width]
        staged[side, shared:, :] = biases[...]
    pl.semaphore_wait(barrier, len(steps))
    for at, (axis, k) in enumerate(steps):
        rows = pl.ds(0, shared) if axis == "tp" else pl.ds(0, out.shape[0])
        if at > 0:
            landing[at, 0, rows] = out[rows, :]
        copy = pltpu.make_async_remote_copy(
            src_ref=landing.at[at, 0, rows] if at > 0 else staged.at[1 - half],
            dst_ref=landing.at[at, 1, rows],
            send_sem=sends.at[at],
            recv_sem=recvs.at[at],
            device_id=peer(axis, k),
            device_id_type=MESH,
        )
        copy.start()
        copy.wait()
        own = landing[at, 0, rows] if at > 0 else staged[half]
        out[rows, :] = own + landing[at, 1, rows]


def sum_all(vectors, biases, axes, collective_id):
    shape = (vectors.shape[0] + biases.shape[0], biases.shape[1])
    steps = 1 + sum(size.bit_length() - 1 for _, size in axes)
    return pl.pallas_call(
        functools.partial(sum_all_kernel, axes),
        out_shape=jax.ShapeDtypeStruct(shape, WIDE),
        in_specs=in_vmem(2),
        out_specs=in_vmem(1)[0],
        scratch_shapes=[
            pltpu.VMEM((2,) + shape, WIDE),
            pltpu.VMEM((steps, 2) + shape, WIDE),
            pltpu.SemaphoreType.DMA((steps,)),
            pltpu.SemaphoreType.DMA((steps,)),
        ],
        compiler_params=pltpu.CompilerParams(collective_id=collective_id, has_side_effects=True),
        name="sum_all",
    )(vectors, biases)


def fetch_parts(rows):
    return next(parts for parts in (2, 3, 1) if rows // 4 % (16 * parts) == 0)


CAST_ROWS = 64


def fetch_kernel(by_column, casts, *refs):
    count = len(by_column)
    shards, small, wides, refs = refs[:count], refs[count], refs[count + 1 : count + 1 + casts], refs[count + 1 + casts :]
    outs, out_small, refs = refs[:count], refs[count], refs[count + 1 :]
    lows, refs = refs[: casts * LAYERS], refs[casts * LAYERS :]
    buffers, (cast_sems, sends, recvs, small_send, small_recv) = refs[:casts], refs[casts:]
    half = lax.axis_index("fsdp")
    ctx = lax.axis_index("ctx")
    pair, across = jnp.bitwise_xor(ctx, 1), jnp.bitwise_xor(ctx, 2)
    peers = ({"fsdp": 1 - half}, {"ctx": across}, {"ctx": pair}, {"ctx": pair})

    barrier = pltpu.get_barrier_semaphore()
    for peer in peers[:3]:
        pl.semaphore_signal(barrier, inc=1, device_id=peer, device_id_type=MESH)
    pl.semaphore_wait(barrier, 3)

    def rows_of(which, quarter, part, base=0):
        parts = fetch_parts(shards[which].shape[0])
        height = shards[which].shape[0] // 4 // parts
        return pl.ds(pl.multiple_of(base + (quarter * parts + part) * height, 16), height)

    def place(which, side, quarter, part):
        rows, cols = shards[which].shape
        if by_column[which]:
            return outs[which].at[rows_of(which, quarter, part), pl.ds(pl.multiple_of(side * cols, 128), cols)]
        return outs[which].at[rows_of(which, quarter, part, side * rows)]

    def copy(which, stage, part, arriving=False):
        quarter = (ctx, ctx, ctx, across)[stage]
        src = shards[which].at[rows_of(which, quarter, part)]
        dst = place(which, half, quarter, part)
        if stage > 0:
            src = dst = place(which, 1 - half, quarter, part)
        if arriving:
            quarter = (ctx, across, pair, jnp.bitwise_xor(ctx, 3))[stage]
            dst = place(which, 1 - half, quarter, part)
        return pltpu.make_async_remote_copy(
            src_ref=src,
            dst_ref=dst,
            send_sem=sends.at[which, stage, part],
            recv_sem=recvs.at[which, stage, part],
            device_id=peers[stage],
            device_id_type=MESH,
        )

    def small_copy(side):
        cols = small.shape[1]
        return pltpu.make_async_remote_copy(
            src_ref=small,
            dst_ref=out_small.at[:, pl.ds(pl.multiple_of(side * cols, 128), cols)],
            send_sem=small_send,
            recv_sem=small_recv,
            device_id=peers[0],
            device_id_type=MESH,
        )

    each = [(which, part) for which in range(count) for part in range(fetch_parts(shards[which].shape[0]))]
    for which, part in each:
        copy(which, 0, part).start()
    small_copy(half).start()
    to_cast = [(layer, which) for layer in range(LAYERS) for which in range(casts)]

    def load(layer, which):
        return pltpu.make_async_copy(
            wides[which].at[layer], buffers[which].at[layer], cast_sems.at[which, layer]
        )

    for layer, which in to_cast:
        load(layer, which).start()
    for shard, out, column in zip((*shards, small), (*outs, out_small), (*by_column, True)):
        rows, cols = shard.shape
        if column:
            out[:, pl.ds(pl.multiple_of(half * cols, 128), cols)] = shard[...]
        else:
            out[pl.ds(pl.multiple_of(half * rows, 16), rows), :] = shard[...]
    for layer, which in to_cast:
        load(layer, which).wait()
        low = lows[which * LAYERS + layer]

        def cast(at, carry):
            rows = pl.ds(pl.multiple_of(at * CAST_ROWS, CAST_ROWS), CAST_ROWS)
            low[rows, :] = buffers[which][layer, rows, :].astype(LOW)
            return carry

        lax.fori_loop(0, low.shape[0] // CAST_ROWS, cast, 0)
    for at in range(len(each) + 1):
        if at < len(each):
            copy(each[at][0], 0, each[at][1], True).wait_recv()
            copy(each[at][0], 1, each[at][1]).start()
            copy(each[at][0], 2, each[at][1]).start()
        if at > 0:
            copy(each[at - 1][0], 1, each[at - 1][1], True).wait_recv()
            copy(each[at - 1][0], 3, each[at - 1][1]).start()
    small_copy(1 - half).wait_recv()
    for stage in (2, 3):
        for which, part in each:
            copy(which, stage, part, True).wait_recv()
    for stage in range(4):
        for which, part in each:
            copy(which, stage, part).wait_send()
    small_copy(half).wait_send()


def fetch_first(shards, by_column, small, wides, collective_id):
    def whole(shape, column):
        return (shape[0], 2 * shape[1]) if column else (2 * shape[0], shape[1])

    shapes = [whole(shard.shape, column) for shard, column in zip(shards, by_column)]
    shapes.append(whole(small.shape, True))
    gathered = len(shapes)
    for wide in wides:
        assert wide.shape[0] == LAYERS and wide.shape[1] % CAST_ROWS == 0
        shapes += [wide.shape[1:]] * LAYERS
    sems = pltpu.SemaphoreType.DMA((len(shards), 4, max(fetch_parts(shard.shape[0]) for shard in shards)))
    return pl.pallas_call(
        functools.partial(fetch_kernel, by_column, len(wides)),
        out_shape=tuple(jax.ShapeDtypeStruct(shape, LOW) for shape in shapes),
        in_specs=in_vmem(gathered) + [pl.BlockSpec(memory_space=pl.ANY)] * len(wides),
        out_specs=tuple(in_vmem(len(shapes))),
        scratch_shapes=[pltpu.VMEM(wide.shape, WIDE) for wide in wides]
        + [
            pltpu.SemaphoreType.DMA((len(wides), LAYERS)),
            sems,
            sems,
            pltpu.SemaphoreType.DMA,
            pltpu.SemaphoreType.DMA,
        ],
        compiler_params=pltpu.CompilerParams(
            collective_id=collective_id, has_side_effects=True, vmem_limit_bytes=40 << 20
        ),
        name="fetch_first",
    )(*shards, small, *wides)


def forward_exchange(partial, residual, bias, gain, shift, n, collective_id):
    rows, width = partial.shape
    return pl.pallas_call(
        functools.partial(forward_exchange_kernel, n, PIECES),
        out_shape=(
            jax.ShapeDtypeStruct((rows, width), LOW),
            jax.ShapeDtypeStruct(residual.shape, WIDE),
        ),
        in_specs=in_vmem(5),
        out_specs=tuple(in_vmem(2)),
        scratch_shapes=exchange_scratch(n, rows, width, PIECES),
        compiler_params=pltpu.CompilerParams(
            collective_id=collective_id, has_side_effects=True, vmem_limit_bytes=40 << 20
        ),
        name="forward_exchange",
    )(partial, residual, bias[None, :], gain[None, :], shift[None, :])


def backward_exchange(partial, grad_out, normal_in, gain, n, collective_id, arrays=(), by_column=()):
    rows, width = partial.shape
    out_shape = (
        jax.ShapeDtypeStruct((rows, width), LOW),
        jax.ShapeDtypeStruct(grad_out.shape, WIDE),
        jax.ShapeDtypeStruct((8, width), WIDE),
    )
    scratch = exchange_scratch(n, rows, width, PIECES)
    kernel, extra = backward_exchange_kernel, ()
    if arrays:
        outs, landings, sems = gradient_shapes(arrays, by_column)
        out_shape = out_shape + outs
        scratch = scratch + landings + [sems] * 2
        kernel, extra = functools.partial(backward_gradient_kernel, by_column), arrays
    return pl.pallas_call(
        functools.partial(kernel, n, PIECES),
        out_shape=out_shape,
        in_specs=in_vmem(4 + len(extra)),
        out_specs=tuple(in_vmem(len(out_shape))),
        scratch_shapes=scratch,
        compiler_params=pltpu.CompilerParams(
            collective_id=collective_id, has_side_effects=True, vmem_limit_bytes=56 << 20
        ),
        name="backward_exchange",
    )(partial, grad_out, normal_in, gain[None, :], *extra)


GROUPS = 2
PARTS = 2 * GROUPS


def part_rows(columns, part, base=0):
    size = columns // GROUPS
    return pl.ds(base + (part % 2) * columns + (part // 2) * size, size)


def group_parts(group):
    return (2 * group, 2 * group + 1)


def group_heads(heads, group):
    assert heads % GROUPS == 0
    size = heads // GROUPS
    return range(heads) if group is None else range(group * size, (group + 1) * size)


def attend_kernel(scale, length, qkv, out, out_wide, log_total, held, high, low_sum, sems_send, sems_recv):
    columns = qkv.shape[0] // 3
    frames = qkv.shape[1]
    heads = columns // HD
    me = lax.axis_index("ctx")

    def partner(r):
        return {"ctx": jnp.bitwise_xor(me, r)}

    barrier = pltpu.get_barrier_semaphore()
    for r in (1, 2):
        pl.semaphore_signal(barrier, inc=1, device_id=partner(r), device_id_type=MESH)
    pl.semaphore_wait(barrier, 2)

    def send(slot, part, to):
        rows, own_rows = part_rows(columns, part), part_rows(columns, part, columns)
        src = qkv.at[own_rows] if slot != 3 else held.at[1, rows]
        return pltpu.make_async_remote_copy(
            src_ref=src,
            dst_ref=held.at[slot - 1, rows],
            send_sem=sems_send.at[slot - 1, part],
            recv_sem=sems_recv.at[slot - 1, part],
            device_id=partner(to),
            device_id_type=MESH,
        )

    for part in range(PARTS):
        send(2, part, 2).start()
    for part in range(PARTS):
        send(1, part, 1).start()

    high[...] = jnp.full_like(high, NEGATIVE)
    low_sum[...] = jnp.zeros_like(low_sum)
    out_wide[...] = jnp.zeros_like(out_wide)
    limit = length[0]

    def block(keys_ref, key_row, value_row, slot, group=None):
        owner = jnp.bitwise_xor(me, slot)
        left = limit - owner * frames
        valid = lax.broadcasted_iota(jnp.int32, (frames, frames), 0) < left
        for h in group_heads(heads, group):
            rows = pl.ds(h * HD, HD)
            keys = keys_ref[pl.ds(key_row + h * HD, HD), :]
            values = keys_ref[pl.ds(value_row + h * HD, HD), :]
            scores = lax.dot_general(
                keys, qkv[rows, :], (((0,), (0,)), ((), ())), preferred_element_type=WIDE
            )
            scores = jnp.where(valid, scores * scale, NEGATIVE)
            before = high[h : h + 1, :]
            now = jnp.maximum(before, jnp.max(scores, axis=0, keepdims=True))
            shrink = jnp.exp(before - now)
            raised = jnp.exp(scores - now)
            low_sum[h : h + 1, :] = low_sum[h : h + 1, :] * shrink + jnp.sum(
                raised, axis=0, keepdims=True
            )
            high[h : h + 1, :] = now
            out_wide[rows, :] = out_wide[rows, :] * shrink + jnp.dot(
                values, raised.astype(LOW), preferred_element_type=WIDE
            )

    block(qkv, columns, 2 * columns, 0)
    for part in range(PARTS):
        send(1, part, 1).wait_recv()
    block(held.at[0], 0, columns, 1)
    for group in range(GROUPS):
        for part in group_parts(group):
            send(2, part, 2).wait_recv()
            send(3, part, 1).start()
        block(held.at[1], 0, columns, 2, group)
    for group in range(GROUPS):
        for part in group_parts(group):
            send(3, part, 1).wait_recv()
        block(held.at[2], 0, columns, 3, group)
    for h in range(heads):
        rows = pl.ds(h * HD, HD)
        total = low_sum[h : h + 1, :]
        done = out_wide[rows, :] / total
        out_wide[rows, :] = done
        out[rows, :] = done.astype(LOW)
        log_total[h : h + 1, :] = high[h : h + 1, :] + jnp.log(total)
    for slot in (1, 2, 3):
        for part in range(PARTS):
            send(slot, part, 2 if slot == 2 else 1).wait_send()


def attend(qkv, length, scale, collective_id):
    columns, frames = qkv.shape[0] // 3, qkv.shape[1]
    return pl.pallas_call(
        functools.partial(attend_kernel, scale),
        out_shape=(
            jax.ShapeDtypeStruct((columns, frames), LOW),
            jax.ShapeDtypeStruct((columns, frames), WIDE),
            jax.ShapeDtypeStruct((8, frames), WIDE),
            jax.ShapeDtypeStruct((3, 2 * columns, frames), LOW),
        ),
        in_specs=[pl.BlockSpec(memory_space=pltpu.SMEM)] + in_vmem(1),
        out_specs=tuple(in_vmem(4)),
        scratch_shapes=[
            pltpu.VMEM((8, frames), WIDE),
            pltpu.VMEM((8, frames), WIDE),
            pltpu.SemaphoreType.DMA((3, PARTS)),
            pltpu.SemaphoreType.DMA((3, PARTS)),
        ],
        compiler_params=pltpu.CompilerParams(
            collective_id=collective_id, has_side_effects=True, vmem_limit_bytes=56 << 20
        ),
        name="attend",
    )(length, qkv)


class LineGather:
    def __init__(self, own, gathered, sends, recvs):
        self.own, self.gathered, self.sends, self.recvs = own, gathered, sends, recvs
        self.n = gathered.shape[0] // own.shape[0]
        self.me = lax.axis_index("tp")
        self.further = (self.me < self.n - 1, self.me > 0)
        self.peers = ({"tp": lax.rem(self.me + 1, self.n)}, {"tp": lax.rem(self.me + self.n - 1, self.n)})

    def greet(self, barrier):
        for way in range(2):

            @pl.when(self.further[way])
            def _():
                pl.semaphore_signal(barrier, inc=1, device_id=self.peers[way], device_id_type=MESH)

        return self.further[0].astype(jnp.int32) + self.further[1].astype(jnp.int32)

    def rows(self, shard):
        size = self.own.shape[0]
        return pl.ds(pl.multiple_of(shard * size, size), size)

    def there(self, way, hops):
        return self.me - hops >= 0 if way == 0 else self.me + hops <= self.n - 1

    def send(self, way, hops):
        shard = self.me - hops if way == 0 else self.me + hops
        rows = self.rows(shard)
        return pltpu.make_async_remote_copy(
            src_ref=self.own if hops == 0 else self.gathered.at[rows],
            dst_ref=self.gathered.at[rows],
            send_sem=self.sends.at[way, hops],
            recv_sem=self.recvs.at[way, hops],
            device_id=self.peers[way],
            device_id_type=MESH,
        )

    def arrival(self, way, hops):
        rows = self.rows(self.me - hops if way == 0 else self.me + hops)
        return pltpu.make_async_remote_copy(
            src_ref=self.gathered.at[rows],
            dst_ref=self.gathered.at[rows],
            send_sem=self.sends.at[way, hops],
            recv_sem=self.recvs.at[way, hops - 1],
            device_id=self.peers[way],
            device_id_type=MESH,
        )

    def hop(self, hops):
        for way in range(2):
            if hops > 0:

                @pl.when(self.there(way, hops))
                def _():
                    self.arrival(way, hops).wait_recv()

            if hops < self.n - 1:

                @pl.when(self.there(way, hops) & self.further[way])
                def _():
                    self.send(way, hops).start()

    def drain(self):
        for hops in range(self.n - 1):
            for way in range(2):

                @pl.when(self.there(way, hops) & self.further[way])
                def _():
                    self.send(way, hops).wait_send()


def attend_back_kernel(scale, sharing, length, qkv, held, grad, out_wide, log_total, *refs):
    if sharing:
        own, grad_qkv, gathered, mine, parts, landed, acc, sems_send, sems_recv, sends, recvs = refs
        share = LineGather(own, gathered, sends, recvs)
    else:
        grad_qkv, mine, parts, landed, acc, sems_send, sems_recv = refs
        share = None
    columns = qkv.shape[0] // 3
    frames = qkv.shape[1]
    heads = columns // HD
    me = lax.axis_index("ctx")

    def partner(r):
        return {"ctx": jnp.bitwise_xor(me, r)}

    barrier = pltpu.get_barrier_semaphore()
    for r in (1, 2):
        pl.semaphore_signal(barrier, inc=1, device_id=partner(r), device_id_type=MESH)
    waiting = 2
    if share is not None:
        waiting = waiting + share.greet(barrier)
    pl.semaphore_wait(barrier, waiting)
    if share is not None:
        share.hop(0)
        gathered[share.rows(share.me), :] = own[...]

    def send(at, part, to):
        rows = part_rows(columns, part)
        return pltpu.make_async_remote_copy(
            src_ref=parts.at[at, rows],
            dst_ref=landed.at[at, rows],
            send_sem=sems_send.at[at, part],
            recv_sem=sems_recv.at[at, part],
            device_id=partner(to),
            device_id_type=MESH,
        )

    acc[...] = jnp.zeros_like(acc)
    limit = length[0]

    def block(keys_ref, key_row, value_row, slot, store, group=None):
        owner = jnp.bitwise_xor(me, slot)
        left = limit - owner * frames
        valid = lax.broadcasted_iota(jnp.int32, (frames, frames), 0) < left
        for h in group_heads(heads, group):
            rows = pl.ds(h * HD, HD)
            keys = keys_ref[pl.ds(key_row + h * HD, HD), :]
            values = keys_ref[pl.ds(value_row + h * HD, HD), :]
            queries = qkv[rows, :]
            upstream = grad[rows, :]
            scores = lax.dot_general(
                keys, queries, (((0,), (0,)), ((), ())), preferred_element_type=WIDE
            )
            weights = jnp.where(valid, jnp.exp(scores * scale - log_total[h : h + 1, :]), 0.0)
            grad_weights = lax.dot_general(
                values, upstream, (((0,), (0,)), ((), ())), preferred_element_type=WIDE
            )
            row_terms = jnp.sum(
                upstream.astype(WIDE) * out_wide[rows, :], axis=0, keepdims=True
            )
            grad_scores = (weights * (grad_weights - row_terms)).astype(LOW)
            acc[rows, :] += jnp.dot(keys, grad_scores, preferred_element_type=WIDE)
            grad_keys = (
                lax.dot_general(
                    queries, grad_scores, (((1,), (1,)), ((), ())), preferred_element_type=WIDE
                )
                * scale
            )
            grad_values = lax.dot_general(
                upstream, weights.astype(LOW), (((1,), (1,)), ((), ())), preferred_element_type=WIDE
            )
            store(h * HD, grad_keys, grad_values)

    def store_part(at):
        def store(row, grad_keys, grad_values):
            parts[at, pl.ds(row, HD), :] = grad_keys.astype(LOW)
            parts[at, pl.ds(columns + row, HD), :] = grad_values.astype(LOW)

        return store

    def store_mine(row, grad_keys, grad_values):
        mine[pl.ds(row, HD), :] = grad_keys
        mine[pl.ds(columns + row, HD), :] = grad_values

    def store_joined(row, grad_keys, grad_values):
        for start, value in ((row, grad_keys), (columns + row, grad_values)):
            rows = pl.ds(start, HD)
            parts[1, rows, :] = (value + landed[0, rows, :].astype(WIDE)).astype(LOW)

    for group in range(GROUPS):
        block(held.at[2], 0, columns, 3, store_part(0), group)
        for part in group_parts(group):
            send(0, part, 1).start()
    for group in range(GROUPS):
        for part in group_parts(group):
            send(0, part, 1).wait_recv()
        block(held.at[1], 0, columns, 2, store_joined, group)
        for part in group_parts(group):
            send(1, part, 2).start()
        if share is not None and group == 0:
            share.hop(1)
    for group in range(GROUPS):
        block(held.at[0], 0, columns, 1, store_part(2), group)
        for part in group_parts(group):
            send(2, part, 1).start()
        if share is not None and group == 0:
            share.hop(2)
    block(qkv, columns, 2 * columns, 0, store_mine)
    grad_qkv[0:columns, :] = (acc[...] * scale).astype(LOW)
    for part in range(PARTS):
        send(2, part, 1).wait_recv()
    for part in range(PARTS):
        send(1, part, 2).wait_recv()
    grad_qkv[columns:, :] = (
        mine[...] + landed[1].astype(WIDE) + landed[2].astype(WIDE)
    ).astype(LOW)
    for at in range(3):
        for part in range(PARTS):
            send(at, part, 2 if at == 1 else 1).wait_send()
    if share is not None:
        for hops in range(3, share.n):
            share.hop(hops)
        share.drain()


def attend_back(qkv, held, grad, out_wide, log_total, length, scale, collective_id, own=None):
    columns, frames = qkv.shape[0] // 3, qkv.shape[1]
    out_shape = (jax.ShapeDtypeStruct((3 * columns, frames), LOW),)
    extra, sems = (), []
    if own is not None:
        n = lax.axis_size("tp")
        assert n >= 3
        out_shape += (jax.ShapeDtypeStruct((n * own.shape[0], own.shape[1]), LOW),)
        extra, sems = (own,), [pltpu.SemaphoreType.DMA((2, n))] * 2
    return pl.pallas_call(
        functools.partial(attend_back_kernel, scale, own is not None),
        out_shape=out_shape,
        in_specs=[pl.BlockSpec(memory_space=pltpu.SMEM)] + in_vmem(5 + len(extra)),
        out_specs=tuple(in_vmem(len(out_shape))),
        scratch_shapes=[
            pltpu.VMEM((2 * columns, frames), WIDE),
            pltpu.VMEM((3, 2 * columns, frames), LOW),
            pltpu.VMEM((3, 2 * columns, frames), LOW),
            pltpu.VMEM((columns, frames), WIDE),
            pltpu.SemaphoreType.DMA((3, PARTS)),
            pltpu.SemaphoreType.DMA((3, PARTS)),
            *sems,
        ],
        compiler_params=pltpu.CompilerParams(
            collective_id=collective_id, has_side_effects=True, vmem_limit_bytes=56 << 20
        ),
        name="attend_back",
    )(length, qkv, held, grad, out_wide, log_total, *extra)


def gelu_value(values):
    return 0.5 * values * (1.0 + lax.erf(values * ROOT_HALF))


def gelu_slope(values):
    return 0.5 * (1.0 + lax.erf(values * ROOT_HALF)) + values * DENSITY * jnp.exp(
        -0.5 * values * values
    )


def product(left_side, right_side, left_axis, right_axis):
    return lax.dot_general(
        left_side,
        right_side,
        (((left_axis,), (right_axis,)), ((), ())),
        preferred_element_type=WIDE,
    )


def per_device(
    hidden,
    cotangent,
    lengths,
    query_weight,
    key_weight,
    value_weight,
    output_weight,
    inner_weight,
    outer_weight,
    query_bias,
    value_bias,
    inner_bias,
    output_bias,
    outer_bias,
    first_gain,
    first_shift,
    second_gain,
    second_shift,
):
    clip_count, rows, width = hidden.shape
    assert clip_count == 1
    assert lax.axis_size("ctx") == 4
    tp_size = lax.axis_size("tp")
    own_rows = rows // tp_size
    columns = query_weight.shape[2]
    hidden_local = inner_weight.shape[2]
    scale = 1.0 / math.sqrt(HD)
    own_start = lax.axis_index("tp") * own_rows

    def own_slice(full):
        return lax.dynamic_slice_in_dim(full, own_start, own_rows, axis=0)

    small = jnp.concatenate(
        [output_bias, outer_bias, first_gain, first_shift, second_gain, second_shift], axis=0
    ).astype(LOW)
    small = jnp.pad(small, ((0, -small.shape[0] % 16), (0, 0)))

    def qkv_shard(layer):
        return jnp.concatenate(
            [query_weight[layer].T, key_weight[layer].T, value_weight[layer].T], axis=0
        ).astype(LOW)

    projections = output_weight.astype(LOW).reshape(-1, output_weight.shape[2])
    if lax.axis_size("fsdp") == 2:
        qkv_first, projections, small, *lows = fetch_first(
            (qkv_shard(0), projections), (True, True), small, (inner_weight, outer_weight), 17
        )
        inner_low, outer_low = lows[:LAYERS], lows[LAYERS:]
    else:
        qkv_first = lax.all_gather(qkv_shard(0), "fsdp", axis=1, tiled=True)
        projections = lax.all_gather(projections, "fsdp", axis=1, tiled=True)
        small = lax.all_gather(small, "fsdp", axis=1, tiled=True)
        inner_low, outer_low = inner_weight.astype(LOW), outer_weight.astype(LOW)
    small = small.astype(WIDE)
    projections = projections.reshape(LAYERS, columns, width)

    def vector(kind, layer):
        return small[kind * LAYERS + layer]

    def fetch(layer):
        qkv = qkv_first
        if layer > 0:
            qkv = lax.all_gather(qkv_shard(layer), "fsdp", axis=1, tiled=True)
        out = projections[layer]
        inner = lax.all_gather(inner_low[layer], "fsdp", axis=0, tiled=True)
        outer = lax.all_gather(outer_low[layer], "fsdp", axis=1, tiled=True)
        return (qkv, out, inner, outer)

    weights = [fetch(layer) for layer in range(LAYERS)]

    hidden_rows = hidden.reshape(rows, width)
    residual = own_slice(hidden_rows)
    hat_full, _ = norm_parts(hidden_rows)
    normed = (hat_full * vector(2, 0) + vector(3, 0)).astype(LOW)
    kept = []
    for layer in range(LAYERS):
        w_qkv, w_out, w_inner, w_outer = weights[layer]
        bias_qkv = jnp.concatenate(
            [query_bias[layer], jnp.zeros_like(query_bias[layer]), value_bias[layer]]
        )
        qkv = (product(w_qkv, normed, 1, 1) + bias_qkv[:, None]).astype(LOW)
        attended, attended_wide, log_total, held = attend(qkv, lengths, scale, 2 * layer)
        branch = product(attended, w_out, 0, 0).astype(LOW)
        normed_two, middle = forward_exchange(
            branch, residual, vector(0, layer), vector(4, layer), vector(5, layer), tp_size, 2 * layer + 4
        )
        inner_pre = product(normed_two, w_inner, 1, 0) + inner_bias[layer]
        active = gelu_value(inner_pre).astype(LOW)
        kept.append(
            (residual, normed, qkv, attended, attended_wide, log_total, held, middle, normed_two, inner_pre, active)
        )
        branch = product(active, w_outer, 1, 0).astype(LOW)
        if layer + 1 < LAYERS:
            normed, residual = forward_exchange(
                branch,
                middle,
                vector(1, layer),
                vector(2, layer + 1),
                vector(3, layer + 1),
                tp_size,
                2 * layer + 5,
            )
        else:
            last_branch, last_middle = branch, middle

    def exchange_back(branch, grad_out, normal_in, gain, collective_id, arrays, by_column):
        if lax.axis_size("fsdp") == 2:
            return backward_exchange(
                branch, grad_out, normal_in, gain, tp_size, collective_id, arrays, by_column
            )
        result = backward_exchange(branch, grad_out, normal_in, gain, tp_size, collective_id)
        for array, column in zip(arrays, by_column):
            axis = 1 if column else 0
            array = lax.psum_scatter(array, ("fsdp", "ctx"), scatter_dimension=axis, tiled=True)
            result += (lax.all_gather(array, "ctx", axis=axis, tiled=True),)
        return result

    grad_rows = cotangent.reshape(rows, width)
    grad_own = own_slice(grad_rows)
    grad_low = grad_rows.astype(LOW)
    outer_bias_sum = jnp.sum(grad_own, axis=0)
    grads = [None] * LAYERS
    vectors = [None] * LAYERS
    biases = [None] * LAYERS
    for layer in reversed(range(LAYERS)):
        w_qkv, w_out, w_inner, w_outer = weights[layer]
        (
            residual,
            normed,
            qkv,
            attended,
            attended_wide,
            log_total,
            held,
            middle,
            normed_two,
            inner_pre,
            active,
        ) = kept[layer]
        grad_active = product(grad_low, w_outer, 1, 1)
        grad_inner = (grad_active * gelu_slope(inner_pre)).astype(LOW)
        branch = product(grad_inner, w_inner, 1, 1).astype(LOW)
        grad_outer_w = product(active, grad_low, 0, 0).astype(LOW)
        grad_inner_w = product(normed_two, grad_inner, 0, 0).astype(LOW)
        grad_mid_low, grad_middle, sums_two, *summed_two = exchange_back(
            branch, grad_own, middle, vector(4, layer), 2 * layer + 8, (grad_inner_w, grad_outer_w), (False, True)
        )
        if layer == LAYERS - 1:
            last_branch, grad_mid_low = lax.optimization_barrier((last_branch, grad_mid_low))
            last_branch = lax.psum_scatter(last_branch, "tp", scatter_dimension=0, tiled=True)
        grad_attended = product(w_out, grad_mid_low, 1, 1).astype(LOW)
        grad_qkv, *shared = attend_back(
            qkv,
            held,
            grad_attended,
            attended_wide,
            log_total,
            lengths,
            scale,
            2 * layer + 12,
            last_rows if layer == 0 else None,
        )
        grad_output_w = product(attended, grad_mid_low, 1, 0).astype(LOW)
        branch = product(grad_qkv, w_qkv, 0, 0).astype(LOW)
        grad_qkv_w = product(grad_qkv, normed, 1, 0).astype(LOW)
        if layer == LAYERS - 1:
            last_branch, branch = lax.optimization_barrier((last_branch, branch))
            last_rows = (last_middle + last_branch.astype(WIDE) + vector(1, layer)).astype(LOW)
        if layer == 0:
            output = shared[0].astype(WIDE)
        grad_low, grad_own, sums_one, *summed_one = exchange_back(
            branch, grad_middle, residual, vector(2, layer), 2 * layer + 9, (grad_qkv_w, grad_output_w), (True, True)
        )
        grads[layer] = (*summed_one, *summed_two)
        vectors[layer] = [
            sums_two[2], outer_bias_sum, sums_one[0], sums_one[1], sums_two[0], sums_two[1]
        ]
        outer_bias_sum = sums_one[2]
        biases[layer] = jnp.concatenate(
            [
                jnp.sum(grad_qkv.astype(WIDE), axis=1),
                jnp.sum(grad_inner.astype(WIDE), axis=0),
            ]
        )
    grad_hidden = grad_low.astype(WIDE)

    shard = output_bias.shape[1]
    flat_biases = jnp.concatenate(biases)
    flat_biases = jnp.pad(flat_biases, (0, -flat_biases.size % (8 * shard))).reshape(-1, shard)
    vector_count = 6 * LAYERS
    small_sums = jnp.stack([row for parts in zip(*vectors) for row in parts])
    if lax.axis_size("fsdp") == 2:
        small_sums = jnp.pad(small_sums, ((0, -vector_count % 8), (0, 0)))
        shared_rows = small_sums.shape[0]
        small_sums = sum_all(
            small_sums, flat_biases, tuple((axis, lax.axis_size(axis)) for axis in ("ctx", "tp")), 16
        )
        vector_sums, bias_sums = small_sums[:vector_count], small_sums[shared_rows:]
    else:
        vector_sums = lax.psum(small_sums, ("fsdp", "ctx", "tp"))
        vector_sums = lax.dynamic_slice_in_dim(vector_sums, lax.axis_index("fsdp") * shard, shard, axis=1)
        bias_sums = lax.psum(flat_biases, ("fsdp", "ctx"))
    vector_sums = vector_sums.reshape(6, LAYERS, shard)
    bias_sums = bias_sums.reshape(-1)[: LAYERS * biases[0].size].reshape(LAYERS, -1)

    def stacked(which):
        return jnp.stack([grads[layer][which] for layer in range(LAYERS)]).astype(WIDE)

    def turned(start):
        return jnp.stack([grads[layer][0][start : start + columns].T for layer in range(LAYERS)]).astype(WIDE)

    return (
        output.reshape(hidden.shape),
        grad_hidden.reshape(hidden.shape),
        turned(0),
        turned(columns),
        turned(2 * columns),
        stacked(1),
        stacked(2),
        stacked(3),
        bias_sums[:, :columns],
        bias_sums[:, 2 * columns : 3 * columns],
        bias_sums[:, 3 * columns :],
        vector_sums[0],
        vector_sums[1],
        vector_sums[2],
        vector_sums[3],
        vector_sums[4],
        vector_sums[5],
    )


def solution(mesh):
    in_specs = (
        P("fsdp", "ctx", None),
        P("fsdp", "ctx", None),
        P("fsdp"),
        P(None, "fsdp", "tp"),
        P(None, "fsdp", "tp"),
        P(None, "fsdp", "tp"),
        P(None, "tp", "fsdp"),
        P(None, "fsdp", "tp"),
        P(None, "tp", "fsdp"),
        P(None, "tp"),
        P(None, "tp"),
        P(None, "tp"),
        P(None, "fsdp"),
        P(None, "fsdp"),
        P(None, "fsdp"),
        P(None, "fsdp"),
        P(None, "fsdp"),
        P(None, "fsdp"),
    )
    out_specs = (
        P("fsdp", "ctx", None),
        P("fsdp", "ctx", None),
        P(None, "fsdp", "tp"),
        P(None, "fsdp", "tp"),
        P(None, "fsdp", "tp"),
        P(None, "tp", "fsdp"),
        P(None, "fsdp", "tp"),
        P(None, "tp", "fsdp"),
        P(None, "tp"),
        P(None, "tp"),
        P(None, "tp"),
        P(None, "fsdp"),
        P(None, "fsdp"),
        P(None, "fsdp"),
        P(None, "fsdp"),
        P(None, "fsdp"),
        P(None, "fsdp"),
    )
    return jax.shard_map(
        per_device, mesh=mesh, in_specs=in_specs, out_specs=out_specs, check_vma=False
    )
```

```python
import functools
import math
import jax
import jax.numpy as jnp
from jax import lax
from jax.experimental import pallas as pl
from jax.experimental.pallas import tpu as pltpu
from jax.sharding import PartitionSpec as P

MESH = pl.DeviceIdType.MESH
LOW = jnp.bfloat16
WIDE = jnp.float32
EPSILON = 1e-05
NEGATIVE = -1e30
HD = 80
PIECES = 4
LAYERS = 2
ROOT_HALF = 1.0 / math.sqrt(2.0)
DENSITY = 1.0 / math.sqrt(2.0 * math.pi)
REDUCE_LAG = 2
GATHER_LAG = 3


def norm_parts(values):
    average = jnp.mean(values, axis=-1, keepdims=True)
    centered = values - average
    spread = jnp.mean(centered * centered, axis=-1, keepdims=True)
    inverse = lax.rsqrt(spread + EPSILON)
    return (centered * inverse, inverse)


def norm_back(upstream, normal_hat, inverse, gain_full):
    scaled = upstream * gain_full
    first_mean = jnp.mean(scaled, axis=-1, keepdims=True)
    second_mean = jnp.mean(scaled * normal_hat, axis=-1, keepdims=True)
    return inverse * (scaled - first_mean - normal_hat * second_mean)


def line_exchange(n, own, pieces, partial, gathered, from_left, from_right, total, sems, finish, side=None):
    rs_send, rs_recv, ag_send, ag_recv = sems
    me = lax.axis_index("tp")
    piece = own // pieces
    to_right, to_left = {"tp": lax.rem(me + 1, n)}, {"tp": lax.rem(me + n - 1, n)}
    has_left, has_right = me > 0, me < n - 1

    barrier = pltpu.get_barrier_semaphore()

    @pl.when(has_left)
    def _():
        pl.semaphore_signal(barrier, inc=1, device_id=to_left, device_id_type=MESH)

    @pl.when(has_right)
    def _():
        pl.semaphore_signal(barrier, inc=1, device_id=to_right, device_id_type=MESH)

    peers = has_left.astype(jnp.int32) + has_right.astype(jnp.int32)
    if side is not None:
        for peer in side.peers:
            pl.semaphore_signal(barrier, inc=1, device_id=peer, device_id_type=MESH)
        peers = peers + len(side.peers)
    pl.semaphore_wait(barrier, peers)
    if side is not None:
        side.start()

    def rows_of(shard, step):
        return pl.ds(pl.multiple_of(shard * own + step * piece, piece), piece)

    def reduce_copy(way, src, shard, step):
        rows = rows_of(shard, step)
        landing = from_left if way == 0 else from_right
        return pltpu.make_async_remote_copy(
            src_ref=src.at[rows],
            dst_ref=landing.at[rows],
            send_sem=rs_send.at[way, shard, step],
            recv_sem=rs_recv.at[way, shard, step],
            device_id=to_right if way == 0 else to_left,
            device_id_type=MESH,
        )

    def gather_copy(way, shard, step):
        rows = rows_of(shard, step)
        return pltpu.make_async_remote_copy(
            src_ref=gathered.at[rows],
            dst_ref=gathered.at[rows],
            send_sem=ag_send.at[way, shard, step],
            recv_sem=ag_recv.at[way, shard, step],
            device_id=to_right if way == 0 else to_left,
            device_id_type=MESH,
        )

    def reduce_one(way, shard, step):
        landing = from_left if way == 0 else from_right
        first = me == 0 if way == 0 else me == n - 1

        @pl.when(first)
        def _():
            reduce_copy(way, partial, shard, step).start()

        @pl.when(jnp.logical_not(first))
        def _():
            rows = rows_of(shard, step)
            reduce_copy(way, partial, shard, step).wait_recv()
            landing[rows, :] = (
                partial[rows, :].astype(WIDE) + landing[rows, :].astype(WIDE)
            ).astype(LOW)
            reduce_copy(way, landing, shard, step).start()

    def finish_one(step):
        rows = rows_of(me, step)
        total[...] = partial[rows, :].astype(WIDE)

        @pl.when(has_left)
        def _():
            reduce_copy(0, partial, me, step).wait_recv()
            total[...] += from_left[rows, :].astype(WIDE)

        @pl.when(has_right)
        def _():
            reduce_copy(1, partial, me, step).wait_recv()
            total[...] += from_right[rows, :].astype(WIDE)

        own_rows = pl.ds(pl.multiple_of(step * piece, piece), piece)
        gathered[rows, :] = finish(own_rows, total[...])

        @pl.when(has_right)
        def _():
            gather_copy(0, me, step).start()

        @pl.when(has_left)
        def _():
            gather_copy(1, me, step).start()

    def forward_one(way, shard, step):
        gather_copy(way, shard, step).wait_recv()

        @pl.when(has_right if way == 0 else has_left)
        def _():
            gather_copy(way, shard, step).start()

    period = n - 1

    def finish_at(device):
        from_start = jnp.where(device > 0, n - 1 - device + REDUCE_LAG * device, 0)
        from_end = jnp.where(device < n - 1, device + REDUCE_LAG * (n - 1 - device), 0)
        return jnp.maximum(from_start, from_end)

    def split(tick, start, length):
        since = tick - start
        clipped = jnp.maximum(since, 0)
        return (since >= 0) & (clipped < length), lax.div(clipped, period), lax.rem(clipped, period)

    def body(tick, carry):
        for way in range(2):
            hops = me if way == 0 else n - 1 - me
            due, step, k = split(tick, REDUCE_LAG * hops, pieces * period)
            shard = n - 1 - k if way == 0 else k
            mine = me < shard if way == 0 else me > shard

            @pl.when(due & mine)
            def _():
                reduce_one(way, shard, step)

        due, step, k = split(tick, finish_at(me), pieces * period)

        @pl.when(due & (k == 0))
        def _():
            finish_one(step)

        for hops in range(1, n):
            for way in range(2):
                shard = me - hops if way == 0 else me + hops
                there = shard >= 0 if way == 0 else shard <= n - 1
                due, step, k = split(
                    tick, finish_at(shard) + GATHER_LAG * hops, pieces * period
                )

                @pl.when(there & due & (k == 0))
                def _():
                    forward_one(way, shard, step)

        if side is not None:
            side.at(tick)
        return carry

    ticks = period * (pieces - 1) + max(REDUCE_LAG, 1) * (n - 1) + GATHER_LAG * (n - 1) + 1
    if side is not None:
        ticks = max(ticks, side.ticks)
    lax.fori_loop(0, ticks, body, 0)
    if side is not None:
        side.drain()

    def drain(step, carry):
        for k in range(n - 1):
            for way in range(2):
                shard = n - 1 - k if way == 0 else k
                sends = me < shard if way == 0 else me > shard

                @pl.when(sends)
                def _():
                    reduce_copy(way, partial, shard, step).wait_send()

        for k in range(n):
            for way in range(2):
                shard = me - k if way == 0 else me + k
                there = shard >= 0 if way == 0 else shard <= n - 1
                further = has_right if way == 0 else has_left

                @pl.when(there & further)
                def _():
                    gather_copy(way, shard, step).wait_send()

        return carry

    lax.fori_loop(0, pieces, drain, 0)


def exchange_scratch(n, rows, width, pieces):
    return [
        pltpu.VMEM((rows, width), LOW),
        pltpu.VMEM((rows, width), LOW),
        pltpu.VMEM((rows // n // pieces, width), WIDE),
        pltpu.SemaphoreType.DMA((2, n, pieces)),
        pltpu.SemaphoreType.DMA((2, n, pieces)),
        pltpu.SemaphoreType.DMA((2, n, pieces)),
        pltpu.SemaphoreType.DMA((2, n, pieces)),
    ]


def forward_fetch_kernel(
    n, pieces, partial, residual, bias, gain, shift, shard, gathered, middle, fetched, from_left, from_right, total,
    rs_send, rs_recv, ag_send, ag_recv, sends, recvs
):
    forward_exchange_kernel(
        n, pieces, partial, residual, bias, gain, shift, gathered, middle, from_left, from_right, total, rs_send, rs_recv,
        ag_send, ag_recv, side=QuartersSide((shard,), (fetched,), sends, recvs)
    )


def forward_exchange_kernel(
    n, pieces, partial, residual, bias, gain, shift, gathered, middle, from_left, from_right, total, *sems, side=None
):
    def finish(rows, value):
        mid = value + residual[rows, :] + bias[...]
        middle[rows, :] = mid
        hat, _ = norm_parts(mid)
        return (hat * gain[...] + shift[...]).astype(LOW)

    line_exchange(
        n, residual.shape[0], pieces, partial, gathered, from_left, from_right, total, sems, finish, side
    )


def backward_exchange_kernel(
    n, pieces, partial, grad_out, normal_in, gain, gathered, grad_in, sums, from_left, from_right, total, *sems, side=None
):
    sums[...] = jnp.zeros_like(sums)

    def finish(rows, upstream):
        hat, inverse = norm_parts(normal_in[rows, :])
        grad = grad_out[rows, :] + norm_back(upstream, hat, inverse, gain[...])
        grad_in[rows, :] = grad
        sums[0:1, :] += jnp.sum(upstream * hat, axis=0, keepdims=True)
        sums[1:2, :] += jnp.sum(upstream, axis=0, keepdims=True)
        sums[2:3, :] += jnp.sum(grad, axis=0, keepdims=True)
        return grad.astype(LOW)

    line_exchange(
        n, grad_out.shape[0], pieces, partial, gathered, from_left, from_right, total, sems, finish, side
    )


def in_vmem(count):
    return [pl.BlockSpec(memory_space=pltpu.VMEM)] * count


class GradientSum:
    LAGS = (0, 3, 6, 9)

    def __init__(self, by_column, arrays, outs, landings, sems):
        self.by_column = by_column
        self.chunks = landings[0].shape[1]
        self.arrays, self.outs, self.landings = arrays, outs, landings
        self.sends, self.recvs = sems
        self.half = lax.axis_index("fsdp")
        self.ctx = lax.axis_index("ctx")
        self.core = lax.rem(self.ctx, 2)
        pair = {"ctx": jnp.bitwise_xor(self.ctx, 1)}
        across = {"ctx": jnp.bitwise_xor(self.ctx, 2)}
        other = {"fsdp": 1 - self.half}
        self.peers = (pair, across, other)
        self.ticks = 2 * (self.chunks - 1) + self.LAGS[3] + 1

    def view(self, which, half, core, chunk):
        rows, cols = self.arrays[which].shape
        if not self.by_column[which]:
            part = rows // 4
            height = part // self.chunks
            start = half * (2 * part) + core * part + chunk * height
            return pl.ds(pl.multiple_of(start, 16), height), slice(None)
        part = rows // 2
        height = part // self.chunks
        start = core * part + chunk * height
        width = cols // 2
        return (
            pl.ds(pl.multiple_of(start, 16), height),
            pl.ds(pl.multiple_of(half * width, 128), width),
        )

    def out_rows(self, which, core, chunk):
        part = self.outs[which].shape[0] // 2
        height = part // self.chunks
        return pl.ds(pl.multiple_of(core * part + chunk * height, 16), height)

    def copy(self, which, stage, chunk, half=0):
        pair, across, other = self.peers
        landing = self.landings[which]
        if stage == 0:
            src = self.arrays[which].at[self.view(which, half, 1 - self.core, chunk)]
            slot, peer = half, pair
        elif stage == 1:
            src = landing.at[1 - self.half, chunk]
            slot, peer = 2, other
        elif stage == 2:
            src = landing.at[2, chunk]
            slot, peer = 3, across
        else:
            src = landing.at[3, chunk]
            slot, peer = 4, pair
        return pltpu.make_async_remote_copy(
            src_ref=src,
            dst_ref=landing.at[slot, chunk],
            send_sem=self.sends.at[which, slot, chunk],
            recv_sem=self.recvs.at[which, slot, chunk],
            device_id=peer,
            device_id_type=MESH,
        )

    def start(self):
        def body(chunk, carry):
            for which in range(len(self.arrays)):
                for half in range(2):
                    self.copy(which, 0, chunk, half).start()
            return carry

        lax.fori_loop(0, self.chunks, body, 0)

    def when_due(self, tick, lag, action):
        since = tick - lag
        clipped = jnp.maximum(since, 0)
        chunk = lax.div(clipped, 2)

        @pl.when((since >= 0) & (lax.rem(clipped, 2) == 0) & (chunk < self.chunks))
        def _():
            for which in range(len(self.arrays)):
                action(which, chunk)

    def at(self, tick):
        def joined(which, chunk):
            landing = self.landings[which]
            for half in range(2):
                self.copy(which, 0, chunk, half).wait_recv()
                rows, cols = self.view(which, half, self.core, chunk)
                landing[half, chunk] = (
                    self.arrays[which][rows, cols].astype(WIDE) + landing[half, chunk].astype(WIDE)
                ).astype(LOW)
            self.copy(which, 1, chunk).start()

        def crossed(which, chunk):
            landing = self.landings[which]
            self.copy(which, 1, chunk).wait_recv()
            landing[2, chunk] = (
                landing[self.half, chunk].astype(WIDE) + landing[2, chunk].astype(WIDE)
            ).astype(LOW)
            self.copy(which, 2, chunk).start()

        def summed(which, chunk):
            landing = self.landings[which]
            self.copy(which, 2, chunk).wait_recv()
            low = (landing[2, chunk].astype(WIDE) + landing[3, chunk].astype(WIDE)).astype(LOW)
            landing[3, chunk] = low
            self.outs[which][self.out_rows(which, self.core, chunk), :] = low
            self.copy(which, 3, chunk).start()

        def shared(which, chunk):
            self.copy(which, 3, chunk).wait_recv()
            self.outs[which][self.out_rows(which, 1 - self.core, chunk), :] = self.landings[which][
                4, chunk
            ]

        for lag, action in zip(self.LAGS, (joined, crossed, summed, shared)):
            self.when_due(tick, lag, action)

    def drain(self):
        def body(chunk, carry):
            for which in range(len(self.arrays)):
                for half in range(2):
                    self.copy(which, 0, chunk, half).wait_send()
                for stage in range(1, 4):
                    self.copy(which, stage, chunk).wait_send()
            return carry

        lax.fori_loop(0, self.chunks, body, 0)


def gradient_shapes(arrays, by_column):
    chunks = 5 if all(by_column) else 10
    outs, landings = (), []
    for array, column in zip(arrays, by_column):
        rows, cols = array.shape
        rows, cols = (rows, cols // 2) if column else (rows // 2, cols)
        outs += (jax.ShapeDtypeStruct((rows, cols), LOW),)
        landings.append(pltpu.VMEM((5, chunks, rows // 2 // chunks, cols), LOW))
    return outs, landings, pltpu.SemaphoreType.DMA((len(arrays), 5, chunks))


def backward_gradient_kernel(by_column, n, pieces, partial, grad_out, normal_in, gain, *refs):
    count = len(by_column)
    arrays, (gathered, grad_in, sums), refs = refs[:count], refs[count : count + 3], refs[count + 3 :]
    outs, (from_left, from_right, total, *sems), refs = refs[:count], refs[count : count + 7], refs[count + 7 :]
    side = GradientSum(by_column, arrays, outs, refs[:count], refs[count:])
    backward_exchange_kernel(
        n, pieces, partial, grad_out, normal_in, gain, gathered, grad_in, sums, from_left, from_right, total, *sems, side=side
    )


def sum_all_kernel(axes, vectors, biases, out, staged, landing, sends, recvs):
    half = lax.axis_index("fsdp")
    shared, width = vectors.shape[0], out.shape[1]
    steps = [("fsdp", 1)] + [(axis, 1 << b) for axis, size in axes for b in range(size.bit_length() - 1)]

    def peer(axis, k):
        return {axis: jnp.bitwise_xor(lax.axis_index(axis), k)}

    barrier = pltpu.get_barrier_semaphore()
    for axis, k in steps:
        pl.semaphore_signal(barrier, inc=1, device_id=peer(axis, k), device_id_type=MESH)
    for side in range(2):
        staged[side, 0:shared, :] = vectors[:, side * width : (side + 1) * width]
        staged[side, shared:, :] = biases[...]
    pl.semaphore_wait(barrier, len(steps))
    for at, (axis, k) in enumerate(steps):
        rows = pl.ds(0, shared) if axis == "tp" else pl.ds(0, out.shape[0])
        if at > 0:
            landing[at, 0, rows] = out[rows, :]
        copy = pltpu.make_async_remote_copy(
            src_ref=landing.at[at, 0, rows] if at > 0 else staged.at[1 - half],
            dst_ref=landing.at[at, 1, rows],
            send_sem=sends.at[at],
            recv_sem=recvs.at[at],
            device_id=peer(axis, k),
            device_id_type=MESH,
        )
        copy.start()
        copy.wait()
        own = landing[at, 0, rows] if at > 0 else staged[half]
        out[rows, :] = own + landing[at, 1, rows]


def sum_all(vectors, biases, axes, collective_id):
    shape = (vectors.shape[0] + biases.shape[0], biases.shape[1])
    steps = 1 + sum(size.bit_length() - 1 for _, size in axes)
    return pl.pallas_call(
        functools.partial(sum_all_kernel, axes),
        out_shape=jax.ShapeDtypeStruct(shape, WIDE),
        in_specs=in_vmem(2),
        out_specs=in_vmem(1)[0],
        scratch_shapes=[
            pltpu.VMEM((2,) + shape, WIDE),
            pltpu.VMEM((steps, 2) + shape, WIDE),
            pltpu.SemaphoreType.DMA((steps,)),
            pltpu.SemaphoreType.DMA((steps,)),
        ],
        compiler_params=pltpu.CompilerParams(collective_id=collective_id, has_side_effects=True),
        name="sum_all",
    )(vectors, biases)


def fetch_parts(rows):
    return next(parts for parts in (2, 3, 1) if rows // 4 % (16 * parts) == 0)


CAST_ROWS = 64


class Quarters:
    def __init__(self, shards, outs, sends, recvs):
        self.shards, self.outs, self.sends, self.recvs = shards, outs, sends, recvs
        self.half = lax.axis_index("fsdp")
        self.ctx = lax.axis_index("ctx")
        self.pair, self.across = jnp.bitwise_xor(self.ctx, 1), jnp.bitwise_xor(self.ctx, 2)
        self.targets = ({"fsdp": 1 - self.half}, {"ctx": self.across}, {"ctx": self.pair}, {"ctx": self.pair})
        self.peers = self.targets[:3]
        self.each = [
            (which, part) for which in range(len(shards)) for part in range(fetch_parts(shards[which].shape[0]))
        ]

    def rows_of(self, which, quarter, part):
        parts = fetch_parts(self.shards[which].shape[0])
        height = self.shards[which].shape[0] // 4 // parts
        return pl.ds(pl.multiple_of((quarter * parts + part) * height, 16), height)

    def place(self, which, side, quarter, part):
        cols = self.shards[which].shape[1]
        return self.outs[which].at[
            self.rows_of(which, quarter, part), pl.ds(pl.multiple_of(side * cols, 128), cols)
        ]

    def copy(self, stage, item, arriving=False):
        which, part = item
        quarter = (self.ctx, self.ctx, self.ctx, self.across)[stage]
        src = self.shards[which].at[self.rows_of(which, quarter, part)]
        dst = self.place(which, self.half, quarter, part)
        if stage > 0:
            src = dst = self.place(which, 1 - self.half, quarter, part)
        if arriving:
            quarter = (self.ctx, self.across, self.pair, jnp.bitwise_xor(self.ctx, 3))[stage]
            dst = self.place(which, 1 - self.half, quarter, part)
        return pltpu.make_async_remote_copy(
            src_ref=src,
            dst_ref=dst,
            send_sem=self.sends.at[which, stage, part],
            recv_sem=self.recvs.at[which, stage, part],
            device_id=self.targets[stage],
            device_id_type=MESH,
        )

    def begin(self):
        for item in self.each:
            self.copy(0, item).start()

    def keep_own(self):
        for shard, out in zip(self.shards, self.outs):
            cols = shard.shape[1]
            out[:, pl.ds(pl.multiple_of(self.half * cols, 128), cols)] = shard[...]

    def crossed(self, item):
        self.copy(0, item, True).wait_recv()
        self.copy(1, item).start()
        self.copy(2, item).start()

    def forwarded(self, item):
        self.copy(1, item, True).wait_recv()
        self.copy(3, item).start()

    def finish(self):
        for stage in (2, 3):
            for item in self.each:
                self.copy(stage, item, True).wait_recv()
        for stage in range(4):
            for item in self.each:
                self.copy(stage, item).wait_send()


class QuartersSide(Quarters):
    CROSSED, APART, FORWARDED = 4, 3, 3

    def start(self):
        self.begin()
        self.keep_own()

    @property
    def ticks(self):
        return self.CROSSED + self.FORWARDED + self.APART * (len(self.each) - 1) + 1

    def at(self, tick):
        for at, item in enumerate(self.each):
            due = self.CROSSED + self.APART * at

            @pl.when(tick == due)
            def _():
                self.crossed(item)

            @pl.when(tick == due + self.FORWARDED)
            def _():
                self.forwarded(item)

    def drain(self):
        self.finish()


def fetch_kernel(counts, jobs, *refs):
    refs = list(refs)

    def take(count):
        taken = refs[:count]
        del refs[:count]
        return taken

    shard_count, small_count, wide_count, low_count = counts
    shards, smalls, wides = take(shard_count), take(small_count), take(wide_count)
    outs, out_smalls, lows = take(shard_count), take(small_count), take(low_count)
    buffers = take(len(jobs))
    cast_sems, sends, recvs, small_sends, small_recvs = refs
    quarters = Quarters(shards, outs, sends, recvs)

    barrier = pltpu.get_barrier_semaphore()
    for peer in quarters.peers:
        pl.semaphore_signal(barrier, inc=1, device_id=peer, device_id_type=MESH)
    pl.semaphore_wait(barrier, 3)

    def small_copy(at, side):
        cols = smalls[at].shape[1]
        return pltpu.make_async_remote_copy(
            src_ref=smalls[at],
            dst_ref=out_smalls[at].at[:, pl.ds(pl.multiple_of(side * cols, 128), cols)],
            send_sem=small_sends.at[at],
            recv_sem=small_recvs.at[at],
            device_id=quarters.peers[0],
            device_id_type=MESH,
        )

    def load(at):
        which, layer, _, _ = jobs[at]
        return pltpu.make_async_copy(wides[which].at[layer], buffers[at], cast_sems.at[at])

    quarters.begin()
    for at in range(small_count):
        small_copy(at, quarters.half).start()
    for at in range(len(jobs)):
        load(at).start()
    quarters.keep_own()
    for small, out in zip(smalls, out_smalls):
        cols = small.shape[1]
        out[:, pl.ds(pl.multiple_of(quarters.half * cols, 128), cols)] = small[...]
    for at, (_, _, low, first) in enumerate(jobs):
        load(at).wait()

        def cast(step, carry):
            start = pl.multiple_of(step * CAST_ROWS, CAST_ROWS)
            lows[low][pl.ds(first + start, CAST_ROWS), :] = buffers[at][pl.ds(start, CAST_ROWS), :].astype(LOW)
            return carry

        lax.fori_loop(0, buffers[at].shape[0] // CAST_ROWS, cast, 0)
    last = len(quarters.each)
    for at in range(last + 1):
        if at < last:
            quarters.crossed(quarters.each[at])
        if at > 0:
            quarters.forwarded(quarters.each[at - 1])
    for at in range(small_count):
        small_copy(at, 1 - quarters.half).wait_recv()
    quarters.finish()
    for at in range(small_count):
        small_copy(at, quarters.half).wait_send()


def quarter_sems(shards):
    most = max(fetch_parts(shard.shape[0]) for shard in shards)
    return [pltpu.SemaphoreType.DMA((len(shards), 4, most))] * 2


def gathered_shape(shard):
    return jax.ShapeDtypeStruct((shard.shape[0], 2 * shard.shape[1]), shard.dtype)


def fetch_first(shards, smalls, wides, jobs, low_shapes, collective_id):
    counts = (len(shards), len(smalls), len(wides), len(low_shapes))
    out_shape = tuple(gathered_shape(array) for array in (*shards, *smalls))
    out_shape += tuple(jax.ShapeDtypeStruct(shape, LOW) for shape in low_shapes)
    return pl.pallas_call(
        functools.partial(fetch_kernel, counts, jobs),
        out_shape=out_shape,
        in_specs=in_vmem(len(shards) + len(smalls)) + [pl.BlockSpec(memory_space=pl.ANY)] * len(wides),
        out_specs=tuple(in_vmem(len(out_shape))),
        scratch_shapes=[pltpu.VMEM(wides[job[0]].shape[1:], WIDE) for job in jobs]
        + [pltpu.SemaphoreType.DMA((len(jobs),))]
        + quarter_sems(shards)
        + [pltpu.SemaphoreType.DMA((len(smalls),))] * 2,
        compiler_params=pltpu.CompilerParams(
            collective_id=collective_id, has_side_effects=True, vmem_limit_bytes=44 << 20
        ),
        name="fetch_first",
    )(*shards, *smalls, *wides)


def forward_exchange(partial, residual, bias, gain, shift, n, collective_id, shard=None):
    rows, width = partial.shape
    out_shape = (
        jax.ShapeDtypeStruct((rows, width), LOW),
        jax.ShapeDtypeStruct(residual.shape, WIDE),
    )
    scratch = exchange_scratch(n, rows, width, PIECES)
    kernel, extra = forward_exchange_kernel, ()
    if shard is not None:
        out_shape += (gathered_shape(shard),)
        scratch = scratch + quarter_sems((shard,))
        kernel, extra = forward_fetch_kernel, (shard,)
    return pl.pallas_call(
        functools.partial(kernel, n, PIECES),
        out_shape=out_shape,
        in_specs=in_vmem(5 + len(extra)),
        out_specs=tuple(in_vmem(len(out_shape))),
        scratch_shapes=scratch,
        compiler_params=pltpu.CompilerParams(
            collective_id=collective_id, has_side_effects=True, vmem_limit_bytes=40 << 20
        ),
        name="forward_exchange",
    )(partial, residual, bias[None, :], gain[None, :], shift[None, :], *extra)


def backward_exchange(partial, grad_out, normal_in, gain, n, collective_id, arrays=(), by_column=()):
    rows, width = partial.shape
    out_shape = (
        jax.ShapeDtypeStruct((rows, width), LOW),
        jax.ShapeDtypeStruct(grad_out.shape, WIDE),
        jax.ShapeDtypeStruct((8, width), WIDE),
    )
    scratch = exchange_scratch(n, rows, width, PIECES)
    kernel, extra = backward_exchange_kernel, ()
    if arrays:
        outs, landings, sems = gradient_shapes(arrays, by_column)
        out_shape = out_shape + outs
        scratch = scratch + landings + [sems] * 2
        kernel, extra = functools.partial(backward_gradient_kernel, by_column), arrays
    return pl.pallas_call(
        functools.partial(kernel, n, PIECES),
        out_shape=out_shape,
        in_specs=in_vmem(4 + len(extra)),
        out_specs=tuple(in_vmem(len(out_shape))),
        scratch_shapes=scratch,
        compiler_params=pltpu.CompilerParams(
            collective_id=collective_id, has_side_effects=True, vmem_limit_bytes=56 << 20
        ),
        name="backward_exchange",
    )(partial, grad_out, normal_in, gain[None, :], *extra)


GROUPS = 2
PARTS = 2 * GROUPS


def part_rows(columns, part, base=0):
    size = columns // GROUPS
    return pl.ds(base + (part % 2) * columns + (part // 2) * size, size)


def group_parts(group):
    return (2 * group, 2 * group + 1)


def group_heads(heads, group):
    assert heads % GROUPS == 0
    size = heads // GROUPS
    return range(heads) if group is None else range(group * size, (group + 1) * size)


def attend_kernel(scale, length, qkv, out, out_wide, log_total, held, high, low_sum, sems_send, sems_recv):
    columns = qkv.shape[0] // 3
    frames = qkv.shape[1]
    heads = columns // HD
    me = lax.axis_index("ctx")

    def partner(r):
        return {"ctx": jnp.bitwise_xor(me, r)}

    barrier = pltpu.get_barrier_semaphore()
    for r in (1, 2):
        pl.semaphore_signal(barrier, inc=1, device_id=partner(r), device_id_type=MESH)
    pl.semaphore_wait(barrier, 2)

    def send(slot, part, to):
        rows, own_rows = part_rows(columns, part), part_rows(columns, part, columns)
        src = qkv.at[own_rows] if slot != 3 else held.at[1, rows]
        return pltpu.make_async_remote_copy(
            src_ref=src,
            dst_ref=held.at[slot - 1, rows],
            send_sem=sems_send.at[slot - 1, part],
            recv_sem=sems_recv.at[slot - 1, part],
            device_id=partner(to),
            device_id_type=MESH,
        )

    for part in range(PARTS):
        send(2, part, 2).start()
    for part in range(PARTS):
        send(1, part, 1).start()

    high[...] = jnp.full_like(high, NEGATIVE)
    low_sum[...] = jnp.zeros_like(low_sum)
    out_wide[...] = jnp.zeros_like(out_wide)
    limit = length[0]

    def block(keys_ref, key_row, value_row, slot, group=None):
        owner = jnp.bitwise_xor(me, slot)
        left = limit - owner * frames
        valid = lax.broadcasted_iota(jnp.int32, (frames, frames), 0) < left
        for h in group_heads(heads, group):
            rows = pl.ds(h * HD, HD)
            keys = keys_ref[pl.ds(key_row + h * HD, HD), :]
            values = keys_ref[pl.ds(value_row + h * HD, HD), :]
            scores = lax.dot_general(
                keys, qkv[rows, :], (((0,), (0,)), ((), ())), preferred_element_type=WIDE
            )
            scores = jnp.where(valid, scores * scale, NEGATIVE)
            before = high[h : h + 1, :]
            now = jnp.maximum(before, jnp.max(scores, axis=0, keepdims=True))
            shrink = jnp.exp(before - now)
            raised = jnp.exp(scores - now)
            low_sum[h : h + 1, :] = low_sum[h : h + 1, :] * shrink + jnp.sum(
                raised, axis=0, keepdims=True
            )
            high[h : h + 1, :] = now
            out_wide[rows, :] = out_wide[rows, :] * shrink + jnp.dot(
                values, raised.astype(LOW), preferred_element_type=WIDE
            )

    block(qkv, columns, 2 * columns, 0)
    for part in range(PARTS):
        send(1, part, 1).wait_recv()
    block(held.at[0], 0, columns, 1)
    for group in range(GROUPS):
        for part in group_parts(group):
            send(2, part, 2).wait_recv()
            send(3, part, 1).start()
        block(held.at[1], 0, columns, 2, group)
    for group in range(GROUPS):
        for part in group_parts(group):
            send(3, part, 1).wait_recv()
        block(held.at[2], 0, columns, 3, group)
    for h in range(heads):
        rows = pl.ds(h * HD, HD)
        total = low_sum[h : h + 1, :]
        done = out_wide[rows, :] / total
        out_wide[rows, :] = done
        out[rows, :] = done.astype(LOW)
        log_total[h : h + 1, :] = high[h : h + 1, :] + jnp.log(total)
    for slot in (1, 2, 3):
        for part in range(PARTS):
            send(slot, part, 2 if slot == 2 else 1).wait_send()


def attend(qkv, length, scale, collective_id):
    columns, frames = qkv.shape[0] // 3, qkv.shape[1]
    return pl.pallas_call(
        functools.partial(attend_kernel, scale),
        out_shape=(
            jax.ShapeDtypeStruct((columns, frames), LOW),
            jax.ShapeDtypeStruct((columns, frames), WIDE),
            jax.ShapeDtypeStruct((8, frames), WIDE),
            jax.ShapeDtypeStruct((3, 2 * columns, frames), LOW),
        ),
        in_specs=[pl.BlockSpec(memory_space=pltpu.SMEM)] + in_vmem(1),
        out_specs=tuple(in_vmem(4)),
        scratch_shapes=[
            pltpu.VMEM((8, frames), WIDE),
            pltpu.VMEM((8, frames), WIDE),
            pltpu.SemaphoreType.DMA((3, PARTS)),
            pltpu.SemaphoreType.DMA((3, PARTS)),
        ],
        compiler_params=pltpu.CompilerParams(
            collective_id=collective_id, has_side_effects=True, vmem_limit_bytes=56 << 20
        ),
        name="attend",
    )(length, qkv)


class LineGather:
    def __init__(self, own, gathered, sends, recvs):
        self.own, self.gathered, self.sends, self.recvs = own, gathered, sends, recvs
        self.n = gathered.shape[0] // own.shape[0]
        self.me = lax.axis_index("tp")
        self.further = (self.me < self.n - 1, self.me > 0)
        self.peers = ({"tp": lax.rem(self.me + 1, self.n)}, {"tp": lax.rem(self.me + self.n - 1, self.n)})

    def greet(self, barrier):
        for way in range(2):

            @pl.when(self.further[way])
            def _():
                pl.semaphore_signal(barrier, inc=1, device_id=self.peers[way], device_id_type=MESH)

        return self.further[0].astype(jnp.int32) + self.further[1].astype(jnp.int32)

    def rows(self, shard):
        size = self.own.shape[0]
        return pl.ds(pl.multiple_of(shard * size, size), size)

    def there(self, way, hops):
        return self.me - hops >= 0 if way == 0 else self.me + hops <= self.n - 1

    def send(self, way, hops):
        shard = self.me - hops if way == 0 else self.me + hops
        rows = self.rows(shard)
        return pltpu.make_async_remote_copy(
            src_ref=self.own if hops == 0 else self.gathered.at[rows],
            dst_ref=self.gathered.at[rows],
            send_sem=self.sends.at[way, hops],
            recv_sem=self.recvs.at[way, hops],
            device_id=self.peers[way],
            device_id_type=MESH,
        )

    def arrival(self, way, hops):
        rows = self.rows(self.me - hops if way == 0 else self.me + hops)
        return pltpu.make_async_remote_copy(
            src_ref=self.gathered.at[rows],
            dst_ref=self.gathered.at[rows],
            send_sem=self.sends.at[way, hops],
            recv_sem=self.recvs.at[way, hops - 1],
            device_id=self.peers[way],
            device_id_type=MESH,
        )

    def hop(self, hops):
        for way in range(2):
            if hops > 0:

                @pl.when(self.there(way, hops))
                def _():
                    self.arrival(way, hops).wait_recv()

            if hops < self.n - 1:

                @pl.when(self.there(way, hops) & self.further[way])
                def _():
                    self.send(way, hops).start()

    def drain(self):
        for hops in range(self.n - 1):
            for way in range(2):

                @pl.when(self.there(way, hops) & self.further[way])
                def _():
                    self.send(way, hops).wait_send()


def attend_back_kernel(scale, sharing, length, qkv, held, grad, out_wide, log_total, *refs):
    if sharing:
        own, grad_qkv, gathered, mine, parts, landed, acc, sems_send, sems_recv, sends, recvs = refs
        share = LineGather(own, gathered, sends, recvs)
    else:
        grad_qkv, mine, parts, landed, acc, sems_send, sems_recv = refs
        share = None
    columns = qkv.shape[0] // 3
    frames = qkv.shape[1]
    heads = columns // HD
    me = lax.axis_index("ctx")

    def partner(r):
        return {"ctx": jnp.bitwise_xor(me, r)}

    barrier = pltpu.get_barrier_semaphore()
    for r in (1, 2):
        pl.semaphore_signal(barrier, inc=1, device_id=partner(r), device_id_type=MESH)
    waiting = 2
    if share is not None:
        waiting = waiting + share.greet(barrier)
    pl.semaphore_wait(barrier, waiting)
    if share is not None:
        share.hop(0)
        gathered[share.rows(share.me), :] = own[...]

    def send(at, part, to):
        rows = part_rows(columns, part)
        return pltpu.make_async_remote_copy(
            src_ref=parts.at[at, rows],
            dst_ref=landed.at[at, rows],
            send_sem=sems_send.at[at, part],
            recv_sem=sems_recv.at[at, part],
            device_id=partner(to),
            device_id_type=MESH,
        )

    acc[...] = jnp.zeros_like(acc)
    limit = length[0]

    def block(keys_ref, key_row, value_row, slot, store, group=None):
        owner = jnp.bitwise_xor(me, slot)
        left = limit - owner * frames
        valid = lax.broadcasted_iota(jnp.int32, (frames, frames), 0) < left
        for h in group_heads(heads, group):
            rows = pl.ds(h * HD, HD)
            keys = keys_ref[pl.ds(key_row + h * HD, HD), :]
            values = keys_ref[pl.ds(value_row + h * HD, HD), :]
            queries = qkv[rows, :]
            upstream = grad[rows, :]
            scores = lax.dot_general(
                keys, queries, (((0,), (0,)), ((), ())), preferred_element_type=WIDE
            )
            weights = jnp.where(valid, jnp.exp(scores * scale - log_total[h : h + 1, :]), 0.0)
            grad_weights = lax.dot_general(
                values, upstream, (((0,), (0,)), ((), ())), preferred_element_type=WIDE
            )
            row_terms = jnp.sum(
                upstream.astype(WIDE) * out_wide[rows, :], axis=0, keepdims=True
            )
            grad_scores = (weights * (grad_weights - row_terms)).astype(LOW)
            acc[rows, :] += jnp.dot(keys, grad_scores, preferred_element_type=WIDE)
            grad_keys = (
                lax.dot_general(
                    queries, grad_scores, (((1,), (1,)), ((), ())), preferred_element_type=WIDE
                )
                * scale
            )
            grad_values = lax.dot_general(
                upstream, weights.astype(LOW), (((1,), (1,)), ((), ())), preferred_element_type=WIDE
            )
            store(h * HD, grad_keys, grad_values)

    def store_part(at):
        def store(row, grad_keys, grad_values):
            parts[at, pl.ds(row, HD), :] = grad_keys.astype(LOW)
            parts[at, pl.ds(columns + row, HD), :] = grad_values.astype(LOW)

        return store

    def store_mine(row, grad_keys, grad_values):
        mine[pl.ds(row, HD), :] = grad_keys
        mine[pl.ds(columns + row, HD), :] = grad_values

    def store_joined(row, grad_keys, grad_values):
        for start, value in ((row, grad_keys), (columns + row, grad_values)):
            rows = pl.ds(start, HD)
            parts[1, rows, :] = (value + landed[0, rows, :].astype(WIDE)).astype(LOW)

    for group in range(GROUPS):
        block(held.at[2], 0, columns, 3, store_part(0), group)
        for part in group_parts(group):
            send(0, part, 1).start()
    for group in range(GROUPS):
        for part in group_parts(group):
            send(0, part, 1).wait_recv()
        block(held.at[1], 0, columns, 2, store_joined, group)
        for part in group_parts(group):
            send(1, part, 2).start()
        if share is not None and group == 0:
            share.hop(1)
    for group in range(GROUPS):
        block(held.at[0], 0, columns, 1, store_part(2), group)
        for part in group_parts(group):
            send(2, part, 1).start()
        if share is not None and group == 0:
            share.hop(2)
    block(qkv, columns, 2 * columns, 0, store_mine)
    grad_qkv[0:columns, :] = (acc[...] * scale).astype(LOW)
    for part in range(PARTS):
        send(2, part, 1).wait_recv()
    for part in range(PARTS):
        send(1, part, 2).wait_recv()
    grad_qkv[columns:, :] = (
        mine[...] + landed[1].astype(WIDE) + landed[2].astype(WIDE)
    ).astype(LOW)
    for at in range(3):
        for part in range(PARTS):
            send(at, part, 2 if at == 1 else 1).wait_send()
    if share is not None:
        for hops in range(3, share.n):
            share.hop(hops)
        share.drain()


def attend_back(qkv, held, grad, out_wide, log_total, length, scale, collective_id, own=None):
    columns, frames = qkv.shape[0] // 3, qkv.shape[1]
    out_shape = (jax.ShapeDtypeStruct((3 * columns, frames), LOW),)
    extra, sems = (), []
    if own is not None:
        n = lax.axis_size("tp")
        assert n >= 3
        out_shape += (jax.ShapeDtypeStruct((n * own.shape[0], own.shape[1]), LOW),)
        extra, sems = (own,), [pltpu.SemaphoreType.DMA((2, n))] * 2
    return pl.pallas_call(
        functools.partial(attend_back_kernel, scale, own is not None),
        out_shape=out_shape,
        in_specs=[pl.BlockSpec(memory_space=pltpu.SMEM)] + in_vmem(5 + len(extra)),
        out_specs=tuple(in_vmem(len(out_shape))),
        scratch_shapes=[
            pltpu.VMEM((2 * columns, frames), WIDE),
            pltpu.VMEM((3, 2 * columns, frames), LOW),
            pltpu.VMEM((3, 2 * columns, frames), LOW),
            pltpu.VMEM((columns, frames), WIDE),
            pltpu.SemaphoreType.DMA((3, PARTS)),
            pltpu.SemaphoreType.DMA((3, PARTS)),
            *sems,
        ],
        compiler_params=pltpu.CompilerParams(
            collective_id=collective_id, has_side_effects=True, vmem_limit_bytes=56 << 20
        ),
        name="attend_back",
    )(length, qkv, held, grad, out_wide, log_total, *extra)


def gelu_value(values):
    return 0.5 * values * (1.0 + lax.erf(values * ROOT_HALF))


def gelu_slope(values):
    return 0.5 * (1.0 + lax.erf(values * ROOT_HALF)) + values * DENSITY * jnp.exp(
        -0.5 * values * values
    )


def product(left_side, right_side, left_axis, right_axis):
    return lax.dot_general(
        left_side,
        right_side,
        (((left_axis,), (right_axis,)), ((), ())),
        preferred_element_type=WIDE,
    )


def per_device(
    hidden,
    cotangent,
    lengths,
    query_weight,
    key_weight,
    value_weight,
    output_weight,
    inner_weight,
    outer_weight,
    query_bias,
    value_bias,
    inner_bias,
    output_bias,
    outer_bias,
    first_gain,
    first_shift,
    second_gain,
    second_shift,
):
    clip_count, rows, width = hidden.shape
    assert clip_count == 1
    assert lax.axis_size("ctx") == 4
    tp_size = lax.axis_size("tp")
    own_rows = rows // tp_size
    columns = query_weight.shape[2]
    hidden_local = inner_weight.shape[2]
    scale = 1.0 / math.sqrt(HD)
    own_start = lax.axis_index("tp") * own_rows

    def own_slice(full):
        return lax.dynamic_slice_in_dim(full, own_start, own_rows, axis=0)

    smalls = (output_bias, outer_bias, first_gain, first_shift, second_gain, second_shift)
    qkv_weights = [jnp.swapaxes(weight, 1, 2) for weight in (query_weight, key_weight, value_weight)]

    def qkv_shard(layer):
        return jnp.concatenate([weight[layer] for weight in qkv_weights], axis=0).astype(LOW)

    def gather(array, axis):
        return lax.all_gather(array, "fsdp", axis=axis, tiled=True)

    projections = output_weight.astype(LOW).reshape(-1, output_weight.shape[2])
    paired = lax.axis_size("fsdp") == 2
    if paired:
        wides = (inner_weight, outer_weight, *qkv_weights)
        jobs = [(which, layer, which * LAYERS + layer, 0) for layer in range(LAYERS) for which in range(2)]
        shapes = [wide.shape[1:] for wide in wides[:2] for _ in range(LAYERS)]
        for layer in range(1, LAYERS):
            jobs += [(2 + at, layer, len(shapes), at * columns) for at in range(3)]
            shapes.append((3 * columns, qkv_weights[0].shape[2]))
        results = fetch_first((qkv_shard(0), projections), smalls, wides, tuple(jobs), shapes, 17)
        qkv_first, projections, *results = results
        smalls, lows = results[: len(smalls)], results[len(smalls) :]
        inner_low, outer_low, qkv_low = lows[:LAYERS], lows[LAYERS : 2 * LAYERS], [None, *lows[2 * LAYERS :]]
    else:
        qkv_first, projections = gather(qkv_shard(0), 1), gather(projections, 1)
        smalls = [gather(small, 1) for small in smalls]
        inner_low, outer_low = inner_weight.astype(LOW), outer_weight.astype(LOW)
        qkv_low = [qkv_shard(layer) for layer in range(LAYERS)]
    projections = projections.reshape(LAYERS, columns, width)
    smalls = [lax.reduce_precision(small, 8, 7) for small in smalls]

    def vector(kind, layer):
        return smalls[kind][layer]

    w_qkvs = [qkv_first] + [None if paired else gather(qkv_low[layer], 1) for layer in range(1, LAYERS)]
    feeds = [(gather(inner_low[layer], 0), gather(outer_low[layer], 1)) for layer in range(LAYERS)]

    hidden_rows = hidden.reshape(rows, width)
    residual = own_slice(hidden_rows)
    hat_full, _ = norm_parts(hidden_rows)
    normed = (hat_full * vector(2, 0) + vector(3, 0)).astype(LOW)
    kept = []
    for layer in range(LAYERS):
        w_qkv, w_out, (w_inner, w_outer) = w_qkvs[layer], projections[layer], feeds[layer]
        bias_qkv = jnp.concatenate(
            [query_bias[layer], jnp.zeros_like(query_bias[layer]), value_bias[layer]]
        )
        qkv = (product(w_qkv, normed, 1, 1) + bias_qkv[:, None]).astype(LOW)
        attended, attended_wide, log_total, held = attend(qkv, lengths, scale, 2 * layer)
        branch = product(attended, w_out, 0, 0).astype(LOW)
        normed_two, middle, *fetched = forward_exchange(
            branch,
            residual,
            vector(0, layer),
            vector(4, layer),
            vector(5, layer),
            tp_size,
            2 * layer + 4,
            qkv_low[layer + 1] if paired and layer + 1 < LAYERS else None,
        )
        if fetched:
            w_qkvs[layer + 1] = fetched[0]
        inner_pre = product(normed_two, w_inner, 1, 0) + inner_bias[layer]
        active, slope = gelu_value(inner_pre).astype(LOW), gelu_slope(inner_pre)
        kept.append(
            (residual, normed, qkv, attended, attended_wide, log_total, held, middle, normed_two, slope, active)
        )
        branch = product(active, w_outer, 1, 0).astype(LOW)
        if layer + 1 < LAYERS:
            normed, residual = forward_exchange(
                branch,
                middle,
                vector(1, layer),
                vector(2, layer + 1),
                vector(3, layer + 1),
                tp_size,
                2 * layer + 5,
            )
        else:
            last_branch, last_middle = branch, middle

    def exchange_back(branch, grad_out, normal_in, gain, collective_id, arrays, by_column):
        if lax.axis_size("fsdp") == 2:
            return backward_exchange(
                branch, grad_out, normal_in, gain, tp_size, collective_id, arrays, by_column
            )
        result = backward_exchange(branch, grad_out, normal_in, gain, tp_size, collective_id)
        for array, column in zip(arrays, by_column):
            axis = 1 if column else 0
            array = lax.psum_scatter(array, ("fsdp", "ctx"), scatter_dimension=axis, tiled=True)
            result += (lax.all_gather(array, "ctx", axis=axis, tiled=True),)
        return result

    grad_rows = cotangent.reshape(rows, width)
    grad_own = own_slice(grad_rows)
    grad_low = grad_rows.astype(LOW)
    outer_bias_sum = jnp.sum(grad_own, axis=0)
    grads = [None] * LAYERS
    vectors = [None] * LAYERS
    biases = [None] * LAYERS
    for layer in reversed(range(LAYERS)):
        w_qkv, w_out, (w_inner, w_outer) = w_qkvs[layer], projections[layer], feeds[layer]
        (
            residual,
            normed,
            qkv,
            attended,
            attended_wide,
            log_total,
            held,
            middle,
            normed_two,
            slope,
            active,
        ) = kept[layer]
        grad_active = product(grad_low, w_outer, 1, 1)
        grad_inner = (grad_active * slope).astype(LOW)
        branch = product(grad_inner, w_inner, 1, 1).astype(LOW)
        split = active.shape[1] // 2
        grad_outer_w = product(active[:, :split], grad_low, 0, 0).astype(LOW)
        grad_outer_rest = product(active[:, split:], grad_low, 0, 0).astype(LOW)
        grad_inner_w = product(normed_two, grad_inner, 0, 0).astype(LOW)
        grad_mid_low, grad_middle, sums_two, *summed_two = exchange_back(
            branch, grad_own, middle, vector(4, layer), 2 * layer + 8, (grad_inner_w, grad_outer_w), (False, True)
        )
        if layer == LAYERS - 1:
            last_branch, grad_mid_low = lax.optimization_barrier((last_branch, grad_mid_low))
            last_branch = lax.psum_scatter(last_branch, "tp", scatter_dimension=0, tiled=True)
        grad_attended = product(w_out, grad_mid_low, 1, 1).astype(LOW)
        grad_qkv, *shared = attend_back(
            qkv,
            held,
            grad_attended,
            attended_wide,
            log_total,
            lengths,
            scale,
            2 * layer + 12,
            last_rows if layer == 0 else None,
        )
        grad_output_w = product(attended, grad_mid_low, 1, 0).astype(LOW)
        branch = product(grad_qkv, w_qkv, 0, 0).astype(LOW)
        grad_qkv_w = product(grad_qkv, normed, 1, 0).astype(LOW)
        if layer == LAYERS - 1:
            last_branch, branch = lax.optimization_barrier((last_branch, branch))
            last_rows = (last_middle + last_branch.astype(WIDE) + vector(1, layer)).astype(LOW)
        if layer == 0:
            output = shared[0].astype(WIDE)
        grad_low, grad_own, sums_one, *summed_one = exchange_back(
            branch, grad_middle, residual, vector(2, layer), 2 * layer + 9, (grad_qkv_w, grad_output_w, grad_outer_rest), (True, True, True)
        )
        grads[layer] = (*summed_one, *summed_two)
        vectors[layer] = [
            sums_two[2], outer_bias_sum, sums_one[0], sums_one[1], sums_two[0], sums_two[1]
        ]
        outer_bias_sum = sums_one[2]
        biases[layer] = jnp.concatenate(
            [
                jnp.sum(grad_qkv.astype(WIDE), axis=1),
                jnp.sum(grad_inner.astype(WIDE), axis=0),
            ]
        )
    grad_hidden = grad_low.astype(WIDE)

    shard = output_bias.shape[1]
    flat_biases = jnp.concatenate(biases)
    flat_biases = jnp.pad(flat_biases, (0, -flat_biases.size % (8 * shard))).reshape(-1, shard)
    vector_count = 6 * LAYERS
    small_sums = jnp.stack([row for parts in zip(*vectors) for row in parts])
    if lax.axis_size("fsdp") == 2:
        small_sums = jnp.pad(small_sums, ((0, -vector_count % 8), (0, 0)))
        shared_rows = small_sums.shape[0]
        small_sums = sum_all(
            small_sums, flat_biases, tuple((axis, lax.axis_size(axis)) for axis in ("ctx", "tp")), 16
        )
        vector_sums, bias_sums = small_sums[:vector_count], small_sums[shared_rows:]
    else:
        vector_sums = lax.psum(small_sums, ("fsdp", "ctx", "tp"))
        vector_sums = lax.dynamic_slice_in_dim(vector_sums, lax.axis_index("fsdp") * shard, shard, axis=1)
        bias_sums = lax.psum(flat_biases, ("fsdp", "ctx"))
    vector_sums = vector_sums.reshape(6, LAYERS, shard)
    bias_sums = bias_sums.reshape(-1)[: LAYERS * biases[0].size].reshape(LAYERS, -1)

    def stacked(which):
        return jnp.stack([grads[layer][which] for layer in range(LAYERS)]).astype(WIDE)

    def joined(first, second):
        return jnp.stack(
            [jnp.concatenate([grads[layer][first], grads[layer][second]]) for layer in range(LAYERS)]
        ).astype(WIDE)

    def turned(start):
        return jnp.stack([grads[layer][0][start : start + columns].T for layer in range(LAYERS)]).astype(WIDE)

    return (
        output.reshape(hidden.shape),
        grad_hidden.reshape(hidden.shape),
        turned(0),
        turned(columns),
        turned(2 * columns),
        stacked(1),
        stacked(3),
        joined(4, 2),
        bias_sums[:, :columns],
        bias_sums[:, 2 * columns : 3 * columns],
        bias_sums[:, 3 * columns :],
        vector_sums[0],
        vector_sums[1],
        vector_sums[2],
        vector_sums[3],
        vector_sums[4],
        vector_sums[5],
    )


def solution(mesh):
    in_specs = (
        P("fsdp", "ctx", None),
        P("fsdp", "ctx", None),
        P("fsdp"),
        P(None, "fsdp", "tp"),
        P(None, "fsdp", "tp"),
        P(None, "fsdp", "tp"),
        P(None, "tp", "fsdp"),
        P(None, "fsdp", "tp"),
        P(None, "tp", "fsdp"),
        P(None, "tp"),
        P(None, "tp"),
        P(None, "tp"),
        P(None, "fsdp"),
        P(None, "fsdp"),
        P(None, "fsdp"),
        P(None, "fsdp"),
        P(None, "fsdp"),
        P(None, "fsdp"),
    )
    out_specs = (
        P("fsdp", "ctx", None),
        P("fsdp", "ctx", None),
        P(None, "fsdp", "tp"),
        P(None, "fsdp", "tp"),
        P(None, "fsdp", "tp"),
        P(None, "tp", "fsdp"),
        P(None, "fsdp", "tp"),
        P(None, "tp", "fsdp"),
        P(None, "tp"),
        P(None, "tp"),
        P(None, "tp"),
        P(None, "fsdp"),
        P(None, "fsdp"),
        P(None, "fsdp"),
        P(None, "fsdp"),
        P(None, "fsdp"),
        P(None, "fsdp"),
    )
    return jax.shard_map(
        per_device, mesh=mesh, in_specs=in_specs, out_specs=out_specs, check_vma=False
    )
```

```python
import functools
import math
import jax
import jax.numpy as jnp
from jax import lax
from jax.experimental import pallas as pl
from jax.experimental.pallas import tpu as pltpu
from jax.sharding import PartitionSpec as P

MESH = pl.DeviceIdType.MESH
LOW = jnp.bfloat16
WIDE = jnp.float32
EPSILON = 1e-05
NEGATIVE = -1e30
HD = 80
PIECES = 4
LAYERS = 2
ROOT_HALF = 1.0 / math.sqrt(2.0)
DENSITY = 1.0 / math.sqrt(2.0 * math.pi)
REDUCE_LAG = 2
GATHER_LAG = 3


def norm_parts(values):
    average = jnp.mean(values, axis=-1, keepdims=True)
    centered = values - average
    spread = jnp.mean(centered * centered, axis=-1, keepdims=True)
    inverse = lax.rsqrt(spread + EPSILON)
    return (centered * inverse, inverse)


def norm_back(upstream, normal_hat, inverse, gain_full):
    scaled = upstream * gain_full
    first_mean = jnp.mean(scaled, axis=-1, keepdims=True)
    second_mean = jnp.mean(scaled * normal_hat, axis=-1, keepdims=True)
    return inverse * (scaled - first_mean - normal_hat * second_mean)


def line_exchange(n, own, pieces, partial, gathered, from_left, from_right, total, sems, finish, side=None):
    rs_send, rs_recv, ag_send, ag_recv = sems
    me = lax.axis_index("tp")
    piece = own // pieces
    to_right, to_left = {"tp": lax.rem(me + 1, n)}, {"tp": lax.rem(me + n - 1, n)}
    has_left, has_right = me > 0, me < n - 1

    barrier = pltpu.get_barrier_semaphore()

    @pl.when(has_left)
    def _():
        pl.semaphore_signal(barrier, inc=1, device_id=to_left, device_id_type=MESH)

    @pl.when(has_right)
    def _():
        pl.semaphore_signal(barrier, inc=1, device_id=to_right, device_id_type=MESH)

    peers = has_left.astype(jnp.int32) + has_right.astype(jnp.int32)
    if side is not None:
        for peer in side.peers:
            pl.semaphore_signal(barrier, inc=1, device_id=peer, device_id_type=MESH)
        peers = peers + len(side.peers)
    pl.semaphore_wait(barrier, peers)
    if side is not None:
        side.start()

    def rows_of(shard, step):
        return pl.ds(pl.multiple_of(shard * own + step * piece, piece), piece)

    def reduce_copy(way, src, shard, step):
        rows = rows_of(shard, step)
        landing = from_left if way == 0 else from_right
        return pltpu.make_async_remote_copy(
            src_ref=src.at[rows],
            dst_ref=landing.at[rows],
            send_sem=rs_send.at[way, shard, step],
            recv_sem=rs_recv.at[way, shard, step],
            device_id=to_right if way == 0 else to_left,
            device_id_type=MESH,
        )

    def gather_copy(way, shard, step):
        rows = rows_of(shard, step)
        return pltpu.make_async_remote_copy(
            src_ref=gathered.at[rows],
            dst_ref=gathered.at[rows],
            send_sem=ag_send.at[way, shard, step],
            recv_sem=ag_recv.at[way, shard, step],
            device_id=to_right if way == 0 else to_left,
            device_id_type=MESH,
        )

    def reduce_one(way, shard, step):
        landing = from_left if way == 0 else from_right
        first = me == 0 if way == 0 else me == n - 1

        @pl.when(first)
        def _():
            reduce_copy(way, partial, shard, step).start()

        @pl.when(jnp.logical_not(first))
        def _():
            rows = rows_of(shard, step)
            reduce_copy(way, partial, shard, step).wait_recv()
            landing[rows, :] = (
                partial[rows, :].astype(WIDE) + landing[rows, :].astype(WIDE)
            ).astype(LOW)
            reduce_copy(way, landing, shard, step).start()

    def finish_one(step):
        rows = rows_of(me, step)
        total[...] = partial[rows, :].astype(WIDE)

        @pl.when(has_left)
        def _():
            reduce_copy(0, partial, me, step).wait_recv()
            total[...] += from_left[rows, :].astype(WIDE)

        @pl.when(has_right)
        def _():
            reduce_copy(1, partial, me, step).wait_recv()
            total[...] += from_right[rows, :].astype(WIDE)

        own_rows = pl.ds(pl.multiple_of(step * piece, piece), piece)
        gathered[rows, :] = finish(own_rows, total[...])

        @pl.when(has_right)
        def _():
            gather_copy(0, me, step).start()

        @pl.when(has_left)
        def _():
            gather_copy(1, me, step).start()

    def forward_one(way, shard, step):
        gather_copy(way, shard, step).wait_recv()

        @pl.when(has_right if way == 0 else has_left)
        def _():
            gather_copy(way, shard, step).start()

    period = n - 1

    def finish_at(device):
        from_start = jnp.where(device > 0, n - 1 - device + REDUCE_LAG * device, 0)
        from_end = jnp.where(device < n - 1, device + REDUCE_LAG * (n - 1 - device), 0)
        return jnp.maximum(from_start, from_end)

    def split(tick, start, length):
        since = tick - start
        clipped = jnp.maximum(since, 0)
        return (since >= 0) & (clipped < length), lax.div(clipped, period), lax.rem(clipped, period)

    def body(tick, carry):
        for way in range(2):
            hops = me if way == 0 else n - 1 - me
            due, step, k = split(tick, REDUCE_LAG * hops, pieces * period)
            shard = n - 1 - k if way == 0 else k
            mine = me < shard if way == 0 else me > shard

            @pl.when(due & mine)
            def _():
                reduce_one(way, shard, step)

        due, step, k = split(tick, finish_at(me), pieces * period)

        @pl.when(due & (k == 0))
        def _():
            finish_one(step)

        for hops in range(1, n):
            for way in range(2):
                shard = me - hops if way == 0 else me + hops
                there = shard >= 0 if way == 0 else shard <= n - 1
                due, step, k = split(
                    tick, finish_at(shard) + GATHER_LAG * hops, pieces * period
                )

                @pl.when(there & due & (k == 0))
                def _():
                    forward_one(way, shard, step)

        if side is not None:
            side.at(tick)
        return carry

    ticks = period * (pieces - 1) + max(REDUCE_LAG, 1) * (n - 1) + GATHER_LAG * (n - 1) + 1
    if side is not None:
        ticks = max(ticks, side.ticks)
    lax.fori_loop(0, ticks, body, 0)
    if side is not None:
        side.drain()

    def drain(step, carry):
        for k in range(n - 1):
            for way in range(2):
                shard = n - 1 - k if way == 0 else k
                sends = me < shard if way == 0 else me > shard

                @pl.when(sends)
                def _():
                    reduce_copy(way, partial, shard, step).wait_send()

        for k in range(n):
            for way in range(2):
                shard = me - k if way == 0 else me + k
                there = shard >= 0 if way == 0 else shard <= n - 1
                further = has_right if way == 0 else has_left

                @pl.when(there & further)
                def _():
                    gather_copy(way, shard, step).wait_send()

        return carry

    lax.fori_loop(0, pieces, drain, 0)


def exchange_scratch(n, rows, width, pieces):
    return [
        pltpu.VMEM((rows, width), LOW),
        pltpu.VMEM((rows, width), LOW),
        pltpu.VMEM((rows // n // pieces, width), WIDE),
        pltpu.SemaphoreType.DMA((2, n, pieces)),
        pltpu.SemaphoreType.DMA((2, n, pieces)),
        pltpu.SemaphoreType.DMA((2, n, pieces)),
        pltpu.SemaphoreType.DMA((2, n, pieces)),
    ]


def forward_fetch_kernel(
    n, pieces, partial, residual, bias, gain, shift, shard, gathered, middle, fetched, from_left, from_right, total,
    rs_send, rs_recv, ag_send, ag_recv, sends, recvs
):
    forward_exchange_kernel(
        n, pieces, partial, residual, bias, gain, shift, gathered, middle, from_left, from_right, total, rs_send, rs_recv,
        ag_send, ag_recv, side=QuartersSide((shard,), (fetched,), sends, recvs)
    )


def forward_exchange_kernel(
    n, pieces, partial, residual, bias, gain, shift, gathered, middle, from_left, from_right, total, *sems, side=None
):
    def finish(rows, value):
        mid = value + residual[rows, :] + bias[...]
        middle[rows, :] = mid
        hat, _ = norm_parts(mid)
        return (hat * gain[...] + shift[...]).astype(LOW)

    line_exchange(
        n, residual.shape[0], pieces, partial, gathered, from_left, from_right, total, sems, finish, side
    )


def backward_exchange_kernel(
    n, pieces, partial, grad_out, normal_in, gain, gathered, grad_in, sums, from_left, from_right, total, *sems, side=None
):
    sums[...] = jnp.zeros_like(sums)

    def finish(rows, upstream):
        hat, inverse = norm_parts(normal_in[rows, :])
        grad = grad_out[rows, :] + norm_back(upstream, hat, inverse, gain[...])
        grad_in[rows, :] = grad
        sums[0:1, :] += jnp.sum(upstream * hat, axis=0, keepdims=True)
        sums[1:2, :] += jnp.sum(upstream, axis=0, keepdims=True)
        sums[2:3, :] += jnp.sum(grad, axis=0, keepdims=True)
        return grad.astype(LOW)

    line_exchange(
        n, grad_out.shape[0], pieces, partial, gathered, from_left, from_right, total, sems, finish, side
    )


def in_vmem(count):
    return [pl.BlockSpec(memory_space=pltpu.VMEM)] * count


class GradientSum:
    LAGS = (0, 3, 6, 9)

    def __init__(self, by_column, arrays, outs, landings, sems):
        self.by_column = by_column
        self.chunks = landings[0].shape[1]
        self.arrays, self.outs, self.landings = arrays, outs, landings
        self.sends, self.recvs = sems
        self.half = lax.axis_index("fsdp")
        self.ctx = lax.axis_index("ctx")
        self.core = lax.rem(self.ctx, 2)
        pair = {"ctx": jnp.bitwise_xor(self.ctx, 1)}
        across = {"ctx": jnp.bitwise_xor(self.ctx, 2)}
        other = {"fsdp": 1 - self.half}
        self.peers = (pair, across, other)
        self.ticks = 2 * (self.chunks - 1) + self.LAGS[3] + 1

    def view(self, which, half, core, chunk):
        rows, cols = self.arrays[which].shape
        if not self.by_column[which]:
            part = rows // 4
            height = part // self.chunks
            start = half * (2 * part) + core * part + chunk * height
            return pl.ds(pl.multiple_of(start, 16), height), slice(None)
        part = rows // 2
        height = part // self.chunks
        start = core * part + chunk * height
        width = cols // 2
        return (
            pl.ds(pl.multiple_of(start, 16), height),
            pl.ds(pl.multiple_of(half * width, 128), width),
        )

    def out_rows(self, which, core, chunk):
        part = self.outs[which].shape[0] // 2
        height = part // self.chunks
        return pl.ds(pl.multiple_of(core * part + chunk * height, 16), height)

    def copy(self, which, stage, chunk, half=0):
        pair, across, other = self.peers
        landing = self.landings[which]
        if stage == 0:
            src = self.arrays[which].at[self.view(which, half, 1 - self.core, chunk)]
            slot, peer = half, pair
        elif stage == 1:
            src = landing.at[1 - self.half, chunk]
            slot, peer = 2, other
        elif stage == 2:
            src = landing.at[2, chunk]
            slot, peer = 3, across
        else:
            src = landing.at[3, chunk]
            slot, peer = 4, pair
        return pltpu.make_async_remote_copy(
            src_ref=src,
            dst_ref=landing.at[slot, chunk],
            send_sem=self.sends.at[which, slot, chunk],
            recv_sem=self.recvs.at[which, slot, chunk],
            device_id=peer,
            device_id_type=MESH,
        )

    def start(self):
        def body(chunk, carry):
            for which in range(len(self.arrays)):
                for half in range(2):
                    self.copy(which, 0, chunk, half).start()
            return carry

        lax.fori_loop(0, self.chunks, body, 0)

    def when_due(self, tick, lag, action):
        since = tick - lag
        clipped = jnp.maximum(since, 0)
        chunk = lax.div(clipped, 2)

        @pl.when((since >= 0) & (lax.rem(clipped, 2) == 0) & (chunk < self.chunks))
        def _():
            for which in range(len(self.arrays)):
                action(which, chunk)

    def at(self, tick):
        def joined(which, chunk):
            landing = self.landings[which]
            for half in range(2):
                self.copy(which, 0, chunk, half).wait_recv()
                rows, cols = self.view(which, half, self.core, chunk)
                landing[half, chunk] = (
                    self.arrays[which][rows, cols].astype(WIDE) + landing[half, chunk].astype(WIDE)
                ).astype(LOW)
            self.copy(which, 1, chunk).start()

        def crossed(which, chunk):
            landing = self.landings[which]
            self.copy(which, 1, chunk).wait_recv()
            landing[2, chunk] = (
                landing[self.half, chunk].astype(WIDE) + landing[2, chunk].astype(WIDE)
            ).astype(LOW)
            self.copy(which, 2, chunk).start()

        def summed(which, chunk):
            landing = self.landings[which]
            self.copy(which, 2, chunk).wait_recv()
            low = (landing[2, chunk].astype(WIDE) + landing[3, chunk].astype(WIDE)).astype(LOW)
            landing[3, chunk] = low
            self.outs[which][self.out_rows(which, self.core, chunk), :] = low
            self.copy(which, 3, chunk).start()

        def shared(which, chunk):
            self.copy(which, 3, chunk).wait_recv()
            self.outs[which][self.out_rows(which, 1 - self.core, chunk), :] = self.landings[which][
                4, chunk
            ]

        for lag, action in zip(self.LAGS, (joined, crossed, summed, shared)):
            self.when_due(tick, lag, action)

    def drain(self):
        def body(chunk, carry):
            for which in range(len(self.arrays)):
                for half in range(2):
                    self.copy(which, 0, chunk, half).wait_send()
                for stage in range(1, 4):
                    self.copy(which, stage, chunk).wait_send()
            return carry

        lax.fori_loop(0, self.chunks, body, 0)


def gradient_shapes(arrays, by_column):
    chunks = 5 if all(by_column) else 10
    outs, landings = (), []
    for array, column in zip(arrays, by_column):
        rows, cols = array.shape
        rows, cols = (rows, cols // 2) if column else (rows // 2, cols)
        outs += (jax.ShapeDtypeStruct((rows, cols), LOW),)
        landings.append(pltpu.VMEM((5, chunks, rows // 2 // chunks, cols), LOW))
    return outs, landings, pltpu.SemaphoreType.DMA((len(arrays), 5, chunks))


def backward_gradient_kernel(by_column, n, pieces, partial, grad_out, normal_in, gain, *refs):
    count = len(by_column)
    arrays, (gathered, grad_in, sums), refs = refs[:count], refs[count : count + 3], refs[count + 3 :]
    outs, (from_left, from_right, total, *sems), refs = refs[:count], refs[count : count + 7], refs[count + 7 :]
    side = GradientSum(by_column, arrays, outs, refs[:count], refs[count:])
    backward_exchange_kernel(
        n, pieces, partial, grad_out, normal_in, gain, gathered, grad_in, sums, from_left, from_right, total, *sems, side=side
    )


def sum_all_kernel(axes, vectors, biases, out, staged, landing, sends, recvs):
    half = lax.axis_index("fsdp")
    shared, width = vectors.shape[0], out.shape[1]
    steps = [("fsdp", 1)] + [(axis, 1 << b) for axis, size in axes for b in range(size.bit_length() - 1)]

    def peer(axis, k):
        return {axis: jnp.bitwise_xor(lax.axis_index(axis), k)}

    barrier = pltpu.get_barrier_semaphore()
    for axis, k in steps:
        pl.semaphore_signal(barrier, inc=1, device_id=peer(axis, k), device_id_type=MESH)
    for side in range(2):
        staged[side, 0:shared, :] = vectors[:, side * width : (side + 1) * width]
        staged[side, shared:, :] = biases[...]
    pl.semaphore_wait(barrier, len(steps))
    for at, (axis, k) in enumerate(steps):
        rows = pl.ds(0, shared) if axis == "tp" else pl.ds(0, out.shape[0])
        if at > 0:
            landing[at, 0, rows] = out[rows, :]
        copy = pltpu.make_async_remote_copy(
            src_ref=landing.at[at, 0, rows] if at > 0 else staged.at[1 - half],
            dst_ref=landing.at[at, 1, rows],
            send_sem=sends.at[at],
            recv_sem=recvs.at[at],
            device_id=peer(axis, k),
            device_id_type=MESH,
        )
        copy.start()
        copy.wait()
        own = landing[at, 0, rows] if at > 0 else staged[half]
        out[rows, :] = own + landing[at, 1, rows]


def sum_all(vectors, biases, axes, collective_id):
    shape = (vectors.shape[0] + biases.shape[0], biases.shape[1])
    steps = 1 + sum(size.bit_length() - 1 for _, size in axes)
    return pl.pallas_call(
        functools.partial(sum_all_kernel, axes),
        out_shape=jax.ShapeDtypeStruct(shape, WIDE),
        in_specs=in_vmem(2),
        out_specs=in_vmem(1)[0],
        scratch_shapes=[
            pltpu.VMEM((2,) + shape, WIDE),
            pltpu.VMEM((steps, 2) + shape, WIDE),
            pltpu.SemaphoreType.DMA((steps,)),
            pltpu.SemaphoreType.DMA((steps,)),
        ],
        compiler_params=pltpu.CompilerParams(
            collective_id=collective_id, has_side_effects=True, vmem_limit_bytes=8 << 20
        ),
        name="sum_all",
    )(vectors, biases)


def fetch_parts(rows):
    return next(parts for parts in (2, 3, 1) if rows // 4 % (16 * parts) == 0)


CAST_ROWS = 64


class Quarters:
    def __init__(self, shards, outs, sends, recvs):
        self.shards, self.outs, self.sends, self.recvs = shards, outs, sends, recvs
        self.half = lax.axis_index("fsdp")
        self.ctx = lax.axis_index("ctx")
        self.pair, self.across = jnp.bitwise_xor(self.ctx, 1), jnp.bitwise_xor(self.ctx, 2)
        self.targets = ({"fsdp": 1 - self.half}, {"ctx": self.across}, {"ctx": self.pair}, {"ctx": self.pair})
        self.peers = self.targets[:3]
        self.each = [
            (which, part) for which in range(len(shards)) for part in range(fetch_parts(shards[which].shape[0]))
        ]

    def rows_of(self, which, quarter, part):
        parts = fetch_parts(self.shards[which].shape[0])
        height = self.shards[which].shape[0] // 4 // parts
        return pl.ds(pl.multiple_of((quarter * parts + part) * height, 16), height)

    def place(self, which, side, quarter, part):
        cols = self.shards[which].shape[1]
        return self.outs[which].at[
            self.rows_of(which, quarter, part), pl.ds(pl.multiple_of(side * cols, 128), cols)
        ]

    def copy(self, stage, item, arriving=False):
        which, part = item
        quarter = (self.ctx, self.ctx, self.ctx, self.across)[stage]
        src = self.shards[which].at[self.rows_of(which, quarter, part)]
        dst = self.place(which, self.half, quarter, part)
        if stage > 0:
            src = dst = self.place(which, 1 - self.half, quarter, part)
        if arriving:
            quarter = (self.ctx, self.across, self.pair, jnp.bitwise_xor(self.ctx, 3))[stage]
            dst = self.place(which, 1 - self.half, quarter, part)
        return pltpu.make_async_remote_copy(
            src_ref=src,
            dst_ref=dst,
            send_sem=self.sends.at[which, stage, part],
            recv_sem=self.recvs.at[which, stage, part],
            device_id=self.targets[stage],
            device_id_type=MESH,
        )

    def begin(self):
        for item in self.each:
            self.copy(0, item).start()

    def keep_own(self):
        for shard, out in zip(self.shards, self.outs):
            cols = shard.shape[1]
            out[:, pl.ds(pl.multiple_of(self.half * cols, 128), cols)] = shard[...]

    def crossed(self, item):
        self.copy(0, item, True).wait_recv()
        self.copy(1, item).start()
        self.copy(2, item).start()

    def forwarded(self, item):
        self.copy(1, item, True).wait_recv()
        self.copy(3, item).start()

    def finish(self):
        for stage in (2, 3):
            for item in self.each:
                self.copy(stage, item, True).wait_recv()
        for stage in range(4):
            for item in self.each:
                self.copy(stage, item).wait_send()


class QuartersSide(Quarters):
    CROSSED, APART, FORWARDED = 4, 3, 3

    def start(self):
        self.begin()
        self.keep_own()

    @property
    def ticks(self):
        return self.CROSSED + self.FORWARDED + self.APART * (len(self.each) - 1) + 1

    def at(self, tick):
        for at, item in enumerate(self.each):
            due = self.CROSSED + self.APART * at

            @pl.when(tick == due)
            def _():
                self.crossed(item)

            @pl.when(tick == due + self.FORWARDED)
            def _():
                self.forwarded(item)

    def drain(self):
        self.finish()


def fetch_kernel(counts, jobs, *refs):
    refs = list(refs)

    def take(count):
        taken = refs[:count]
        del refs[:count]
        return taken

    shard_count, small_count, wide_count, low_count = counts
    shards, smalls, wides = take(shard_count), take(small_count), take(wide_count)
    outs, out_smalls, lows = take(shard_count), take(small_count), take(low_count)
    buffers = take(len(jobs))
    cast_sems, sends, recvs, small_sends, small_recvs = refs
    quarters = Quarters(shards, outs, sends, recvs)

    barrier = pltpu.get_barrier_semaphore()
    for peer in quarters.peers:
        pl.semaphore_signal(barrier, inc=1, device_id=peer, device_id_type=MESH)
    pl.semaphore_wait(barrier, 3)

    def small_copy(at, side):
        cols = smalls[at].shape[1]
        return pltpu.make_async_remote_copy(
            src_ref=smalls[at],
            dst_ref=out_smalls[at].at[:, pl.ds(pl.multiple_of(side * cols, 128), cols)],
            send_sem=small_sends.at[at],
            recv_sem=small_recvs.at[at],
            device_id=quarters.peers[0],
            device_id_type=MESH,
        )

    def load(at):
        which, layer, _, _ = jobs[at]
        return pltpu.make_async_copy(wides[which].at[layer], buffers[at], cast_sems.at[at])

    quarters.begin()
    for at in range(small_count):
        small_copy(at, quarters.half).start()
    for at in range(len(jobs)):
        load(at).start()
    quarters.keep_own()
    for small, out in zip(smalls, out_smalls):
        cols = small.shape[1]
        out[:, pl.ds(pl.multiple_of(quarters.half * cols, 128), cols)] = small[...]
    for at, (_, _, low, first) in enumerate(jobs):
        load(at).wait()

        def cast(step, carry):
            start = pl.multiple_of(step * CAST_ROWS, CAST_ROWS)
            lows[low][pl.ds(first + start, CAST_ROWS), :] = buffers[at][pl.ds(start, CAST_ROWS), :].astype(LOW)
            return carry

        lax.fori_loop(0, buffers[at].shape[0] // CAST_ROWS, cast, 0)
    last = len(quarters.each)
    for at in range(last + 1):
        if at < last:
            quarters.crossed(quarters.each[at])
        if at > 0:
            quarters.forwarded(quarters.each[at - 1])
    for at in range(small_count):
        small_copy(at, 1 - quarters.half).wait_recv()
    quarters.finish()
    for at in range(small_count):
        small_copy(at, quarters.half).wait_send()


def quarter_sems(shards):
    most = max(fetch_parts(shard.shape[0]) for shard in shards)
    return [pltpu.SemaphoreType.DMA((len(shards), 4, most))] * 2


def gathered_shape(shard):
    return jax.ShapeDtypeStruct((shard.shape[0], 2 * shard.shape[1]), shard.dtype)


def fetch_first(shards, smalls, wides, jobs, low_shapes, collective_id):
    counts = (len(shards), len(smalls), len(wides), len(low_shapes))
    out_shape = tuple(gathered_shape(array) for array in (*shards, *smalls))
    out_shape += tuple(jax.ShapeDtypeStruct(shape, LOW) for shape in low_shapes)
    return pl.pallas_call(
        functools.partial(fetch_kernel, counts, jobs),
        out_shape=out_shape,
        in_specs=in_vmem(len(shards) + len(smalls)) + [pl.BlockSpec(memory_space=pl.ANY)] * len(wides),
        out_specs=tuple(in_vmem(len(out_shape))),
        scratch_shapes=[pltpu.VMEM(wides[job[0]].shape[1:], WIDE) for job in jobs]
        + [pltpu.SemaphoreType.DMA((len(jobs),))]
        + quarter_sems(shards)
        + [pltpu.SemaphoreType.DMA((len(smalls),))] * 2,
        compiler_params=pltpu.CompilerParams(
            collective_id=collective_id, has_side_effects=True, vmem_limit_bytes=44 << 20
        ),
        name="fetch_first",
    )(*shards, *smalls, *wides)


def forward_exchange(partial, residual, bias, gain, shift, n, collective_id, shard=None):
    rows, width = partial.shape
    out_shape = (
        jax.ShapeDtypeStruct((rows, width), LOW),
        jax.ShapeDtypeStruct(residual.shape, WIDE),
    )
    scratch = exchange_scratch(n, rows, width, PIECES)
    kernel, extra = forward_exchange_kernel, ()
    if shard is not None:
        out_shape += (gathered_shape(shard),)
        scratch = scratch + quarter_sems((shard,))
        kernel, extra = forward_fetch_kernel, (shard,)
    return pl.pallas_call(
        functools.partial(kernel, n, PIECES),
        out_shape=out_shape,
        in_specs=in_vmem(5 + len(extra)),
        out_specs=tuple(in_vmem(len(out_shape))),
        scratch_shapes=scratch,
        compiler_params=pltpu.CompilerParams(
            collective_id=collective_id, has_side_effects=True, vmem_limit_bytes=14 << 20
        ),
        name="forward_exchange",
    )(partial, residual, bias[None, :], gain[None, :], shift[None, :], *extra)


def backward_exchange(partial, grad_out, normal_in, gain, n, collective_id, arrays=(), by_column=()):
    rows, width = partial.shape
    out_shape = (
        jax.ShapeDtypeStruct((rows, width), LOW),
        jax.ShapeDtypeStruct(grad_out.shape, WIDE),
        jax.ShapeDtypeStruct((8, width), WIDE),
    )
    scratch = exchange_scratch(n, rows, width, PIECES)
    kernel, extra = backward_exchange_kernel, ()
    if arrays:
        outs, landings, sems = gradient_shapes(arrays, by_column)
        out_shape = out_shape + outs
        scratch = scratch + landings + [sems] * 2
        kernel, extra = functools.partial(backward_gradient_kernel, by_column), arrays
    return pl.pallas_call(
        functools.partial(kernel, n, PIECES),
        out_shape=out_shape,
        in_specs=in_vmem(4 + len(extra)),
        out_specs=tuple(in_vmem(len(out_shape))),
        scratch_shapes=scratch,
        compiler_params=pltpu.CompilerParams(
            collective_id=collective_id, has_side_effects=True, vmem_limit_bytes=24 << 20
        ),
        name="backward_exchange",
    )(partial, grad_out, normal_in, gain[None, :], *extra)


GROUPS = 2
PARTS = 2 * GROUPS


def part_rows(columns, part, base=0):
    size = columns // GROUPS
    return pl.ds(base + (part % 2) * columns + (part // 2) * size, size)


def group_parts(group):
    return (2 * group, 2 * group + 1)


def group_heads(heads, group):
    assert heads % GROUPS == 0
    size = heads // GROUPS
    return range(heads) if group is None else range(group * size, (group + 1) * size)


def attend_kernel(scale, length, qkv, out, out_wide, log_total, held, high, low_sum, sems_send, sems_recv):
    columns = qkv.shape[0] // 3
    frames = qkv.shape[1]
    heads = columns // HD
    me = lax.axis_index("ctx")

    def partner(r):
        return {"ctx": jnp.bitwise_xor(me, r)}

    barrier = pltpu.get_barrier_semaphore()
    for r in (1, 2):
        pl.semaphore_signal(barrier, inc=1, device_id=partner(r), device_id_type=MESH)
    pl.semaphore_wait(barrier, 2)

    def send(slot, part, to):
        rows, own_rows = part_rows(columns, part), part_rows(columns, part, columns)
        src = qkv.at[own_rows] if slot != 3 else held.at[1, rows]
        return pltpu.make_async_remote_copy(
            src_ref=src,
            dst_ref=held.at[slot - 1, rows],
            send_sem=sems_send.at[slot - 1, part],
            recv_sem=sems_recv.at[slot - 1, part],
            device_id=partner(to),
            device_id_type=MESH,
        )

    for part in range(PARTS):
        send(2, part, 2).start()
    for part in range(PARTS):
        send(1, part, 1).start()

    high[...] = jnp.full_like(high, NEGATIVE)
    low_sum[...] = jnp.zeros_like(low_sum)
    out_wide[...] = jnp.zeros_like(out_wide)
    limit = length[0]

    def block(keys_ref, key_row, value_row, slot, group=None):
        owner = jnp.bitwise_xor(me, slot)
        left = limit - owner * frames
        valid = lax.broadcasted_iota(jnp.int32, (frames, frames), 0) < left
        for h in group_heads(heads, group):
            rows = pl.ds(h * HD, HD)
            keys = keys_ref[pl.ds(key_row + h * HD, HD), :]
            values = keys_ref[pl.ds(value_row + h * HD, HD), :]
            scores = lax.dot_general(
                keys, qkv[rows, :], (((0,), (0,)), ((), ())), preferred_element_type=WIDE
            )
            scores = jnp.where(valid, scores * scale, NEGATIVE)
            before = high[h : h + 1, :]
            now = jnp.maximum(before, jnp.max(scores, axis=0, keepdims=True))
            shrink = jnp.exp(before - now)
            raised = jnp.exp(scores - now)
            low_sum[h : h + 1, :] = low_sum[h : h + 1, :] * shrink + jnp.sum(
                raised, axis=0, keepdims=True
            )
            high[h : h + 1, :] = now
            out_wide[rows, :] = out_wide[rows, :] * shrink + jnp.dot(
                values, raised.astype(LOW), preferred_element_type=WIDE
            )

    block(qkv, columns, 2 * columns, 0)
    for part in range(PARTS):
        send(1, part, 1).wait_recv()
    block(held.at[0], 0, columns, 1)
    for group in range(GROUPS):
        for part in group_parts(group):
            send(2, part, 2).wait_recv()
            send(3, part, 1).start()
        block(held.at[1], 0, columns, 2, group)
    for group in range(GROUPS):
        for part in group_parts(group):
            send(3, part, 1).wait_recv()
        block(held.at[2], 0, columns, 3, group)
    for h in range(heads):
        rows = pl.ds(h * HD, HD)
        total = low_sum[h : h + 1, :]
        done = out_wide[rows, :] / total
        out_wide[rows, :] = done
        out[rows, :] = done.astype(LOW)
        log_total[h : h + 1, :] = high[h : h + 1, :] + jnp.log(total)
    for slot in (1, 2, 3):
        for part in range(PARTS):
            send(slot, part, 2 if slot == 2 else 1).wait_send()


def attend(qkv, length, scale, collective_id):
    columns, frames = qkv.shape[0] // 3, qkv.shape[1]
    return pl.pallas_call(
        functools.partial(attend_kernel, scale),
        out_shape=(
            jax.ShapeDtypeStruct((columns, frames), LOW),
            jax.ShapeDtypeStruct((columns, frames), WIDE),
            jax.ShapeDtypeStruct((8, frames), WIDE),
            jax.ShapeDtypeStruct((3, 2 * columns, frames), LOW),
        ),
        in_specs=[pl.BlockSpec(memory_space=pltpu.SMEM)] + in_vmem(1),
        out_specs=tuple(in_vmem(4)),
        scratch_shapes=[
            pltpu.VMEM((8, frames), WIDE),
            pltpu.VMEM((8, frames), WIDE),
            pltpu.SemaphoreType.DMA((3, PARTS)),
            pltpu.SemaphoreType.DMA((3, PARTS)),
        ],
        compiler_params=pltpu.CompilerParams(
            collective_id=collective_id, has_side_effects=True, vmem_limit_bytes=18 << 20
        ),
        name="attend",
    )(length, qkv)


class LineGather:
    def __init__(self, own, gathered, sends, recvs):
        self.own, self.gathered, self.sends, self.recvs = own, gathered, sends, recvs
        self.n = gathered.shape[0] // own.shape[0]
        self.me = lax.axis_index("tp")
        self.further = (self.me < self.n - 1, self.me > 0)
        self.peers = ({"tp": lax.rem(self.me + 1, self.n)}, {"tp": lax.rem(self.me + self.n - 1, self.n)})

    def greet(self, barrier):
        for way in range(2):

            @pl.when(self.further[way])
            def _():
                pl.semaphore_signal(barrier, inc=1, device_id=self.peers[way], device_id_type=MESH)

        return self.further[0].astype(jnp.int32) + self.further[1].astype(jnp.int32)

    def rows(self, shard):
        size = self.own.shape[0]
        return pl.ds(pl.multiple_of(shard * size, size), size)

    def there(self, way, hops):
        return self.me - hops >= 0 if way == 0 else self.me + hops <= self.n - 1

    def send(self, way, hops):
        shard = self.me - hops if way == 0 else self.me + hops
        rows = self.rows(shard)
        return pltpu.make_async_remote_copy(
            src_ref=self.own if hops == 0 else self.gathered.at[rows],
            dst_ref=self.gathered.at[rows],
            send_sem=self.sends.at[way, hops],
            recv_sem=self.recvs.at[way, hops],
            device_id=self.peers[way],
            device_id_type=MESH,
        )

    def arrival(self, way, hops):
        rows = self.rows(self.me - hops if way == 0 else self.me + hops)
        return pltpu.make_async_remote_copy(
            src_ref=self.gathered.at[rows],
            dst_ref=self.gathered.at[rows],
            send_sem=self.sends.at[way, hops],
            recv_sem=self.recvs.at[way, hops - 1],
            device_id=self.peers[way],
            device_id_type=MESH,
        )

    def hop(self, hops):
        for way in range(2):
            if hops > 0:

                @pl.when(self.there(way, hops))
                def _():
                    self.arrival(way, hops).wait_recv()

            if hops < self.n - 1:

                @pl.when(self.there(way, hops) & self.further[way])
                def _():
                    self.send(way, hops).start()

    def drain(self):
        for hops in range(self.n - 1):
            for way in range(2):

                @pl.when(self.there(way, hops) & self.further[way])
                def _():
                    self.send(way, hops).wait_send()


def attend_back_kernel(scale, sharing, length, qkv, held, grad, out_wide, log_total, *refs):
    if sharing:
        own, grad_qkv, gathered, mine, parts, landed, acc, sems_send, sems_recv, sends, recvs = refs
        share = LineGather(own, gathered, sends, recvs)
    else:
        grad_qkv, mine, parts, landed, acc, sems_send, sems_recv = refs
        share = None
    columns = qkv.shape[0] // 3
    frames = qkv.shape[1]
    heads = columns // HD
    me = lax.axis_index("ctx")

    def partner(r):
        return {"ctx": jnp.bitwise_xor(me, r)}

    barrier = pltpu.get_barrier_semaphore()
    for r in (1, 2):
        pl.semaphore_signal(barrier, inc=1, device_id=partner(r), device_id_type=MESH)
    waiting = 2
    if share is not None:
        waiting = waiting + share.greet(barrier)
    pl.semaphore_wait(barrier, waiting)
    if share is not None:
        share.hop(0)
        gathered[share.rows(share.me), :] = own[...]

    def send(at, part, to):
        rows = part_rows(columns, part)
        return pltpu.make_async_remote_copy(
            src_ref=parts.at[at, rows],
            dst_ref=landed.at[at, rows],
            send_sem=sems_send.at[at, part],
            recv_sem=sems_recv.at[at, part],
            device_id=partner(to),
            device_id_type=MESH,
        )

    acc[...] = jnp.zeros_like(acc)
    limit = length[0]

    def block(keys_ref, key_row, value_row, slot, store, group=None):
        owner = jnp.bitwise_xor(me, slot)
        left = limit - owner * frames
        valid = lax.broadcasted_iota(jnp.int32, (frames, frames), 0) < left
        for h in group_heads(heads, group):
            rows = pl.ds(h * HD, HD)
            keys = keys_ref[pl.ds(key_row + h * HD, HD), :]
            values = keys_ref[pl.ds(value_row + h * HD, HD), :]
            queries = qkv[rows, :]
            upstream = grad[rows, :]
            scores = lax.dot_general(
                keys, queries, (((0,), (0,)), ((), ())), preferred_element_type=WIDE
            )
            weights = jnp.where(valid, jnp.exp(scores * scale - log_total[h : h + 1, :]), 0.0)
            grad_weights = lax.dot_general(
                values, upstream, (((0,), (0,)), ((), ())), preferred_element_type=WIDE
            )
            row_terms = jnp.sum(
                upstream.astype(WIDE) * out_wide[rows, :], axis=0, keepdims=True
            )
            grad_scores = (weights * (grad_weights - row_terms)).astype(LOW)
            acc[rows, :] += jnp.dot(keys, grad_scores, preferred_element_type=WIDE)
            grad_keys = (
                lax.dot_general(
                    queries, grad_scores, (((1,), (1,)), ((), ())), preferred_element_type=WIDE
                )
                * scale
            )
            grad_values = lax.dot_general(
                upstream, weights.astype(LOW), (((1,), (1,)), ((), ())), preferred_element_type=WIDE
            )
            store(h * HD, grad_keys, grad_values)

    def store_part(at):
        def store(row, grad_keys, grad_values):
            parts[at, pl.ds(row, HD), :] = grad_keys.astype(LOW)
            parts[at, pl.ds(columns + row, HD), :] = grad_values.astype(LOW)

        return store

    def store_mine(row, grad_keys, grad_values):
        mine[pl.ds(row, HD), :] = grad_keys
        mine[pl.ds(columns + row, HD), :] = grad_values

    def store_joined(row, grad_keys, grad_values):
        for start, value in ((row, grad_keys), (columns + row, grad_values)):
            rows = pl.ds(start, HD)
            parts[1, rows, :] = (value + landed[0, rows, :].astype(WIDE)).astype(LOW)

    for group in range(GROUPS):
        block(held.at[2], 0, columns, 3, store_part(0), group)
        for part in group_parts(group):
            send(0, part, 1).start()
    for group in range(GROUPS):
        for part in group_parts(group):
            send(0, part, 1).wait_recv()
        block(held.at[1], 0, columns, 2, store_joined, group)
        for part in group_parts(group):
            send(1, part, 2).start()
        if share is not None and group == 0:
            share.hop(1)
    for group in range(GROUPS):
        block(held.at[0], 0, columns, 1, store_part(2), group)
        for part in group_parts(group):
            send(2, part, 1).start()
        if share is not None and group == 0:
            share.hop(2)
    block(qkv, columns, 2 * columns, 0, store_mine)
    grad_qkv[0:columns, :] = (acc[...] * scale).astype(LOW)
    for part in range(PARTS):
        send(2, part, 1).wait_recv()
    for part in range(PARTS):
        send(1, part, 2).wait_recv()
    grad_qkv[columns:, :] = (
        mine[...] + landed[1].astype(WIDE) + landed[2].astype(WIDE)
    ).astype(LOW)
    for at in range(3):
        for part in range(PARTS):
            send(at, part, 2 if at == 1 else 1).wait_send()
    if share is not None:
        for hops in range(3, share.n):
            share.hop(hops)
        share.drain()


def attend_back(qkv, held, grad, out_wide, log_total, length, scale, collective_id, own=None):
    columns, frames = qkv.shape[0] // 3, qkv.shape[1]
    out_shape = (jax.ShapeDtypeStruct((3 * columns, frames), LOW),)
    extra, sems = (), []
    if own is not None:
        n = lax.axis_size("tp")
        assert n >= 3
        out_shape += (jax.ShapeDtypeStruct((n * own.shape[0], own.shape[1]), LOW),)
        extra, sems = (own,), [pltpu.SemaphoreType.DMA((2, n))] * 2
    return pl.pallas_call(
        functools.partial(attend_back_kernel, scale, own is not None),
        out_shape=out_shape,
        in_specs=[pl.BlockSpec(memory_space=pltpu.SMEM)] + in_vmem(5 + len(extra)),
        out_specs=tuple(in_vmem(len(out_shape))),
        scratch_shapes=[
            pltpu.VMEM((2 * columns, frames), WIDE),
            pltpu.VMEM((3, 2 * columns, frames), LOW),
            pltpu.VMEM((3, 2 * columns, frames), LOW),
            pltpu.VMEM((columns, frames), WIDE),
            pltpu.SemaphoreType.DMA((3, PARTS)),
            pltpu.SemaphoreType.DMA((3, PARTS)),
            *sems,
        ],
        compiler_params=pltpu.CompilerParams(
            collective_id=collective_id, has_side_effects=True, vmem_limit_bytes=20 << 20
        ),
        name="attend_back",
    )(length, qkv, held, grad, out_wide, log_total, *extra)


def gelu_value(values):
    return 0.5 * values * (1.0 + lax.erf(values * ROOT_HALF))


def gelu_slope(values):
    return 0.5 * (1.0 + lax.erf(values * ROOT_HALF)) + values * DENSITY * jnp.exp(
        -0.5 * values * values
    )


def product(left_side, right_side, left_axis, right_axis):
    return lax.dot_general(
        left_side,
        right_side,
        (((left_axis,), (right_axis,)), ((), ())),
        preferred_element_type=WIDE,
    )


def per_device(
    hidden,
    cotangent,
    lengths,
    query_weight,
    key_weight,
    value_weight,
    output_weight,
    inner_weight,
    outer_weight,
    query_bias,
    value_bias,
    inner_bias,
    output_bias,
    outer_bias,
    first_gain,
    first_shift,
    second_gain,
    second_shift,
):
    clip_count, rows, width = hidden.shape
    assert clip_count == 1
    assert lax.axis_size("ctx") == 4
    tp_size = lax.axis_size("tp")
    own_rows = rows // tp_size
    columns = query_weight.shape[2]
    hidden_local = inner_weight.shape[2]
    scale = 1.0 / math.sqrt(HD)
    own_start = lax.axis_index("tp") * own_rows

    def own_slice(full):
        return lax.dynamic_slice_in_dim(full, own_start, own_rows, axis=0)

    smalls = (output_bias, outer_bias, first_gain, first_shift, second_gain, second_shift)
    qkv_weights = [jnp.swapaxes(weight, 1, 2) for weight in (query_weight, key_weight, value_weight)]

    def qkv_shard(layer):
        return jnp.concatenate([weight[layer] for weight in qkv_weights], axis=0).astype(LOW)

    def gather(array, axis):
        return lax.all_gather(array, "fsdp", axis=axis, tiled=True)

    projections = output_weight.astype(LOW).reshape(-1, output_weight.shape[2])
    paired = lax.axis_size("fsdp") == 2
    if paired:
        wides = (inner_weight, outer_weight, *qkv_weights)
        jobs = [(which, layer, which * LAYERS + layer, 0) for layer in range(LAYERS) for which in range(2)]
        shapes = [wide.shape[1:] for wide in wides[:2] for _ in range(LAYERS)]
        for layer in range(1, LAYERS):
            jobs += [(2 + at, layer, len(shapes), at * columns) for at in range(3)]
            shapes.append((3 * columns, qkv_weights[0].shape[2]))
        results = fetch_first((qkv_shard(0), projections), smalls, wides, tuple(jobs), shapes, 17)
        qkv_first, projections, *results = results
        smalls, lows = results[: len(smalls)], results[len(smalls) :]
        inner_low, outer_low, qkv_low = lows[:LAYERS], lows[LAYERS : 2 * LAYERS], [None, *lows[2 * LAYERS :]]
    else:
        qkv_first, projections = gather(qkv_shard(0), 1), gather(projections, 1)
        smalls = [gather(small, 1) for small in smalls]
        inner_low, outer_low = inner_weight.astype(LOW), outer_weight.astype(LOW)
        qkv_low = [qkv_shard(layer) for layer in range(LAYERS)]
    projections = projections.reshape(LAYERS, columns, width)
    smalls = [lax.reduce_precision(small, 8, 7) for small in smalls]

    def vector(kind, layer):
        return smalls[kind][layer]

    w_qkvs = [qkv_first] + [None if paired else gather(qkv_low[layer], 1) for layer in range(1, LAYERS)]
    feeds = [(gather(inner_low[layer], 0), gather(outer_low[layer], 1)) for layer in range(LAYERS)]

    hidden_rows = hidden.reshape(rows, width)
    residual = own_slice(hidden_rows)
    hat_full, _ = norm_parts(hidden_rows)
    normed = (hat_full * vector(2, 0) + vector(3, 0)).astype(LOW)
    kept = []
    for layer in range(LAYERS):
        w_qkv, w_out, (w_inner, w_outer) = w_qkvs[layer], projections[layer], feeds[layer]
        bias_qkv = jnp.concatenate(
            [query_bias[layer], jnp.zeros_like(query_bias[layer]), value_bias[layer]]
        )
        qkv = (product(w_qkv, normed, 1, 1) + bias_qkv[:, None]).astype(LOW)
        attended, attended_wide, log_total, held = attend(qkv, lengths, scale, 2 * layer)
        branch = product(attended, w_out, 0, 0).astype(LOW)
        normed_two, middle, *fetched = forward_exchange(
            branch,
            residual,
            vector(0, layer),
            vector(4, layer),
            vector(5, layer),
            tp_size,
            2 * layer + 4,
            qkv_low[layer + 1] if paired and layer + 1 < LAYERS else None,
        )
        if fetched:
            w_qkvs[layer + 1] = fetched[0]
        inner_pre = product(normed_two, w_inner, 1, 0) + inner_bias[layer]
        active, slope = gelu_value(inner_pre).astype(LOW), gelu_slope(inner_pre)
        kept.append(
            (residual, normed, qkv, attended, attended_wide, log_total, held, middle, normed_two, slope, active)
        )
        branch = product(active, w_outer, 1, 0).astype(LOW)
        if layer + 1 < LAYERS:
            normed, residual = forward_exchange(
                branch,
                middle,
                vector(1, layer),
                vector(2, layer + 1),
                vector(3, layer + 1),
                tp_size,
                2 * layer + 5,
            )
        else:
            last_branch, last_middle = branch, middle

    def exchange_back(branch, grad_out, normal_in, gain, collective_id, arrays, by_column):
        if lax.axis_size("fsdp") == 2:
            return backward_exchange(
                branch, grad_out, normal_in, gain, tp_size, collective_id, arrays, by_column
            )
        result = backward_exchange(branch, grad_out, normal_in, gain, tp_size, collective_id)
        for array, column in zip(arrays, by_column):
            axis = 1 if column else 0
            array = lax.psum_scatter(array, ("fsdp", "ctx"), scatter_dimension=axis, tiled=True)
            result += (lax.all_gather(array, "ctx", axis=axis, tiled=True),)
        return result

    grad_rows = cotangent.reshape(rows, width)
    grad_own = own_slice(grad_rows)
    grad_low = grad_rows.astype(LOW)
    outer_bias_sum = jnp.sum(grad_own, axis=0)
    grads = [None] * LAYERS
    vectors = [None] * LAYERS
    biases = [None] * LAYERS
    for layer in reversed(range(LAYERS)):
        w_qkv, w_out, (w_inner, w_outer) = w_qkvs[layer], projections[layer], feeds[layer]
        (
            residual,
            normed,
            qkv,
            attended,
            attended_wide,
            log_total,
            held,
            middle,
            normed_two,
            slope,
            active,
        ) = kept[layer]
        grad_active = product(grad_low, w_outer, 1, 1)
        grad_inner = (grad_active * slope).astype(LOW)
        branch = product(grad_inner, w_inner, 1, 1).astype(LOW)
        grad_outer_w = product(active, grad_low, 0, 0).astype(LOW)
        grad_inner_w = product(normed_two, grad_inner, 0, 0).astype(LOW)
        grad_mid_low, grad_middle, sums_two, *summed_two = exchange_back(
            branch, grad_own, middle, vector(4, layer), 2 * layer + 8, (grad_inner_w, grad_outer_w), (False, True)
        )
        if layer == LAYERS - 1:
            last_branch, grad_mid_low = lax.optimization_barrier((last_branch, grad_mid_low))
            last_branch = lax.psum_scatter(last_branch, "tp", scatter_dimension=0, tiled=True)
        grad_attended = product(w_out, grad_mid_low, 1, 1).astype(LOW)
        grad_qkv, *shared = attend_back(
            qkv,
            held,
            grad_attended,
            attended_wide,
            log_total,
            lengths,
            scale,
            2 * layer + 12,
            last_rows if layer == 0 else None,
        )
        grad_output_w = product(attended, grad_mid_low, 1, 0).astype(LOW)
        branch = product(grad_qkv, w_qkv, 0, 0).astype(LOW)
        grad_qkv_w = product(grad_qkv, normed, 1, 0).astype(LOW)
        if layer == LAYERS - 1:
            last_branch, branch = lax.optimization_barrier((last_branch, branch))
            last_rows = (last_middle + last_branch.astype(WIDE) + vector(1, layer)).astype(LOW)
        if layer == 0:
            output = shared[0].astype(WIDE)
        grad_low, grad_own, sums_one, *summed_one = exchange_back(
            branch, grad_middle, residual, vector(2, layer), 2 * layer + 9, (grad_qkv_w, grad_output_w), (True, True)
        )
        grads[layer] = (*summed_one, *summed_two)
        vectors[layer] = [
            sums_two[2], outer_bias_sum, sums_one[0], sums_one[1], sums_two[0], sums_two[1]
        ]
        outer_bias_sum = sums_one[2]
        biases[layer] = jnp.concatenate(
            [
                jnp.sum(grad_qkv.astype(WIDE), axis=1),
                jnp.sum(grad_inner.astype(WIDE), axis=0),
            ]
        )
    grad_hidden = grad_low.astype(WIDE)

    shard = output_bias.shape[1]
    flat_biases = jnp.concatenate(biases)
    flat_biases = jnp.pad(flat_biases, (0, -flat_biases.size % (8 * shard))).reshape(-1, shard)
    vector_count = 6 * LAYERS
    small_sums = jnp.stack([row for parts in zip(*vectors) for row in parts])
    if lax.axis_size("fsdp") == 2:
        small_sums = jnp.pad(small_sums, ((0, -vector_count % 8), (0, 0)))
        shared_rows = small_sums.shape[0]
        small_sums = sum_all(
            small_sums, flat_biases, tuple((axis, lax.axis_size(axis)) for axis in ("ctx", "tp")), 16
        )
        vector_sums, bias_sums = small_sums[:vector_count], small_sums[shared_rows:]
    else:
        vector_sums = lax.psum(small_sums, ("fsdp", "ctx", "tp"))
        vector_sums = lax.dynamic_slice_in_dim(vector_sums, lax.axis_index("fsdp") * shard, shard, axis=1)
        bias_sums = lax.psum(flat_biases, ("fsdp", "ctx"))
    vector_sums = vector_sums.reshape(6, LAYERS, shard)
    bias_sums = bias_sums.reshape(-1)[: LAYERS * biases[0].size].reshape(LAYERS, -1)

    def stacked(which):
        return jnp.stack([grads[layer][which] for layer in range(LAYERS)]).astype(WIDE)

    def turned(start):
        return jnp.stack([grads[layer][0][start : start + columns].T for layer in range(LAYERS)]).astype(WIDE)

    return (
        output.reshape(hidden.shape),
        grad_hidden.reshape(hidden.shape),
        turned(0),
        turned(columns),
        turned(2 * columns),
        stacked(1),
        stacked(2),
        stacked(3),
        bias_sums[:, :columns],
        bias_sums[:, 2 * columns : 3 * columns],
        bias_sums[:, 3 * columns :],
        vector_sums[0],
        vector_sums[1],
        vector_sums[2],
        vector_sums[3],
        vector_sums[4],
        vector_sums[5],
    )


def solution(mesh):
    in_specs = (
        P("fsdp", "ctx", None),
        P("fsdp", "ctx", None),
        P("fsdp"),
        P(None, "fsdp", "tp"),
        P(None, "fsdp", "tp"),
        P(None, "fsdp", "tp"),
        P(None, "tp", "fsdp"),
        P(None, "fsdp", "tp"),
        P(None, "tp", "fsdp"),
        P(None, "tp"),
        P(None, "tp"),
        P(None, "tp"),
        P(None, "fsdp"),
        P(None, "fsdp"),
        P(None, "fsdp"),
        P(None, "fsdp"),
        P(None, "fsdp"),
        P(None, "fsdp"),
    )
    out_specs = (
        P("fsdp", "ctx", None),
        P("fsdp", "ctx", None),
        P(None, "fsdp", "tp"),
        P(None, "fsdp", "tp"),
        P(None, "fsdp", "tp"),
        P(None, "tp", "fsdp"),
        P(None, "fsdp", "tp"),
        P(None, "tp", "fsdp"),
        P(None, "tp"),
        P(None, "tp"),
        P(None, "tp"),
        P(None, "fsdp"),
        P(None, "fsdp"),
        P(None, "fsdp"),
        P(None, "fsdp"),
        P(None, "fsdp"),
        P(None, "fsdp"),
    )
    return jax.shard_map(
        per_device, mesh=mesh, in_specs=in_specs, out_specs=out_specs, check_vma=False
    )
```

```python
import functools
import math
import jax
import jax.numpy as jnp
from jax import lax
from jax.experimental import pallas as pl
from jax.experimental.pallas import tpu as pltpu
from jax.sharding import PartitionSpec as P

MESH = pl.DeviceIdType.MESH
LOW = jnp.bfloat16
WIDE = jnp.float32
EPSILON = 1e-05
NEGATIVE = -1e30
HD = 80
PIECES = 4
LAYERS = 2
ROOT_HALF = 1.0 / math.sqrt(2.0)
DENSITY = 1.0 / math.sqrt(2.0 * math.pi)
REDUCE_LAG = 2
GATHER_LAG = 3


def norm_parts(values):
    average = jnp.mean(values, axis=-1, keepdims=True)
    centered = values - average
    spread = jnp.mean(centered * centered, axis=-1, keepdims=True)
    inverse = lax.rsqrt(spread + EPSILON)
    return (centered * inverse, inverse)


def norm_back(upstream, normal_hat, inverse, gain_full):
    scaled = upstream * gain_full
    first_mean = jnp.mean(scaled, axis=-1, keepdims=True)
    second_mean = jnp.mean(scaled * normal_hat, axis=-1, keepdims=True)
    return inverse * (scaled - first_mean - normal_hat * second_mean)


def line_exchange(n, own, pieces, partial, gathered, from_left, from_right, total, sems, finish, side=None):
    rs_send, rs_recv, ag_send, ag_recv = sems
    me = lax.axis_index("tp")
    piece = own // pieces
    to_right, to_left = {"tp": lax.rem(me + 1, n)}, {"tp": lax.rem(me + n - 1, n)}
    has_left, has_right = me > 0, me < n - 1

    barrier = pltpu.get_barrier_semaphore()

    @pl.when(has_left)
    def _():
        pl.semaphore_signal(barrier, inc=1, device_id=to_left, device_id_type=MESH)

    @pl.when(has_right)
    def _():
        pl.semaphore_signal(barrier, inc=1, device_id=to_right, device_id_type=MESH)

    peers = has_left.astype(jnp.int32) + has_right.astype(jnp.int32)
    if side is not None:
        for peer in side.peers:
            pl.semaphore_signal(barrier, inc=1, device_id=peer, device_id_type=MESH)
        peers = peers + len(side.peers)
    pl.semaphore_wait(barrier, peers)
    if side is not None:
        side.start()

    def rows_of(shard, step):
        return pl.ds(pl.multiple_of(shard * own + step * piece, piece), piece)

    def reduce_copy(way, src, shard, step):
        rows = rows_of(shard, step)
        landing = from_left if way == 0 else from_right
        return pltpu.make_async_remote_copy(
            src_ref=src.at[rows],
            dst_ref=landing.at[rows],
            send_sem=rs_send.at[way, shard, step],
            recv_sem=rs_recv.at[way, shard, step],
            device_id=to_right if way == 0 else to_left,
            device_id_type=MESH,
        )

    def gather_copy(way, shard, step):
        rows = rows_of(shard, step)
        return pltpu.make_async_remote_copy(
            src_ref=gathered.at[rows],
            dst_ref=gathered.at[rows],
            send_sem=ag_send.at[way, shard, step],
            recv_sem=ag_recv.at[way, shard, step],
            device_id=to_right if way == 0 else to_left,
            device_id_type=MESH,
        )

    def reduce_one(way, shard, step):
        landing = from_left if way == 0 else from_right
        first = me == 0 if way == 0 else me == n - 1

        @pl.when(first)
        def _():
            reduce_copy(way, partial, shard, step).start()

        @pl.when(jnp.logical_not(first))
        def _():
            rows = rows_of(shard, step)
            reduce_copy(way, partial, shard, step).wait_recv()
            landing[rows, :] = (
                partial[rows, :].astype(WIDE) + landing[rows, :].astype(WIDE)
            ).astype(LOW)
            reduce_copy(way, landing, shard, step).start()

    def finish_one(step):
        rows = rows_of(me, step)
        total[...] = partial[rows, :].astype(WIDE)

        @pl.when(has_left)
        def _():
            reduce_copy(0, partial, me, step).wait_recv()
            total[...] += from_left[rows, :].astype(WIDE)

        @pl.when(has_right)
        def _():
            reduce_copy(1, partial, me, step).wait_recv()
            total[...] += from_right[rows, :].astype(WIDE)

        own_rows = pl.ds(pl.multiple_of(step * piece, piece), piece)
        gathered[rows, :] = finish(own_rows, total[...])

        @pl.when(has_right)
        def _():
            gather_copy(0, me, step).start()

        @pl.when(has_left)
        def _():
            gather_copy(1, me, step).start()

    def forward_one(way, shard, step):
        gather_copy(way, shard, step).wait_recv()

        @pl.when(has_right if way == 0 else has_left)
        def _():
            gather_copy(way, shard, step).start()

    period = n - 1

    def finish_at(device):
        from_start = jnp.where(device > 0, n - 1 - device + REDUCE_LAG * device, 0)
        from_end = jnp.where(device < n - 1, device + REDUCE_LAG * (n - 1 - device), 0)
        return jnp.maximum(from_start, from_end)

    def split(tick, start, length):
        since = tick - start
        clipped = jnp.maximum(since, 0)
        return (since >= 0) & (clipped < length), lax.div(clipped, period), lax.rem(clipped, period)

    def body(tick, carry):
        for way in range(2):
            hops = me if way == 0 else n - 1 - me
            due, step, k = split(tick, REDUCE_LAG * hops, pieces * period)
            shard = n - 1 - k if way == 0 else k
            mine = me < shard if way == 0 else me > shard

            @pl.when(due & mine)
            def _():
                reduce_one(way, shard, step)

        due, step, k = split(tick, finish_at(me), pieces * period)

        @pl.when(due & (k == 0))
        def _():
            finish_one(step)

        for hops in range(1, n):
            for way in range(2):
                shard = me - hops if way == 0 else me + hops
                there = shard >= 0 if way == 0 else shard <= n - 1
                due, step, k = split(
                    tick, finish_at(shard) + GATHER_LAG * hops, pieces * period
                )

                @pl.when(there & due & (k == 0))
                def _():
                    forward_one(way, shard, step)

        if side is not None:
            side.at(tick)
        return carry

    ticks = period * (pieces - 1) + max(REDUCE_LAG, 1) * (n - 1) + GATHER_LAG * (n - 1) + 1
    if side is not None:
        ticks = max(ticks, side.ticks)
    lax.fori_loop(0, ticks, body, 0)
    if side is not None:
        side.drain()

    def drain(step, carry):
        for k in range(n - 1):
            for way in range(2):
                shard = n - 1 - k if way == 0 else k
                sends = me < shard if way == 0 else me > shard

                @pl.when(sends)
                def _():
                    reduce_copy(way, partial, shard, step).wait_send()

        for k in range(n):
            for way in range(2):
                shard = me - k if way == 0 else me + k
                there = shard >= 0 if way == 0 else shard <= n - 1
                further = has_right if way == 0 else has_left

                @pl.when(there & further)
                def _():
                    gather_copy(way, shard, step).wait_send()

        return carry

    lax.fori_loop(0, pieces, drain, 0)


def exchange_scratch(n, rows, width, pieces):
    return [
        pltpu.VMEM((rows, width), LOW),
        pltpu.VMEM((rows, width), LOW),
        pltpu.VMEM((rows // n // pieces, width), WIDE),
        pltpu.SemaphoreType.DMA((2, n, pieces)),
        pltpu.SemaphoreType.DMA((2, n, pieces)),
        pltpu.SemaphoreType.DMA((2, n, pieces)),
        pltpu.SemaphoreType.DMA((2, n, pieces)),
    ]


def forward_fetch_kernel(
    n, pieces, partial, residual, bias, gain, shift, shard, gathered, middle, fetched, from_left, from_right, total,
    rs_send, rs_recv, ag_send, ag_recv, sends, recvs
):
    forward_exchange_kernel(
        n, pieces, partial, residual, bias, gain, shift, gathered, middle, from_left, from_right, total, rs_send, rs_recv,
        ag_send, ag_recv, side=QuartersSide((shard,), (fetched,), sends, recvs)
    )


def forward_exchange_kernel(
    n, pieces, partial, residual, bias, gain, shift, gathered, middle, from_left, from_right, total, *sems, side=None
):
    def finish(rows, value):
        mid = value + residual[rows, :] + bias[...]
        middle[rows, :] = mid
        hat, _ = norm_parts(mid)
        return (hat * gain[...] + shift[...]).astype(LOW)

    line_exchange(
        n, residual.shape[0], pieces, partial, gathered, from_left, from_right, total, sems, finish, side
    )


def backward_exchange_kernel(
    n, pieces, partial, grad_out, normal_in, gain, gathered, grad_in, sums, from_left, from_right, total, *sems, side=None
):
    sums[...] = jnp.zeros_like(sums)

    def finish(rows, upstream):
        hat, inverse = norm_parts(normal_in[rows, :])
        grad = grad_out[rows, :] + norm_back(upstream, hat, inverse, gain[...])
        grad_in[rows, :] = grad
        sums[0:1, :] += jnp.sum(upstream * hat, axis=0, keepdims=True)
        sums[1:2, :] += jnp.sum(upstream, axis=0, keepdims=True)
        sums[2:3, :] += jnp.sum(grad, axis=0, keepdims=True)
        return grad.astype(LOW)

    line_exchange(
        n, grad_out.shape[0], pieces, partial, gathered, from_left, from_right, total, sems, finish, side
    )


def in_vmem(count):
    return [pl.BlockSpec(memory_space=pltpu.VMEM)] * count


class GradientSum:
    LAGS = (0, 3, 6, 9)

    def __init__(self, by_column, arrays, outs, landings, sems):
        self.by_column = by_column
        self.chunks = landings[0].shape[1]
        self.arrays, self.outs, self.landings = arrays, outs, landings
        self.sends, self.recvs = sems
        self.half = lax.axis_index("fsdp")
        self.ctx = lax.axis_index("ctx")
        self.core = lax.rem(self.ctx, 2)
        pair = {"ctx": jnp.bitwise_xor(self.ctx, 1)}
        across = {"ctx": jnp.bitwise_xor(self.ctx, 2)}
        other = {"fsdp": 1 - self.half}
        self.peers = (pair, across, other)
        self.ticks = 2 * (self.chunks - 1) + self.LAGS[3] + 1

    def view(self, which, half, core, chunk):
        rows, cols = self.arrays[which].shape
        if not self.by_column[which]:
            part = rows // 4
            height = part // self.chunks
            start = half * (2 * part) + core * part + chunk * height
            return pl.ds(pl.multiple_of(start, 16), height), slice(None)
        part = rows // 2
        height = part // self.chunks
        start = core * part + chunk * height
        width = cols // 2
        return (
            pl.ds(pl.multiple_of(start, 16), height),
            pl.ds(pl.multiple_of(half * width, 128), width),
        )

    def out_rows(self, which, core, chunk):
        part = self.outs[which].shape[0] // 2
        height = part // self.chunks
        return pl.ds(pl.multiple_of(core * part + chunk * height, 16), height)

    def copy(self, which, stage, chunk, half=0):
        pair, across, other = self.peers
        landing = self.landings[which]
        if stage == 0:
            src = self.arrays[which].at[self.view(which, half, 1 - self.core, chunk)]
            slot, peer = half, pair
        elif stage == 1:
            src = landing.at[1 - self.half, chunk]
            slot, peer = 2, other
        elif stage == 2:
            src = landing.at[2, chunk]
            slot, peer = 3, across
        else:
            src = landing.at[3, chunk]
            slot, peer = 4, pair
        return pltpu.make_async_remote_copy(
            src_ref=src,
            dst_ref=landing.at[slot, chunk],
            send_sem=self.sends.at[which, slot, chunk],
            recv_sem=self.recvs.at[which, slot, chunk],
            device_id=peer,
            device_id_type=MESH,
        )

    def start(self):
        def body(chunk, carry):
            for which in range(len(self.arrays)):
                for half in range(2):
                    self.copy(which, 0, chunk, half).start()
            return carry

        lax.fori_loop(0, self.chunks, body, 0)

    def when_due(self, tick, lag, action):
        since = tick - lag
        clipped = jnp.maximum(since, 0)
        chunk = lax.div(clipped, 2)

        @pl.when((since >= 0) & (lax.rem(clipped, 2) == 0) & (chunk < self.chunks))
        def _():
            for which in range(len(self.arrays)):
                action(which, chunk)

    def at(self, tick):
        def joined(which, chunk):
            landing = self.landings[which]
            for half in range(2):
                self.copy(which, 0, chunk, half).wait_recv()
                rows, cols = self.view(which, half, self.core, chunk)
                landing[half, chunk] = (
                    self.arrays[which][rows, cols].astype(WIDE) + landing[half, chunk].astype(WIDE)
                ).astype(LOW)
            self.copy(which, 1, chunk).start()

        def crossed(which, chunk):
            landing = self.landings[which]
            self.copy(which, 1, chunk).wait_recv()
            landing[2, chunk] = (
                landing[self.half, chunk].astype(WIDE) + landing[2, chunk].astype(WIDE)
            ).astype(LOW)
            self.copy(which, 2, chunk).start()

        def summed(which, chunk):
            landing = self.landings[which]
            self.copy(which, 2, chunk).wait_recv()
            low = (landing[2, chunk].astype(WIDE) + landing[3, chunk].astype(WIDE)).astype(LOW)
            landing[3, chunk] = low
            self.outs[which][self.out_rows(which, self.core, chunk), :] = low
            self.copy(which, 3, chunk).start()

        def shared(which, chunk):
            self.copy(which, 3, chunk).wait_recv()
            self.outs[which][self.out_rows(which, 1 - self.core, chunk), :] = self.landings[which][
                4, chunk
            ]

        for lag, action in zip(self.LAGS, (joined, crossed, summed, shared)):
            self.when_due(tick, lag, action)

    def drain(self):
        def body(chunk, carry):
            for which in range(len(self.arrays)):
                for half in range(2):
                    self.copy(which, 0, chunk, half).wait_send()
                for stage in range(1, 4):
                    self.copy(which, stage, chunk).wait_send()
            return carry

        lax.fori_loop(0, self.chunks, body, 0)


def gradient_shapes(arrays, by_column):
    chunks = 5 if all(by_column) else 10
    outs, landings = (), []
    for array, column in zip(arrays, by_column):
        rows, cols = array.shape
        rows, cols = (rows, cols // 2) if column else (rows // 2, cols)
        outs += (jax.ShapeDtypeStruct((rows, cols), LOW),)
        landings.append(pltpu.VMEM((5, chunks, rows // 2 // chunks, cols), LOW))
    return outs, landings, pltpu.SemaphoreType.DMA((len(arrays), 5, chunks))


def backward_gradient_kernel(by_column, n, pieces, partial, grad_out, normal_in, gain, *refs):
    count = len(by_column)
    arrays, (gathered, grad_in, sums), refs = refs[:count], refs[count : count + 3], refs[count + 3 :]
    outs, (from_left, from_right, total, *sems), refs = refs[:count], refs[count : count + 7], refs[count + 7 :]
    side = GradientSum(by_column, arrays, outs, refs[:count], refs[count:])
    backward_exchange_kernel(
        n, pieces, partial, grad_out, normal_in, gain, gathered, grad_in, sums, from_left, from_right, total, *sems, side=side
    )


def sum_all_kernel(axes, vectors, biases, out, staged, landing, sends, recvs):
    half = lax.axis_index("fsdp")
    shared, width = vectors.shape[0], out.shape[1]
    steps = [("fsdp", 1)] + [(axis, 1 << b) for axis, size in axes for b in range(size.bit_length() - 1)]

    def peer(axis, k):
        return {axis: jnp.bitwise_xor(lax.axis_index(axis), k)}

    barrier = pltpu.get_barrier_semaphore()
    for axis, k in steps:
        pl.semaphore_signal(barrier, inc=1, device_id=peer(axis, k), device_id_type=MESH)
    for side in range(2):
        staged[side, 0:shared, :] = vectors[:, side * width : (side + 1) * width]
        staged[side, shared:, :] = biases[...]
    pl.semaphore_wait(barrier, len(steps))
    for at, (axis, k) in enumerate(steps):
        rows = pl.ds(0, shared) if axis == "tp" else pl.ds(0, out.shape[0])
        if at > 0:
            landing[at, 0, rows] = out[rows, :]
        copy = pltpu.make_async_remote_copy(
            src_ref=landing.at[at, 0, rows] if at > 0 else staged.at[1 - half],
            dst_ref=landing.at[at, 1, rows],
            send_sem=sends.at[at],
            recv_sem=recvs.at[at],
            device_id=peer(axis, k),
            device_id_type=MESH,
        )
        copy.start()
        copy.wait()
        own = landing[at, 0, rows] if at > 0 else staged[half]
        out[rows, :] = own + landing[at, 1, rows]


def sum_all(vectors, biases, axes, collective_id):
    shape = (vectors.shape[0] + biases.shape[0], biases.shape[1])
    steps = 1 + sum(size.bit_length() - 1 for _, size in axes)
    return pl.pallas_call(
        functools.partial(sum_all_kernel, axes),
        out_shape=jax.ShapeDtypeStruct(shape, WIDE),
        in_specs=in_vmem(2),
        out_specs=in_vmem(1)[0],
        scratch_shapes=[
            pltpu.VMEM((2,) + shape, WIDE),
            pltpu.VMEM((steps, 2) + shape, WIDE),
            pltpu.SemaphoreType.DMA((steps,)),
            pltpu.SemaphoreType.DMA((steps,)),
        ],
        compiler_params=pltpu.CompilerParams(
            collective_id=collective_id, has_side_effects=True, vmem_limit_bytes=8 << 20
        ),
        name="sum_all",
    )(vectors, biases)


def fetch_parts(rows):
    return next(parts for parts in (2, 3, 1) if rows // 4 % (16 * parts) == 0)


CAST_ROWS = 64
FIRST_GAIN, FIRST_SHIFT = 2, 3


class Quarters:
    def __init__(self, shards, outs, sends, recvs):
        self.shards, self.outs, self.sends, self.recvs = shards, outs, sends, recvs
        self.half = lax.axis_index("fsdp")
        self.ctx = lax.axis_index("ctx")
        self.pair, self.across = jnp.bitwise_xor(self.ctx, 1), jnp.bitwise_xor(self.ctx, 2)
        self.targets = ({"fsdp": 1 - self.half}, {"ctx": self.across}, {"ctx": self.pair}, {"ctx": self.pair})
        self.peers = self.targets[:3]
        self.each = [
            (which, part) for which in range(len(shards)) for part in range(fetch_parts(shards[which].shape[0]))
        ]

    def rows_of(self, which, quarter, part):
        parts = fetch_parts(self.shards[which].shape[0])
        height = self.shards[which].shape[0] // 4 // parts
        return pl.ds(pl.multiple_of((quarter * parts + part) * height, 16), height)

    def place(self, which, side, quarter, part):
        cols = self.shards[which].shape[1]
        return self.outs[which].at[
            self.rows_of(which, quarter, part), pl.ds(pl.multiple_of(side * cols, 128), cols)
        ]

    def copy(self, stage, item, arriving=False):
        which, part = item
        quarter = (self.ctx, self.ctx, self.ctx, self.across)[stage]
        src = self.shards[which].at[self.rows_of(which, quarter, part)]
        dst = self.place(which, self.half, quarter, part)
        if stage > 0:
            src = dst = self.place(which, 1 - self.half, quarter, part)
        if arriving:
            quarter = (self.ctx, self.across, self.pair, jnp.bitwise_xor(self.ctx, 3))[stage]
            dst = self.place(which, 1 - self.half, quarter, part)
        return pltpu.make_async_remote_copy(
            src_ref=src,
            dst_ref=dst,
            send_sem=self.sends.at[which, stage, part],
            recv_sem=self.recvs.at[which, stage, part],
            device_id=self.targets[stage],
            device_id_type=MESH,
        )

    def begin(self):
        for item in self.each:
            self.copy(0, item).start()

    def keep_own(self):
        for shard, out in zip(self.shards, self.outs):
            cols = shard.shape[1]
            out[:, pl.ds(pl.multiple_of(self.half * cols, 128), cols)] = shard[...]

    def crossed(self, item):
        self.copy(0, item, True).wait_recv()
        self.copy(1, item).start()
        self.copy(2, item).start()

    def forwarded(self, item):
        self.copy(1, item, True).wait_recv()
        self.copy(3, item).start()

    def finish(self):
        for stage in (2, 3):
            for item in self.each:
                self.copy(stage, item, True).wait_recv()
        for stage in range(4):
            for item in self.each:
                self.copy(stage, item).wait_send()


class QuartersSide(Quarters):
    CROSSED, APART, FORWARDED = 6, 5, 4

    def start(self):
        self.begin()
        self.keep_own()

    @property
    def ticks(self):
        return self.CROSSED + self.FORWARDED + self.APART * (len(self.each) - 1) + 1

    def at(self, tick):
        for at, item in enumerate(self.each):
            due = self.CROSSED + self.APART * at

            @pl.when(tick == due)
            def _():
                self.crossed(item)

            @pl.when(tick == due + self.FORWARDED)
            def _():
                self.forwarded(item)

    def drain(self):
        self.finish()


def fetch_kernel(counts, jobs, *refs):
    refs = list(refs)

    def take(count):
        taken = refs[:count]
        del refs[:count]
        return taken

    shard_count, small_count, wide_count, low_count = counts
    shards, smalls, wides, (frames,) = take(shard_count), take(small_count), take(wide_count), take(1)
    outs, out_smalls, lows, (normed,) = take(shard_count), take(small_count), take(low_count), take(1)
    buffers, (frame_buffer,) = take(len(jobs)), take(1)
    cast_sems, sends, recvs, small_sends, small_recvs = refs
    quarters = Quarters(shards, outs, sends, recvs)

    barrier = pltpu.get_barrier_semaphore()
    for peer in quarters.peers:
        pl.semaphore_signal(barrier, inc=1, device_id=peer, device_id_type=MESH)
    pl.semaphore_wait(barrier, 3)

    def small_copy(at, side):
        cols = smalls[at].shape[1]
        return pltpu.make_async_remote_copy(
            src_ref=smalls[at],
            dst_ref=out_smalls[at].at[:, pl.ds(pl.multiple_of(side * cols, 128), cols)],
            send_sem=small_sends.at[at],
            recv_sem=small_recvs.at[at],
            device_id=quarters.peers[0],
            device_id_type=MESH,
        )

    def load(at):
        which, layer, _, _ = jobs[at]
        return pltpu.make_async_copy(wides[which].at[layer], buffers[at], cast_sems.at[at])

    frame_load = pltpu.make_async_copy(frames, frame_buffer, cast_sems.at[len(jobs)])

    def norm(step, carry):
        rows = pl.ds(pl.multiple_of(step * CAST_ROWS, CAST_ROWS), CAST_ROWS)
        hat, _ = norm_parts(frame_buffer[rows, :])
        normed[rows, :] = (hat * out_smalls[FIRST_GAIN][0:1, :] + out_smalls[FIRST_SHIFT][0:1, :]).astype(LOW)
        return carry

    for at in range(small_count):
        small_copy(at, quarters.half).start()
    quarters.begin()
    for at in range(len(jobs)):
        load(at).start()
    frame_load.start()
    quarters.keep_own()
    for small, out in zip(smalls, out_smalls):
        cols = small.shape[1]
        out[:, pl.ds(pl.multiple_of(quarters.half * cols, 128), cols)] = small[...]
    for at, (_, _, low, first) in enumerate(jobs):
        load(at).wait()

        def cast(step, carry):
            start = pl.multiple_of(step * CAST_ROWS, CAST_ROWS)
            lows[low][pl.ds(first + start, CAST_ROWS), :] = buffers[at][pl.ds(start, CAST_ROWS), :].astype(LOW)
            return carry

        lax.fori_loop(0, buffers[at].shape[0] // CAST_ROWS, cast, 0)
    for at in range(small_count):
        small_copy(at, 1 - quarters.half).wait_recv()
        out_smalls[at][...] = out_smalls[at][...].astype(LOW).astype(WIDE)
    last = len(quarters.each)
    for at in range(last + 1):
        if at < last:
            quarters.crossed(quarters.each[at])
        if at > 0:
            quarters.forwarded(quarters.each[at - 1])
        if at == fetch_parts(shards[0].shape[0]):
            frame_load.wait()
            lax.fori_loop(0, normed.shape[0] // CAST_ROWS, norm, 0)
    quarters.finish()
    for at in range(small_count):
        small_copy(at, quarters.half).wait_send()


def quarter_sems(shards):
    most = max(fetch_parts(shard.shape[0]) for shard in shards)
    return [pltpu.SemaphoreType.DMA((len(shards), 4, most))] * 2


def gathered_shape(shard):
    return jax.ShapeDtypeStruct((shard.shape[0], 2 * shard.shape[1]), shard.dtype)


def fetch_first(shards, smalls, wides, frames, jobs, low_shapes, collective_id):
    counts = (len(shards), len(smalls), len(wides), len(low_shapes))
    out_shape = tuple(gathered_shape(array) for array in (*shards, *smalls))
    out_shape += tuple(jax.ShapeDtypeStruct(shape, LOW) for shape in (*low_shapes, frames.shape))
    return pl.pallas_call(
        functools.partial(fetch_kernel, counts, jobs),
        out_shape=out_shape,
        in_specs=in_vmem(len(shards) + len(smalls)) + [pl.BlockSpec(memory_space=pl.ANY)] * (len(wides) + 1),
        out_specs=tuple(in_vmem(len(out_shape))),
        scratch_shapes=[pltpu.VMEM(wides[job[0]].shape[1:], WIDE) for job in jobs]
        + [pltpu.VMEM(frames.shape, WIDE), pltpu.SemaphoreType.DMA((len(jobs) + 1,))]
        + quarter_sems(shards)
        + [pltpu.SemaphoreType.DMA((len(smalls),))] * 2,
        compiler_params=pltpu.CompilerParams(
            collective_id=collective_id, has_side_effects=True, vmem_limit_bytes=42 << 20
        ),
        name="fetch_first",
    )(*shards, *smalls, *wides, frames)


def forward_exchange(partial, residual, bias, gain, shift, n, collective_id, shard=None):
    rows, width = partial.shape
    out_shape = (
        jax.ShapeDtypeStruct((rows, width), LOW),
        jax.ShapeDtypeStruct(residual.shape, WIDE),
    )
    scratch = exchange_scratch(n, rows, width, PIECES)
    kernel, extra = forward_exchange_kernel, ()
    if shard is not None:
        out_shape += (gathered_shape(shard),)
        scratch = scratch + quarter_sems((shard,))
        kernel, extra = forward_fetch_kernel, (shard,)
    return pl.pallas_call(
        functools.partial(kernel, n, PIECES),
        out_shape=out_shape,
        in_specs=in_vmem(5 + len(extra)),
        out_specs=tuple(in_vmem(len(out_shape))),
        scratch_shapes=scratch,
        compiler_params=pltpu.CompilerParams(
            collective_id=collective_id, has_side_effects=True, vmem_limit_bytes=12 << 20
        ),
        name="forward_exchange",
    )(partial, residual, bias[None, :], gain[None, :], shift[None, :], *extra)


def backward_exchange(partial, grad_out, normal_in, gain, n, collective_id, arrays=(), by_column=()):
    rows, width = partial.shape
    out_shape = (
        jax.ShapeDtypeStruct((rows, width), LOW),
        jax.ShapeDtypeStruct(grad_out.shape, WIDE),
        jax.ShapeDtypeStruct((8, width), WIDE),
    )
    scratch = exchange_scratch(n, rows, width, PIECES)
    kernel, extra = backward_exchange_kernel, ()
    if arrays:
        outs, landings, sems = gradient_shapes(arrays, by_column)
        out_shape = out_shape + outs
        scratch = scratch + landings + [sems] * 2
        kernel, extra = functools.partial(backward_gradient_kernel, by_column), arrays
    return pl.pallas_call(
        functools.partial(kernel, n, PIECES),
        out_shape=out_shape,
        in_specs=in_vmem(4 + len(extra)),
        out_specs=tuple(in_vmem(len(out_shape))),
        scratch_shapes=scratch,
        compiler_params=pltpu.CompilerParams(
            collective_id=collective_id, has_side_effects=True, vmem_limit_bytes=20 << 20
        ),
        name="backward_exchange",
    )(partial, grad_out, normal_in, gain[None, :], *extra)


GROUPS = 2
PARTS = 2 * GROUPS


def part_rows(columns, part, base=0):
    size = columns // GROUPS
    return pl.ds(base + (part % 2) * columns + (part // 2) * size, size)


def group_parts(group):
    return (2 * group, 2 * group + 1)


def group_heads(heads, group):
    assert heads % GROUPS == 0
    size = heads // GROUPS
    return range(heads) if group is None else range(group * size, (group + 1) * size)


def attend_kernel(scale, length, qkv, out, out_wide, log_total, held, high, low_sum, sems_send, sems_recv):
    columns = qkv.shape[0] // 3
    frames = qkv.shape[1]
    heads = columns // HD
    me = lax.axis_index("ctx")

    def partner(r):
        return {"ctx": jnp.bitwise_xor(me, r)}

    barrier = pltpu.get_barrier_semaphore()
    for r in (1, 2):
        pl.semaphore_signal(barrier, inc=1, device_id=partner(r), device_id_type=MESH)
    pl.semaphore_wait(barrier, 2)

    def send(slot, part, to):
        rows, own_rows = part_rows(columns, part), part_rows(columns, part, columns)
        src = qkv.at[own_rows] if slot != 3 else held.at[1, rows]
        return pltpu.make_async_remote_copy(
            src_ref=src,
            dst_ref=held.at[slot - 1, rows],
            send_sem=sems_send.at[slot - 1, part],
            recv_sem=sems_recv.at[slot - 1, part],
            device_id=partner(to),
            device_id_type=MESH,
        )

    for part in range(PARTS):
        send(2, part, 2).start()
    for part in range(PARTS):
        send(1, part, 1).start()

    high[...] = jnp.full_like(high, NEGATIVE)
    low_sum[...] = jnp.zeros_like(low_sum)
    out_wide[...] = jnp.zeros_like(out_wide)
    limit = length[0]

    def block(keys_ref, key_row, value_row, slot, group=None):
        owner = jnp.bitwise_xor(me, slot)
        left = limit - owner * frames
        valid = lax.broadcasted_iota(jnp.int32, (frames, frames), 0) < left
        for h in group_heads(heads, group):
            rows = pl.ds(h * HD, HD)
            keys = keys_ref[pl.ds(key_row + h * HD, HD), :]
            values = keys_ref[pl.ds(value_row + h * HD, HD), :]
            scores = lax.dot_general(
                keys, qkv[rows, :], (((0,), (0,)), ((), ())), preferred_element_type=WIDE
            )
            scores = jnp.where(valid, scores * scale, NEGATIVE)
            before = high[h : h + 1, :]
            now = jnp.maximum(before, jnp.max(scores, axis=0, keepdims=True))
            shrink = jnp.exp(before - now)
            raised = jnp.exp(scores - now)
            low_sum[h : h + 1, :] = low_sum[h : h + 1, :] * shrink + jnp.sum(
                raised, axis=0, keepdims=True
            )
            high[h : h + 1, :] = now
            out_wide[rows, :] = out_wide[rows, :] * shrink + jnp.dot(
                values, raised.astype(LOW), preferred_element_type=WIDE
            )

    block(qkv, columns, 2 * columns, 0)
    for part in range(PARTS):
        send(1, part, 1).wait_recv()
    block(held.at[0], 0, columns, 1)
    for group in range(GROUPS):
        for part in group_parts(group):
            send(2, part, 2).wait_recv()
            send(3, part, 1).start()
        block(held.at[1], 0, columns, 2, group)
    for group in range(GROUPS):
        for part in group_parts(group):
            send(3, part, 1).wait_recv()
        block(held.at[2], 0, columns, 3, group)
    for h in range(heads):
        rows = pl.ds(h * HD, HD)
        total = low_sum[h : h + 1, :]
        done = out_wide[rows, :] / total
        out_wide[rows, :] = done
        out[rows, :] = done.astype(LOW)
        log_total[h : h + 1, :] = high[h : h + 1, :] + jnp.log(total)
    for slot in (1, 2, 3):
        for part in range(PARTS):
            send(slot, part, 2 if slot == 2 else 1).wait_send()


def attend(qkv, length, scale, collective_id):
    columns, frames = qkv.shape[0] // 3, qkv.shape[1]
    return pl.pallas_call(
        functools.partial(attend_kernel, scale),
        out_shape=(
            jax.ShapeDtypeStruct((columns, frames), LOW),
            jax.ShapeDtypeStruct((columns, frames), WIDE),
            jax.ShapeDtypeStruct((8, frames), WIDE),
            jax.ShapeDtypeStruct((3, 2 * columns, frames), LOW),
        ),
        in_specs=[pl.BlockSpec(memory_space=pltpu.SMEM)] + in_vmem(1),
        out_specs=tuple(in_vmem(4)),
        scratch_shapes=[
            pltpu.VMEM((8, frames), WIDE),
            pltpu.VMEM((8, frames), WIDE),
            pltpu.SemaphoreType.DMA((3, PARTS)),
            pltpu.SemaphoreType.DMA((3, PARTS)),
        ],
        compiler_params=pltpu.CompilerParams(
            collective_id=collective_id, has_side_effects=True, vmem_limit_bytes=16 << 20
        ),
        name="attend",
    )(length, qkv)


class LineGather:
    def __init__(self, own, gathered, sends, recvs):
        self.own, self.gathered, self.sends, self.recvs = own, gathered, sends, recvs
        self.n = gathered.shape[0] // own.shape[0]
        self.me = lax.axis_index("tp")
        self.further = (self.me < self.n - 1, self.me > 0)
        self.peers = ({"tp": lax.rem(self.me + 1, self.n)}, {"tp": lax.rem(self.me + self.n - 1, self.n)})

    def greet(self, barrier):
        for way in range(2):

            @pl.when(self.further[way])
            def _():
                pl.semaphore_signal(barrier, inc=1, device_id=self.peers[way], device_id_type=MESH)

        return self.further[0].astype(jnp.int32) + self.further[1].astype(jnp.int32)

    def rows(self, shard):
        size = self.own.shape[0]
        return pl.ds(pl.multiple_of(shard * size, size), size)

    def there(self, way, hops):
        return self.me - hops >= 0 if way == 0 else self.me + hops <= self.n - 1

    def send(self, way, hops):
        shard = self.me - hops if way == 0 else self.me + hops
        rows = self.rows(shard)
        return pltpu.make_async_remote_copy(
            src_ref=self.own if hops == 0 else self.gathered.at[rows],
            dst_ref=self.gathered.at[rows],
            send_sem=self.sends.at[way, hops],
            recv_sem=self.recvs.at[way, hops],
            device_id=self.peers[way],
            device_id_type=MESH,
        )

    def arrival(self, way, hops):
        rows = self.rows(self.me - hops if way == 0 else self.me + hops)
        return pltpu.make_async_remote_copy(
            src_ref=self.gathered.at[rows],
            dst_ref=self.gathered.at[rows],
            send_sem=self.sends.at[way, hops],
            recv_sem=self.recvs.at[way, hops - 1],
            device_id=self.peers[way],
            device_id_type=MESH,
        )

    def hop(self, hops):
        for way in range(2):
            if hops > 0:

                @pl.when(self.there(way, hops))
                def _():
                    self.arrival(way, hops).wait_recv()

            if hops < self.n - 1:

                @pl.when(self.there(way, hops) & self.further[way])
                def _():
                    self.send(way, hops).start()

    def drain(self):
        for hops in range(self.n - 1):
            for way in range(2):

                @pl.when(self.there(way, hops) & self.further[way])
                def _():
                    self.send(way, hops).wait_send()


def attend_back_kernel(scale, sharing, length, qkv, held, grad, out_wide, log_total, *refs):
    if sharing:
        own, grad_qkv, gathered, mine, parts, landed, acc, sems_send, sems_recv, sends, recvs = refs
        share = LineGather(own, gathered, sends, recvs)
    else:
        grad_qkv, mine, parts, landed, acc, sems_send, sems_recv = refs
        share = None
    columns = qkv.shape[0] // 3
    frames = qkv.shape[1]
    heads = columns // HD
    me = lax.axis_index("ctx")

    def partner(r):
        return {"ctx": jnp.bitwise_xor(me, r)}

    barrier = pltpu.get_barrier_semaphore()
    for r in (1, 2):
        pl.semaphore_signal(barrier, inc=1, device_id=partner(r), device_id_type=MESH)
    waiting = 2
    if share is not None:
        waiting = waiting + share.greet(barrier)
    pl.semaphore_wait(barrier, waiting)
    if share is not None:
        share.hop(0)
        gathered[share.rows(share.me), :] = own[...]

    def send(at, part, to):
        rows = part_rows(columns, part)
        return pltpu.make_async_remote_copy(
            src_ref=parts.at[at, rows],
            dst_ref=landed.at[at, rows],
            send_sem=sems_send.at[at, part],
            recv_sem=sems_recv.at[at, part],
            device_id=partner(to),
            device_id_type=MESH,
        )

    acc[...] = jnp.zeros_like(acc)
    limit = length[0]

    def block(keys_ref, key_row, value_row, slot, store, group=None):
        owner = jnp.bitwise_xor(me, slot)
        left = limit - owner * frames
        valid = lax.broadcasted_iota(jnp.int32, (frames, frames), 0) < left
        for h in group_heads(heads, group):
            rows = pl.ds(h * HD, HD)
            keys = keys_ref[pl.ds(key_row + h * HD, HD), :]
            values = keys_ref[pl.ds(value_row + h * HD, HD), :]
            queries = qkv[rows, :]
            upstream = grad[rows, :]
            scores = lax.dot_general(
                keys, queries, (((0,), (0,)), ((), ())), preferred_element_type=WIDE
            )
            weights = jnp.where(valid, jnp.exp(scores * scale - log_total[h : h + 1, :]), 0.0)
            grad_weights = lax.dot_general(
                values, upstream, (((0,), (0,)), ((), ())), preferred_element_type=WIDE
            )
            row_terms = jnp.sum(
                upstream.astype(WIDE) * out_wide[rows, :], axis=0, keepdims=True
            )
            grad_scores = (weights * (grad_weights - row_terms)).astype(LOW)
            acc[rows, :] += jnp.dot(keys, grad_scores, preferred_element_type=WIDE)
            grad_keys = (
                lax.dot_general(
                    queries, grad_scores, (((1,), (1,)), ((), ())), preferred_element_type=WIDE
                )
                * scale
            )
            grad_values = lax.dot_general(
                upstream, weights.astype(LOW), (((1,), (1,)), ((), ())), preferred_element_type=WIDE
            )
            store(h * HD, grad_keys, grad_values)

    def store_part(at):
        def store(row, grad_keys, grad_values):
            parts[at, pl.ds(row, HD), :] = grad_keys.astype(LOW)
            parts[at, pl.ds(columns + row, HD), :] = grad_values.astype(LOW)

        return store

    def store_mine(row, grad_keys, grad_values):
        mine[pl.ds(row, HD), :] = grad_keys
        mine[pl.ds(columns + row, HD), :] = grad_values

    def store_joined(row, grad_keys, grad_values):
        for start, value in ((row, grad_keys), (columns + row, grad_values)):
            rows = pl.ds(start, HD)
            parts[1, rows, :] = (value + landed[0, rows, :].astype(WIDE)).astype(LOW)

    for group in range(GROUPS):
        block(held.at[2], 0, columns, 3, store_part(0), group)
        for part in group_parts(group):
            send(0, part, 1).start()
    for group in range(GROUPS):
        for part in group_parts(group):
            send(0, part, 1).wait_recv()
        block(held.at[1], 0, columns, 2, store_joined, group)
        for part in group_parts(group):
            send(1, part, 2).start()
        if share is not None and group == 0:
            share.hop(1)
    for group in range(GROUPS):
        block(held.at[0], 0, columns, 1, store_part(2), group)
        for part in group_parts(group):
            send(2, part, 1).start()
        if share is not None and group == 0:
            share.hop(2)
    block(qkv, columns, 2 * columns, 0, store_mine)
    grad_qkv[0:columns, :] = (acc[...] * scale).astype(LOW)
    for part in range(PARTS):
        send(2, part, 1).wait_recv()
    for part in range(PARTS):
        send(1, part, 2).wait_recv()
    grad_qkv[columns:, :] = (
        mine[...] + landed[1].astype(WIDE) + landed[2].astype(WIDE)
    ).astype(LOW)
    for at in range(3):
        for part in range(PARTS):
            send(at, part, 2 if at == 1 else 1).wait_send()
    if share is not None:
        for hops in range(3, share.n):
            share.hop(hops)
        share.drain()


def attend_back(qkv, held, grad, out_wide, log_total, length, scale, collective_id, own=None):
    columns, frames = qkv.shape[0] // 3, qkv.shape[1]
    out_shape = (jax.ShapeDtypeStruct((3 * columns, frames), LOW),)
    extra, sems = (), []
    if own is not None:
        n = lax.axis_size("tp")
        assert n >= 3
        out_shape += (jax.ShapeDtypeStruct((n * own.shape[0], own.shape[1]), LOW),)
        extra, sems = (own,), [pltpu.SemaphoreType.DMA((2, n))] * 2
    return pl.pallas_call(
        functools.partial(attend_back_kernel, scale, own is not None),
        out_shape=out_shape,
        in_specs=[pl.BlockSpec(memory_space=pltpu.SMEM)] + in_vmem(5 + len(extra)),
        out_specs=tuple(in_vmem(len(out_shape))),
        scratch_shapes=[
            pltpu.VMEM((2 * columns, frames), WIDE),
            pltpu.VMEM((3, 2 * columns, frames), LOW),
            pltpu.VMEM((3, 2 * columns, frames), LOW),
            pltpu.VMEM((columns, frames), WIDE),
            pltpu.SemaphoreType.DMA((3, PARTS)),
            pltpu.SemaphoreType.DMA((3, PARTS)),
            *sems,
        ],
        compiler_params=pltpu.CompilerParams(
            collective_id=collective_id, has_side_effects=True, vmem_limit_bytes=18 << 20
        ),
        name="attend_back",
    )(length, qkv, held, grad, out_wide, log_total, *extra)


def gelu_value(values):
    return 0.5 * values * (1.0 + lax.erf(values * ROOT_HALF))


def gelu_slope(values):
    return 0.5 * (1.0 + lax.erf(values * ROOT_HALF)) + values * DENSITY * jnp.exp(
        -0.5 * values * values
    )


def product(left_side, right_side, left_axis, right_axis):
    return lax.dot_general(
        left_side,
        right_side,
        (((left_axis,), (right_axis,)), ((), ())),
        preferred_element_type=WIDE,
    )


def per_device(
    hidden,
    cotangent,
    lengths,
    query_weight,
    key_weight,
    value_weight,
    output_weight,
    inner_weight,
    outer_weight,
    query_bias,
    value_bias,
    inner_bias,
    output_bias,
    outer_bias,
    first_gain,
    first_shift,
    second_gain,
    second_shift,
):
    clip_count, rows, width = hidden.shape
    assert clip_count == 1
    assert lax.axis_size("ctx") == 4
    tp_size = lax.axis_size("tp")
    own_rows = rows // tp_size
    columns = query_weight.shape[2]
    hidden_local = inner_weight.shape[2]
    scale = 1.0 / math.sqrt(HD)
    own_start = lax.axis_index("tp") * own_rows

    def own_slice(full):
        return lax.dynamic_slice_in_dim(full, own_start, own_rows, axis=0)

    hidden_rows = hidden.reshape(rows, width)
    smalls = (output_bias, outer_bias, first_gain, first_shift, second_gain, second_shift)
    qkv_weights = [jnp.swapaxes(weight, 1, 2) for weight in (query_weight, key_weight, value_weight)]

    def qkv_shard(layer):
        return jnp.concatenate([weight[layer] for weight in qkv_weights], axis=0).astype(LOW)

    def gather(array, axis):
        return lax.all_gather(array, "fsdp", axis=axis, tiled=True)

    projections = output_weight.astype(LOW).reshape(-1, output_weight.shape[2])
    paired = lax.axis_size("fsdp") == 2
    if paired:
        wides = (inner_weight, outer_weight, *qkv_weights)
        jobs = [(which, layer, which * LAYERS + layer, 0) for layer in range(LAYERS) for which in range(2)]
        shapes = [wide.shape[1:] for wide in wides[:2] for _ in range(LAYERS)]
        for layer in range(1, LAYERS):
            jobs += [(2 + at, layer, len(shapes), at * columns) for at in range(3)]
            shapes.append((3 * columns, qkv_weights[0].shape[2]))
        results = fetch_first((qkv_shard(0), projections), smalls, wides, hidden_rows, tuple(jobs), shapes, 17)
        qkv_first, projections, *results, normed = results
        smalls, lows = results[: len(smalls)], results[len(smalls) :]
        inner_low, outer_low, qkv_low = lows[:LAYERS], lows[LAYERS : 2 * LAYERS], [None, *lows[2 * LAYERS :]]
    else:
        qkv_first, projections = gather(qkv_shard(0), 1), gather(projections, 1)
        smalls = [gather(small, 1) for small in smalls]
        inner_low, outer_low = inner_weight.astype(LOW), outer_weight.astype(LOW)
        qkv_low = [qkv_shard(layer) for layer in range(LAYERS)]
        smalls = [lax.reduce_precision(small, 8, 7) for small in smalls]
        hat_full, _ = norm_parts(hidden_rows)
        normed = (hat_full * smalls[FIRST_GAIN][0] + smalls[FIRST_SHIFT][0]).astype(LOW)
    projections = projections.reshape(LAYERS, columns, width)

    def vector(kind, layer):
        return smalls[kind][layer]

    w_qkvs = [qkv_first] + [gather(qkv_low[layer], 1) for layer in range(1, LAYERS)]
    w_inners = [gather(inner_low[layer], 0) for layer in range(LAYERS)]
    carried = paired and tp_size == 4
    w_outers = [None if carried and layer == 0 else gather(outer_low[layer], 1) for layer in range(LAYERS)]

    residual = own_slice(hidden_rows)
    kept = []
    for layer in range(LAYERS):
        w_qkv, w_out, w_inner = w_qkvs[layer], projections[layer], w_inners[layer]
        bias_qkv = jnp.concatenate(
            [query_bias[layer], jnp.zeros_like(query_bias[layer]), value_bias[layer]]
        )
        qkv = (product(w_qkv, normed, 1, 1) + bias_qkv[:, None]).astype(LOW)
        attended, attended_wide, log_total, held = attend(qkv, lengths, scale, 2 * layer)
        branch = product(attended, w_out, 0, 0).astype(LOW)
        normed_two, middle, *fetched = forward_exchange(
            branch,
            residual,
            vector(0, layer),
            vector(4, layer),
            vector(5, layer),
            tp_size,
            2 * layer + 4,
            outer_low[layer] if carried and layer == 0 else None,
        )
        if fetched:
            w_outers[layer] = fetched[0]
        inner_pre = product(normed_two, w_inner, 1, 0) + inner_bias[layer]
        active, slope = gelu_value(inner_pre).astype(LOW), gelu_slope(inner_pre)
        kept.append(
            (residual, normed, qkv, attended, attended_wide, log_total, held, middle, normed_two, slope, active)
        )
        branch = product(active, w_outers[layer], 1, 0).astype(LOW)
        if layer + 1 < LAYERS:
            normed, residual = forward_exchange(
                branch,
                middle,
                vector(1, layer),
                vector(2, layer + 1),
                vector(3, layer + 1),
                tp_size,
                2 * layer + 5,
            )
        else:
            last_branch, last_middle = branch, middle

    def exchange_back(branch, grad_out, normal_in, gain, collective_id, arrays, by_column):
        if lax.axis_size("fsdp") == 2:
            return backward_exchange(
                branch, grad_out, normal_in, gain, tp_size, collective_id, arrays, by_column
            )
        result = backward_exchange(branch, grad_out, normal_in, gain, tp_size, collective_id)
        for array, column in zip(arrays, by_column):
            axis = 1 if column else 0
            array = lax.psum_scatter(array, ("fsdp", "ctx"), scatter_dimension=axis, tiled=True)
            result += (lax.all_gather(array, "ctx", axis=axis, tiled=True),)
        return result

    grad_rows = cotangent.reshape(rows, width)
    grad_own = own_slice(grad_rows)
    grad_low = grad_rows.astype(LOW)
    outer_bias_sum = jnp.sum(grad_own, axis=0)
    grads = [None] * LAYERS
    vectors = [None] * LAYERS
    biases = [None] * LAYERS
    for layer in reversed(range(LAYERS)):
        w_qkv, w_out, w_inner, w_outer = w_qkvs[layer], projections[layer], w_inners[layer], w_outers[layer]
        (
            residual,
            normed,
            qkv,
            attended,
            attended_wide,
            log_total,
            held,
            middle,
            normed_two,
            slope,
            active,
        ) = kept[layer]
        grad_active = product(grad_low, w_outer, 1, 1)
        grad_inner = (grad_active * slope).astype(LOW)
        branch = product(grad_inner, w_inner, 1, 1).astype(LOW)
        grad_outer_w = product(active, grad_low, 0, 0).astype(LOW)
        grad_inner_w = product(normed_two, grad_inner, 0, 0).astype(LOW)
        grad_mid_low, grad_middle, sums_two, *summed_two = exchange_back(
            branch, grad_own, middle, vector(4, layer), 2 * layer + 8, (grad_inner_w, grad_outer_w), (False, True)
        )
        if layer == LAYERS - 1:
            last_branch, grad_mid_low = lax.optimization_barrier((last_branch, grad_mid_low))
            last_branch = lax.psum_scatter(last_branch, "tp", scatter_dimension=0, tiled=True)
        grad_attended = product(w_out, grad_mid_low, 1, 1).astype(LOW)
        grad_qkv, *shared = attend_back(
            qkv,
            held,
            grad_attended,
            attended_wide,
            log_total,
            lengths,
            scale,
            2 * layer + 12,
            last_rows if layer == 0 else None,
        )
        grad_output_w = product(attended, grad_mid_low, 1, 0).astype(LOW)
        branch = product(grad_qkv, w_qkv, 0, 0).astype(LOW)
        grad_qkv_w = product(grad_qkv, normed, 1, 0).astype(LOW)
        if layer == LAYERS - 1:
            last_branch, branch = lax.optimization_barrier((last_branch, branch))
            last_rows = (last_middle + last_branch.astype(WIDE) + vector(1, layer)).astype(LOW)
        if layer == 0:
            output = shared[0].astype(WIDE)
        grad_low, grad_own, sums_one, *summed_one = exchange_back(
            branch, grad_middle, residual, vector(2, layer), 2 * layer + 9, (grad_qkv_w, grad_output_w), (True, True)
        )
        grads[layer] = (*summed_one, *summed_two)
        vectors[layer] = [
            sums_two[2], outer_bias_sum, sums_one[0], sums_one[1], sums_two[0], sums_two[1]
        ]
        outer_bias_sum = sums_one[2]
        biases[layer] = jnp.concatenate(
            [
                jnp.sum(grad_qkv.astype(WIDE), axis=1),
                jnp.sum(grad_inner.astype(WIDE), axis=0),
            ]
        )
    grad_hidden = grad_low.astype(WIDE)

    shard = output_bias.shape[1]
    flat_biases = jnp.concatenate(biases)
    flat_biases = jnp.pad(flat_biases, (0, -flat_biases.size % (8 * shard))).reshape(-1, shard)
    vector_count = 6 * LAYERS
    small_sums = jnp.stack([row for parts in zip(*vectors) for row in parts])
    if lax.axis_size("fsdp") == 2:
        small_sums = jnp.pad(small_sums, ((0, -vector_count % 8), (0, 0)))
        shared_rows = small_sums.shape[0]
        small_sums = sum_all(
            small_sums, flat_biases, tuple((axis, lax.axis_size(axis)) for axis in ("ctx", "tp")), 16
        )
        vector_sums, bias_sums = small_sums[:vector_count], small_sums[shared_rows:]
    else:
        vector_sums = lax.psum(small_sums, ("fsdp", "ctx", "tp"))
        vector_sums = lax.dynamic_slice_in_dim(vector_sums, lax.axis_index("fsdp") * shard, shard, axis=1)
        bias_sums = lax.psum(flat_biases, ("fsdp", "ctx"))
    vector_sums = vector_sums.reshape(6, LAYERS, shard)
    bias_sums = bias_sums.reshape(-1)[: LAYERS * biases[0].size].reshape(LAYERS, -1)

    def stacked(which):
        return jnp.stack([grads[layer][which] for layer in range(LAYERS)]).astype(WIDE)

    def turned(start):
        return jnp.stack([grads[layer][0][start : start + columns].T for layer in range(LAYERS)]).astype(WIDE)

    return (
        output.reshape(hidden.shape),
        grad_hidden.reshape(hidden.shape),
        turned(0),
        turned(columns),
        turned(2 * columns),
        stacked(1),
        stacked(2),
        stacked(3),
        bias_sums[:, :columns],
        bias_sums[:, 2 * columns : 3 * columns],
        bias_sums[:, 3 * columns :],
        vector_sums[0],
        vector_sums[1],
        vector_sums[2],
        vector_sums[3],
        vector_sums[4],
        vector_sums[5],
    )


def solution(mesh):
    in_specs = (
        P("fsdp", "ctx", None),
        P("fsdp", "ctx", None),
        P("fsdp"),
        P(None, "fsdp", "tp"),
        P(None, "fsdp", "tp"),
        P(None, "fsdp", "tp"),
        P(None, "tp", "fsdp"),
        P(None, "fsdp", "tp"),
        P(None, "tp", "fsdp"),
        P(None, "tp"),
        P(None, "tp"),
        P(None, "tp"),
        P(None, "fsdp"),
        P(None, "fsdp"),
        P(None, "fsdp"),
        P(None, "fsdp"),
        P(None, "fsdp"),
        P(None, "fsdp"),
    )
    out_specs = (
        P("fsdp", "ctx", None),
        P("fsdp", "ctx", None),
        P(None, "fsdp", "tp"),
        P(None, "fsdp", "tp"),
        P(None, "fsdp", "tp"),
        P(None, "tp", "fsdp"),
        P(None, "fsdp", "tp"),
        P(None, "tp", "fsdp"),
        P(None, "tp"),
        P(None, "tp"),
        P(None, "tp"),
        P(None, "fsdp"),
        P(None, "fsdp"),
        P(None, "fsdp"),
        P(None, "fsdp"),
        P(None, "fsdp"),
        P(None, "fsdp"),
    )
    return jax.shard_map(
        per_device, mesh=mesh, in_specs=in_specs, out_specs=out_specs, check_vma=False
    )
```

```python
import functools
import math
import jax
import jax.numpy as jnp
from jax import lax
from jax.experimental import pallas as pl
from jax.experimental.pallas import tpu as pltpu
from jax.sharding import PartitionSpec as P

MESH = pl.DeviceIdType.MESH
LOW = jnp.bfloat16
WIDE = jnp.float32
EPSILON = 1e-05
NEGATIVE = -1e30
HD = 80
PIECES = 4
LAYERS = 2
ROOT_HALF = 1.0 / math.sqrt(2.0)
DENSITY = 1.0 / math.sqrt(2.0 * math.pi)
REDUCE_LAG = 2
GATHER_LAG = 3


def norm_parts(values):
    average = jnp.mean(values, axis=-1, keepdims=True)
    centered = values - average
    spread = jnp.mean(centered * centered, axis=-1, keepdims=True)
    inverse = lax.rsqrt(spread + EPSILON)
    return (centered * inverse, inverse)


def norm_back(upstream, normal_hat, inverse, gain_full):
    scaled = upstream * gain_full
    first_mean = jnp.mean(scaled, axis=-1, keepdims=True)
    second_mean = jnp.mean(scaled * normal_hat, axis=-1, keepdims=True)
    return inverse * (scaled - first_mean - normal_hat * second_mean)


def line_exchange(n, own, pieces, partial, gathered, from_left, from_right, total, sems, finish, side=None):
    rs_send, rs_recv, ag_send, ag_recv = sems
    me = lax.axis_index("tp")
    piece = own // pieces
    to_right, to_left = {"tp": lax.rem(me + 1, n)}, {"tp": lax.rem(me + n - 1, n)}
    has_left, has_right = me > 0, me < n - 1

    barrier = pltpu.get_barrier_semaphore()

    @pl.when(has_left)
    def _():
        pl.semaphore_signal(barrier, inc=1, device_id=to_left, device_id_type=MESH)

    @pl.when(has_right)
    def _():
        pl.semaphore_signal(barrier, inc=1, device_id=to_right, device_id_type=MESH)

    peers = has_left.astype(jnp.int32) + has_right.astype(jnp.int32)
    if side is not None:
        for peer in side.peers:
            pl.semaphore_signal(barrier, inc=1, device_id=peer, device_id_type=MESH)
        peers = peers + len(side.peers)
    pl.semaphore_wait(barrier, peers)
    if side is not None:
        side.start()

    def rows_of(shard, step):
        return pl.ds(pl.multiple_of(shard * own + step * piece, piece), piece)

    def reduce_copy(way, src, shard, step):
        rows = rows_of(shard, step)
        landing = from_left if way == 0 else from_right
        return pltpu.make_async_remote_copy(
            src_ref=src.at[rows],
            dst_ref=landing.at[rows],
            send_sem=rs_send.at[way, shard, step],
            recv_sem=rs_recv.at[way, shard, step],
            device_id=to_right if way == 0 else to_left,
            device_id_type=MESH,
        )

    def gather_copy(way, shard, step):
        rows = rows_of(shard, step)
        return pltpu.make_async_remote_copy(
            src_ref=gathered.at[rows],
            dst_ref=gathered.at[rows],
            send_sem=ag_send.at[way, shard, step],
            recv_sem=ag_recv.at[way, shard, step],
            device_id=to_right if way == 0 else to_left,
            device_id_type=MESH,
        )

    def reduce_one(way, shard, step):
        landing = from_left if way == 0 else from_right
        first = me == 0 if way == 0 else me == n - 1

        @pl.when(first)
        def _():
            reduce_copy(way, partial, shard, step).start()

        @pl.when(jnp.logical_not(first))
        def _():
            rows = rows_of(shard, step)
            reduce_copy(way, partial, shard, step).wait_recv()
            landing[rows, :] = (
                partial[rows, :].astype(WIDE) + landing[rows, :].astype(WIDE)
            ).astype(LOW)
            reduce_copy(way, landing, shard, step).start()

    def finish_one(step):
        rows = rows_of(me, step)
        total[...] = partial[rows, :].astype(WIDE)

        @pl.when(has_left)
        def _():
            reduce_copy(0, partial, me, step).wait_recv()
            total[...] += from_left[rows, :].astype(WIDE)

        @pl.when(has_right)
        def _():
            reduce_copy(1, partial, me, step).wait_recv()
            total[...] += from_right[rows, :].astype(WIDE)

        own_rows = pl.ds(pl.multiple_of(step * piece, piece), piece)
        gathered[rows, :] = finish(own_rows, total[...])

        @pl.when(has_right)
        def _():
            gather_copy(0, me, step).start()

        @pl.when(has_left)
        def _():
            gather_copy(1, me, step).start()

    def forward_one(way, shard, step):
        gather_copy(way, shard, step).wait_recv()

        @pl.when(has_right if way == 0 else has_left)
        def _():
            gather_copy(way, shard, step).start()

    period = n - 1

    def finish_at(device):
        from_start = jnp.where(device > 0, n - 1 - device + REDUCE_LAG * device, 0)
        from_end = jnp.where(device < n - 1, device + REDUCE_LAG * (n - 1 - device), 0)
        return jnp.maximum(from_start, from_end)

    def split(tick, start, length):
        since = tick - start
        clipped = jnp.maximum(since, 0)
        return (since >= 0) & (clipped < length), lax.div(clipped, period), lax.rem(clipped, period)

    def body(tick, carry):
        for way in range(2):
            hops = me if way == 0 else n - 1 - me
            due, step, k = split(tick, REDUCE_LAG * hops, pieces * period)
            shard = n - 1 - k if way == 0 else k
            mine = me < shard if way == 0 else me > shard

            @pl.when(due & mine)
            def _():
                reduce_one(way, shard, step)

        due, step, k = split(tick, finish_at(me), pieces * period)

        @pl.when(due & (k == 0))
        def _():
            finish_one(step)

        for hops in range(1, n):
            for way in range(2):
                shard = me - hops if way == 0 else me + hops
                there = shard >= 0 if way == 0 else shard <= n - 1
                due, step, k = split(
                    tick, finish_at(shard) + GATHER_LAG * hops, pieces * period
                )

                @pl.when(there & due & (k == 0))
                def _():
                    forward_one(way, shard, step)

        if side is not None:
            side.at(tick)
        return carry

    ticks = period * (pieces - 1) + max(REDUCE_LAG, 1) * (n - 1) + GATHER_LAG * (n - 1) + 1
    if side is not None:
        ticks = max(ticks, side.ticks)
    lax.fori_loop(0, ticks, body, 0)
    if side is not None:
        side.drain()

    def drain(step, carry):
        for k in range(n - 1):
            for way in range(2):
                shard = n - 1 - k if way == 0 else k
                sends = me < shard if way == 0 else me > shard

                @pl.when(sends)
                def _():
                    reduce_copy(way, partial, shard, step).wait_send()

        for k in range(n):
            for way in range(2):
                shard = me - k if way == 0 else me + k
                there = shard >= 0 if way == 0 else shard <= n - 1
                further = has_right if way == 0 else has_left

                @pl.when(there & further)
                def _():
                    gather_copy(way, shard, step).wait_send()

        return carry

    lax.fori_loop(0, pieces, drain, 0)


def exchange_scratch(n, rows, width, pieces):
    return [
        pltpu.VMEM((rows, width), LOW),
        pltpu.VMEM((rows, width), LOW),
        pltpu.VMEM((rows // n // pieces, width), WIDE),
        pltpu.SemaphoreType.DMA((2, n, pieces)),
        pltpu.SemaphoreType.DMA((2, n, pieces)),
        pltpu.SemaphoreType.DMA((2, n, pieces)),
        pltpu.SemaphoreType.DMA((2, n, pieces)),
    ]


def forward_fetch_kernel(
    n, pieces, partial, residual, bias, gain, shift, shard, gathered, middle, fetched, from_left, from_right, total,
    rs_send, rs_recv, ag_send, ag_recv, sends, recvs
):
    forward_exchange_kernel(
        n, pieces, partial, residual, bias, gain, shift, gathered, middle, from_left, from_right, total, rs_send, rs_recv,
        ag_send, ag_recv, side=QuartersSide((shard,), (fetched,), sends, recvs)
    )


def forward_exchange_kernel(
    n, pieces, partial, residual, bias, gain, shift, gathered, middle, from_left, from_right, total, *sems, side=None
):
    def finish(rows, value):
        mid = value + residual[rows, :] + bias[...]
        middle[rows, :] = mid
        hat, _ = norm_parts(mid)
        return (hat * gain[...] + shift[...]).astype(LOW)

    line_exchange(
        n, residual.shape[0], pieces, partial, gathered, from_left, from_right, total, sems, finish, side
    )


def backward_exchange_kernel(
    n, pieces, partial, grad_out, normal_in, gain, gathered, grad_in, sums, from_left, from_right, total, *sems, side=None
):
    sums[...] = jnp.zeros_like(sums)

    def finish(rows, upstream):
        hat, inverse = norm_parts(normal_in[rows, :])
        grad = grad_out[rows, :] + norm_back(upstream, hat, inverse, gain[...])
        grad_in[rows, :] = grad
        sums[0:1, :] += jnp.sum(upstream * hat, axis=0, keepdims=True)
        sums[1:2, :] += jnp.sum(upstream, axis=0, keepdims=True)
        sums[2:3, :] += jnp.sum(grad, axis=0, keepdims=True)
        return grad.astype(LOW)

    line_exchange(
        n, grad_out.shape[0], pieces, partial, gathered, from_left, from_right, total, sems, finish, side
    )


def in_vmem(count):
    return [pl.BlockSpec(memory_space=pltpu.VMEM)] * count


class GradientSum:
    LAGS = (0, 3, 6, 9)

    def __init__(self, by_column, arrays, outs, landings, sems):
        self.by_column = by_column
        self.chunks = landings[0].shape[1]
        self.arrays, self.outs, self.landings = arrays, outs, landings
        self.sends, self.recvs, self.stores = sems
        self.half = lax.axis_index("fsdp")
        self.ctx = lax.axis_index("ctx")
        self.core = lax.rem(self.ctx, 2)
        pair = {"ctx": jnp.bitwise_xor(self.ctx, 1)}
        across = {"ctx": jnp.bitwise_xor(self.ctx, 2)}
        other = {"fsdp": 1 - self.half}
        self.peers = (pair, across, other)
        self.ticks = 2 * (self.chunks - 1) + self.LAGS[3] + 1

    def view(self, which, half, core, chunk):
        rows, cols = self.arrays[which].shape
        if not self.by_column[which]:
            part = rows // 4
            height = part // self.chunks
            start = half * (2 * part) + core * part + chunk * height
            return pl.ds(pl.multiple_of(start, 16), height), slice(None)
        part = rows // 2
        height = part // self.chunks
        start = core * part + chunk * height
        width = cols // 2
        return (
            pl.ds(pl.multiple_of(start, 16), height),
            pl.ds(pl.multiple_of(half * width, 128), width),
        )

    def out_rows(self, which, core, chunk):
        part = self.outs[which].shape[0] // 2
        height = part // self.chunks
        return pl.ds(pl.multiple_of(core * part + chunk * height, 16), height)

    def store(self, which, whose, chunk):
        core = self.core if whose == 0 else 1 - self.core
        return pltpu.make_async_copy(
            self.landings[which].at[3 + whose, chunk],
            self.outs[which].at[self.out_rows(which, core, chunk)],
            self.stores.at[which, whose, chunk],
        )

    def copy(self, which, stage, chunk, half=0):
        pair, across, other = self.peers
        landing = self.landings[which]
        if stage == 0:
            src = self.arrays[which].at[self.view(which, half, 1 - self.core, chunk)]
            slot, peer = half, pair
        elif stage == 1:
            src = landing.at[1 - self.half, chunk]
            slot, peer = 2, other
        elif stage == 2:
            src = landing.at[2, chunk]
            slot, peer = 3, across
        else:
            src = landing.at[3, chunk]
            slot, peer = 4, pair
        return pltpu.make_async_remote_copy(
            src_ref=src,
            dst_ref=landing.at[slot, chunk],
            send_sem=self.sends.at[which, slot, chunk],
            recv_sem=self.recvs.at[which, slot, chunk],
            device_id=peer,
            device_id_type=MESH,
        )

    def start(self):
        def body(chunk, carry):
            for which in range(len(self.arrays)):
                for half in range(2):
                    self.copy(which, 0, chunk, half).start()
            return carry

        lax.fori_loop(0, self.chunks, body, 0)

    def when_due(self, tick, lag, action):
        since = tick - lag
        clipped = jnp.maximum(since, 0)
        chunk = lax.div(clipped, 2)

        @pl.when((since >= 0) & (lax.rem(clipped, 2) == 0) & (chunk < self.chunks))
        def _():
            for which in range(len(self.arrays)):
                action(which, chunk)

    def at(self, tick):
        def joined(which, chunk):
            landing = self.landings[which]
            for half in range(2):
                self.copy(which, 0, chunk, half).wait_recv()
                rows, cols = self.view(which, half, self.core, chunk)
                landing[half, chunk] = (
                    self.arrays[which][rows, cols].astype(WIDE) + landing[half, chunk].astype(WIDE)
                ).astype(LOW)
            self.copy(which, 1, chunk).start()

        def crossed(which, chunk):
            landing = self.landings[which]
            self.copy(which, 1, chunk).wait_recv()
            landing[2, chunk] = (
                landing[self.half, chunk].astype(WIDE) + landing[2, chunk].astype(WIDE)
            ).astype(LOW)
            self.copy(which, 2, chunk).start()

        def summed(which, chunk):
            landing = self.landings[which]
            self.copy(which, 2, chunk).wait_recv()
            low = (landing[2, chunk].astype(WIDE) + landing[3, chunk].astype(WIDE)).astype(LOW)
            landing[3, chunk] = low
            self.copy(which, 3, chunk).start()
            self.store(which, 0, chunk).start()

        def shared(which, chunk):
            self.copy(which, 3, chunk).wait_recv()
            self.store(which, 1, chunk).start()

        for lag, action in zip(self.LAGS, (joined, crossed, summed, shared)):
            self.when_due(tick, lag, action)

    def drain(self):
        def body(chunk, carry):
            for which in range(len(self.arrays)):
                for half in range(2):
                    self.copy(which, 0, chunk, half).wait_send()
                for stage in range(1, 4):
                    self.copy(which, stage, chunk).wait_send()
                for whose in range(2):
                    self.store(which, whose, chunk).wait()
            return carry

        lax.fori_loop(0, self.chunks, body, 0)


def gradient_shapes(arrays, by_column):
    chunks = 5 if all(by_column) else 10
    outs, landings = (), []
    for array, column in zip(arrays, by_column):
        rows, cols = array.shape
        rows, cols = (rows, cols // 2) if column else (rows // 2, cols)
        outs += (pltpu.HBM((rows, cols), LOW),)
        landings.append(pltpu.VMEM((5, chunks, rows // 2 // chunks, cols), LOW))
    sems = [pltpu.SemaphoreType.DMA((len(arrays), 5, chunks))] * 2
    return outs, landings, sems + [pltpu.SemaphoreType.DMA((len(arrays), 2, chunks))]


def backward_gradient_kernel(by_column, n, pieces, partial, grad_out, normal_in, gain, *refs):
    count = len(by_column)
    arrays, (gathered, grad_in, sums), refs = refs[:count], refs[count : count + 3], refs[count + 3 :]
    outs, (from_left, from_right, total, *sems), refs = refs[:count], refs[count : count + 7], refs[count + 7 :]
    side = GradientSum(by_column, arrays, outs, refs[:count], refs[count:])
    backward_exchange_kernel(
        n, pieces, partial, grad_out, normal_in, gain, gathered, grad_in, sums, from_left, from_right, total, *sems, side=side
    )


def sum_all_kernel(axes, vectors, biases, out, staged, landing, sends, recvs):
    half = lax.axis_index("fsdp")
    shared, width = vectors.shape[0], out.shape[1]
    steps = [("fsdp", 1)] + [(axis, 1 << b) for axis, size in axes for b in range(size.bit_length() - 1)]

    def peer(axis, k):
        return {axis: jnp.bitwise_xor(lax.axis_index(axis), k)}

    barrier = pltpu.get_barrier_semaphore()
    for axis, k in steps:
        pl.semaphore_signal(barrier, inc=1, device_id=peer(axis, k), device_id_type=MESH)
    for side in range(2):
        staged[side, 0:shared, :] = vectors[:, side * width : (side + 1) * width]
        staged[side, shared:, :] = biases[...]
    pl.semaphore_wait(barrier, len(steps))
    for at, (axis, k) in enumerate(steps):
        rows = pl.ds(0, shared) if axis == "tp" else pl.ds(0, out.shape[0])
        if at > 0:
            landing[at, 0, rows] = out[rows, :]
        copy = pltpu.make_async_remote_copy(
            src_ref=landing.at[at, 0, rows] if at > 0 else staged.at[1 - half],
            dst_ref=landing.at[at, 1, rows],
            send_sem=sends.at[at],
            recv_sem=recvs.at[at],
            device_id=peer(axis, k),
            device_id_type=MESH,
        )
        copy.start()
        copy.wait()
        own = landing[at, 0, rows] if at > 0 else staged[half]
        out[rows, :] = own + landing[at, 1, rows]


def sum_all(vectors, biases, axes, collective_id):
    shape = (vectors.shape[0] + biases.shape[0], biases.shape[1])
    steps = 1 + sum(size.bit_length() - 1 for _, size in axes)
    return pl.pallas_call(
        functools.partial(sum_all_kernel, axes),
        out_shape=jax.ShapeDtypeStruct(shape, WIDE),
        in_specs=in_vmem(2),
        out_specs=in_vmem(1)[0],
        scratch_shapes=[
            pltpu.VMEM((2,) + shape, WIDE),
            pltpu.VMEM((steps, 2) + shape, WIDE),
            pltpu.SemaphoreType.DMA((steps,)),
            pltpu.SemaphoreType.DMA((steps,)),
        ],
        compiler_params=pltpu.CompilerParams(
            collective_id=collective_id, has_side_effects=True, vmem_limit_bytes=8 << 20
        ),
        name="sum_all",
    )(vectors, biases)


def fetch_parts(rows):
    return next(parts for parts in (2, 3, 1) if rows // 4 % (16 * parts) == 0)


CAST_ROWS = 64
FIRST_GAIN, FIRST_SHIFT = 2, 3


class Quarters:
    def __init__(self, shards, outs, sends, recvs):
        self.shards, self.outs, self.sends, self.recvs = shards, outs, sends, recvs
        self.half = lax.axis_index("fsdp")
        self.ctx = lax.axis_index("ctx")
        self.pair, self.across = jnp.bitwise_xor(self.ctx, 1), jnp.bitwise_xor(self.ctx, 2)
        self.targets = ({"fsdp": 1 - self.half}, {"ctx": self.across}, {"ctx": self.pair}, {"ctx": self.pair})
        self.peers = self.targets[:3]
        self.each = [
            (which, part) for which in range(len(shards)) for part in range(fetch_parts(shards[which].shape[0]))
        ]

    def rows_of(self, which, quarter, part):
        parts = fetch_parts(self.shards[which].shape[0])
        height = self.shards[which].shape[0] // 4 // parts
        return pl.ds(pl.multiple_of((quarter * parts + part) * height, 16), height)

    def place(self, which, side, quarter, part):
        cols = self.shards[which].shape[1]
        return self.outs[which].at[
            self.rows_of(which, quarter, part), pl.ds(pl.multiple_of(side * cols, 128), cols)
        ]

    def copy(self, stage, item, arriving=False):
        which, part = item
        quarter = (self.ctx, self.ctx, self.ctx, self.across)[stage]
        src = self.shards[which].at[self.rows_of(which, quarter, part)]
        dst = self.place(which, self.half, quarter, part)
        if stage > 0:
            src = dst = self.place(which, 1 - self.half, quarter, part)
        if arriving:
            quarter = (self.ctx, self.across, self.pair, jnp.bitwise_xor(self.ctx, 3))[stage]
            dst = self.place(which, 1 - self.half, quarter, part)
        return pltpu.make_async_remote_copy(
            src_ref=src,
            dst_ref=dst,
            send_sem=self.sends.at[which, stage, part],
            recv_sem=self.recvs.at[which, stage, part],
            device_id=self.targets[stage],
            device_id_type=MESH,
        )

    def begin(self):
        for item in self.each:
            self.copy(0, item).start()

    def keep_own(self):
        for shard, out in zip(self.shards, self.outs):
            cols = shard.shape[1]
            out[:, pl.ds(pl.multiple_of(self.half * cols, 128), cols)] = shard[...]

    def crossed(self, item):
        self.copy(0, item, True).wait_recv()
        self.copy(1, item).start()
        self.copy(2, item).start()

    def forwarded(self, item):
        self.copy(1, item, True).wait_recv()
        self.copy(3, item).start()

    def finish(self):
        for stage in (2, 3):
            for item in self.each:
                self.copy(stage, item, True).wait_recv()
        for stage in range(4):
            for item in self.each:
                self.copy(stage, item).wait_send()


class QuartersSide(Quarters):
    CROSSED, APART, FORWARDED = 6, 5, 4

    def start(self):
        self.begin()
        self.keep_own()

    @property
    def ticks(self):
        return self.CROSSED + self.FORWARDED + self.APART * (len(self.each) - 1) + 1

    def at(self, tick):
        for at, item in enumerate(self.each):
            due = self.CROSSED + self.APART * at

            @pl.when(tick == due)
            def _():
                self.crossed(item)

            @pl.when(tick == due + self.FORWARDED)
            def _():
                self.forwarded(item)

    def drain(self):
        self.finish()


def fetch_kernel(counts, jobs, *refs):
    refs = list(refs)

    def take(count):
        taken = refs[:count]
        del refs[:count]
        return taken

    shard_count, small_count, wide_count, low_count = counts
    shards, smalls, wides, (frames,) = take(shard_count), take(small_count), take(wide_count), take(1)
    outs, out_smalls, lows, (normed,) = take(shard_count), take(small_count), take(low_count), take(1)
    buffers, (frame_buffer,) = take(len(jobs)), take(1)
    cast_sems, sends, recvs, small_sends, small_recvs = refs
    quarters = Quarters(shards, outs, sends, recvs)

    barrier = pltpu.get_barrier_semaphore()
    for peer in quarters.peers:
        pl.semaphore_signal(barrier, inc=1, device_id=peer, device_id_type=MESH)
    pl.semaphore_wait(barrier, 3)

    def small_copy(at, side):
        cols = smalls[at].shape[1]
        return pltpu.make_async_remote_copy(
            src_ref=smalls[at],
            dst_ref=out_smalls[at].at[:, pl.ds(pl.multiple_of(side * cols, 128), cols)],
            send_sem=small_sends.at[at],
            recv_sem=small_recvs.at[at],
            device_id=quarters.peers[0],
            device_id_type=MESH,
        )

    def load(at):
        which, layer, _, _ = jobs[at]
        return pltpu.make_async_copy(wides[which].at[layer], buffers[at], cast_sems.at[at])

    frame_load = pltpu.make_async_copy(frames, frame_buffer, cast_sems.at[len(jobs)])

    def norm(step, carry):
        rows = pl.ds(pl.multiple_of(step * CAST_ROWS, CAST_ROWS), CAST_ROWS)
        hat, _ = norm_parts(frame_buffer[rows, :])
        normed[rows, :] = (hat * out_smalls[FIRST_GAIN][0:1, :] + out_smalls[FIRST_SHIFT][0:1, :]).astype(LOW)
        return carry

    for at in range(small_count):
        small_copy(at, quarters.half).start()
    quarters.begin()
    for at in range(len(jobs)):
        load(at).start()
    frame_load.start()
    quarters.keep_own()
    for small, out in zip(smalls, out_smalls):
        cols = small.shape[1]
        out[:, pl.ds(pl.multiple_of(quarters.half * cols, 128), cols)] = small[...]
    for at, (_, _, low, first) in enumerate(jobs):
        load(at).wait()

        def cast(step, carry):
            start = pl.multiple_of(step * CAST_ROWS, CAST_ROWS)
            lows[low][pl.ds(first + start, CAST_ROWS), :] = buffers[at][pl.ds(start, CAST_ROWS), :].astype(LOW)
            return carry

        lax.fori_loop(0, buffers[at].shape[0] // CAST_ROWS, cast, 0)
    for at in range(small_count):
        small_copy(at, 1 - quarters.half).wait_recv()
        out_smalls[at][...] = out_smalls[at][...].astype(LOW).astype(WIDE)
    last = len(quarters.each)
    for at in range(last + 1):
        if at < last:
            quarters.crossed(quarters.each[at])
        if at > 0:
            quarters.forwarded(quarters.each[at - 1])
        if at == fetch_parts(shards[0].shape[0]):
            frame_load.wait()
            lax.fori_loop(0, normed.shape[0] // CAST_ROWS, norm, 0)
    quarters.finish()
    for at in range(small_count):
        small_copy(at, quarters.half).wait_send()


def quarter_sems(shards):
    most = max(fetch_parts(shard.shape[0]) for shard in shards)
    return [pltpu.SemaphoreType.DMA((len(shards), 4, most))] * 2


def gathered_shape(shard):
    return jax.ShapeDtypeStruct((shard.shape[0], 2 * shard.shape[1]), shard.dtype)


def fetch_first(shards, smalls, wides, frames, jobs, low_shapes, collective_id):
    counts = (len(shards), len(smalls), len(wides), len(low_shapes))
    out_shape = tuple(gathered_shape(array) for array in (*shards, *smalls))
    out_shape += tuple(jax.ShapeDtypeStruct(shape, LOW) for shape in (*low_shapes, frames.shape))
    return pl.pallas_call(
        functools.partial(fetch_kernel, counts, jobs),
        out_shape=out_shape,
        in_specs=in_vmem(len(shards) + len(smalls)) + [pl.BlockSpec(memory_space=pl.ANY)] * (len(wides) + 1),
        out_specs=tuple(in_vmem(len(out_shape))),
        scratch_shapes=[pltpu.VMEM(wides[job[0]].shape[1:], WIDE) for job in jobs]
        + [pltpu.VMEM(frames.shape, WIDE), pltpu.SemaphoreType.DMA((len(jobs) + 1,))]
        + quarter_sems(shards)
        + [pltpu.SemaphoreType.DMA((len(smalls),))] * 2,
        compiler_params=pltpu.CompilerParams(
            collective_id=collective_id, has_side_effects=True, vmem_limit_bytes=42 << 20
        ),
        name="fetch_first",
    )(*shards, *smalls, *wides, frames)


def forward_exchange(partial, residual, bias, gain, shift, n, collective_id, shard=None):
    rows, width = partial.shape
    out_shape = (
        jax.ShapeDtypeStruct((rows, width), LOW),
        jax.ShapeDtypeStruct(residual.shape, WIDE),
    )
    scratch = exchange_scratch(n, rows, width, PIECES)
    kernel, extra = forward_exchange_kernel, ()
    if shard is not None:
        out_shape += (gathered_shape(shard),)
        scratch = scratch + quarter_sems((shard,))
        kernel, extra = forward_fetch_kernel, (shard,)
    return pl.pallas_call(
        functools.partial(kernel, n, PIECES),
        out_shape=out_shape,
        in_specs=in_vmem(5 + len(extra)),
        out_specs=tuple(in_vmem(len(out_shape))),
        scratch_shapes=scratch,
        compiler_params=pltpu.CompilerParams(
            collective_id=collective_id, has_side_effects=True, vmem_limit_bytes=12 << 20
        ),
        name="forward_exchange",
    )(partial, residual, bias[None, :], gain[None, :], shift[None, :], *extra)


def backward_exchange(partial, grad_out, normal_in, gain, n, collective_id, arrays=(), by_column=()):
    rows, width = partial.shape
    out_shape = (
        jax.ShapeDtypeStruct((rows, width), LOW),
        jax.ShapeDtypeStruct(grad_out.shape, WIDE),
        jax.ShapeDtypeStruct((8, width), WIDE),
    )
    scratch = exchange_scratch(n, rows, width, PIECES)
    kernel, extra = backward_exchange_kernel, ()
    if arrays:
        outs, landings, sems = gradient_shapes(arrays, by_column)
        out_shape = out_shape + outs
        scratch = scratch + landings + sems
        kernel, extra = functools.partial(backward_gradient_kernel, by_column), arrays
    return pl.pallas_call(
        functools.partial(kernel, n, PIECES),
        out_shape=out_shape,
        in_specs=in_vmem(4 + len(extra)),
        out_specs=tuple(in_vmem(3) + [pl.BlockSpec(memory_space=pltpu.HBM)] * len(extra)),
        scratch_shapes=scratch,
        compiler_params=pltpu.CompilerParams(
            collective_id=collective_id, has_side_effects=True, vmem_limit_bytes=20 << 20
        ),
        name="backward_exchange",
    )(partial, grad_out, normal_in, gain[None, :], *extra)


GROUPS = 2
PARTS = 2 * GROUPS


def part_rows(columns, part, base=0):
    size = columns // GROUPS
    return pl.ds(base + (part % 2) * columns + (part // 2) * size, size)


def group_parts(group):
    return (2 * group, 2 * group + 1)


def group_heads(heads, group):
    assert heads % GROUPS == 0
    size = heads // GROUPS
    return range(heads) if group is None else range(group * size, (group + 1) * size)


def attend_kernel(scale, length, qkv, out, out_wide, log_total, held, high, low_sum, sems_send, sems_recv):
    columns = qkv.shape[0] // 3
    frames = qkv.shape[1]
    heads = columns // HD
    me = lax.axis_index("ctx")

    def partner(r):
        return {"ctx": jnp.bitwise_xor(me, r)}

    barrier = pltpu.get_barrier_semaphore()
    for r in (1, 2):
        pl.semaphore_signal(barrier, inc=1, device_id=partner(r), device_id_type=MESH)
    pl.semaphore_wait(barrier, 2)

    def send(slot, part, to):
        rows, own_rows = part_rows(columns, part), part_rows(columns, part, columns)
        src = qkv.at[own_rows] if slot != 3 else held.at[1, rows]
        return pltpu.make_async_remote_copy(
            src_ref=src,
            dst_ref=held.at[slot - 1, rows],
            send_sem=sems_send.at[slot - 1, part],
            recv_sem=sems_recv.at[slot - 1, part],
            device_id=partner(to),
            device_id_type=MESH,
        )

    for part in range(PARTS):
        send(2, part, 2).start()
    for part in range(PARTS):
        send(1, part, 1).start()

    high[...] = jnp.full_like(high, NEGATIVE)
    low_sum[...] = jnp.zeros_like(low_sum)
    out_wide[...] = jnp.zeros_like(out_wide)
    limit = length[0]

    def block(keys_ref, key_row, value_row, slot, group=None):
        owner = jnp.bitwise_xor(me, slot)
        left = limit - owner * frames
        valid = lax.broadcasted_iota(jnp.int32, (frames, frames), 0) < left
        for h in group_heads(heads, group):
            rows = pl.ds(h * HD, HD)
            keys = keys_ref[pl.ds(key_row + h * HD, HD), :]
            values = keys_ref[pl.ds(value_row + h * HD, HD), :]
            scores = lax.dot_general(
                keys, qkv[rows, :], (((0,), (0,)), ((), ())), preferred_element_type=WIDE
            )
            scores = jnp.where(valid, scores * scale, NEGATIVE)
            before = high[h : h + 1, :]
            now = jnp.maximum(before, jnp.max(scores, axis=0, keepdims=True))
            shrink = jnp.exp(before - now)
            raised = jnp.exp(scores - now)
            low_sum[h : h + 1, :] = low_sum[h : h + 1, :] * shrink + jnp.sum(
                raised, axis=0, keepdims=True
            )
            high[h : h + 1, :] = now
            out_wide[rows, :] = out_wide[rows, :] * shrink + jnp.dot(
                values, raised.astype(LOW), preferred_element_type=WIDE
            )

    block(qkv, columns, 2 * columns, 0)
    for part in range(PARTS):
        send(1, part, 1).wait_recv()
    block(held.at[0], 0, columns, 1)
    for group in range(GROUPS):
        for part in group_parts(group):
            send(2, part, 2).wait_recv()
            send(3, part, 1).start()
        block(held.at[1], 0, columns, 2, group)
    for group in range(GROUPS):
        for part in group_parts(group):
            send(3, part, 1).wait_recv()
        block(held.at[2], 0, columns, 3, group)
    for h in range(heads):
        rows = pl.ds(h * HD, HD)
        total = low_sum[h : h + 1, :]
        done = out_wide[rows, :] / total
        out_wide[rows, :] = done
        out[rows, :] = done.astype(LOW)
        log_total[h : h + 1, :] = high[h : h + 1, :] + jnp.log(total)
    for slot in (1, 2, 3):
        for part in range(PARTS):
            send(slot, part, 2 if slot == 2 else 1).wait_send()


def attend(qkv, length, scale, collective_id):
    columns, frames = qkv.shape[0] // 3, qkv.shape[1]
    return pl.pallas_call(
        functools.partial(attend_kernel, scale),
        out_shape=(
            jax.ShapeDtypeStruct((columns, frames), LOW),
            jax.ShapeDtypeStruct((columns, frames), WIDE),
            jax.ShapeDtypeStruct((8, frames), WIDE),
            jax.ShapeDtypeStruct((3, 2 * columns, frames), LOW),
        ),
        in_specs=[pl.BlockSpec(memory_space=pltpu.SMEM)] + in_vmem(1),
        out_specs=tuple(in_vmem(4)),
        scratch_shapes=[
            pltpu.VMEM((8, frames), WIDE),
            pltpu.VMEM((8, frames), WIDE),
            pltpu.SemaphoreType.DMA((3, PARTS)),
            pltpu.SemaphoreType.DMA((3, PARTS)),
        ],
        compiler_params=pltpu.CompilerParams(
            collective_id=collective_id, has_side_effects=True, vmem_limit_bytes=16 << 20
        ),
        name="attend",
    )(length, qkv)


class LineGather:
    def __init__(self, own, gathered, sends, recvs):
        self.own, self.gathered, self.sends, self.recvs = own, gathered, sends, recvs
        self.n = gathered.shape[0] // own.shape[0]
        self.me = lax.axis_index("tp")
        self.further = (self.me < self.n - 1, self.me > 0)
        self.peers = ({"tp": lax.rem(self.me + 1, self.n)}, {"tp": lax.rem(self.me + self.n - 1, self.n)})

    def greet(self, barrier):
        for way in range(2):

            @pl.when(self.further[way])
            def _():
                pl.semaphore_signal(barrier, inc=1, device_id=self.peers[way], device_id_type=MESH)

        return self.further[0].astype(jnp.int32) + self.further[1].astype(jnp.int32)

    def rows(self, shard):
        size = self.own.shape[0]
        return pl.ds(pl.multiple_of(shard * size, size), size)

    def there(self, way, hops):
        return self.me - hops >= 0 if way == 0 else self.me + hops <= self.n - 1

    def send(self, way, hops):
        shard = self.me - hops if way == 0 else self.me + hops
        rows = self.rows(shard)
        return pltpu.make_async_remote_copy(
            src_ref=self.own if hops == 0 else self.gathered.at[rows],
            dst_ref=self.gathered.at[rows],
            send_sem=self.sends.at[way, hops],
            recv_sem=self.recvs.at[way, hops],
            device_id=self.peers[way],
            device_id_type=MESH,
        )

    def arrival(self, way, hops):
        rows = self.rows(self.me - hops if way == 0 else self.me + hops)
        return pltpu.make_async_remote_copy(
            src_ref=self.gathered.at[rows],
            dst_ref=self.gathered.at[rows],
            send_sem=self.sends.at[way, hops],
            recv_sem=self.recvs.at[way, hops - 1],
            device_id=self.peers[way],
            device_id_type=MESH,
        )

    def hop(self, hops):
        for way in range(2):
            if hops > 0:

                @pl.when(self.there(way, hops))
                def _():
                    self.arrival(way, hops).wait_recv()

            if hops < self.n - 1:

                @pl.when(self.there(way, hops) & self.further[way])
                def _():
                    self.send(way, hops).start()

    def drain(self):
        for hops in range(self.n - 1):
            for way in range(2):

                @pl.when(self.there(way, hops) & self.further[way])
                def _():
                    self.send(way, hops).wait_send()


def attend_back_kernel(scale, sharing, length, qkv, held, grad, out_wide, log_total, *refs):
    if sharing:
        own, grad_qkv, gathered, mine, parts, landed, acc, sems_send, sems_recv, sends, recvs = refs
        share = LineGather(own, gathered, sends, recvs)
    else:
        grad_qkv, mine, parts, landed, acc, sems_send, sems_recv = refs
        share = None
    columns = qkv.shape[0] // 3
    frames = qkv.shape[1]
    heads = columns // HD
    me = lax.axis_index("ctx")

    def partner(r):
        return {"ctx": jnp.bitwise_xor(me, r)}

    barrier = pltpu.get_barrier_semaphore()
    for r in (1, 2):
        pl.semaphore_signal(barrier, inc=1, device_id=partner(r), device_id_type=MESH)
    waiting = 2
    if share is not None:
        waiting = waiting + share.greet(barrier)
    pl.semaphore_wait(barrier, waiting)
    if share is not None:
        share.hop(0)
        gathered[share.rows(share.me), :] = own[...]

    def send(at, part, to):
        rows = part_rows(columns, part)
        return pltpu.make_async_remote_copy(
            src_ref=parts.at[at, rows],
            dst_ref=landed.at[at, rows],
            send_sem=sems_send.at[at, part],
            recv_sem=sems_recv.at[at, part],
            device_id=partner(to),
            device_id_type=MESH,
        )

    acc[...] = jnp.zeros_like(acc)
    limit = length[0]

    def block(keys_ref, key_row, value_row, slot, store, group=None):
        owner = jnp.bitwise_xor(me, slot)
        left = limit - owner * frames
        valid = lax.broadcasted_iota(jnp.int32, (frames, frames), 0) < left
        for h in group_heads(heads, group):
            rows = pl.ds(h * HD, HD)
            keys = keys_ref[pl.ds(key_row + h * HD, HD), :]
            values = keys_ref[pl.ds(value_row + h * HD, HD), :]
            queries = qkv[rows, :]
            upstream = grad[rows, :]
            scores = lax.dot_general(
                keys, queries, (((0,), (0,)), ((), ())), preferred_element_type=WIDE
            )
            weights = jnp.where(valid, jnp.exp(scores * scale - log_total[h : h + 1, :]), 0.0)
            grad_weights = lax.dot_general(
                values, upstream, (((0,), (0,)), ((), ())), preferred_element_type=WIDE
            )
            row_terms = jnp.sum(
                upstream.astype(WIDE) * out_wide[rows, :], axis=0, keepdims=True
            )
            grad_scores = (weights * (grad_weights - row_terms)).astype(LOW)
            acc[rows, :] += jnp.dot(keys, grad_scores, preferred_element_type=WIDE)
            grad_keys = (
                lax.dot_general(
                    queries, grad_scores, (((1,), (1,)), ((), ())), preferred_element_type=WIDE
                )
                * scale
            )
            grad_values = lax.dot_general(
                upstream, weights.astype(LOW), (((1,), (1,)), ((), ())), preferred_element_type=WIDE
            )
            store(h * HD, grad_keys, grad_values)

    def store_part(at):
        def store(row, grad_keys, grad_values):
            parts[at, pl.ds(row, HD), :] = grad_keys.astype(LOW)
            parts[at, pl.ds(columns + row, HD), :] = grad_values.astype(LOW)

        return store

    def store_mine(row, grad_keys, grad_values):
        mine[pl.ds(row, HD), :] = grad_keys
        mine[pl.ds(columns + row, HD), :] = grad_values

    def store_joined(row, grad_keys, grad_values):
        for start, value in ((row, grad_keys), (columns + row, grad_values)):
            rows = pl.ds(start, HD)
            parts[1, rows, :] = (value + landed[0, rows, :].astype(WIDE)).astype(LOW)

    for group in range(GROUPS):
        block(held.at[2], 0, columns, 3, store_part(0), group)
        for part in group_parts(group):
            send(0, part, 1).start()
    for group in range(GROUPS):
        for part in group_parts(group):
            send(0, part, 1).wait_recv()
        block(held.at[1], 0, columns, 2, store_joined, group)
        for part in group_parts(group):
            send(1, part, 2).start()
        if share is not None and group == 0:
            share.hop(1)
    for group in range(GROUPS):
        block(held.at[0], 0, columns, 1, store_part(2), group)
        for part in group_parts(group):
            send(2, part, 1).start()
        if share is not None and group == 0:
            share.hop(2)
    block(qkv, columns, 2 * columns, 0, store_mine)
    grad_qkv[0:columns, :] = (acc[...] * scale).astype(LOW)
    for part in range(PARTS):
        send(2, part, 1).wait_recv()
    for part in range(PARTS):
        send(1, part, 2).wait_recv()
    grad_qkv[columns:, :] = (
        mine[...] + landed[1].astype(WIDE) + landed[2].astype(WIDE)
    ).astype(LOW)
    for at in range(3):
        for part in range(PARTS):
            send(at, part, 2 if at == 1 else 1).wait_send()
    if share is not None:
        for hops in range(3, share.n):
            share.hop(hops)
        share.drain()


def attend_back(qkv, held, grad, out_wide, log_total, length, scale, collective_id, own=None):
    columns, frames = qkv.shape[0] // 3, qkv.shape[1]
    out_shape = (jax.ShapeDtypeStruct((3 * columns, frames), LOW),)
    extra, sems = (), []
    if own is not None:
        n = lax.axis_size("tp")
        assert n >= 3
        out_shape += (jax.ShapeDtypeStruct((n * own.shape[0], own.shape[1]), LOW),)
        extra, sems = (own,), [pltpu.SemaphoreType.DMA((2, n))] * 2
    return pl.pallas_call(
        functools.partial(attend_back_kernel, scale, own is not None),
        out_shape=out_shape,
        in_specs=[pl.BlockSpec(memory_space=pltpu.SMEM)] + in_vmem(5 + len(extra)),
        out_specs=tuple(in_vmem(len(out_shape))),
        scratch_shapes=[
            pltpu.VMEM((2 * columns, frames), WIDE),
            pltpu.VMEM((3, 2 * columns, frames), LOW),
            pltpu.VMEM((3, 2 * columns, frames), LOW),
            pltpu.VMEM((columns, frames), WIDE),
            pltpu.SemaphoreType.DMA((3, PARTS)),
            pltpu.SemaphoreType.DMA((3, PARTS)),
            *sems,
        ],
        compiler_params=pltpu.CompilerParams(
            collective_id=collective_id, has_side_effects=True, vmem_limit_bytes=18 << 20
        ),
        name="attend_back",
    )(length, qkv, held, grad, out_wide, log_total, *extra)


def gelu_value(values):
    return 0.5 * values * (1.0 + lax.erf(values * ROOT_HALF))


def gelu_slope(values):
    return 0.5 * (1.0 + lax.erf(values * ROOT_HALF)) + values * DENSITY * jnp.exp(
        -0.5 * values * values
    )


def product(left_side, right_side, left_axis, right_axis):
    return lax.dot_general(
        left_side,
        right_side,
        (((left_axis,), (right_axis,)), ((), ())),
        preferred_element_type=WIDE,
    )


def per_device(
    hidden,
    cotangent,
    lengths,
    query_weight,
    key_weight,
    value_weight,
    output_weight,
    inner_weight,
    outer_weight,
    query_bias,
    value_bias,
    inner_bias,
    output_bias,
    outer_bias,
    first_gain,
    first_shift,
    second_gain,
    second_shift,
):
    clip_count, rows, width = hidden.shape
    assert clip_count == 1
    assert lax.axis_size("ctx") == 4
    tp_size = lax.axis_size("tp")
    own_rows = rows // tp_size
    columns = query_weight.shape[2]
    hidden_local = inner_weight.shape[2]
    scale = 1.0 / math.sqrt(HD)
    own_start = lax.axis_index("tp") * own_rows

    def own_slice(full):
        return lax.dynamic_slice_in_dim(full, own_start, own_rows, axis=0)

    hidden_rows = hidden.reshape(rows, width)
    smalls = (output_bias, outer_bias, first_gain, first_shift, second_gain, second_shift)
    qkv_weights = [jnp.swapaxes(weight, 1, 2) for weight in (query_weight, key_weight, value_weight)]

    def qkv_shard(layer):
        return jnp.concatenate([weight[layer] for weight in qkv_weights], axis=0).astype(LOW)

    def gather(array, axis):
        return lax.all_gather(array, "fsdp", axis=axis, tiled=True)

    projections = output_weight.astype(LOW).reshape(-1, output_weight.shape[2])
    paired = lax.axis_size("fsdp") == 2
    if paired:
        wides = (inner_weight, outer_weight, *qkv_weights)
        jobs = [(which, layer, which * LAYERS + layer, 0) for layer in range(LAYERS) for which in range(2)]
        shapes = [wide.shape[1:] for wide in wides[:2] for _ in range(LAYERS)]
        for layer in range(1, LAYERS):
            jobs += [(2 + at, layer, len(shapes), at * columns) for at in range(3)]
            shapes.append((3 * columns, qkv_weights[0].shape[2]))
        wides += (cotangent,)
        jobs.append((len(wides) - 1, 0, len(shapes), 0))
        shapes.append(cotangent.shape[1:])
        results = fetch_first((qkv_shard(0), projections), smalls, wides, hidden_rows, tuple(jobs), shapes, 17)
        qkv_first, projections, *results, normed = results
        smalls, lows = results[: len(smalls)], results[len(smalls) :]
        *lows, grad_low = lows
        inner_low, outer_low, qkv_low = lows[:LAYERS], lows[LAYERS : 2 * LAYERS], [None, *lows[2 * LAYERS :]]
    else:
        qkv_first, projections = gather(qkv_shard(0), 1), gather(projections, 1)
        smalls = [gather(small, 1) for small in smalls]
        inner_low, outer_low = inner_weight.astype(LOW), outer_weight.astype(LOW)
        qkv_low = [qkv_shard(layer) for layer in range(LAYERS)]
        grad_low = cotangent.reshape(rows, width).astype(LOW)
        smalls = [lax.reduce_precision(small, 8, 7) for small in smalls]
        hat_full, _ = norm_parts(hidden_rows)
        normed = (hat_full * smalls[FIRST_GAIN][0] + smalls[FIRST_SHIFT][0]).astype(LOW)
    projections = projections.reshape(LAYERS, columns, width)

    def vector(kind, layer):
        return smalls[kind][layer]

    w_qkvs = [qkv_first] + [gather(qkv_low[layer], 1) for layer in range(1, LAYERS)]
    w_inners = [gather(inner_low[layer], 0) for layer in range(LAYERS)]
    carried = paired and tp_size == 4
    w_outers = [None if carried and layer == 0 else gather(outer_low[layer], 1) for layer in range(LAYERS)]

    residual = own_slice(hidden_rows)
    kept = []
    for layer in range(LAYERS):
        w_qkv, w_out, w_inner = w_qkvs[layer], projections[layer], w_inners[layer]
        bias_qkv = jnp.concatenate(
            [query_bias[layer], jnp.zeros_like(query_bias[layer]), value_bias[layer]]
        )
        qkv = (product(w_qkv, normed, 1, 1) + bias_qkv[:, None]).astype(LOW)
        attended, attended_wide, log_total, held = attend(qkv, lengths, scale, 2 * layer)
        branch = product(attended, w_out, 0, 0).astype(LOW)
        normed_two, middle, *fetched = forward_exchange(
            branch,
            residual,
            vector(0, layer),
            vector(4, layer),
            vector(5, layer),
            tp_size,
            2 * layer + 4,
            outer_low[layer] if carried and layer == 0 else None,
        )
        if fetched:
            w_outers[layer] = fetched[0]
        inner_pre = product(normed_two, w_inner, 1, 0) + inner_bias[layer]
        active, slope = gelu_value(inner_pre).astype(LOW), gelu_slope(inner_pre)
        kept.append(
            (residual, normed, qkv, attended, attended_wide, log_total, held, middle, normed_two, slope, active)
        )
        branch = product(active, w_outers[layer], 1, 0).astype(LOW)
        if layer + 1 < LAYERS:
            normed, residual = forward_exchange(
                branch,
                middle,
                vector(1, layer),
                vector(2, layer + 1),
                vector(3, layer + 1),
                tp_size,
                2 * layer + 5,
            )
        else:
            last_branch, last_middle = branch, middle

    def exchange_back(branch, grad_out, normal_in, gain, collective_id, arrays, by_column):
        if lax.axis_size("fsdp") == 2:
            return backward_exchange(
                branch, grad_out, normal_in, gain, tp_size, collective_id, arrays, by_column
            )
        result = backward_exchange(branch, grad_out, normal_in, gain, tp_size, collective_id)
        for array, column in zip(arrays, by_column):
            axis = 1 if column else 0
            array = lax.psum_scatter(array, ("fsdp", "ctx"), scatter_dimension=axis, tiled=True)
            result += (lax.all_gather(array, "ctx", axis=axis, tiled=True),)
        return result

    grad_rows = cotangent.reshape(rows, width)
    grad_own = own_slice(grad_rows)
    outer_bias_sum = jnp.sum(grad_own, axis=0)
    grads = [None] * LAYERS
    vectors = [None] * LAYERS
    biases = [None] * LAYERS
    for layer in reversed(range(LAYERS)):
        w_qkv, w_out, w_inner, w_outer = w_qkvs[layer], projections[layer], w_inners[layer], w_outers[layer]
        (
            residual,
            normed,
            qkv,
            attended,
            attended_wide,
            log_total,
            held,
            middle,
            normed_two,
            slope,
            active,
        ) = kept[layer]
        grad_active = product(grad_low, w_outer, 1, 1)
        grad_inner = (grad_active * slope).astype(LOW)
        branch = product(grad_inner, w_inner, 1, 1).astype(LOW)
        grad_outer_w = product(active, grad_low, 0, 0).astype(LOW)
        grad_inner_w = product(normed_two, grad_inner, 0, 0).astype(LOW)
        grad_mid_low, grad_middle, sums_two, *summed_two = exchange_back(
            branch, grad_own, middle, vector(4, layer), 2 * layer + 8, (grad_inner_w, grad_outer_w), (False, True)
        )
        if layer == LAYERS - 1:
            last_branch, grad_mid_low = lax.optimization_barrier((last_branch, grad_mid_low))
            last_branch = lax.psum_scatter(last_branch, "tp", scatter_dimension=0, tiled=True)
        grad_attended = product(w_out, grad_mid_low, 1, 1).astype(LOW)
        grad_qkv, *shared = attend_back(
            qkv,
            held,
            grad_attended,
            attended_wide,
            log_total,
            lengths,
            scale,
            2 * layer + 12,
            last_rows if layer == 0 else None,
        )
        grad_output_w = product(attended, grad_mid_low, 1, 0).astype(LOW)
        branch = product(grad_qkv, w_qkv, 0, 0).astype(LOW)
        grad_qkv_w = product(grad_qkv, normed, 1, 0).astype(LOW)
        if layer == LAYERS - 1:
            last_branch, branch = lax.optimization_barrier((last_branch, branch))
            last_rows = (last_middle + last_branch.astype(WIDE) + vector(1, layer)).astype(LOW)
        if layer == 0:
            output = shared[0].astype(WIDE)
        grad_low, grad_own, sums_one, *summed_one = exchange_back(
            branch, grad_middle, residual, vector(2, layer), 2 * layer + 9, (grad_qkv_w, grad_output_w), (True, True)
        )
        grads[layer] = (*summed_one, *summed_two)
        vectors[layer] = [
            sums_two[2], outer_bias_sum, sums_one[0], sums_one[1], sums_two[0], sums_two[1]
        ]
        outer_bias_sum = sums_one[2]
        biases[layer] = jnp.concatenate(
            [
                jnp.sum(grad_qkv.astype(WIDE), axis=1),
                jnp.sum(grad_inner.astype(WIDE), axis=0),
            ]
        )
    grad_hidden = grad_low.astype(WIDE)

    shard = output_bias.shape[1]
    flat_biases = jnp.concatenate(biases)
    flat_biases = jnp.pad(flat_biases, (0, -flat_biases.size % (8 * shard))).reshape(-1, shard)
    vector_count = 6 * LAYERS
    small_sums = jnp.stack([row for parts in zip(*vectors) for row in parts])
    if lax.axis_size("fsdp") == 2:
        small_sums = jnp.pad(small_sums, ((0, -vector_count % 8), (0, 0)))
        shared_rows = small_sums.shape[0]
        small_sums = sum_all(
            small_sums, flat_biases, tuple((axis, lax.axis_size(axis)) for axis in ("ctx", "tp")), 16
        )
        vector_sums, bias_sums = small_sums[:vector_count], small_sums[shared_rows:]
    else:
        vector_sums = lax.psum(small_sums, ("fsdp", "ctx", "tp"))
        vector_sums = lax.dynamic_slice_in_dim(vector_sums, lax.axis_index("fsdp") * shard, shard, axis=1)
        bias_sums = lax.psum(flat_biases, ("fsdp", "ctx"))
    vector_sums = vector_sums.reshape(6, LAYERS, shard)
    bias_sums = bias_sums.reshape(-1)[: LAYERS * biases[0].size].reshape(LAYERS, -1)

    def stacked(which):
        return jnp.stack([grads[layer][which] for layer in range(LAYERS)]).astype(WIDE)

    def turned(start):
        return jnp.stack([grads[layer][0][start : start + columns].T for layer in range(LAYERS)]).astype(WIDE)

    return (
        output.reshape(hidden.shape),
        grad_hidden.reshape(hidden.shape),
        turned(0),
        turned(columns),
        turned(2 * columns),
        stacked(1),
        stacked(2),
        stacked(3),
        bias_sums[:, :columns],
        bias_sums[:, 2 * columns : 3 * columns],
        bias_sums[:, 3 * columns :],
        vector_sums[0],
        vector_sums[1],
        vector_sums[2],
        vector_sums[3],
        vector_sums[4],
        vector_sums[5],
    )


def solution(mesh):
    in_specs = (
        P("fsdp", "ctx", None),
        P("fsdp", "ctx", None),
        P("fsdp"),
        P(None, "fsdp", "tp"),
        P(None, "fsdp", "tp"),
        P(None, "fsdp", "tp"),
        P(None, "tp", "fsdp"),
        P(None, "fsdp", "tp"),
        P(None, "tp", "fsdp"),
        P(None, "tp"),
        P(None, "tp"),
        P(None, "tp"),
        P(None, "fsdp"),
        P(None, "fsdp"),
        P(None, "fsdp"),
        P(None, "fsdp"),
        P(None, "fsdp"),
        P(None, "fsdp"),
    )
    out_specs = (
        P("fsdp", "ctx", None),
        P("fsdp", "ctx", None),
        P(None, "fsdp", "tp"),
        P(None, "fsdp", "tp"),
        P(None, "fsdp", "tp"),
        P(None, "tp", "fsdp"),
        P(None, "fsdp", "tp"),
        P(None, "tp", "fsdp"),
        P(None, "tp"),
        P(None, "tp"),
        P(None, "tp"),
        P(None, "fsdp"),
        P(None, "fsdp"),
        P(None, "fsdp"),
        P(None, "fsdp"),
        P(None, "fsdp"),
        P(None, "fsdp"),
    )
    return jax.shard_map(
        per_device, mesh=mesh, in_specs=in_specs, out_specs=out_specs, check_vma=False
    )
```

```python
import functools
import math
import jax
import jax.numpy as jnp
from jax import lax
from jax.experimental import pallas as pl
from jax.experimental.pallas import tpu as pltpu
from jax.sharding import PartitionSpec as P

MESH = pl.DeviceIdType.MESH
LOW = jnp.bfloat16
WIDE = jnp.float32
EPSILON = 1e-05
NEGATIVE = -1e30
HD = 80
PIECES = 4
LAYERS = 2
ROOT_HALF = 1.0 / math.sqrt(2.0)
DENSITY = 1.0 / math.sqrt(2.0 * math.pi)
REDUCE_LAG = 2
GATHER_LAG = 3


def norm_parts(values):
    average = jnp.mean(values, axis=-1, keepdims=True)
    centered = values - average
    spread = jnp.mean(centered * centered, axis=-1, keepdims=True)
    inverse = lax.rsqrt(spread + EPSILON)
    return (centered * inverse, inverse)


def norm_back(upstream, normal_hat, inverse, gain_full):
    scaled = upstream * gain_full
    first_mean = jnp.mean(scaled, axis=-1, keepdims=True)
    second_mean = jnp.mean(scaled * normal_hat, axis=-1, keepdims=True)
    return inverse * (scaled - first_mean - normal_hat * second_mean)


def line_exchange(n, own, pieces, partial, gathered, from_left, from_right, total, sems, finish, side=None):
    rs_send, rs_recv, ag_send, ag_recv = sems
    me = lax.axis_index("tp")
    piece = own // pieces
    to_right, to_left = {"tp": lax.rem(me + 1, n)}, {"tp": lax.rem(me + n - 1, n)}
    has_left, has_right = me > 0, me < n - 1

    barrier = pltpu.get_barrier_semaphore()

    @pl.when(has_left)
    def _():
        pl.semaphore_signal(barrier, inc=1, device_id=to_left, device_id_type=MESH)

    @pl.when(has_right)
    def _():
        pl.semaphore_signal(barrier, inc=1, device_id=to_right, device_id_type=MESH)

    peers = has_left.astype(jnp.int32) + has_right.astype(jnp.int32)
    if side is not None:
        for peer in side.peers:
            pl.semaphore_signal(barrier, inc=1, device_id=peer, device_id_type=MESH)
        peers = peers + len(side.peers)
    pl.semaphore_wait(barrier, peers)
    if side is not None:
        side.start()

    def rows_of(shard, step):
        return pl.ds(pl.multiple_of(shard * own + step * piece, piece), piece)

    def reduce_copy(way, src, shard, step):
        rows = rows_of(shard, step)
        landing = from_left if way == 0 else from_right
        return pltpu.make_async_remote_copy(
            src_ref=src.at[rows],
            dst_ref=landing.at[rows],
            send_sem=rs_send.at[way, shard, step],
            recv_sem=rs_recv.at[way, shard, step],
            device_id=to_right if way == 0 else to_left,
            device_id_type=MESH,
        )

    def gather_copy(way, shard, step):
        rows = rows_of(shard, step)
        return pltpu.make_async_remote_copy(
            src_ref=gathered.at[rows],
            dst_ref=gathered.at[rows],
            send_sem=ag_send.at[way, shard, step],
            recv_sem=ag_recv.at[way, shard, step],
            device_id=to_right if way == 0 else to_left,
            device_id_type=MESH,
        )

    def reduce_one(way, shard, step):
        landing = from_left if way == 0 else from_right
        first = me == 0 if way == 0 else me == n - 1

        @pl.when(first)
        def _():
            reduce_copy(way, partial, shard, step).start()

        @pl.when(jnp.logical_not(first))
        def _():
            rows = rows_of(shard, step)
            reduce_copy(way, partial, shard, step).wait_recv()
            landing[rows, :] = (
                partial[rows, :].astype(WIDE) + landing[rows, :].astype(WIDE)
            ).astype(LOW)
            reduce_copy(way, landing, shard, step).start()

    def finish_one(step):
        rows = rows_of(me, step)
        total[...] = partial[rows, :].astype(WIDE)

        @pl.when(has_left)
        def _():
            reduce_copy(0, partial, me, step).wait_recv()
            total[...] += from_left[rows, :].astype(WIDE)

        @pl.when(has_right)
        def _():
            reduce_copy(1, partial, me, step).wait_recv()
            total[...] += from_right[rows, :].astype(WIDE)

        own_rows = pl.ds(pl.multiple_of(step * piece, piece), piece)
        gathered[rows, :] = finish(own_rows, total[...])

        @pl.when(has_right)
        def _():
            gather_copy(0, me, step).start()

        @pl.when(has_left)
        def _():
            gather_copy(1, me, step).start()

    def forward_one(way, shard, step):
        gather_copy(way, shard, step).wait_recv()

        @pl.when(has_right if way == 0 else has_left)
        def _():
            gather_copy(way, shard, step).start()

    period = n - 1

    def finish_at(device):
        from_start = jnp.where(device > 0, n - 1 - device + REDUCE_LAG * device, 0)
        from_end = jnp.where(device < n - 1, device + REDUCE_LAG * (n - 1 - device), 0)
        return jnp.maximum(from_start, from_end)

    def split(tick, start, length):
        since = tick - start
        clipped = jnp.maximum(since, 0)
        return (since >= 0) & (clipped < length), lax.div(clipped, period), lax.rem(clipped, period)

    def body(tick, carry):
        for way in range(2):
            hops = me if way == 0 else n - 1 - me
            due, step, k = split(tick, REDUCE_LAG * hops, pieces * period)
            shard = n - 1 - k if way == 0 else k
            mine = me < shard if way == 0 else me > shard

            @pl.when(due & mine)
            def _():
                reduce_one(way, shard, step)

        due, step, k = split(tick, finish_at(me), pieces * period)

        @pl.when(due & (k == 0))
        def _():
            finish_one(step)

        for hops in range(1, n):
            for way in range(2):
                shard = me - hops if way == 0 else me + hops
                there = shard >= 0 if way == 0 else shard <= n - 1
                due, step, k = split(
                    tick, finish_at(shard) + GATHER_LAG * hops, pieces * period
                )

                @pl.when(there & due & (k == 0))
                def _():
                    forward_one(way, shard, step)

        if side is not None:
            side.at(tick)
        return carry

    ticks = period * (pieces - 1) + max(REDUCE_LAG, 1) * (n - 1) + GATHER_LAG * (n - 1) + 1
    if side is not None:
        ticks = max(ticks, side.ticks)
    lax.fori_loop(0, ticks, body, 0)
    if side is not None:
        side.drain()

    def drain(step, carry):
        for k in range(n - 1):
            for way in range(2):
                shard = n - 1 - k if way == 0 else k
                sends = me < shard if way == 0 else me > shard

                @pl.when(sends)
                def _():
                    reduce_copy(way, partial, shard, step).wait_send()

        for k in range(n):
            for way in range(2):
                shard = me - k if way == 0 else me + k
                there = shard >= 0 if way == 0 else shard <= n - 1
                further = has_right if way == 0 else has_left

                @pl.when(there & further)
                def _():
                    gather_copy(way, shard, step).wait_send()

        return carry

    lax.fori_loop(0, pieces, drain, 0)


def exchange_scratch(n, rows, width, pieces):
    return [
        pltpu.VMEM((rows, width), LOW),
        pltpu.VMEM((rows, width), LOW),
        pltpu.VMEM((rows // n // pieces, width), WIDE),
        pltpu.SemaphoreType.DMA((2, n, pieces)),
        pltpu.SemaphoreType.DMA((2, n, pieces)),
        pltpu.SemaphoreType.DMA((2, n, pieces)),
        pltpu.SemaphoreType.DMA((2, n, pieces)),
    ]


def forward_fetch_kernel(
    n, pieces, partial, residual, bias, gain, shift, shard, gathered, middle, fetched, from_left, from_right, total,
    rs_send, rs_recv, ag_send, ag_recv, sends, recvs
):
    forward_exchange_kernel(
        n, pieces, partial, residual, bias, gain, shift, gathered, middle, from_left, from_right, total, rs_send, rs_recv,
        ag_send, ag_recv, side=QuartersSide((shard,), (fetched,), sends, recvs)
    )


def forward_exchange_kernel(
    n, pieces, partial, residual, bias, gain, shift, gathered, middle, from_left, from_right, total, *sems, side=None
):
    def finish(rows, value):
        mid = value + residual[rows, :] + bias[...]
        middle[rows, :] = mid
        hat, _ = norm_parts(mid)
        return (hat * gain[...] + shift[...]).astype(LOW)

    line_exchange(
        n, residual.shape[0], pieces, partial, gathered, from_left, from_right, total, sems, finish, side
    )


def backward_exchange_kernel(
    n, pieces, partial, grad_out, normal_in, gain, gathered, grad_in, sums, from_left, from_right, total, *sems, side=None
):
    sums[...] = jnp.zeros_like(sums)

    def finish(rows, upstream):
        hat, inverse = norm_parts(normal_in[rows, :])
        grad = grad_out[rows, :] + norm_back(upstream, hat, inverse, gain[...])
        grad_in[rows, :] = grad
        sums[0:1, :] += jnp.sum(upstream * hat, axis=0, keepdims=True)
        sums[1:2, :] += jnp.sum(upstream, axis=0, keepdims=True)
        sums[2:3, :] += jnp.sum(grad, axis=0, keepdims=True)
        return grad.astype(LOW)

    line_exchange(
        n, grad_out.shape[0], pieces, partial, gathered, from_left, from_right, total, sems, finish, side
    )


def in_vmem(count):
    return [pl.BlockSpec(memory_space=pltpu.VMEM)] * count


class GradientSum:
    LAGS = (0, 3, 6, 9)

    def __init__(self, by_column, arrays, outs, landings, sems):
        self.by_column = by_column
        self.chunks = landings[0].shape[1]
        self.arrays, self.outs, self.landings = arrays, outs, landings
        self.sends, self.recvs, self.stores = sems
        self.half = lax.axis_index("fsdp")
        self.ctx = lax.axis_index("ctx")
        self.core = lax.rem(self.ctx, 2)
        pair = {"ctx": jnp.bitwise_xor(self.ctx, 1)}
        across = {"ctx": jnp.bitwise_xor(self.ctx, 2)}
        other = {"fsdp": 1 - self.half}
        self.peers = (pair, across, other)
        self.ticks = 2 * (self.chunks - 1) + self.LAGS[3] + 1

    def view(self, which, half, core, chunk):
        rows, cols = self.arrays[which].shape
        if not self.by_column[which]:
            part = rows // 4
            height = part // self.chunks
            start = half * (2 * part) + core * part + chunk * height
            return pl.ds(pl.multiple_of(start, 16), height), slice(None)
        part = rows // 2
        height = part // self.chunks
        start = core * part + chunk * height
        width = cols // 2
        return (
            pl.ds(pl.multiple_of(start, 16), height),
            pl.ds(pl.multiple_of(half * width, 128), width),
        )

    def out_rows(self, which, core, chunk):
        part = self.outs[which].shape[0] // 2
        height = part // self.chunks
        return pl.ds(pl.multiple_of(core * part + chunk * height, 16), height)

    def store(self, which, whose, chunk):
        core = self.core if whose == 0 else 1 - self.core
        return pltpu.make_async_copy(
            self.landings[which].at[3 + whose, chunk],
            self.outs[which].at[self.out_rows(which, core, chunk)],
            self.stores.at[which, whose, chunk],
        )

    def copy(self, which, stage, chunk, half=0):
        pair, across, other = self.peers
        landing = self.landings[which]
        if stage == 0:
            src = self.arrays[which].at[self.view(which, half, 1 - self.core, chunk)]
            slot, peer = half, pair
        elif stage == 1:
            src = landing.at[1 - self.half, chunk]
            slot, peer = 2, other
        elif stage == 2:
            src = landing.at[2, chunk]
            slot, peer = 3, across
        else:
            src = landing.at[3, chunk]
            slot, peer = 4, pair
        return pltpu.make_async_remote_copy(
            src_ref=src,
            dst_ref=landing.at[slot, chunk],
            send_sem=self.sends.at[which, slot, chunk],
            recv_sem=self.recvs.at[which, slot, chunk],
            device_id=peer,
            device_id_type=MESH,
        )

    def start(self):
        def body(chunk, carry):
            for which in range(len(self.arrays)):
                for half in range(2):
                    self.copy(which, 0, chunk, half).start()
            return carry

        lax.fori_loop(0, self.chunks, body, 0)

    def when_due(self, tick, lag, action):
        since = tick - lag
        clipped = jnp.maximum(since, 0)
        chunk = lax.div(clipped, 2)

        @pl.when((since >= 0) & (lax.rem(clipped, 2) == 0) & (chunk < self.chunks))
        def _():
            for which in range(len(self.arrays)):
                action(which, chunk)

    def at(self, tick):
        def joined(which, chunk):
            landing = self.landings[which]
            for half in range(2):
                self.copy(which, 0, chunk, half).wait_recv()
                rows, cols = self.view(which, half, self.core, chunk)
                landing[half, chunk] = (
                    self.arrays[which][rows, cols].astype(WIDE) + landing[half, chunk].astype(WIDE)
                ).astype(LOW)
            self.copy(which, 1, chunk).start()

        def crossed(which, chunk):
            landing = self.landings[which]
            self.copy(which, 1, chunk).wait_recv()
            landing[2, chunk] = (
                landing[self.half, chunk].astype(WIDE) + landing[2, chunk].astype(WIDE)
            ).astype(LOW)
            self.copy(which, 2, chunk).start()

        def summed(which, chunk):
            landing = self.landings[which]
            self.copy(which, 2, chunk).wait_recv()
            low = (landing[2, chunk].astype(WIDE) + landing[3, chunk].astype(WIDE)).astype(LOW)
            landing[3, chunk] = low
            self.copy(which, 3, chunk).start()
            self.store(which, 0, chunk).start()

        def shared(which, chunk):
            self.copy(which, 3, chunk).wait_recv()
            self.store(which, 1, chunk).start()

        for lag, action in zip(self.LAGS, (joined, crossed, summed, shared)):
            self.when_due(tick, lag, action)

    def drain(self):
        def body(chunk, carry):
            for which in range(len(self.arrays)):
                for half in range(2):
                    self.copy(which, 0, chunk, half).wait_send()
                for stage in range(1, 4):
                    self.copy(which, stage, chunk).wait_send()
                for whose in range(2):
                    self.store(which, whose, chunk).wait()
            return carry

        lax.fori_loop(0, self.chunks, body, 0)


def gradient_shapes(arrays, by_column):
    chunks = 5 if all(by_column) else 10
    outs, landings = (), []
    for array, column in zip(arrays, by_column):
        rows, cols = array.shape
        rows, cols = (rows, cols // 2) if column else (rows // 2, cols)
        outs += (pltpu.HBM((rows, cols), LOW),)
        landings.append(pltpu.VMEM((5, chunks, rows // 2 // chunks, cols), LOW))
    sems = [pltpu.SemaphoreType.DMA((len(arrays), 5, chunks))] * 2
    return outs, landings, sems + [pltpu.SemaphoreType.DMA((len(arrays), 2, chunks))]


def backward_gradient_kernel(by_column, n, pieces, partial, grad_out, normal_in, gain, *refs):
    count = len(by_column)
    arrays, (gathered, grad_in, sums), refs = refs[:count], refs[count : count + 3], refs[count + 3 :]
    outs, (from_left, from_right, total, *sems), refs = refs[:count], refs[count : count + 7], refs[count + 7 :]
    side = GradientSum(by_column, arrays, outs, refs[:count], refs[count:])
    backward_exchange_kernel(
        n, pieces, partial, grad_out, normal_in, gain, gathered, grad_in, sums, from_left, from_right, total, *sems, side=side
    )


def sum_all_kernel(axes, vectors, biases, out, staged, landing, sends, recvs):
    half = lax.axis_index("fsdp")
    shared, width = vectors.shape[0], out.shape[1]
    steps = [("fsdp", 1)] + [(axis, 1 << b) for axis, size in axes for b in range(size.bit_length() - 1)]

    def peer(axis, k):
        return {axis: jnp.bitwise_xor(lax.axis_index(axis), k)}

    barrier = pltpu.get_barrier_semaphore()
    for axis, k in steps:
        pl.semaphore_signal(barrier, inc=1, device_id=peer(axis, k), device_id_type=MESH)
    for side in range(2):
        staged[side, 0:shared, :] = vectors[:, side * width : (side + 1) * width]
        staged[side, shared:, :] = biases[...]
    pl.semaphore_wait(barrier, len(steps))
    for at, (axis, k) in enumerate(steps):
        rows = pl.ds(0, shared) if axis == "tp" else pl.ds(0, out.shape[0])
        if at > 0:
            landing[at, 0, rows] = out[rows, :]
        copy = pltpu.make_async_remote_copy(
            src_ref=landing.at[at, 0, rows] if at > 0 else staged.at[1 - half],
            dst_ref=landing.at[at, 1, rows],
            send_sem=sends.at[at],
            recv_sem=recvs.at[at],
            device_id=peer(axis, k),
            device_id_type=MESH,
        )
        copy.start()
        copy.wait()
        own = landing[at, 0, rows] if at > 0 else staged[half]
        out[rows, :] = own + landing[at, 1, rows]


def sum_all(vectors, biases, axes, collective_id):
    shape = (vectors.shape[0] + biases.shape[0], biases.shape[1])
    steps = 1 + sum(size.bit_length() - 1 for _, size in axes)
    return pl.pallas_call(
        functools.partial(sum_all_kernel, axes),
        out_shape=jax.ShapeDtypeStruct(shape, WIDE),
        in_specs=in_vmem(2),
        out_specs=in_vmem(1)[0],
        scratch_shapes=[
            pltpu.VMEM((2,) + shape, WIDE),
            pltpu.VMEM((steps, 2) + shape, WIDE),
            pltpu.SemaphoreType.DMA((steps,)),
            pltpu.SemaphoreType.DMA((steps,)),
        ],
        compiler_params=pltpu.CompilerParams(
            collective_id=collective_id, has_side_effects=True, vmem_limit_bytes=8 << 20
        ),
        name="sum_all",
    )(vectors, biases)


def fetch_parts(rows):
    return next(parts for parts in (2, 3, 1) if rows // 4 % (16 * parts) == 0)


CAST_ROWS = 64
FIRST_GAIN, FIRST_SHIFT = 2, 3


class Quarters:
    def __init__(self, shards, outs, sends, recvs):
        self.shards, self.outs, self.sends, self.recvs = shards, outs, sends, recvs
        self.half = lax.axis_index("fsdp")
        self.ctx = lax.axis_index("ctx")
        self.pair, self.across = jnp.bitwise_xor(self.ctx, 1), jnp.bitwise_xor(self.ctx, 2)
        self.targets = ({"fsdp": 1 - self.half}, {"ctx": self.across}, {"ctx": self.pair}, {"ctx": self.pair})
        self.peers = self.targets[:3]
        self.each = [
            (which, part) for which in range(len(shards)) for part in range(fetch_parts(shards[which].shape[0]))
        ]

    def rows_of(self, which, quarter, part):
        parts = fetch_parts(self.shards[which].shape[0])
        height = self.shards[which].shape[0] // 4 // parts
        return pl.ds(pl.multiple_of((quarter * parts + part) * height, 16), height)

    def place(self, which, side, quarter, part):
        cols = self.shards[which].shape[1]
        return self.outs[which].at[
            self.rows_of(which, quarter, part), pl.ds(pl.multiple_of(side * cols, 128), cols)
        ]

    def copy(self, stage, item, arriving=False):
        which, part = item
        quarter = (self.ctx, self.ctx, self.ctx, self.across)[stage]
        src = self.shards[which].at[self.rows_of(which, quarter, part)]
        dst = self.place(which, self.half, quarter, part)
        if stage > 0:
            src = dst = self.place(which, 1 - self.half, quarter, part)
        if arriving:
            quarter = (self.ctx, self.across, self.pair, jnp.bitwise_xor(self.ctx, 3))[stage]
            dst = self.place(which, 1 - self.half, quarter, part)
        return pltpu.make_async_remote_copy(
            src_ref=src,
            dst_ref=dst,
            send_sem=self.sends.at[which, stage, part],
            recv_sem=self.recvs.at[which, stage, part],
            device_id=self.targets[stage],
            device_id_type=MESH,
        )

    def begin(self):
        for item in self.each:
            self.copy(0, item).start()

    def keep_own(self):
        for shard, out in zip(self.shards, self.outs):
            cols = shard.shape[1]
            out[:, pl.ds(pl.multiple_of(self.half * cols, 128), cols)] = shard[...]

    def crossed(self, item):
        self.copy(0, item, True).wait_recv()
        self.copy(1, item).start()
        self.copy(2, item).start()

    def forwarded(self, item):
        self.copy(1, item, True).wait_recv()
        self.copy(3, item).start()

    def finish(self):
        for stage in (2, 3):
            for item in self.each:
                self.copy(stage, item, True).wait_recv()
        for stage in range(4):
            for item in self.each:
                self.copy(stage, item).wait_send()


class QuartersSide(Quarters):
    CROSSED, APART, FORWARDED = 6, 5, 4

    def start(self):
        self.begin()
        self.keep_own()

    @property
    def ticks(self):
        return self.CROSSED + self.FORWARDED + self.APART * (len(self.each) - 1) + 1

    def at(self, tick):
        for at, item in enumerate(self.each):
            due = self.CROSSED + self.APART * at

            @pl.when(tick == due)
            def _():
                self.crossed(item)

            @pl.when(tick == due + self.FORWARDED)
            def _():
                self.forwarded(item)

    def drain(self):
        self.finish()


def fetch_kernel(counts, jobs, *refs):
    refs = list(refs)

    def take(count):
        taken = refs[:count]
        del refs[:count]
        return taken

    shard_count, small_count, wide_count, low_count = counts
    shards, smalls, wides, (frames,) = take(shard_count), take(small_count), take(wide_count), take(1)
    outs, out_smalls, lows, (normed,) = take(shard_count), take(small_count), take(low_count), take(1)
    buffers, (frame_buffer,), stages = take(len(jobs)), take(1), take(low_count)
    store_sems, cast_sems, sends, recvs, small_sends, small_recvs = refs
    quarters = Quarters(shards, outs, sends, recvs)

    barrier = pltpu.get_barrier_semaphore()
    for peer in quarters.peers:
        pl.semaphore_signal(barrier, inc=1, device_id=peer, device_id_type=MESH)
    pl.semaphore_wait(barrier, 3)

    def small_copy(at, side):
        cols = smalls[at].shape[1]
        return pltpu.make_async_remote_copy(
            src_ref=smalls[at],
            dst_ref=out_smalls[at].at[:, pl.ds(pl.multiple_of(side * cols, 128), cols)],
            send_sem=small_sends.at[at],
            recv_sem=small_recvs.at[at],
            device_id=quarters.peers[0],
            device_id_type=MESH,
        )

    def store(low):
        return pltpu.make_async_copy(stages[low], lows[low], store_sems.at[low])

    def load(at):
        which, layer, _, _ = jobs[at]
        return pltpu.make_async_copy(wides[which].at[layer], buffers[at], cast_sems.at[at])

    frame_load = pltpu.make_async_copy(frames, frame_buffer, cast_sems.at[len(jobs)])

    def norm(step, carry):
        rows = pl.ds(pl.multiple_of(step * CAST_ROWS, CAST_ROWS), CAST_ROWS)
        hat, _ = norm_parts(frame_buffer[rows, :])
        normed[rows, :] = (hat * out_smalls[FIRST_GAIN][0:1, :] + out_smalls[FIRST_SHIFT][0:1, :]).astype(LOW)
        return carry

    for at in range(small_count):
        small_copy(at, quarters.half).start()
    quarters.begin()
    for at in range(len(jobs)):
        load(at).start()
    frame_load.start()
    quarters.keep_own()
    for small, out in zip(smalls, out_smalls):
        cols = small.shape[1]
        out[:, pl.ds(pl.multiple_of(quarters.half * cols, 128), cols)] = small[...]
    for at, (_, _, low, first) in enumerate(jobs):
        load(at).wait()

        def cast(step, carry):
            start = pl.multiple_of(step * CAST_ROWS, CAST_ROWS)
            stages[low][pl.ds(first + start, CAST_ROWS), :] = buffers[at][pl.ds(start, CAST_ROWS), :].astype(LOW)
            return carry

        lax.fori_loop(0, buffers[at].shape[0] // CAST_ROWS, cast, 0)
        if first + buffers[at].shape[0] == lows[low].shape[0]:
            store(low).start()
    for at in range(small_count):
        small_copy(at, 1 - quarters.half).wait_recv()
        out_smalls[at][...] = out_smalls[at][...].astype(LOW).astype(WIDE)
    last = len(quarters.each)
    for at in range(last + 1):
        if at < last:
            quarters.crossed(quarters.each[at])
        if at > 0:
            quarters.forwarded(quarters.each[at - 1])
        if at == fetch_parts(shards[0].shape[0]):
            frame_load.wait()
            lax.fori_loop(0, normed.shape[0] // CAST_ROWS, norm, 0)
    quarters.finish()
    for at in range(small_count):
        small_copy(at, quarters.half).wait_send()
    for low in range(low_count):
        store(low).wait()


def quarter_sems(shards):
    most = max(fetch_parts(shard.shape[0]) for shard in shards)
    return [pltpu.SemaphoreType.DMA((len(shards), 4, most))] * 2


def gathered_shape(shard):
    return jax.ShapeDtypeStruct((shard.shape[0], 2 * shard.shape[1]), shard.dtype)


def fetch_first(shards, smalls, wides, frames, jobs, low_shapes, collective_id):
    counts = (len(shards), len(smalls), len(wides), len(low_shapes))
    out_shape = tuple(gathered_shape(array) for array in (*shards, *smalls))
    gathered = len(out_shape)
    out_shape += tuple(pltpu.HBM(shape, LOW) for shape in low_shapes)
    out_shape += (jax.ShapeDtypeStruct(frames.shape, LOW),)
    return pl.pallas_call(
        functools.partial(fetch_kernel, counts, jobs),
        out_shape=out_shape,
        in_specs=in_vmem(len(shards) + len(smalls)) + [pl.BlockSpec(memory_space=pl.ANY)] * (len(wides) + 1),
        out_specs=tuple(
            in_vmem(gathered) + [pl.BlockSpec(memory_space=pltpu.HBM)] * len(low_shapes) + in_vmem(1)
        ),
        scratch_shapes=[pltpu.VMEM(wides[job[0]].shape[1:], WIDE) for job in jobs]
        + [pltpu.VMEM(frames.shape, WIDE)]
        + [pltpu.VMEM(shape, LOW) for shape in low_shapes]
        + [pltpu.SemaphoreType.DMA((len(low_shapes),)), pltpu.SemaphoreType.DMA((len(jobs) + 1,))]
        + quarter_sems(shards)
        + [pltpu.SemaphoreType.DMA((len(smalls),))] * 2,
        compiler_params=pltpu.CompilerParams(
            collective_id=collective_id, has_side_effects=True, vmem_limit_bytes=40 << 20
        ),
        name="fetch_first",
    )(*shards, *smalls, *wides, frames)


def forward_exchange(partial, residual, bias, gain, shift, n, collective_id, shard=None):
    rows, width = partial.shape
    out_shape = (
        jax.ShapeDtypeStruct((rows, width), LOW),
        jax.ShapeDtypeStruct(residual.shape, WIDE),
    )
    scratch = exchange_scratch(n, rows, width, PIECES)
    kernel, extra = forward_exchange_kernel, ()
    if shard is not None:
        out_shape += (gathered_shape(shard),)
        scratch = scratch + quarter_sems((shard,))
        kernel, extra = forward_fetch_kernel, (shard,)
    return pl.pallas_call(
        functools.partial(kernel, n, PIECES),
        out_shape=out_shape,
        in_specs=in_vmem(5 + len(extra)),
        out_specs=tuple(in_vmem(len(out_shape))),
        scratch_shapes=scratch,
        compiler_params=pltpu.CompilerParams(
            collective_id=collective_id, has_side_effects=True, vmem_limit_bytes=12 << 20
        ),
        name="forward_exchange",
    )(partial, residual, bias[None, :], gain[None, :], shift[None, :], *extra)


def backward_exchange(partial, grad_out, normal_in, gain, n, collective_id, arrays=(), by_column=()):
    rows, width = partial.shape
    out_shape = (
        jax.ShapeDtypeStruct((rows, width), LOW),
        jax.ShapeDtypeStruct(grad_out.shape, WIDE),
        jax.ShapeDtypeStruct((8, width), WIDE),
    )
    scratch = exchange_scratch(n, rows, width, PIECES)
    kernel, extra = backward_exchange_kernel, ()
    if arrays:
        outs, landings, sems = gradient_shapes(arrays, by_column)
        out_shape = out_shape + outs
        scratch = scratch + landings + sems
        kernel, extra = functools.partial(backward_gradient_kernel, by_column), arrays
    return pl.pallas_call(
        functools.partial(kernel, n, PIECES),
        out_shape=out_shape,
        in_specs=in_vmem(4 + len(extra)),
        out_specs=tuple(in_vmem(3) + [pl.BlockSpec(memory_space=pltpu.HBM)] * len(extra)),
        scratch_shapes=scratch,
        compiler_params=pltpu.CompilerParams(
            collective_id=collective_id, has_side_effects=True, vmem_limit_bytes=20 << 20
        ),
        name="backward_exchange",
    )(partial, grad_out, normal_in, gain[None, :], *extra)


GROUPS = 2
PARTS = 2 * GROUPS


def part_rows(columns, part, base=0):
    size = columns // GROUPS
    return pl.ds(base + (part % 2) * columns + (part // 2) * size, size)


def group_parts(group):
    return (2 * group, 2 * group + 1)


def group_heads(heads, group):
    assert heads % GROUPS == 0
    size = heads // GROUPS
    return range(heads) if group is None else range(group * size, (group + 1) * size)


def attend_kernel(scale, length, qkv, out, out_wide, log_total, held, high, low_sum, sems_send, sems_recv):
    columns = qkv.shape[0] // 3
    frames = qkv.shape[1]
    heads = columns // HD
    me = lax.axis_index("ctx")

    def partner(r):
        return {"ctx": jnp.bitwise_xor(me, r)}

    barrier = pltpu.get_barrier_semaphore()
    for r in (1, 2):
        pl.semaphore_signal(barrier, inc=1, device_id=partner(r), device_id_type=MESH)
    pl.semaphore_wait(barrier, 2)

    def send(slot, part, to):
        rows, own_rows = part_rows(columns, part), part_rows(columns, part, columns)
        src = qkv.at[own_rows] if slot != 3 else held.at[1, rows]
        return pltpu.make_async_remote_copy(
            src_ref=src,
            dst_ref=held.at[slot - 1, rows],
            send_sem=sems_send.at[slot - 1, part],
            recv_sem=sems_recv.at[slot - 1, part],
            device_id=partner(to),
            device_id_type=MESH,
        )

    for part in range(PARTS):
        send(2, part, 2).start()
    for part in range(PARTS):
        send(1, part, 1).start()

    high[...] = jnp.full_like(high, NEGATIVE)
    low_sum[...] = jnp.zeros_like(low_sum)
    out_wide[...] = jnp.zeros_like(out_wide)
    limit = length[0]

    def block(keys_ref, key_row, value_row, slot, group=None):
        owner = jnp.bitwise_xor(me, slot)
        left = limit - owner * frames
        valid = lax.broadcasted_iota(jnp.int32, (frames, frames), 0) < left
        for h in group_heads(heads, group):
            rows = pl.ds(h * HD, HD)
            keys = keys_ref[pl.ds(key_row + h * HD, HD), :]
            values = keys_ref[pl.ds(value_row + h * HD, HD), :]
            scores = lax.dot_general(
                keys, qkv[rows, :], (((0,), (0,)), ((), ())), preferred_element_type=WIDE
            )
            scores = jnp.where(valid, scores * scale, NEGATIVE)
            before = high[h : h + 1, :]
            now = jnp.maximum(before, jnp.max(scores, axis=0, keepdims=True))
            shrink = jnp.exp(before - now)
            raised = jnp.exp(scores - now)
            low_sum[h : h + 1, :] = low_sum[h : h + 1, :] * shrink + jnp.sum(
                raised, axis=0, keepdims=True
            )
            high[h : h + 1, :] = now
            out_wide[rows, :] = out_wide[rows, :] * shrink + jnp.dot(
                values, raised.astype(LOW), preferred_element_type=WIDE
            )

    block(qkv, columns, 2 * columns, 0)
    for part in range(PARTS):
        send(1, part, 1).wait_recv()
    block(held.at[0], 0, columns, 1)
    for group in range(GROUPS):
        for part in group_parts(group):
            send(2, part, 2).wait_recv()
            send(3, part, 1).start()
        block(held.at[1], 0, columns, 2, group)
    for group in range(GROUPS):
        for part in group_parts(group):
            send(3, part, 1).wait_recv()
        block(held.at[2], 0, columns, 3, group)
    for h in range(heads):
        rows = pl.ds(h * HD, HD)
        total = low_sum[h : h + 1, :]
        done = out_wide[rows, :] / total
        out_wide[rows, :] = done
        out[rows, :] = done.astype(LOW)
        log_total[h : h + 1, :] = high[h : h + 1, :] + jnp.log(total)
    for slot in (1, 2, 3):
        for part in range(PARTS):
            send(slot, part, 2 if slot == 2 else 1).wait_send()


def attend(qkv, length, scale, collective_id):
    columns, frames = qkv.shape[0] // 3, qkv.shape[1]
    return pl.pallas_call(
        functools.partial(attend_kernel, scale),
        out_shape=(
            jax.ShapeDtypeStruct((columns, frames), LOW),
            jax.ShapeDtypeStruct((columns, frames), WIDE),
            jax.ShapeDtypeStruct((8, frames), WIDE),
            jax.ShapeDtypeStruct((3, 2 * columns, frames), LOW),
        ),
        in_specs=[pl.BlockSpec(memory_space=pltpu.SMEM)] + in_vmem(1),
        out_specs=tuple(in_vmem(4)),
        scratch_shapes=[
            pltpu.VMEM((8, frames), WIDE),
            pltpu.VMEM((8, frames), WIDE),
            pltpu.SemaphoreType.DMA((3, PARTS)),
            pltpu.SemaphoreType.DMA((3, PARTS)),
        ],
        compiler_params=pltpu.CompilerParams(
            collective_id=collective_id, has_side_effects=True, vmem_limit_bytes=16 << 20
        ),
        name="attend",
    )(length, qkv)


class LineGather:
    def __init__(self, own, gathered, sends, recvs):
        self.own, self.gathered, self.sends, self.recvs = own, gathered, sends, recvs
        self.n = gathered.shape[0] // own.shape[0]
        self.me = lax.axis_index("tp")
        self.further = (self.me < self.n - 1, self.me > 0)
        self.peers = ({"tp": lax.rem(self.me + 1, self.n)}, {"tp": lax.rem(self.me + self.n - 1, self.n)})

    def greet(self, barrier):
        for way in range(2):

            @pl.when(self.further[way])
            def _():
                pl.semaphore_signal(barrier, inc=1, device_id=self.peers[way], device_id_type=MESH)

        return self.further[0].astype(jnp.int32) + self.further[1].astype(jnp.int32)

    def rows(self, shard):
        size = self.own.shape[0]
        return pl.ds(pl.multiple_of(shard * size, size), size)

    def there(self, way, hops):
        return self.me - hops >= 0 if way == 0 else self.me + hops <= self.n - 1

    def send(self, way, hops):
        shard = self.me - hops if way == 0 else self.me + hops
        rows = self.rows(shard)
        return pltpu.make_async_remote_copy(
            src_ref=self.own if hops == 0 else self.gathered.at[rows],
            dst_ref=self.gathered.at[rows],
            send_sem=self.sends.at[way, hops],
            recv_sem=self.recvs.at[way, hops],
            device_id=self.peers[way],
            device_id_type=MESH,
        )

    def arrival(self, way, hops):
        rows = self.rows(self.me - hops if way == 0 else self.me + hops)
        return pltpu.make_async_remote_copy(
            src_ref=self.gathered.at[rows],
            dst_ref=self.gathered.at[rows],
            send_sem=self.sends.at[way, hops],
            recv_sem=self.recvs.at[way, hops - 1],
            device_id=self.peers[way],
            device_id_type=MESH,
        )

    def hop(self, hops):
        for way in range(2):
            if hops > 0:

                @pl.when(self.there(way, hops))
                def _():
                    self.arrival(way, hops).wait_recv()

            if hops < self.n - 1:

                @pl.when(self.there(way, hops) & self.further[way])
                def _():
                    self.send(way, hops).start()

    def drain(self):
        for hops in range(self.n - 1):
            for way in range(2):

                @pl.when(self.there(way, hops) & self.further[way])
                def _():
                    self.send(way, hops).wait_send()


def attend_back_kernel(scale, sharing, length, qkv, held, grad, out_wide, log_total, *refs):
    if sharing:
        own, grad_qkv, gathered, mine, parts, landed, acc, sems_send, sems_recv, sends, recvs = refs
        share = LineGather(own, gathered, sends, recvs)
    else:
        grad_qkv, mine, parts, landed, acc, sems_send, sems_recv = refs
        share = None
    columns = qkv.shape[0] // 3
    frames = qkv.shape[1]
    heads = columns // HD
    me = lax.axis_index("ctx")

    def partner(r):
        return {"ctx": jnp.bitwise_xor(me, r)}

    barrier = pltpu.get_barrier_semaphore()
    for r in (1, 2):
        pl.semaphore_signal(barrier, inc=1, device_id=partner(r), device_id_type=MESH)
    waiting = 2
    if share is not None:
        waiting = waiting + share.greet(barrier)
    pl.semaphore_wait(barrier, waiting)
    if share is not None:
        share.hop(0)
        gathered[share.rows(share.me), :] = own[...]

    def send(at, part, to):
        rows = part_rows(columns, part)
        return pltpu.make_async_remote_copy(
            src_ref=parts.at[at, rows],
            dst_ref=landed.at[at, rows],
            send_sem=sems_send.at[at, part],
            recv_sem=sems_recv.at[at, part],
            device_id=partner(to),
            device_id_type=MESH,
        )

    acc[...] = jnp.zeros_like(acc)
    limit = length[0]

    def block(keys_ref, key_row, value_row, slot, store, group=None):
        owner = jnp.bitwise_xor(me, slot)
        left = limit - owner * frames
        valid = lax.broadcasted_iota(jnp.int32, (frames, frames), 0) < left
        for h in group_heads(heads, group):
            rows = pl.ds(h * HD, HD)
            keys = keys_ref[pl.ds(key_row + h * HD, HD), :]
            values = keys_ref[pl.ds(value_row + h * HD, HD), :]
            queries = qkv[rows, :]
            upstream = grad[rows, :]
            scores = lax.dot_general(
                keys, queries, (((0,), (0,)), ((), ())), preferred_element_type=WIDE
            )
            weights = jnp.where(valid, jnp.exp(scores * scale - log_total[h : h + 1, :]), 0.0)
            grad_weights = lax.dot_general(
                values, upstream, (((0,), (0,)), ((), ())), preferred_element_type=WIDE
            )
            row_terms = jnp.sum(
                upstream.astype(WIDE) * out_wide[rows, :], axis=0, keepdims=True
            )
            grad_scores = (weights * (grad_weights - row_terms)).astype(LOW)
            acc[rows, :] += jnp.dot(keys, grad_scores, preferred_element_type=WIDE)
            grad_keys = (
                lax.dot_general(
                    queries, grad_scores, (((1,), (1,)), ((), ())), preferred_element_type=WIDE
                )
                * scale
            )
            grad_values = lax.dot_general(
                upstream, weights.astype(LOW), (((1,), (1,)), ((), ())), preferred_element_type=WIDE
            )
            store(h * HD, grad_keys, grad_values)

    def store_part(at):
        def store(row, grad_keys, grad_values):
            parts[at, pl.ds(row, HD), :] = grad_keys.astype(LOW)
            parts[at, pl.ds(columns + row, HD), :] = grad_values.astype(LOW)

        return store

    def store_mine(row, grad_keys, grad_values):
        mine[pl.ds(row, HD), :] = grad_keys
        mine[pl.ds(columns + row, HD), :] = grad_values

    def store_joined(row, grad_keys, grad_values):
        for start, value in ((row, grad_keys), (columns + row, grad_values)):
            rows = pl.ds(start, HD)
            parts[1, rows, :] = (value + landed[0, rows, :].astype(WIDE)).astype(LOW)

    for group in range(GROUPS):
        block(held.at[2], 0, columns, 3, store_part(0), group)
        for part in group_parts(group):
            send(0, part, 1).start()
    for group in range(GROUPS):
        for part in group_parts(group):
            send(0, part, 1).wait_recv()
        block(held.at[1], 0, columns, 2, store_joined, group)
        for part in group_parts(group):
            send(1, part, 2).start()
        if share is not None and group == 0:
            share.hop(1)
    for group in range(GROUPS):
        block(held.at[0], 0, columns, 1, store_part(2), group)
        for part in group_parts(group):
            send(2, part, 1).start()
        if share is not None and group == 0:
            share.hop(2)
    block(qkv, columns, 2 * columns, 0, store_mine)
    grad_qkv[0:columns, :] = (acc[...] * scale).astype(LOW)
    for part in range(PARTS):
        send(2, part, 1).wait_recv()
    for part in range(PARTS):
        send(1, part, 2).wait_recv()
    grad_qkv[columns:, :] = (
        mine[...] + landed[1].astype(WIDE) + landed[2].astype(WIDE)
    ).astype(LOW)
    for at in range(3):
        for part in range(PARTS):
            send(at, part, 2 if at == 1 else 1).wait_send()
    if share is not None:
        for hops in range(3, share.n):
            share.hop(hops)
        share.drain()


def attend_back(qkv, held, grad, out_wide, log_total, length, scale, collective_id, own=None):
    columns, frames = qkv.shape[0] // 3, qkv.shape[1]
    out_shape = (jax.ShapeDtypeStruct((3 * columns, frames), LOW),)
    extra, sems = (), []
    if own is not None:
        n = lax.axis_size("tp")
        assert n >= 3
        out_shape += (jax.ShapeDtypeStruct((n * own.shape[0], own.shape[1]), LOW),)
        extra, sems = (own,), [pltpu.SemaphoreType.DMA((2, n))] * 2
    return pl.pallas_call(
        functools.partial(attend_back_kernel, scale, own is not None),
        out_shape=out_shape,
        in_specs=[pl.BlockSpec(memory_space=pltpu.SMEM)] + in_vmem(5 + len(extra)),
        out_specs=tuple(in_vmem(len(out_shape))),
        scratch_shapes=[
            pltpu.VMEM((2 * columns, frames), WIDE),
            pltpu.VMEM((3, 2 * columns, frames), LOW),
            pltpu.VMEM((3, 2 * columns, frames), LOW),
            pltpu.VMEM((columns, frames), WIDE),
            pltpu.SemaphoreType.DMA((3, PARTS)),
            pltpu.SemaphoreType.DMA((3, PARTS)),
            *sems,
        ],
        compiler_params=pltpu.CompilerParams(
            collective_id=collective_id, has_side_effects=True, vmem_limit_bytes=18 << 20
        ),
        name="attend_back",
    )(length, qkv, held, grad, out_wide, log_total, *extra)


def gelu_value(values):
    return 0.5 * values * (1.0 + lax.erf(values * ROOT_HALF))


def gelu_slope(values):
    return 0.5 * (1.0 + lax.erf(values * ROOT_HALF)) + values * DENSITY * jnp.exp(
        -0.5 * values * values
    )


def product(left_side, right_side, left_axis, right_axis):
    return lax.dot_general(
        left_side,
        right_side,
        (((left_axis,), (right_axis,)), ((), ())),
        preferred_element_type=WIDE,
    )


def per_device(
    hidden,
    cotangent,
    lengths,
    query_weight,
    key_weight,
    value_weight,
    output_weight,
    inner_weight,
    outer_weight,
    query_bias,
    value_bias,
    inner_bias,
    output_bias,
    outer_bias,
    first_gain,
    first_shift,
    second_gain,
    second_shift,
):
    clip_count, rows, width = hidden.shape
    assert clip_count == 1
    assert lax.axis_size("ctx") == 4
    tp_size = lax.axis_size("tp")
    own_rows = rows // tp_size
    columns = query_weight.shape[2]
    hidden_local = inner_weight.shape[2]
    scale = 1.0 / math.sqrt(HD)
    own_start = lax.axis_index("tp") * own_rows

    def own_slice(full):
        return lax.dynamic_slice_in_dim(full, own_start, own_rows, axis=0)

    hidden_rows = hidden.reshape(rows, width)
    smalls = (output_bias, outer_bias, first_gain, first_shift, second_gain, second_shift)
    qkv_weights = [jnp.swapaxes(weight, 1, 2) for weight in (query_weight, key_weight, value_weight)]

    def qkv_shard(layer):
        return jnp.concatenate([weight[layer] for weight in qkv_weights], axis=0).astype(LOW)

    def gather(array, axis):
        return lax.all_gather(array, "fsdp", axis=axis, tiled=True)

    projections = output_weight.astype(LOW).reshape(-1, output_weight.shape[2])
    paired = lax.axis_size("fsdp") == 2
    if paired:
        wides = (inner_weight, outer_weight, *qkv_weights)
        jobs = [(which, layer, which * LAYERS + layer, 0) for layer in range(LAYERS) for which in range(2)]
        shapes = [wide.shape[1:] for wide in wides[:2] for _ in range(LAYERS)]
        for layer in range(1, LAYERS):
            jobs += [(2 + at, layer, len(shapes), at * columns) for at in range(3)]
            shapes.append((3 * columns, qkv_weights[0].shape[2]))
        wides += (cotangent,)
        jobs.append((len(wides) - 1, 0, len(shapes), 0))
        shapes.append(cotangent.shape[1:])
        results = fetch_first((qkv_shard(0), projections), smalls, wides, hidden_rows, tuple(jobs), shapes, 17)
        qkv_first, projections, *results, normed = results
        smalls, lows = results[: len(smalls)], results[len(smalls) :]
        *lows, grad_low = lows
        inner_low, outer_low, qkv_low = lows[:LAYERS], lows[LAYERS : 2 * LAYERS], [None, *lows[2 * LAYERS :]]
    else:
        qkv_first, projections = gather(qkv_shard(0), 1), gather(projections, 1)
        smalls = [gather(small, 1) for small in smalls]
        inner_low, outer_low = inner_weight.astype(LOW), outer_weight.astype(LOW)
        qkv_low = [qkv_shard(layer) for layer in range(LAYERS)]
        grad_low = cotangent.reshape(rows, width).astype(LOW)
        smalls = [lax.reduce_precision(small, 8, 7) for small in smalls]
        hat_full, _ = norm_parts(hidden_rows)
        normed = (hat_full * smalls[FIRST_GAIN][0] + smalls[FIRST_SHIFT][0]).astype(LOW)
    projections = projections.reshape(LAYERS, columns, width)

    def vector(kind, layer):
        return smalls[kind][layer]

    w_qkvs = [qkv_first] + [gather(qkv_low[layer], 1) for layer in range(1, LAYERS)]
    w_inners = [gather(inner_low[layer], 0) for layer in range(LAYERS)]
    carried = paired and tp_size == 4
    w_outers = [None if carried and layer == 0 else gather(outer_low[layer], 1) for layer in range(LAYERS)]

    residual = own_slice(hidden_rows)
    kept = []
    for layer in range(LAYERS):
        w_qkv, w_out, w_inner = w_qkvs[layer], projections[layer], w_inners[layer]
        bias_qkv = jnp.concatenate(
            [query_bias[layer], jnp.zeros_like(query_bias[layer]), value_bias[layer]]
        )
        qkv = (product(w_qkv, normed, 1, 1) + bias_qkv[:, None]).astype(LOW)
        attended, attended_wide, log_total, held = attend(qkv, lengths, scale, 2 * layer)
        branch = product(attended, w_out, 0, 0).astype(LOW)
        normed_two, middle, *fetched = forward_exchange(
            branch,
            residual,
            vector(0, layer),
            vector(4, layer),
            vector(5, layer),
            tp_size,
            2 * layer + 4,
            outer_low[layer] if carried and layer == 0 else None,
        )
        if fetched:
            w_outers[layer] = fetched[0]
        inner_pre = product(normed_two, w_inner, 1, 0) + inner_bias[layer]
        active, slope = gelu_value(inner_pre).astype(LOW), gelu_slope(inner_pre)
        kept.append(
            (residual, normed, qkv, attended, attended_wide, log_total, held, middle, normed_two, slope, active)
        )
        branch = product(active, w_outers[layer], 1, 0).astype(LOW)
        if layer + 1 < LAYERS:
            normed, residual = forward_exchange(
                branch,
                middle,
                vector(1, layer),
                vector(2, layer + 1),
                vector(3, layer + 1),
                tp_size,
                2 * layer + 5,
            )
        else:
            last_branch, last_middle = branch, middle

    def exchange_back(branch, grad_out, normal_in, gain, collective_id, arrays, by_column):
        if lax.axis_size("fsdp") == 2:
            return backward_exchange(
                branch, grad_out, normal_in, gain, tp_size, collective_id, arrays, by_column
            )
        result = backward_exchange(branch, grad_out, normal_in, gain, tp_size, collective_id)
        for array, column in zip(arrays, by_column):
            axis = 1 if column else 0
            array = lax.psum_scatter(array, ("fsdp", "ctx"), scatter_dimension=axis, tiled=True)
            result += (lax.all_gather(array, "ctx", axis=axis, tiled=True),)
        return result

    grad_rows = cotangent.reshape(rows, width)
    grad_own = own_slice(grad_rows)
    outer_bias_sum = jnp.sum(grad_own, axis=0)
    grads = [None] * LAYERS
    vectors = [None] * LAYERS
    biases = [None] * LAYERS
    for layer in reversed(range(LAYERS)):
        w_qkv, w_out, w_inner, w_outer = w_qkvs[layer], projections[layer], w_inners[layer], w_outers[layer]
        (
            residual,
            normed,
            qkv,
            attended,
            attended_wide,
            log_total,
            held,
            middle,
            normed_two,
            slope,
            active,
        ) = kept[layer]
        grad_active = product(grad_low, w_outer, 1, 1)
        grad_inner = (grad_active * slope).astype(LOW)
        branch = product(grad_inner, w_inner, 1, 1).astype(LOW)
        grad_outer_w = product(active, grad_low, 0, 0).astype(LOW)
        grad_inner_w = product(normed_two, grad_inner, 0, 0).astype(LOW)
        grad_mid_low, grad_middle, sums_two, *summed_two = exchange_back(
            branch, grad_own, middle, vector(4, layer), 2 * layer + 8, (grad_inner_w, grad_outer_w), (False, True)
        )
        if layer == LAYERS - 1:
            last_branch, grad_mid_low = lax.optimization_barrier((last_branch, grad_mid_low))
            last_branch = lax.psum_scatter(last_branch, "tp", scatter_dimension=0, tiled=True)
        grad_attended = product(w_out, grad_mid_low, 1, 1).astype(LOW)
        grad_qkv, *shared = attend_back(
            qkv,
            held,
            grad_attended,
            attended_wide,
            log_total,
            lengths,
            scale,
            2 * layer + 12,
            last_rows if layer == 0 else None,
        )
        grad_output_w = product(attended, grad_mid_low, 1, 0).astype(LOW)
        branch = product(grad_qkv, w_qkv, 0, 0).astype(LOW)
        grad_qkv_w = product(grad_qkv, normed, 1, 0).astype(LOW)
        if layer == LAYERS - 1:
            last_branch, branch = lax.optimization_barrier((last_branch, branch))
            last_rows = (last_middle + last_branch.astype(WIDE) + vector(1, layer)).astype(LOW)
        if layer == 0:
            output = shared[0].astype(WIDE)
        grad_low, grad_own, sums_one, *summed_one = exchange_back(
            branch, grad_middle, residual, vector(2, layer), 2 * layer + 9, (grad_qkv_w, grad_output_w), (True, True)
        )
        grads[layer] = (*summed_one, *summed_two)
        vectors[layer] = [
            sums_two[2], outer_bias_sum, sums_one[0], sums_one[1], sums_two[0], sums_two[1]
        ]
        outer_bias_sum = sums_one[2]
        biases[layer] = jnp.concatenate(
            [
                jnp.sum(grad_qkv.astype(WIDE), axis=1),
                jnp.sum(grad_inner.astype(WIDE), axis=0),
            ]
        )
    grad_hidden = grad_low.astype(WIDE)

    shard = output_bias.shape[1]
    flat_biases = jnp.concatenate(biases)
    flat_biases = jnp.pad(flat_biases, (0, -flat_biases.size % (8 * shard))).reshape(-1, shard)
    vector_count = 6 * LAYERS
    small_sums = jnp.stack([row for parts in zip(*vectors) for row in parts])
    if lax.axis_size("fsdp") == 2:
        small_sums = jnp.pad(small_sums, ((0, -vector_count % 8), (0, 0)))
        shared_rows = small_sums.shape[0]
        small_sums = sum_all(
            small_sums, flat_biases, tuple((axis, lax.axis_size(axis)) for axis in ("ctx", "tp")), 16
        )
        vector_sums, bias_sums = small_sums[:vector_count], small_sums[shared_rows:]
    else:
        vector_sums = lax.psum(small_sums, ("fsdp", "ctx", "tp"))
        vector_sums = lax.dynamic_slice_in_dim(vector_sums, lax.axis_index("fsdp") * shard, shard, axis=1)
        bias_sums = lax.psum(flat_biases, ("fsdp", "ctx"))
    vector_sums = vector_sums.reshape(6, LAYERS, shard)
    bias_sums = bias_sums.reshape(-1)[: LAYERS * biases[0].size].reshape(LAYERS, -1)

    def stacked(which):
        return jnp.stack([grads[layer][which] for layer in range(LAYERS)]).astype(WIDE)

    def turned(start):
        return jnp.stack([grads[layer][0][start : start + columns].T for layer in range(LAYERS)]).astype(WIDE)

    return (
        output.reshape(hidden.shape),
        grad_hidden.reshape(hidden.shape),
        turned(0),
        turned(columns),
        turned(2 * columns),
        stacked(1),
        stacked(2),
        stacked(3),
        bias_sums[:, :columns],
        bias_sums[:, 2 * columns : 3 * columns],
        bias_sums[:, 3 * columns :],
        vector_sums[0],
        vector_sums[1],
        vector_sums[2],
        vector_sums[3],
        vector_sums[4],
        vector_sums[5],
    )


def solution(mesh):
    in_specs = (
        P("fsdp", "ctx", None),
        P("fsdp", "ctx", None),
        P("fsdp"),
        P(None, "fsdp", "tp"),
        P(None, "fsdp", "tp"),
        P(None, "fsdp", "tp"),
        P(None, "tp", "fsdp"),
        P(None, "fsdp", "tp"),
        P(None, "tp", "fsdp"),
        P(None, "tp"),
        P(None, "tp"),
        P(None, "tp"),
        P(None, "fsdp"),
        P(None, "fsdp"),
        P(None, "fsdp"),
        P(None, "fsdp"),
        P(None, "fsdp"),
        P(None, "fsdp"),
    )
    out_specs = (
        P("fsdp", "ctx", None),
        P("fsdp", "ctx", None),
        P(None, "fsdp", "tp"),
        P(None, "fsdp", "tp"),
        P(None, "fsdp", "tp"),
        P(None, "tp", "fsdp"),
        P(None, "fsdp", "tp"),
        P(None, "tp", "fsdp"),
        P(None, "tp"),
        P(None, "tp"),
        P(None, "tp"),
        P(None, "fsdp"),
        P(None, "fsdp"),
        P(None, "fsdp"),
        P(None, "fsdp"),
        P(None, "fsdp"),
        P(None, "fsdp"),
    )
    return jax.shard_map(
        per_device, mesh=mesh, in_specs=in_specs, out_specs=out_specs, check_vma=False
    )
```

```python
import functools
import math
import jax
import jax.numpy as jnp
from jax import lax
from jax.experimental import pallas as pl
from jax.experimental.pallas import tpu as pltpu
from jax.sharding import PartitionSpec as P

MESH = pl.DeviceIdType.MESH
LOW = jnp.bfloat16
WIDE = jnp.float32
EPSILON = 1e-05
NEGATIVE = -1e30
HD = 80
PIECES = 4
LAYERS = 2
ROOT_HALF = 1.0 / math.sqrt(2.0)
DENSITY = 1.0 / math.sqrt(2.0 * math.pi)
REDUCE_LAG = 2
GATHER_LAG = 2


def norm_parts(values):
    average = jnp.mean(values, axis=-1, keepdims=True)
    centered = values - average
    spread = jnp.mean(centered * centered, axis=-1, keepdims=True)
    inverse = lax.rsqrt(spread + EPSILON)
    return (centered * inverse, inverse)


def norm_back(upstream, normal_hat, inverse, gain_full):
    scaled = upstream * gain_full
    first_mean = jnp.mean(scaled, axis=-1, keepdims=True)
    second_mean = jnp.mean(scaled * normal_hat, axis=-1, keepdims=True)
    return inverse * (scaled - first_mean - normal_hat * second_mean)


def line_exchange(n, own, pieces, partial, gathered, from_left, from_right, total, sems, finish, side=None):
    rs_send, rs_recv, ag_send, ag_recv = sems
    me = lax.axis_index("tp")
    piece = own // pieces
    to_right, to_left = {"tp": lax.rem(me + 1, n)}, {"tp": lax.rem(me + n - 1, n)}
    has_left, has_right = me > 0, me < n - 1

    barrier = pltpu.get_barrier_semaphore()

    @pl.when(has_left)
    def _():
        pl.semaphore_signal(barrier, inc=1, device_id=to_left, device_id_type=MESH)

    @pl.when(has_right)
    def _():
        pl.semaphore_signal(barrier, inc=1, device_id=to_right, device_id_type=MESH)

    peers = has_left.astype(jnp.int32) + has_right.astype(jnp.int32)
    if side is not None:
        for peer in side.peers:
            pl.semaphore_signal(barrier, inc=1, device_id=peer, device_id_type=MESH)
        peers = peers + len(side.peers)
    pl.semaphore_wait(barrier, peers)
    if side is not None:
        side.start()

    def rows_of(shard, step):
        return pl.ds(pl.multiple_of(shard * own + step * piece, piece), piece)

    def reduce_copy(way, src, shard, step):
        rows = rows_of(shard, step)
        landing = from_left if way == 0 else from_right
        return pltpu.make_async_remote_copy(
            src_ref=src.at[rows],
            dst_ref=landing.at[rows],
            send_sem=rs_send.at[way, shard, step],
            recv_sem=rs_recv.at[way, shard, step],
            device_id=to_right if way == 0 else to_left,
            device_id_type=MESH,
        )

    def gather_copy(way, shard, step):
        rows = rows_of(shard, step)
        return pltpu.make_async_remote_copy(
            src_ref=gathered.at[rows],
            dst_ref=gathered.at[rows],
            send_sem=ag_send.at[way, shard, step],
            recv_sem=ag_recv.at[way, shard, step],
            device_id=to_right if way == 0 else to_left,
            device_id_type=MESH,
        )

    def reduce_one(way, shard, step):
        landing = from_left if way == 0 else from_right
        first = me == 0 if way == 0 else me == n - 1

        @pl.when(first)
        def _():
            reduce_copy(way, partial, shard, step).start()

        @pl.when(jnp.logical_not(first))
        def _():
            rows = rows_of(shard, step)
            reduce_copy(way, partial, shard, step).wait_recv()
            landing[rows, :] = (
                partial[rows, :].astype(WIDE) + landing[rows, :].astype(WIDE)
            ).astype(LOW)
            reduce_copy(way, landing, shard, step).start()

    def finish_one(step):
        rows = rows_of(me, step)
        total[...] = partial[rows, :].astype(WIDE)

        @pl.when(has_left)
        def _():
            reduce_copy(0, partial, me, step).wait_recv()
            total[...] += from_left[rows, :].astype(WIDE)

        @pl.when(has_right)
        def _():
            reduce_copy(1, partial, me, step).wait_recv()
            total[...] += from_right[rows, :].astype(WIDE)

        own_rows = pl.ds(pl.multiple_of(step * piece, piece), piece)
        gathered[rows, :] = finish(own_rows, total[...])

        @pl.when(has_right)
        def _():
            gather_copy(0, me, step).start()

        @pl.when(has_left)
        def _():
            gather_copy(1, me, step).start()

    def forward_one(way, shard, step):
        gather_copy(way, shard, step).wait_recv()

        @pl.when(has_right if way == 0 else has_left)
        def _():
            gather_copy(way, shard, step).start()

    period = n - 1

    def finish_at(device):
        from_start = jnp.where(device > 0, n - 1 - device + REDUCE_LAG * device, 0)
        from_end = jnp.where(device < n - 1, device + REDUCE_LAG * (n - 1 - device), 0)
        return jnp.maximum(from_start, from_end)

    def split(tick, start, length):
        since = tick - start
        clipped = jnp.maximum(since, 0)
        return (since >= 0) & (clipped < length), lax.div(clipped, period), lax.rem(clipped, period)

    def body(tick, carry):
        for way in range(2):
            hops = me if way == 0 else n - 1 - me
            due, step, k = split(tick, REDUCE_LAG * hops, pieces * period)
            shard = n - 1 - k if way == 0 else k
            mine = me < shard if way == 0 else me > shard

            @pl.when(due & mine)
            def _():
                reduce_one(way, shard, step)

        due, step, k = split(tick, finish_at(me), pieces * period)

        @pl.when(due & (k == 0))
        def _():
            finish_one(step)

        for hops in range(1, n):
            for way in range(2):
                shard = me - hops if way == 0 else me + hops
                there = shard >= 0 if way == 0 else shard <= n - 1
                due, step, k = split(
                    tick, finish_at(shard) + GATHER_LAG * hops, pieces * period
                )

                @pl.when(there & due & (k == 0))
                def _():
                    forward_one(way, shard, step)

        if side is not None:
            side.at(tick)
        return carry

    ticks = period * (pieces - 1) + max(REDUCE_LAG, 1) * (n - 1) + GATHER_LAG * (n - 1) + 1
    if side is not None:
        ticks = max(ticks, side.ticks)
    lax.fori_loop(0, ticks, body, 0)
    if side is not None:
        side.drain()

    def drain(step, carry):
        for k in range(n - 1):
            for way in range(2):
                shard = n - 1 - k if way == 0 else k
                sends = me < shard if way == 0 else me > shard

                @pl.when(sends)
                def _():
                    reduce_copy(way, partial, shard, step).wait_send()

        for k in range(n):
            for way in range(2):
                shard = me - k if way == 0 else me + k
                there = shard >= 0 if way == 0 else shard <= n - 1
                further = has_right if way == 0 else has_left

                @pl.when(there & further)
                def _():
                    gather_copy(way, shard, step).wait_send()

        return carry

    lax.fori_loop(0, pieces, drain, 0)


def exchange_scratch(n, rows, width, pieces):
    return [
        pltpu.VMEM((rows, width), LOW),
        pltpu.VMEM((rows, width), LOW),
        pltpu.VMEM((rows // n // pieces, width), WIDE),
        pltpu.SemaphoreType.DMA((2, n, pieces)),
        pltpu.SemaphoreType.DMA((2, n, pieces)),
        pltpu.SemaphoreType.DMA((2, n, pieces)),
        pltpu.SemaphoreType.DMA((2, n, pieces)),
    ]


def forward_fetch_kernel(
    n, pieces, partial, residual, bias, gain, shift, shard, gathered, middle, fetched, from_left, from_right, total,
    rs_send, rs_recv, ag_send, ag_recv, sends, recvs
):
    forward_exchange_kernel(
        n, pieces, partial, residual, bias, gain, shift, gathered, middle, from_left, from_right, total, rs_send, rs_recv,
        ag_send, ag_recv, side=QuartersSide((shard,), (fetched,), sends, recvs)
    )


def forward_exchange_kernel(
    n, pieces, partial, residual, bias, gain, shift, gathered, middle, from_left, from_right, total, *sems, side=None
):
    def finish(rows, value):
        mid = value + residual[rows, :] + bias[...]
        middle[rows, :] = mid
        hat, _ = norm_parts(mid)
        return (hat * gain[...] + shift[...]).astype(LOW)

    line_exchange(
        n, residual.shape[0], pieces, partial, gathered, from_left, from_right, total, sems, finish, side
    )


def backward_exchange_kernel(
    n, pieces, partial, grad_out, normal_in, gain, gathered, grad_in, sums, from_left, from_right, total, *sems, side=None
):
    sums[...] = jnp.zeros_like(sums)

    def finish(rows, upstream):
        hat, inverse = norm_parts(normal_in[rows, :])
        grad = grad_out[rows, :] + norm_back(upstream, hat, inverse, gain[...])
        grad_in[rows, :] = grad
        sums[0:1, :] += jnp.sum(upstream * hat, axis=0, keepdims=True)
        sums[1:2, :] += jnp.sum(upstream, axis=0, keepdims=True)
        sums[2:3, :] += jnp.sum(grad, axis=0, keepdims=True)
        return grad.astype(LOW)

    line_exchange(
        n, grad_out.shape[0], pieces, partial, gathered, from_left, from_right, total, sems, finish, side
    )


def in_vmem(count):
    return [pl.BlockSpec(memory_space=pltpu.VMEM)] * count


class GradientSum:
    LAGS = (0, 3, 6, 9)

    def __init__(self, by_column, arrays, outs, landings, sems):
        self.by_column = by_column
        self.chunks = landings[0].shape[1]
        self.arrays, self.outs, self.landings = arrays, outs, landings
        self.sends, self.recvs, self.stores = sems
        self.half = lax.axis_index("fsdp")
        self.ctx = lax.axis_index("ctx")
        self.core = lax.rem(self.ctx, 2)
        pair = {"ctx": jnp.bitwise_xor(self.ctx, 1)}
        across = {"ctx": jnp.bitwise_xor(self.ctx, 2)}
        other = {"fsdp": 1 - self.half}
        self.peers = (pair, across, other)
        self.ticks = 2 * (self.chunks - 1) + self.LAGS[3] + 1

    def view(self, which, half, core, chunk):
        rows, cols = self.arrays[which].shape
        if not self.by_column[which]:
            part = rows // 4
            height = part // self.chunks
            start = half * (2 * part) + core * part + chunk * height
            return pl.ds(pl.multiple_of(start, 16), height), slice(None)
        part = rows // 2
        height = part // self.chunks
        start = core * part + chunk * height
        width = cols // 2
        return (
            pl.ds(pl.multiple_of(start, 16), height),
            pl.ds(pl.multiple_of(half * width, 128), width),
        )

    def out_rows(self, which, core, chunk):
        part = self.outs[which].shape[0] // 2
        height = part // self.chunks
        return pl.ds(pl.multiple_of(core * part + chunk * height, 16), height)

    def store(self, which, whose, chunk):
        core = self.core if whose == 0 else 1 - self.core
        return pltpu.make_async_copy(
            self.landings[which].at[3 + whose, chunk],
            self.outs[which].at[self.out_rows(which, core, chunk)],
            self.stores.at[which, whose, chunk],
        )

    def copy(self, which, stage, chunk, half=0):
        pair, across, other = self.peers
        landing = self.landings[which]
        if stage == 0:
            src = self.arrays[which].at[self.view(which, half, 1 - self.core, chunk)]
            slot, peer = half, pair
        elif stage == 1:
            src = landing.at[1 - self.half, chunk]
            slot, peer = 2, other
        elif stage == 2:
            src = landing.at[2, chunk]
            slot, peer = 3, across
        else:
            src = landing.at[3, chunk]
            slot, peer = 4, pair
        return pltpu.make_async_remote_copy(
            src_ref=src,
            dst_ref=landing.at[slot, chunk],
            send_sem=self.sends.at[which, slot, chunk],
            recv_sem=self.recvs.at[which, slot, chunk],
            device_id=peer,
            device_id_type=MESH,
        )

    def start(self):
        def body(chunk, carry):
            for which in range(len(self.arrays)):
                for half in range(2):
                    self.copy(which, 0, chunk, half).start()
            return carry

        lax.fori_loop(0, self.chunks, body, 0)

    def when_due(self, tick, lag, action):
        since = tick - lag
        clipped = jnp.maximum(since, 0)
        chunk = lax.div(clipped, 2)

        @pl.when((since >= 0) & (lax.rem(clipped, 2) == 0) & (chunk < self.chunks))
        def _():
            for which in range(len(self.arrays)):
                action(which, chunk)

    def at(self, tick):
        def joined(which, chunk):
            landing = self.landings[which]
            for half in range(2):
                self.copy(which, 0, chunk, half).wait_recv()
                rows, cols = self.view(which, half, self.core, chunk)
                landing[half, chunk] = (
                    self.arrays[which][rows, cols].astype(WIDE) + landing[half, chunk].astype(WIDE)
                ).astype(LOW)
            self.copy(which, 1, chunk).start()

        def crossed(which, chunk):
            landing = self.landings[which]
            self.copy(which, 1, chunk).wait_recv()
            landing[2, chunk] = (
                landing[self.half, chunk].astype(WIDE) + landing[2, chunk].astype(WIDE)
            ).astype(LOW)
            self.copy(which, 2, chunk).start()

        def summed(which, chunk):
            landing = self.landings[which]
            self.copy(which, 2, chunk).wait_recv()
            low = (landing[2, chunk].astype(WIDE) + landing[3, chunk].astype(WIDE)).astype(LOW)
            landing[3, chunk] = low
            self.copy(which, 3, chunk).start()
            self.store(which, 0, chunk).start()

        def shared(which, chunk):
            self.copy(which, 3, chunk).wait_recv()
            self.store(which, 1, chunk).start()

        for lag, action in zip(self.LAGS, (joined, crossed, summed, shared)):
            self.when_due(tick, lag, action)

    def drain(self):
        def body(chunk, carry):
            for which in range(len(self.arrays)):
                for half in range(2):
                    self.copy(which, 0, chunk, half).wait_send()
                for stage in range(1, 4):
                    self.copy(which, stage, chunk).wait_send()
                for whose in range(2):
                    self.store(which, whose, chunk).wait()
            return carry

        lax.fori_loop(0, self.chunks, body, 0)


def gradient_shapes(arrays, by_column):
    chunks = 5 if all(by_column) else 10
    outs, landings = (), []
    for array, column in zip(arrays, by_column):
        rows, cols = array.shape
        rows, cols = (rows, cols // 2) if column else (rows // 2, cols)
        outs += (pltpu.HBM((rows, cols), LOW),)
        landings.append(pltpu.VMEM((5, chunks, rows // 2 // chunks, cols), LOW))
    sems = [pltpu.SemaphoreType.DMA((len(arrays), 5, chunks))] * 2
    return outs, landings, sems + [pltpu.SemaphoreType.DMA((len(arrays), 2, chunks))]


def backward_gradient_kernel(by_column, n, pieces, partial, grad_out, normal_in, gain, *refs):
    count = len(by_column)
    arrays, (gathered, grad_in, sums), refs = refs[:count], refs[count : count + 3], refs[count + 3 :]
    outs, (from_left, from_right, total, *sems), refs = refs[:count], refs[count : count + 7], refs[count + 7 :]
    side = GradientSum(by_column, arrays, outs, refs[:count], refs[count:])
    backward_exchange_kernel(
        n, pieces, partial, grad_out, normal_in, gain, gathered, grad_in, sums, from_left, from_right, total, *sems, side=side
    )


def sum_all_kernel(axes, vectors, biases, out, staged, landing, sends, recvs):
    half = lax.axis_index("fsdp")
    shared, width = vectors.shape[0], out.shape[1]
    steps = [("fsdp", 1)] + [(axis, 1 << b) for axis, size in axes for b in range(size.bit_length() - 1)]

    def peer(axis, k):
        return {axis: jnp.bitwise_xor(lax.axis_index(axis), k)}

    barrier = pltpu.get_barrier_semaphore()
    for axis, k in steps:
        pl.semaphore_signal(barrier, inc=1, device_id=peer(axis, k), device_id_type=MESH)
    for side in range(2):
        staged[side, 0:shared, :] = vectors[:, side * width : (side + 1) * width]
        staged[side, shared:, :] = biases[...]
    pl.semaphore_wait(barrier, len(steps))
    for at, (axis, k) in enumerate(steps):
        rows = pl.ds(0, shared) if axis == "tp" else pl.ds(0, out.shape[0])
        if at > 0:
            landing[at, 0, rows] = out[rows, :]
        copy = pltpu.make_async_remote_copy(
            src_ref=landing.at[at, 0, rows] if at > 0 else staged.at[1 - half],
            dst_ref=landing.at[at, 1, rows],
            send_sem=sends.at[at],
            recv_sem=recvs.at[at],
            device_id=peer(axis, k),
            device_id_type=MESH,
        )
        copy.start()
        copy.wait()
        own = landing[at, 0, rows] if at > 0 else staged[half]
        out[rows, :] = own + landing[at, 1, rows]


def sum_all(vectors, biases, axes, collective_id):
    shape = (vectors.shape[0] + biases.shape[0], biases.shape[1])
    steps = 1 + sum(size.bit_length() - 1 for _, size in axes)
    return pl.pallas_call(
        functools.partial(sum_all_kernel, axes),
        out_shape=jax.ShapeDtypeStruct(shape, WIDE),
        in_specs=in_vmem(2),
        out_specs=in_vmem(1)[0],
        scratch_shapes=[
            pltpu.VMEM((2,) + shape, WIDE),
            pltpu.VMEM((steps, 2) + shape, WIDE),
            pltpu.SemaphoreType.DMA((steps,)),
            pltpu.SemaphoreType.DMA((steps,)),
        ],
        compiler_params=pltpu.CompilerParams(
            collective_id=collective_id, has_side_effects=True, vmem_limit_bytes=8 << 20
        ),
        name="sum_all",
    )(vectors, biases)


def fetch_parts(rows):
    return next(parts for parts in (2, 3, 1) if rows // 4 % (16 * parts) == 0)


CAST_ROWS = 64
FIRST_GAIN, FIRST_SHIFT = 2, 3


class Quarters:
    def __init__(self, shards, outs, sends, recvs):
        self.shards, self.outs, self.sends, self.recvs = shards, outs, sends, recvs
        self.half = lax.axis_index("fsdp")
        self.ctx = lax.axis_index("ctx")
        self.pair, self.across = jnp.bitwise_xor(self.ctx, 1), jnp.bitwise_xor(self.ctx, 2)
        self.targets = ({"fsdp": 1 - self.half}, {"ctx": self.across}, {"ctx": self.pair}, {"ctx": self.pair})
        self.peers = self.targets[:3]
        self.each = [
            (which, part) for which in range(len(shards)) for part in range(fetch_parts(shards[which].shape[0]))
        ]

    def rows_of(self, which, quarter, part):
        parts = fetch_parts(self.shards[which].shape[0])
        height = self.shards[which].shape[0] // 4 // parts
        return pl.ds(pl.multiple_of((quarter * parts + part) * height, 16), height)

    def place(self, which, side, quarter, part):
        cols = self.shards[which].shape[1]
        return self.outs[which].at[
            self.rows_of(which, quarter, part), pl.ds(pl.multiple_of(side * cols, 128), cols)
        ]

    def copy(self, stage, item, arriving=False):
        which, part = item
        quarter = (self.ctx, self.ctx, self.ctx, self.across)[stage]
        src = self.shards[which].at[self.rows_of(which, quarter, part)]
        dst = self.place(which, self.half, quarter, part)
        if stage > 0:
            src = dst = self.place(which, 1 - self.half, quarter, part)
        if arriving:
            quarter = (self.ctx, self.across, self.pair, jnp.bitwise_xor(self.ctx, 3))[stage]
            dst = self.place(which, 1 - self.half, quarter, part)
        return pltpu.make_async_remote_copy(
            src_ref=src,
            dst_ref=dst,
            send_sem=self.sends.at[which, stage, part],
            recv_sem=self.recvs.at[which, stage, part],
            device_id=self.targets[stage],
            device_id_type=MESH,
        )

    def begin(self):
        for item in self.each:
            self.copy(0, item).start()

    def keep_own(self):
        for shard, out in zip(self.shards, self.outs):
            cols = shard.shape[1]
            out[:, pl.ds(pl.multiple_of(self.half * cols, 128), cols)] = shard[...]

    def crossed(self, item):
        self.copy(0, item, True).wait_recv()
        self.copy(1, item).start()
        self.copy(2, item).start()

    def forwarded(self, item):
        self.copy(1, item, True).wait_recv()
        self.copy(3, item).start()

    def finish(self):
        for stage in (2, 3):
            for item in self.each:
                self.copy(stage, item, True).wait_recv()
        for stage in range(4):
            for item in self.each:
                self.copy(stage, item).wait_send()


class QuartersSide(Quarters):
    CROSSED, APART, FORWARDED = 6, 5, 4

    def start(self):
        self.begin()
        self.keep_own()

    @property
    def ticks(self):
        return self.CROSSED + self.FORWARDED + self.APART * (len(self.each) - 1) + 1

    def at(self, tick):
        for at, item in enumerate(self.each):
            due = self.CROSSED + self.APART * at

            @pl.when(tick == due)
            def _():
                self.crossed(item)

            @pl.when(tick == due + self.FORWARDED)
            def _():
                self.forwarded(item)

    def drain(self):
        self.finish()


def fetch_kernel(counts, jobs, *refs):
    refs = list(refs)

    def take(count):
        taken = refs[:count]
        del refs[:count]
        return taken

    shard_count, small_count, wide_count, low_count = counts
    shards, smalls, wides, (frames,) = take(shard_count), take(small_count), take(wide_count), take(1)
    outs, out_smalls, lows, (normed,) = take(shard_count), take(small_count), take(low_count), take(1)
    buffers, (frame_buffer,), stages = take(len(jobs)), take(1), take(low_count)
    store_sems, cast_sems, sends, recvs, small_sends, small_recvs = refs
    quarters = Quarters(shards, outs, sends, recvs)

    barrier = pltpu.get_barrier_semaphore()
    for peer in quarters.peers:
        pl.semaphore_signal(barrier, inc=1, device_id=peer, device_id_type=MESH)
    pl.semaphore_wait(barrier, 3)

    def small_copy(at, side):
        cols = smalls[at].shape[1]
        return pltpu.make_async_remote_copy(
            src_ref=smalls[at],
            dst_ref=out_smalls[at].at[:, pl.ds(pl.multiple_of(side * cols, 128), cols)],
            send_sem=small_sends.at[at],
            recv_sem=small_recvs.at[at],
            device_id=quarters.peers[0],
            device_id_type=MESH,
        )

    def store(low):
        return pltpu.make_async_copy(stages[low], lows[low], store_sems.at[low])

    def load(at):
        which, layer, _, _ = jobs[at]
        return pltpu.make_async_copy(wides[which].at[layer], buffers[at], cast_sems.at[at])

    frame_load = pltpu.make_async_copy(frames, frame_buffer, cast_sems.at[len(jobs)])

    def norm(step, carry):
        rows = pl.ds(pl.multiple_of(step * CAST_ROWS, CAST_ROWS), CAST_ROWS)
        hat, _ = norm_parts(frame_buffer[rows, :])
        normed[rows, :] = (hat * out_smalls[FIRST_GAIN][0:1, :] + out_smalls[FIRST_SHIFT][0:1, :]).astype(LOW)
        return carry

    for at in range(small_count):
        small_copy(at, quarters.half).start()
    quarters.begin()
    for at in range(len(jobs)):
        load(at).start()
    frame_load.start()
    quarters.keep_own()
    for small, out in zip(smalls, out_smalls):
        cols = small.shape[1]
        out[:, pl.ds(pl.multiple_of(quarters.half * cols, 128), cols)] = small[...]
    for at, (_, _, low, first) in enumerate(jobs):
        load(at).wait()

        def cast(step, carry):
            start = pl.multiple_of(step * CAST_ROWS, CAST_ROWS)
            stages[low][pl.ds(first + start, CAST_ROWS), :] = buffers[at][pl.ds(start, CAST_ROWS), :].astype(LOW)
            return carry

        lax.fori_loop(0, buffers[at].shape[0] // CAST_ROWS, cast, 0)
        if first + buffers[at].shape[0] == lows[low].shape[0]:
            store(low).start()
    for at in range(small_count):
        small_copy(at, 1 - quarters.half).wait_recv()
        out_smalls[at][...] = out_smalls[at][...].astype(LOW).astype(WIDE)
    last = len(quarters.each)
    for at in range(last + 1):
        if at < last:
            quarters.crossed(quarters.each[at])
        if at > 0:
            quarters.forwarded(quarters.each[at - 1])
        if at == fetch_parts(shards[0].shape[0]):
            frame_load.wait()
            lax.fori_loop(0, normed.shape[0] // CAST_ROWS, norm, 0)
    quarters.finish()
    for at in range(small_count):
        small_copy(at, quarters.half).wait_send()
    for low in range(low_count):
        store(low).wait()


def quarter_sems(shards):
    most = max(fetch_parts(shard.shape[0]) for shard in shards)
    return [pltpu.SemaphoreType.DMA((len(shards), 4, most))] * 2


def gathered_shape(shard):
    return jax.ShapeDtypeStruct((shard.shape[0], 2 * shard.shape[1]), shard.dtype)


def fetch_first(shards, smalls, wides, frames, jobs, low_shapes, collective_id):
    counts = (len(shards), len(smalls), len(wides), len(low_shapes))
    out_shape = tuple(gathered_shape(array) for array in (*shards, *smalls))
    gathered = len(out_shape)
    out_shape += tuple(pltpu.HBM(shape, LOW) for shape in low_shapes)
    out_shape += (jax.ShapeDtypeStruct(frames.shape, LOW),)
    return pl.pallas_call(
        functools.partial(fetch_kernel, counts, jobs),
        out_shape=out_shape,
        in_specs=in_vmem(len(shards) + len(smalls)) + [pl.BlockSpec(memory_space=pl.ANY)] * (len(wides) + 1),
        out_specs=tuple(
            in_vmem(gathered) + [pl.BlockSpec(memory_space=pltpu.HBM)] * len(low_shapes) + in_vmem(1)
        ),
        scratch_shapes=[pltpu.VMEM(wides[job[0]].shape[1:], WIDE) for job in jobs]
        + [pltpu.VMEM(frames.shape, WIDE)]
        + [pltpu.VMEM(shape, LOW) for shape in low_shapes]
        + [pltpu.SemaphoreType.DMA((len(low_shapes),)), pltpu.SemaphoreType.DMA((len(jobs) + 1,))]
        + quarter_sems(shards)
        + [pltpu.SemaphoreType.DMA((len(smalls),))] * 2,
        compiler_params=pltpu.CompilerParams(
            collective_id=collective_id, has_side_effects=True, vmem_limit_bytes=40 << 20
        ),
        name="fetch_first",
    )(*shards, *smalls, *wides, frames)


def forward_exchange(partial, residual, bias, gain, shift, n, collective_id, shard=None):
    rows, width = partial.shape
    out_shape = (
        jax.ShapeDtypeStruct((rows, width), LOW),
        jax.ShapeDtypeStruct(residual.shape, WIDE),
    )
    scratch = exchange_scratch(n, rows, width, PIECES)
    kernel, extra = forward_exchange_kernel, ()
    if shard is not None:
        out_shape += (gathered_shape(shard),)
        scratch = scratch + quarter_sems((shard,))
        kernel, extra = forward_fetch_kernel, (shard,)
    return pl.pallas_call(
        functools.partial(kernel, n, PIECES),
        out_shape=out_shape,
        in_specs=in_vmem(5 + len(extra)),
        out_specs=tuple(in_vmem(len(out_shape))),
        scratch_shapes=scratch,
        compiler_params=pltpu.CompilerParams(
            collective_id=collective_id, has_side_effects=True, vmem_limit_bytes=12 << 20
        ),
        name="forward_exchange",
    )(partial, residual, bias[None, :], gain[None, :], shift[None, :], *extra)


def backward_exchange(partial, grad_out, normal_in, gain, n, collective_id, arrays=(), by_column=()):
    rows, width = partial.shape
    out_shape = (
        jax.ShapeDtypeStruct((rows, width), LOW),
        jax.ShapeDtypeStruct(grad_out.shape, WIDE),
        jax.ShapeDtypeStruct((8, width), WIDE),
    )
    scratch = exchange_scratch(n, rows, width, PIECES)
    kernel, extra = backward_exchange_kernel, ()
    if arrays:
        outs, landings, sems = gradient_shapes(arrays, by_column)
        out_shape = out_shape + outs
        scratch = scratch + landings + sems
        kernel, extra = functools.partial(backward_gradient_kernel, by_column), arrays
    return pl.pallas_call(
        functools.partial(kernel, n, PIECES),
        out_shape=out_shape,
        in_specs=in_vmem(4 + len(extra)),
        out_specs=tuple(in_vmem(3) + [pl.BlockSpec(memory_space=pltpu.HBM)] * len(extra)),
        scratch_shapes=scratch,
        compiler_params=pltpu.CompilerParams(
            collective_id=collective_id, has_side_effects=True, vmem_limit_bytes=20 << 20
        ),
        name="backward_exchange",
    )(partial, grad_out, normal_in, gain[None, :], *extra)


GROUPS = 2
PARTS = 2 * GROUPS


def part_rows(columns, part, base=0):
    size = columns // GROUPS
    return pl.ds(base + (part % 2) * columns + (part // 2) * size, size)


def group_parts(group):
    return (2 * group, 2 * group + 1)


def group_heads(heads, group):
    assert heads % GROUPS == 0
    size = heads // GROUPS
    return range(heads) if group is None else range(group * size, (group + 1) * size)


def attend_kernel(scale, length, qkv, out, out_wide, log_total, held, high, low_sum, sems_send, sems_recv):
    columns = qkv.shape[0] // 3
    frames = qkv.shape[1]
    heads = columns // HD
    me = lax.axis_index("ctx")

    def partner(r):
        return {"ctx": jnp.bitwise_xor(me, r)}

    barrier = pltpu.get_barrier_semaphore()
    for r in (1, 2):
        pl.semaphore_signal(barrier, inc=1, device_id=partner(r), device_id_type=MESH)
    pl.semaphore_wait(barrier, 2)

    def send(slot, part, to):
        rows, own_rows = part_rows(columns, part), part_rows(columns, part, columns)
        src = qkv.at[own_rows] if slot != 3 else held.at[1, rows]
        return pltpu.make_async_remote_copy(
            src_ref=src,
            dst_ref=held.at[slot - 1, rows],
            send_sem=sems_send.at[slot - 1, part],
            recv_sem=sems_recv.at[slot - 1, part],
            device_id=partner(to),
            device_id_type=MESH,
        )

    for part in range(PARTS):
        send(2, part, 2).start()
    for part in range(PARTS):
        send(1, part, 1).start()

    high[...] = jnp.full_like(high, NEGATIVE)
    low_sum[...] = jnp.zeros_like(low_sum)
    out_wide[...] = jnp.zeros_like(out_wide)
    limit = length[0]

    def block(keys_ref, key_row, value_row, slot, group=None):
        owner = jnp.bitwise_xor(me, slot)
        left = limit - owner * frames
        valid = lax.broadcasted_iota(jnp.int32, (frames, frames), 0) < left
        for h in group_heads(heads, group):
            rows = pl.ds(h * HD, HD)
            keys = keys_ref[pl.ds(key_row + h * HD, HD), :]
            values = keys_ref[pl.ds(value_row + h * HD, HD), :]
            scores = lax.dot_general(
                keys, qkv[rows, :], (((0,), (0,)), ((), ())), preferred_element_type=WIDE
            )
            scores = jnp.where(valid, scores * scale, NEGATIVE)
            before = high[h : h + 1, :]
            now = jnp.maximum(before, jnp.max(scores, axis=0, keepdims=True))
            shrink = jnp.exp(before - now)
            raised = jnp.exp(scores - now)
            low_sum[h : h + 1, :] = low_sum[h : h + 1, :] * shrink + jnp.sum(
                raised, axis=0, keepdims=True
            )
            high[h : h + 1, :] = now
            out_wide[rows, :] = out_wide[rows, :] * shrink + jnp.dot(
                values, raised.astype(LOW), preferred_element_type=WIDE
            )

    block(qkv, columns, 2 * columns, 0)
    for part in range(PARTS):
        send(1, part, 1).wait_recv()
    block(held.at[0], 0, columns, 1)
    for group in range(GROUPS):
        for part in group_parts(group):
            send(2, part, 2).wait_recv()
            send(3, part, 1).start()
        block(held.at[1], 0, columns, 2, group)
    for group in range(GROUPS):
        for part in group_parts(group):
            send(3, part, 1).wait_recv()
        block(held.at[2], 0, columns, 3, group)
    for h in range(heads):
        rows = pl.ds(h * HD, HD)
        total = low_sum[h : h + 1, :]
        done = out_wide[rows, :] / total
        out_wide[rows, :] = done
        out[rows, :] = done.astype(LOW)
        log_total[h : h + 1, :] = high[h : h + 1, :] + jnp.log(total)
    for slot in (1, 2, 3):
        for part in range(PARTS):
            send(slot, part, 2 if slot == 2 else 1).wait_send()


def attend(qkv, length, scale, collective_id):
    columns, frames = qkv.shape[0] // 3, qkv.shape[1]
    return pl.pallas_call(
        functools.partial(attend_kernel, scale),
        out_shape=(
            jax.ShapeDtypeStruct((columns, frames), LOW),
            jax.ShapeDtypeStruct((columns, frames), WIDE),
            jax.ShapeDtypeStruct((8, frames), WIDE),
            jax.ShapeDtypeStruct((3, 2 * columns, frames), LOW),
        ),
        in_specs=[pl.BlockSpec(memory_space=pltpu.SMEM)] + in_vmem(1),
        out_specs=tuple(in_vmem(4)),
        scratch_shapes=[
            pltpu.VMEM((8, frames), WIDE),
            pltpu.VMEM((8, frames), WIDE),
            pltpu.SemaphoreType.DMA((3, PARTS)),
            pltpu.SemaphoreType.DMA((3, PARTS)),
        ],
        compiler_params=pltpu.CompilerParams(
            collective_id=collective_id, has_side_effects=True, vmem_limit_bytes=16 << 20
        ),
        name="attend",
    )(length, qkv)


class LineGather:
    def __init__(self, own, gathered, sends, recvs):
        self.own, self.gathered, self.sends, self.recvs = own, gathered, sends, recvs
        self.n = gathered.shape[0] // own.shape[0]
        self.me = lax.axis_index("tp")
        self.further = (self.me < self.n - 1, self.me > 0)
        self.peers = ({"tp": lax.rem(self.me + 1, self.n)}, {"tp": lax.rem(self.me + self.n - 1, self.n)})

    def greet(self, barrier):
        for way in range(2):

            @pl.when(self.further[way])
            def _():
                pl.semaphore_signal(barrier, inc=1, device_id=self.peers[way], device_id_type=MESH)

        return self.further[0].astype(jnp.int32) + self.further[1].astype(jnp.int32)

    def rows(self, shard):
        size = self.own.shape[0]
        return pl.ds(pl.multiple_of(shard * size, size), size)

    def there(self, way, hops):
        return self.me - hops >= 0 if way == 0 else self.me + hops <= self.n - 1

    def send(self, way, hops):
        shard = self.me - hops if way == 0 else self.me + hops
        rows = self.rows(shard)
        return pltpu.make_async_remote_copy(
            src_ref=self.own if hops == 0 else self.gathered.at[rows],
            dst_ref=self.gathered.at[rows],
            send_sem=self.sends.at[way, hops],
            recv_sem=self.recvs.at[way, hops],
            device_id=self.peers[way],
            device_id_type=MESH,
        )

    def arrival(self, way, hops):
        rows = self.rows(self.me - hops if way == 0 else self.me + hops)
        return pltpu.make_async_remote_copy(
            src_ref=self.gathered.at[rows],
            dst_ref=self.gathered.at[rows],
            send_sem=self.sends.at[way, hops],
            recv_sem=self.recvs.at[way, hops - 1],
            device_id=self.peers[way],
            device_id_type=MESH,
        )

    def hop(self, hops):
        for way in range(2):
            if hops > 0:

                @pl.when(self.there(way, hops))
                def _():
                    self.arrival(way, hops).wait_recv()

            if hops < self.n - 1:

                @pl.when(self.there(way, hops) & self.further[way])
                def _():
                    self.send(way, hops).start()

    def drain(self):
        for hops in range(self.n - 1):
            for way in range(2):

                @pl.when(self.there(way, hops) & self.further[way])
                def _():
                    self.send(way, hops).wait_send()


def attend_back_kernel(scale, sharing, length, qkv, held, grad, out_wide, log_total, *refs):
    if sharing:
        own, grad_qkv, gathered, mine, parts, landed, acc, sems_send, sems_recv, sends, recvs = refs
        share = LineGather(own, gathered, sends, recvs)
    else:
        grad_qkv, mine, parts, landed, acc, sems_send, sems_recv = refs
        share = None
    columns = qkv.shape[0] // 3
    frames = qkv.shape[1]
    heads = columns // HD
    me = lax.axis_index("ctx")

    def partner(r):
        return {"ctx": jnp.bitwise_xor(me, r)}

    barrier = pltpu.get_barrier_semaphore()
    for r in (1, 2):
        pl.semaphore_signal(barrier, inc=1, device_id=partner(r), device_id_type=MESH)
    waiting = 2
    if share is not None:
        waiting = waiting + share.greet(barrier)
    pl.semaphore_wait(barrier, waiting)
    if share is not None:
        share.hop(0)
        gathered[share.rows(share.me), :] = own[...]

    def send(at, part, to):
        rows = part_rows(columns, part)
        return pltpu.make_async_remote_copy(
            src_ref=parts.at[at, rows],
            dst_ref=landed.at[at, rows],
            send_sem=sems_send.at[at, part],
            recv_sem=sems_recv.at[at, part],
            device_id=partner(to),
            device_id_type=MESH,
        )

    acc[...] = jnp.zeros_like(acc)
    limit = length[0]

    def block(keys_ref, key_row, value_row, slot, store, group=None):
        owner = jnp.bitwise_xor(me, slot)
        left = limit - owner * frames
        valid = lax.broadcasted_iota(jnp.int32, (frames, frames), 0) < left
        for h in group_heads(heads, group):
            rows = pl.ds(h * HD, HD)
            keys = keys_ref[pl.ds(key_row + h * HD, HD), :]
            values = keys_ref[pl.ds(value_row + h * HD, HD), :]
            queries = qkv[rows, :]
            upstream = grad[rows, :]
            scores = lax.dot_general(
                keys, queries, (((0,), (0,)), ((), ())), preferred_element_type=WIDE
            )
            weights = jnp.where(valid, jnp.exp(scores * scale - log_total[h : h + 1, :]), 0.0)
            grad_weights = lax.dot_general(
                values, upstream, (((0,), (0,)), ((), ())), preferred_element_type=WIDE
            )
            row_terms = jnp.sum(
                upstream.astype(WIDE) * out_wide[rows, :], axis=0, keepdims=True
            )
            grad_scores = (weights * (grad_weights - row_terms)).astype(LOW)
            acc[rows, :] += jnp.dot(keys, grad_scores, preferred_element_type=WIDE)
            grad_keys = (
                lax.dot_general(
                    queries, grad_scores, (((1,), (1,)), ((), ())), preferred_element_type=WIDE
                )
                * scale
            )
            grad_values = lax.dot_general(
                upstream, weights.astype(LOW), (((1,), (1,)), ((), ())), preferred_element_type=WIDE
            )
            store(h * HD, grad_keys, grad_values)

    def store_part(at):
        def store(row, grad_keys, grad_values):
            parts[at, pl.ds(row, HD), :] = grad_keys.astype(LOW)
            parts[at, pl.ds(columns + row, HD), :] = grad_values.astype(LOW)

        return store

    def store_mine(row, grad_keys, grad_values):
        mine[pl.ds(row, HD), :] = grad_keys
        mine[pl.ds(columns + row, HD), :] = grad_values

    def store_joined(row, grad_keys, grad_values):
        for start, value in ((row, grad_keys), (columns + row, grad_values)):
            rows = pl.ds(start, HD)
            parts[1, rows, :] = (value + landed[0, rows, :].astype(WIDE)).astype(LOW)

    for group in range(GROUPS):
        block(held.at[2], 0, columns, 3, store_part(0), group)
        for part in group_parts(group):
            send(0, part, 1).start()
    for group in range(GROUPS):
        for part in group_parts(group):
            send(0, part, 1).wait_recv()
        block(held.at[1], 0, columns, 2, store_joined, group)
        for part in group_parts(group):
            send(1, part, 2).start()
        if share is not None and group == 0:
            share.hop(1)
    for group in range(GROUPS):
        block(held.at[0], 0, columns, 1, store_part(2), group)
        for part in group_parts(group):
            send(2, part, 1).start()
        if share is not None and group == 0:
            share.hop(2)
    block(qkv, columns, 2 * columns, 0, store_mine)
    grad_qkv[0:columns, :] = (acc[...] * scale).astype(LOW)
    for part in range(PARTS):
        send(2, part, 1).wait_recv()
    for part in range(PARTS):
        send(1, part, 2).wait_recv()
    grad_qkv[columns:, :] = (
        mine[...] + landed[1].astype(WIDE) + landed[2].astype(WIDE)
    ).astype(LOW)
    for at in range(3):
        for part in range(PARTS):
            send(at, part, 2 if at == 1 else 1).wait_send()
    if share is not None:
        for hops in range(3, share.n):
            share.hop(hops)
        share.drain()


def attend_back(qkv, held, grad, out_wide, log_total, length, scale, collective_id, own=None):
    columns, frames = qkv.shape[0] // 3, qkv.shape[1]
    out_shape = (jax.ShapeDtypeStruct((3 * columns, frames), LOW),)
    extra, sems = (), []
    if own is not None:
        n = lax.axis_size("tp")
        assert n >= 3
        out_shape += (jax.ShapeDtypeStruct((n * own.shape[0], own.shape[1]), LOW),)
        extra, sems = (own,), [pltpu.SemaphoreType.DMA((2, n))] * 2
    return pl.pallas_call(
        functools.partial(attend_back_kernel, scale, own is not None),
        out_shape=out_shape,
        in_specs=[pl.BlockSpec(memory_space=pltpu.SMEM)] + in_vmem(5 + len(extra)),
        out_specs=tuple(in_vmem(len(out_shape))),
        scratch_shapes=[
            pltpu.VMEM((2 * columns, frames), WIDE),
            pltpu.VMEM((3, 2 * columns, frames), LOW),
            pltpu.VMEM((3, 2 * columns, frames), LOW),
            pltpu.VMEM((columns, frames), WIDE),
            pltpu.SemaphoreType.DMA((3, PARTS)),
            pltpu.SemaphoreType.DMA((3, PARTS)),
            *sems,
        ],
        compiler_params=pltpu.CompilerParams(
            collective_id=collective_id, has_side_effects=True, vmem_limit_bytes=18 << 20
        ),
        name="attend_back",
    )(length, qkv, held, grad, out_wide, log_total, *extra)


def gelu_value(values):
    return 0.5 * values * (1.0 + lax.erf(values * ROOT_HALF))


def gelu_slope(values):
    return 0.5 * (1.0 + lax.erf(values * ROOT_HALF)) + values * DENSITY * jnp.exp(
        -0.5 * values * values
    )


def product(left_side, right_side, left_axis, right_axis):
    return lax.dot_general(
        left_side,
        right_side,
        (((left_axis,), (right_axis,)), ((), ())),
        preferred_element_type=WIDE,
    )


def per_device(
    hidden,
    cotangent,
    lengths,
    query_weight,
    key_weight,
    value_weight,
    output_weight,
    inner_weight,
    outer_weight,
    query_bias,
    value_bias,
    inner_bias,
    output_bias,
    outer_bias,
    first_gain,
    first_shift,
    second_gain,
    second_shift,
):
    clip_count, rows, width = hidden.shape
    assert clip_count == 1
    assert lax.axis_size("ctx") == 4
    tp_size = lax.axis_size("tp")
    own_rows = rows // tp_size
    columns = query_weight.shape[2]
    hidden_local = inner_weight.shape[2]
    scale = 1.0 / math.sqrt(HD)
    own_start = lax.axis_index("tp") * own_rows

    def own_slice(full):
        return lax.dynamic_slice_in_dim(full, own_start, own_rows, axis=0)

    hidden_rows = hidden.reshape(rows, width)
    smalls = (output_bias, outer_bias, first_gain, first_shift, second_gain, second_shift)
    qkv_weights = [jnp.swapaxes(weight, 1, 2) for weight in (query_weight, key_weight, value_weight)]

    def qkv_shard(layer):
        return jnp.concatenate([weight[layer] for weight in qkv_weights], axis=0).astype(LOW)

    def gather(array, axis):
        return lax.all_gather(array, "fsdp", axis=axis, tiled=True)

    projections = output_weight.astype(LOW).reshape(-1, output_weight.shape[2])
    paired = lax.axis_size("fsdp") == 2
    if paired:
        wides = (inner_weight, outer_weight, *qkv_weights)
        jobs = [(which, layer, which * LAYERS + layer, 0) for layer in range(LAYERS) for which in range(2)]
        shapes = [wide.shape[1:] for wide in wides[:2] for _ in range(LAYERS)]
        for layer in range(1, LAYERS):
            jobs += [(2 + at, layer, len(shapes), at * columns) for at in range(3)]
            shapes.append((3 * columns, qkv_weights[0].shape[2]))
        wides += (cotangent,)
        jobs.append((len(wides) - 1, 0, len(shapes), 0))
        shapes.append(cotangent.shape[1:])
        results = fetch_first((qkv_shard(0), projections), smalls, wides, hidden_rows, tuple(jobs), shapes, 17)
        qkv_first, projections, *results, normed = results
        smalls, lows = results[: len(smalls)], results[len(smalls) :]
        *lows, grad_low = lows
        inner_low, outer_low, qkv_low = lows[:LAYERS], lows[LAYERS : 2 * LAYERS], [None, *lows[2 * LAYERS :]]
    else:
        qkv_first, projections = gather(qkv_shard(0), 1), gather(projections, 1)
        smalls = [gather(small, 1) for small in smalls]
        inner_low, outer_low = inner_weight.astype(LOW), outer_weight.astype(LOW)
        qkv_low = [qkv_shard(layer) for layer in range(LAYERS)]
        grad_low = cotangent.reshape(rows, width).astype(LOW)
        smalls = [lax.reduce_precision(small, 8, 7) for small in smalls]
        hat_full, _ = norm_parts(hidden_rows)
        normed = (hat_full * smalls[FIRST_GAIN][0] + smalls[FIRST_SHIFT][0]).astype(LOW)
    projections = projections.reshape(LAYERS, columns, width)

    def vector(kind, layer):
        return smalls[kind][layer]

    w_qkvs = [qkv_first] + [gather(qkv_low[layer], 1) for layer in range(1, LAYERS)]
    w_inners = [gather(inner_low[layer], 0) for layer in range(LAYERS)]
    carried = paired and tp_size == 4
    w_outers = [None if carried and layer == 0 else gather(outer_low[layer], 1) for layer in range(LAYERS)]

    residual = own_slice(hidden_rows)
    kept = []
    for layer in range(LAYERS):
        w_qkv, w_out, w_inner = w_qkvs[layer], projections[layer], w_inners[layer]
        bias_qkv = jnp.concatenate(
            [query_bias[layer], jnp.zeros_like(query_bias[layer]), value_bias[layer]]
        )
        qkv = (product(w_qkv, normed, 1, 1) + bias_qkv[:, None]).astype(LOW)
        attended, attended_wide, log_total, held = attend(qkv, lengths, scale, 2 * layer)
        branch = product(attended, w_out, 0, 0).astype(LOW)
        normed_two, middle, *fetched = forward_exchange(
            branch,
            residual,
            vector(0, layer),
            vector(4, layer),
            vector(5, layer),
            tp_size,
            2 * layer + 4,
            outer_low[layer] if carried and layer == 0 else None,
        )
        if fetched:
            w_outers[layer] = fetched[0]
        inner_pre = product(normed_two, w_inner, 1, 0) + inner_bias[layer]
        active, slope = gelu_value(inner_pre).astype(LOW), gelu_slope(inner_pre)
        kept.append(
            (residual, normed, qkv, attended, attended_wide, log_total, held, middle, normed_two, slope, active)
        )
        branch = product(active, w_outers[layer], 1, 0).astype(LOW)
        if layer + 1 < LAYERS:
            normed, residual = forward_exchange(
                branch,
                middle,
                vector(1, layer),
                vector(2, layer + 1),
                vector(3, layer + 1),
                tp_size,
                2 * layer + 5,
            )
        else:
            last_branch, last_middle = branch, middle

    def exchange_back(branch, grad_out, normal_in, gain, collective_id, arrays, by_column):
        if lax.axis_size("fsdp") == 2:
            return backward_exchange(
                branch, grad_out, normal_in, gain, tp_size, collective_id, arrays, by_column
            )
        result = backward_exchange(branch, grad_out, normal_in, gain, tp_size, collective_id)
        for array, column in zip(arrays, by_column):
            axis = 1 if column else 0
            array = lax.psum_scatter(array, ("fsdp", "ctx"), scatter_dimension=axis, tiled=True)
            result += (lax.all_gather(array, "ctx", axis=axis, tiled=True),)
        return result

    grad_rows = cotangent.reshape(rows, width)
    grad_own = own_slice(grad_rows)
    outer_bias_sum = jnp.sum(grad_own, axis=0)
    grads = [None] * LAYERS
    vectors = [None] * LAYERS
    biases = [None] * LAYERS
    for layer in reversed(range(LAYERS)):
        w_qkv, w_out, w_inner, w_outer = w_qkvs[layer], projections[layer], w_inners[layer], w_outers[layer]
        (
            residual,
            normed,
            qkv,
            attended,
            attended_wide,
            log_total,
            held,
            middle,
            normed_two,
            slope,
            active,
        ) = kept[layer]
        grad_active = product(grad_low, w_outer, 1, 1)
        grad_inner = (grad_active * slope).astype(LOW)
        branch = product(grad_inner, w_inner, 1, 1).astype(LOW)
        grad_outer_w = product(active, grad_low, 0, 0).astype(LOW)
        grad_inner_w = product(normed_two, grad_inner, 0, 0).astype(LOW)
        grad_mid_low, grad_middle, sums_two, *summed_two = exchange_back(
            branch, grad_own, middle, vector(4, layer), 2 * layer + 8, (grad_inner_w, grad_outer_w), (False, True)
        )
        if layer == LAYERS - 1:
            last_branch, grad_mid_low = lax.optimization_barrier((last_branch, grad_mid_low))
            last_branch = lax.psum_scatter(last_branch, "tp", scatter_dimension=0, tiled=True)
        grad_attended = product(w_out, grad_mid_low, 1, 1).astype(LOW)
        grad_qkv, *shared = attend_back(
            qkv,
            held,
            grad_attended,
            attended_wide,
            log_total,
            lengths,
            scale,
            2 * layer + 12,
            last_rows if layer == 0 else None,
        )
        grad_output_w = product(attended, grad_mid_low, 1, 0).astype(LOW)
        branch = product(grad_qkv, w_qkv, 0, 0).astype(LOW)
        grad_qkv_w = product(grad_qkv, normed, 1, 0).astype(LOW)
        if layer == LAYERS - 1:
            last_branch, branch = lax.optimization_barrier((last_branch, branch))
            last_rows = (last_middle + last_branch.astype(WIDE) + vector(1, layer)).astype(LOW)
        if layer == 0:
            output = shared[0].astype(WIDE)
        grad_low, grad_own, sums_one, *summed_one = exchange_back(
            branch, grad_middle, residual, vector(2, layer), 2 * layer + 9, (grad_qkv_w, grad_output_w), (True, True)
        )
        grads[layer] = (*summed_one, *summed_two)
        vectors[layer] = [
            sums_two[2], outer_bias_sum, sums_one[0], sums_one[1], sums_two[0], sums_two[1]
        ]
        outer_bias_sum = sums_one[2]
        biases[layer] = jnp.concatenate(
            [
                jnp.sum(grad_qkv.astype(WIDE), axis=1),
                jnp.sum(grad_inner.astype(WIDE), axis=0),
            ]
        )
    grad_hidden = grad_low.astype(WIDE)

    shard = output_bias.shape[1]
    flat_biases = jnp.concatenate(biases)
    flat_biases = jnp.pad(flat_biases, (0, -flat_biases.size % (8 * shard))).reshape(-1, shard)
    vector_count = 6 * LAYERS
    small_sums = jnp.stack([row for parts in zip(*vectors) for row in parts])
    if lax.axis_size("fsdp") == 2:
        small_sums = jnp.pad(small_sums, ((0, -vector_count % 8), (0, 0)))
        shared_rows = small_sums.shape[0]
        small_sums = sum_all(
            small_sums, flat_biases, tuple((axis, lax.axis_size(axis)) for axis in ("ctx", "tp")), 16
        )
        vector_sums, bias_sums = small_sums[:vector_count], small_sums[shared_rows:]
    else:
        vector_sums = lax.psum(small_sums, ("fsdp", "ctx", "tp"))
        vector_sums = lax.dynamic_slice_in_dim(vector_sums, lax.axis_index("fsdp") * shard, shard, axis=1)
        bias_sums = lax.psum(flat_biases, ("fsdp", "ctx"))
    vector_sums = vector_sums.reshape(6, LAYERS, shard)
    bias_sums = bias_sums.reshape(-1)[: LAYERS * biases[0].size].reshape(LAYERS, -1)

    def stacked(which):
        return jnp.stack([grads[layer][which] for layer in range(LAYERS)]).astype(WIDE)

    def turned(start):
        return jnp.stack([grads[layer][0][start : start + columns].T for layer in range(LAYERS)]).astype(WIDE)

    return (
        output.reshape(hidden.shape),
        grad_hidden.reshape(hidden.shape),
        turned(0),
        turned(columns),
        turned(2 * columns),
        stacked(1),
        stacked(2),
        stacked(3),
        bias_sums[:, :columns],
        bias_sums[:, 2 * columns : 3 * columns],
        bias_sums[:, 3 * columns :],
        vector_sums[0],
        vector_sums[1],
        vector_sums[2],
        vector_sums[3],
        vector_sums[4],
        vector_sums[5],
    )


def solution(mesh):
    in_specs = (
        P("fsdp", "ctx", None),
        P("fsdp", "ctx", None),
        P("fsdp"),
        P(None, "fsdp", "tp"),
        P(None, "fsdp", "tp"),
        P(None, "fsdp", "tp"),
        P(None, "tp", "fsdp"),
        P(None, "fsdp", "tp"),
        P(None, "tp", "fsdp"),
        P(None, "tp"),
        P(None, "tp"),
        P(None, "tp"),
        P(None, "fsdp"),
        P(None, "fsdp"),
        P(None, "fsdp"),
        P(None, "fsdp"),
        P(None, "fsdp"),
        P(None, "fsdp"),
    )
    out_specs = (
        P("fsdp", "ctx", None),
        P("fsdp", "ctx", None),
        P(None, "fsdp", "tp"),
        P(None, "fsdp", "tp"),
        P(None, "fsdp", "tp"),
        P(None, "tp", "fsdp"),
        P(None, "fsdp", "tp"),
        P(None, "tp", "fsdp"),
        P(None, "tp"),
        P(None, "tp"),
        P(None, "tp"),
        P(None, "fsdp"),
        P(None, "fsdp"),
        P(None, "fsdp"),
        P(None, "fsdp"),
        P(None, "fsdp"),
        P(None, "fsdp"),
    )
    return jax.shard_map(
        per_device, mesh=mesh, in_specs=in_specs, out_specs=out_specs, check_vma=False
    )
```
